32 devices in a mesh: dp: 8 (over y, x, core), tensor: 4 (over z).
Axes of the slice: x: 2, y: 2, z: 4, core: 2. Of those that a mesh axis runs over, the one named last changes fastest.
Arguments:
- hidden_in: bfloat16 [8192, 768], P(('dp', 'tensor')), may hold values from -6 to 6
- prev_logits: float32 [8192, 12], P('dp'), may hold values from -6 to 6
- routes: int32 [2, 8192, 2], P(None, 'dp'), may hold values from 0 to 11, all different within a row; in each aligned block of 1024 rows (0 to 1023, 1024 to 2047, ..., all dimensions but the last counted through in order) at most 256 rows name the same one
- span_starts: int32 [8, 2], P('dp'), may hold values from 0 to 768, as said below
- attn_norm: bfloat16 [2, 768], P(None, ('dp', 'tensor')), may hold values from 0.5 to 1.5
- qkv_weight: bfloat16 [2, 768, 3, 768], P(None, 'dp', None, 'tensor'), may hold values from -0.21875 to 0.21875
- out_weight: bfloat16 [2, 768, 768], P(None, 'tensor', 'dp'), may hold values from -0.875 to 0.875
- moe_norm: bfloat16 [2, 768], P(None, ('dp', 'tensor')), may hold values from 0.5 to 1.5
- router: bfloat16 [2, 768, 12], P(None, ('dp', 'tensor')), may hold values from -0.109375 to 0.109375
- gate_mix: bfloat16 [2, 12, 12], replicated, may hold values from -0.875 to 0.875
- const_vec: bfloat16 [2, 2, 768], P(None, None, ('dp', 'tensor')), may hold values from -6 to 6
- const_mix: bfloat16 [2, 2, 768, 2], P(None, None, ('dp', 'tensor')), may hold values from -0.21875 to 0.21875
- up_weight: bfloat16 [2, 8, 768, 2, 2048], P(None, None, 'dp', None, 'tensor'), may hold values from -0.21875 to 0.21875
- down_weight: bfloat16 [2, 8, 2048, 768], P(None, None, 'tensor', 'dp'), may hold values from -0.25 to 0.25
- out_grad: bfloat16 [8192, 768], P(('dp', 'tensor')), may hold values from -6 to 6
Outputs:
- hidden_out: float32 [8192, 768], P(('dp', 'tensor'))
- in_grad: float32 [8192, 768], P(('dp', 'tensor'))
- attn_norm_grad: float32 [2, 768], P(None, ('dp', 'tensor'))
- qkv_grad: float32 [2, 768, 3, 768], P(None, 'dp', None, 'tensor')
- out_weight_grad: float32 [2, 768, 768], P(None, 'tensor', 'dp')
- moe_norm_grad: float32 [2, 768], P(None, ('dp', 'tensor'))
- router_grad: float32 [2, 768, 12], P(None, ('dp', 'tensor'))
- gate_mix_grad: float32 [2, 12, 12], replicated
- const_vec_grad: float32 [2, 2, 768], P(None, None, ('dp', 'tensor'))
- const_mix_grad: float32 [2, 2, 768, 2], P(None, None, ('dp', 'tensor'))
- up_grad: float32 [2, 8, 768, 2, 2048], P(None, None, 'dp', None, 'tensor')
- down_grad: float32 [2, 8, 2048, 768], P(None, None, 'tensor', 'dp')
The draws below stay inside these ranges and needn't reach their ends.
Inputs may be any that keep to these rules, and one draw needn't show every extreme that they name: `routes`: numbers below 8 are feed-forward experts, 8 the zero expert, 9 the copy expert, 10 and 11 the constant experts. A token's two numbers differ, and in every layer no number is named by more than 256 tokens of one sequence. Span k of a sequence covers positions span_starts to span_starts + 255, all within positions k * 512 to (k + 1) * 512 - 1.
All inputs are finite; a program needn't handle non-finite values.
Results may differ from the reference program's by a relative error of at most 0.035.
Values may be sent and summed in bfloat16 or wider, within the bound.
A program may use at most 384 MiB of HBM per device.

```python
import math
import jax
import jax.numpy as jnp
import numpy as np
from jax import lax

D = 768
HEADS = 12
HEAD = 64
FF = 2048
EXPERTS = 8
NEXP = 12
TOPK = 2
LAYERS = 2
PIC = 256
NPIC = 2
SEQ_LEN = 1024
SEQS = 8
TOKENS = 8192
CAP = 256
QBLOCK = 512


def draw_span_starts(key, part):
    segment = SEQ_LEN // NPIC
    room = segment - PIC + 1
    offsets = jax.random.randint(key, (SEQS, NPIC), 0, room, dtype=jnp.int32)
    offsets = offsets.at[0, NPIC - 1].set(room - 1).at[SEQS - 1, 0].set(0)
    bases = jnp.arange(NPIC, dtype=jnp.int32) * segment
    return (bases[None, :] + offsets).astype(jnp.int32)


def block_scale(rng, shape, shards, smallest, top_value):
    def one(axis_at, blocks):
        steps = jax.random.uniform(jax.random.fold_in(jax.random.fold_in(rng, 6), axis_at), (blocks,), jnp.float32, smallest / len(shards), top_value / len(shards))
        return jnp.repeat(jnp.exp(steps), shape[axis_at] // blocks).reshape((-1,) + (1,) * (len(shape) - axis_at - 1))

    factor_of = one(*shards[0])
    for cut in shards[1:]:
        factor_of = factor_of * one(*cut)
    return factor_of


def shared_out(key, own, number, rows, count, top, bound, lean):
    ranking = jax.random.permutation(key, count)
    packed, ordinary = portions_of(count, rows * top, bound, lean, True), portions_of(count, rows * top, bound, lean, False)
    places = jnp.arange(count)

    def named(tallies, offset_by):
        used = int((tallies > 0).sum())
        fixed = max(1, used // 4)
        moved = fixed + (places - fixed + offset_by * (used - fixed)) % max(1, count - fixed)
        return jnp.zeros((count,), jnp.int32).at[ranking[jnp.where(places < fixed, places, moved)]].set(jnp.asarray(tallies, jnp.int32))

    tallies = jnp.where(number % 4 == 0, named(packed, number // 4), named(ordinary, number - number // 4 - 1))
    mixed = jax.random.permutation(jax.random.fold_in(own, 3), count)
    donor, receiver = mixed[0:count // 2 * 2:2], mixed[1:count // 2 * 2:2]
    slack = jnp.minimum(tallies[donor] - 1, bound - tallies[receiver]) // 2
    slack = jnp.where((donor == ranking[0]) | (receiver == ranking[0]) | (tallies[receiver] == 0), 0, jnp.maximum(slack, 0))
    moved = jax.random.randint(jax.random.fold_in(own, 4), (count // 2,), 0, 1 << 20) % (slack + 1)
    tallies = tallies.at[donor].add(-moved).at[receiver].add(moved)
    members = jnp.searchsorted(jnp.cumsum(tallies), jnp.arange(rows * top), side="right").astype(jnp.int32)
    table = members.reshape(top, rows).T
    table = table[jax.random.permutation(jax.random.fold_in(own, 1), rows)]
    offset_by = jax.random.randint(jax.random.fold_in(own, 2), (rows, 1), 0, top)
    return jnp.take_along_axis(table, (jnp.arange(top)[None, :] + offset_by) % top, axis=1)


def portions_of(count, total, reach, skew, full):
    portions = [(1 << 20) // math.isqrt(rank ** skew) + 1 for rank in range(1, count + 1)]
    largest = reach if full else min(reach, max(-(-total // count), total * portions[0] // sum(portions)))
    least = 1 if total - largest >= count - 1 else 0
    holding, surplus = [largest] + [least] * (count - 1), total - largest - least * (count - 1)
    while surplus > 0:
        free = [i for i in range(1, count) if holding[i] < largest] or [i for i in range(1, count) if holding[i] < reach]
        pool, budget = sum([portions[i] for i in free]), surplus
        for i in free:
            more = min(reach - holding[i], max(1, budget * portions[i] // pool), surplus)
            holding[i] = holding[i] + more
            surplus = surplus - more
    return np.array(holding)


def gaussian(rng, extent, deviation, reach, shards=(), kind=jnp.bfloat16):
    values = jax.random.normal(rng, extent, jnp.float32) * deviation
    if len(shards) > 0:
        values = block_scale(rng, extent, shards, -0.22, 0.18) * values
    return jnp.clip(values, min=-reach, max=reach).astype(kind)


def setup_inputs(seed: int = 0) -> dict:
    arg_keys = jax.random.split(jax.random.key(seed), 16)
    hidden_in = gaussian(arg_keys[0], (TOKENS, D), 1.0, 6.0, ((0, 32),))
    prev_logits = gaussian(arg_keys[1], (TOKENS, NEXP), 1.0, 6.0, ((0, 8),), jnp.float32)
    routes_keys = jax.random.split(jax.random.fold_in(arg_keys[2], 1), LAYERS * TOKENS // SEQ_LEN)
    routes_turns = jax.random.permutation(jax.random.fold_in(arg_keys[2], 3), LAYERS * TOKENS // SEQ_LEN)
    routes = jax.vmap(lambda own, number: shared_out(jax.random.fold_in(arg_keys[2], 2), own, number, SEQ_LEN, NEXP, TOPK, CAP, 1))(routes_keys, routes_turns).reshape((LAYERS, TOKENS, TOPK))
    span_starts = draw_span_starts(jax.random.fold_in(arg_keys[15], 71), 0)
    attn_norm = jnp.clip(1.0 + 0.1 * jax.random.normal(arg_keys[4], (LAYERS, D), jnp.float32), 0.5, 1.5).astype(jnp.bfloat16)
    qkv_weight = gaussian(arg_keys[5], (LAYERS, D, 3, D), D ** -0.5, 0.21875, ((1, 8), (3, 4)))
    out_weight = gaussian(arg_keys[6], (LAYERS, D, D), (D // 16) ** -0.5, 0.875, ((1, 4), (2, 8)))
    moe_norm = jnp.clip(1.0 + 0.1 * jax.random.normal(arg_keys[7], (LAYERS, D), jnp.float32), 0.5, 1.5).astype(jnp.bfloat16)
    router = gaussian(arg_keys[8], (LAYERS, D, NEXP), (4 * D) ** -0.5, 0.109375, ((1, 32),))
    gate_mix = gaussian(arg_keys[9], (LAYERS, NEXP, NEXP), (4 * NEXP) ** -0.5, 0.875)
    const_vec = gaussian(arg_keys[10], (LAYERS, 2, D), 1.0, 6.0, ((2, 32),))
    const_mix = gaussian(arg_keys[11], (LAYERS, 2, D, 2), D ** -0.5, 0.21875, ((2, 32),))
    up_weight = gaussian(arg_keys[12], (LAYERS, EXPERTS, D, 2, FF), D ** -0.5, 0.21875, ((2, 8), (4, 4)))
    down_weight = gaussian(arg_keys[13], (LAYERS, EXPERTS, FF, D), (FF // 4) ** -0.5, 0.25, ((2, 4), (3, 8)))
    out_grad = gaussian(arg_keys[14], (TOKENS, D), 1.0, 6.0, ((0, 32),))
    return dict(hidden_in=hidden_in, prev_logits=prev_logits, routes=routes, span_starts=span_starts, attn_norm=attn_norm, qkv_weight=qkv_weight, out_weight=out_weight, moe_norm=moe_norm, router=router, gate_mix=gate_mix, const_vec=const_vec, const_mix=const_mix, up_weight=up_weight, down_weight=down_weight, out_grad=out_grad)


@jax.custom_vjp
def low(v):
    return lax.optimization_barrier(v.astype(jnp.bfloat16)).astype(jnp.float32)

@jax.custom_vjp
def low_back(v):
    return v

def low_keep(v):
    return (low(v), None)

def low_pass(kept, grad):
    return (grad,)

def back_keep(v):
    return (v, None)

def back_low(kept, grad):
    return (low(grad),)
low.defvjp(low_keep, low_pass)
low_back.defvjp(back_keep, back_low)
EPS = 1e-06
HIGH = lax.Precision.HIGHEST

def rms_scale(values, gain):
    return values * lax.rsqrt(lax.optimization_barrier(jnp.mean(values * values, axis=-1, keepdims=True)) + EPS) * gain

def span_marks(starts):
    places = jnp.arange(SEQ_LEN, dtype=jnp.int32)
    inside = (places[:, None] >= starts[None, :]) & (places[:, None] < starts[None, :] + PIC)
    labels = jnp.arange(1, NPIC + 1, dtype=jnp.int32)
    return lax.optimization_barrier(jnp.sum(jnp.where(inside, labels[None, :], 0), axis=1, dtype=jnp.int32))

def allowed_keys(start_row, span_ids):
    places = jnp.arange(SEQ_LEN, dtype=jnp.int32)
    query_pos = start_row + jnp.arange(QBLOCK, dtype=jnp.int32)
    query_ids = lax.dynamic_slice_in_dim(span_ids, start_row, QBLOCK, 0)
    causal = places[None, :] <= query_pos[:, None]
    picture = (query_ids[:, None] == span_ids[None, :]) & (query_ids[:, None] > 0)
    return causal | picture

def attention(triple, span_ids):
    queries, key_rows, value_rows = (triple[0], triple[1], triple[2])
    factor = HEAD ** (-0.5)

    def one_block(block_at):
        start_row = block_at * QBLOCK
        block_q = lax.dynamic_slice_in_dim(queries, start_row, QBLOCK, 0)
        scores = low_back(jnp.einsum('qhe,khe->hqk', block_q, key_rows, precision=HIGH) * factor)
        scores = jnp.where(allowed_keys(start_row, span_ids)[None], scores, -1e+30)
        attn_probs = low(jax.nn.softmax(scores, axis=-1))
        return jnp.einsum('hqk,khe->qhe', attn_probs, value_rows, precision=HIGH)
    blocks = lax.map(jax.checkpoint(one_block), jnp.arange(SEQ_LEN // QBLOCK, dtype=jnp.int32))
    return blocks.reshape(SEQ_LEN, HEADS * HEAD)

def dispatch(route_ids):
    flat_ids = route_ids.reshape(-1)
    hit_table = (flat_ids[:, None] == jnp.arange(NEXP, dtype=jnp.int32)[None, :]).astype(jnp.int32)
    slots = lax.optimization_barrier(jnp.sum((jnp.cumsum(hit_table, axis=0, dtype=jnp.int32) - 1) * hit_table, axis=1, dtype=jnp.int32))
    is_ffn = flat_ids < EXPERTS
    target = jnp.where(is_ffn, flat_ids * CAP + slots, EXPERTS * CAP).astype(jnp.int32)
    pick_ids = jnp.arange(flat_ids.shape[0], dtype=jnp.int32)
    owner_ids = jnp.zeros((EXPERTS * CAP,), jnp.int32).at[target].set(pick_ids, mode='drop')
    return (is_ffn, target, owner_ids)

def layer_forward(hidden, previous, route_ids, span_ids, params):
    attn_gain, triple_w, w_out, moe_gain, w_router, w_mix, const_v, const_m, w_up, w_down = params
    normed = low(rms_scale(hidden, attn_gain))
    triple = jnp.einsum('sd,dcf->csf', normed, triple_w, precision=HIGH)
    triple = low_back(low(triple)).reshape(3, SEQ_LEN, HEADS, HEAD)
    attended = low_back(low(attention(triple, span_ids)))
    hidden = hidden + low_back(jnp.dot(attended, w_out, precision=HIGH))
    moe_in = low(rms_scale(hidden, moe_gain))
    logits = jnp.dot(moe_in, w_router, precision=HIGH) + jnp.dot(previous, w_mix, precision=HIGH)
    gate_pair = jax.nn.softmax(jnp.take_along_axis(logits, route_ids, axis=1), axis=1)
    is_ffn, target, owner_ids = dispatch(route_ids)
    expert_in = moe_in[owner_ids // 2].reshape(EXPERTS, CAP, D)
    gate_up = low_back(jnp.einsum('ecd,edgf->ecgf', expert_in, w_up, precision=HIGH))
    swiglu = low(jax.nn.silu(gate_up[:, :, 0]) * gate_up[:, :, 1])
    expert_rows = low_back(jnp.einsum('ecf,efd->ecd', swiglu, w_down, precision=HIGH)).reshape(EXPERTS * CAP, D)
    picked = expert_rows[jnp.where(is_ffn, target, 0)].reshape(SEQ_LEN, TOPK, D)
    ffn_gates = gate_pair * is_ffn.reshape(SEQ_LEN, TOPK)
    routed = low_back(lax.optimization_barrier(jnp.sum(ffn_gates[:, :, None] * picked, axis=1)))
    copy_gate = lax.optimization_barrier(jnp.sum(gate_pair * (route_ids == EXPERTS + 1), axis=1))
    side_sum = copy_gate[:, None] * moe_in
    for const_at in range(2):
        const_gate = lax.optimization_barrier(jnp.sum(gate_pair * (route_ids == EXPERTS + 2 + const_at), axis=1))
        const_alpha = jax.nn.softmax(jnp.dot(moe_in, const_m[const_at], precision=HIGH), axis=1)
        const_out = const_alpha[:, 0:1] * moe_in + const_alpha[:, 1:2] * const_v[const_at][None, :]
        side_sum = side_sum + const_gate[:, None] * const_out
    return (hidden + routed + side_sum, logits)

def reference(hidden_in, prev_logits, routes, span_starts, attn_norm, qkv_weight, out_weight, moe_norm, router, gate_mix, const_vec, const_mix, up_weight, down_weight, out_grad):
    params = tuple((item.astype(jnp.float32) for item in (attn_norm, qkv_weight, out_weight, moe_norm, router, gate_mix, const_vec, const_mix, up_weight, down_weight)))

    def forward(hidden, previous, route_pair, span_ids, weights):
        for layer_at in range(LAYERS):
            hidden, previous = layer_forward(hidden, previous, route_pair[layer_at], span_ids, tuple((item[layer_at] for item in weights)))
        return hidden
    seq_hidden = hidden_in.astype(jnp.float32).reshape(SEQS, SEQ_LEN, D)
    seq_prev = prev_logits.reshape(SEQS, SEQ_LEN, NEXP)
    seq_routes = jnp.transpose(routes.reshape(LAYERS, SEQS, SEQ_LEN, TOPK), (1, 0, 2, 3))
    seq_cot = out_grad.astype(jnp.float32).reshape(SEQS, SEQ_LEN, D)

    def per_sequence(totals, inputs):
        hidden, previous, route_pair, starts, cotangent = inputs
        span_ids = span_marks(starts)
        result, pullback = jax.vjp(lambda start_h, weights: forward(start_h, previous, route_pair, span_ids, weights), hidden, params)
        grad_h, grad_w = pullback(cotangent)
        totals = tuple((total_item + grad_item for total_item, grad_item in zip(totals, grad_w)))
        return (totals, (result, grad_h))
    zeros_w = tuple((jnp.zeros_like(item) for item in params))
    totals, outputs = lax.scan(per_sequence, zeros_w, (seq_hidden, seq_prev, seq_routes, span_starts, seq_cot))
    results, grads = outputs
    return (results.reshape(TOKENS, D), grads.reshape(TOKENS, D), totals[0], totals[1], totals[2], totals[3], totals[4], totals[5], totals[6], totals[7], totals[8], totals[9])
```

```python
import functools

import jax
import jax.numpy as jnp
from jax import lax
from jax.experimental import pallas as pl
from jax.experimental.pallas import tpu as pltpu
from jax.sharding import PartitionSpec as P

HEAD = 64
EXPERTS = 8
NEXP = 12
TOPK = 2
PIC = 256
LANES = 128

EPS = 1e-06
HIGH = lax.Precision.HIGHEST
MESH = pl.DeviceIdType.MESH
F32 = jnp.float32
BF16 = jnp.bfloat16
VMEM_SPEC = pl.BlockSpec(memory_space=pltpu.VMEM)
VMEM_LIMIT = 60 * 1024 * 1024


def dot(a, b):
    return jnp.dot(a, b, preferred_element_type=F32)


def dot_nt(a, b):
    return lax.dot_general(a, b, (((1,), (1,)), ((), ())), preferred_element_type=F32)


def dot_tn(a, b):
    return lax.dot_general(a, b, (((0,), (0,)), ((), ())), preferred_element_type=F32)


def everyone_kernel(count, inner, reduce, x_ref, out_ref, *scratch):
    if reduce:
        land, send_sems, recv_sems = scratch
    else:
        land, (send_sems, recv_sems) = out_ref, scratch
    me = lax.axis_index("dp") * inner + lax.axis_index("tensor")

    def place(other):
        return (lax.div(other, inner), lax.rem(other, inner))

    barrier = pltpu.get_barrier_semaphore()

    def greet(step, carry):
        other = lax.rem(me + step, count)
        pl.semaphore_signal(barrier, inc=1, device_id=place(other), device_id_type=MESH)
        return carry

    lax.fori_loop(1, count, greet, 0)
    pl.semaphore_wait(barrier, count - 1)

    def copy_to(other):
        return pltpu.make_async_remote_copy(
            src_ref=x_ref.at[other] if reduce else x_ref,
            dst_ref=land.at[me],
            send_sem=send_sems.at[other],
            recv_sem=recv_sems.at[me],
            device_id=place(other),
            device_id_type=MESH,
        )

    def send(step, carry):
        copy_to(lax.rem(me + step, count)).start()
        return carry

    lax.fori_loop(1, count, send, 0)
    land[me] = x_ref[me] if reduce else x_ref[...]

    def finish(step, carry):
        other = lax.rem(me + count - step, count)
        pltpu.make_async_remote_copy(
            src_ref=x_ref.at[other] if reduce else x_ref,
            dst_ref=land.at[other],
            send_sem=send_sems.at[other],
            recv_sem=recv_sems.at[other],
            device_id=place(other),
            device_id_type=MESH,
        ).wait()
        return carry

    lax.fori_loop(1, count, finish, 0)
    if reduce:
        out_ref[...] = jnp.sum(land[...], axis=0)


def everyone(values, reduce, collective_id):
    inner = lax.axis_size("tensor")
    count = lax.axis_size("dp") * inner
    tail = values.shape[1:] if reduce else values.shape
    scratch = [pltpu.SemaphoreType.DMA((count,)), pltpu.SemaphoreType.DMA((count,))]
    if reduce:
        scratch = [pltpu.VMEM((count,) + tail, values.dtype)] + scratch
    return pl.pallas_call(
        functools.partial(everyone_kernel, count, inner, reduce),
        out_shape=jax.ShapeDtypeStruct(tail if reduce else (count,) + tail, values.dtype),
        in_specs=[VMEM_SPEC],
        out_specs=VMEM_SPEC,
        scratch_shapes=scratch,
        compiler_params=pltpu.CompilerParams(
            collective_id=collective_id, has_side_effects=True, vmem_limit_bytes=VMEM_LIMIT
        ),
        name="everyone",
    )(values)


def normed(values, gain):
    return values * lax.rsqrt(jnp.mean(values * values, axis=-1, keepdims=True) + EPS) * gain


def line_kernel(kind, nt, chunks, extra, *refs):
    refs = list(refs)
    has_sum = kind != "start"
    has_gather = kind != "end"
    part = refs.pop(0) if has_sum else None
    if kind == "start":
        x_ref, gain_ref = refs.pop(0), refs.pop(0)
    elif kind == "fwd":
        extra_ref, gain_ref = refs.pop(0), refs.pop(0)
    elif kind == "last":
        extra_ref, og_ref = refs.pop(0), refs.pop(0)
    else:
        extra_ref = refs.pop(0) if extra else None
        base_ref, skip_ref, gain_ref = refs.pop(0), refs.pop(0), refs.pop(0)
    own_ref = refs.pop(0) if has_sum else None
    gg_ref = refs.pop(0) if kind in ("bwd", "end") else None
    all_ref = refs.pop(0) if has_gather else None
    if has_sum:
        from_left, from_right, tx, acc, rs_send, rl_sem, rr_sem = refs[:7]
        refs = refs[7:]
    if has_gather:
        ag_right, ag_left, ag_recv = refs[:3]

    me = lax.axis_index("tensor")
    has_l, has_r = me > 0, me < nt - 1
    left, right = jnp.maximum(me - 1, 0), jnp.minimum(me + 1, nt - 1)

    barrier = pltpu.get_barrier_semaphore()

    @pl.when(has_l)
    def _():
        pl.semaphore_signal(barrier, inc=1, device_id={"tensor": left}, device_id_type=MESH)

    @pl.when(has_r)
    def _():
        pl.semaphore_signal(barrier, inc=1, device_id={"tensor": right}, device_id_type=MESH)

    pl.semaphore_wait(barrier, has_l.astype(jnp.int32) + has_r.astype(jnp.int32))

    def copy(src, dst, send_sem, recv_sem, to):
        return pltpu.make_async_remote_copy(
            src_ref=src,
            dst_ref=dst,
            send_sem=send_sem,
            recv_sem=recv_sem,
            device_id={"tensor": to},
            device_id_type=MESH,
        )

    def sum_right(j, c, src):
        return copy(src, from_left.at[j, c], rs_send.at[j, c], rl_sem.at[j, c], right)

    def sum_left(j, c, src):
        return copy(src, from_right.at[j, c], rs_send.at[j, c], rr_sem.at[j, c], left)

    def spread_right(j, c):
        block = all_ref.at[j, c]
        return copy(block, block, ag_right.at[j, c], ag_recv.at[j, c], right)

    def spread_left(j, c):
        block = all_ref.at[j, c]
        return copy(block, block, ag_left.at[j, c], ag_recv.at[j, c], left)

    def offer(c):
        @pl.when(has_r)
        def _():
            spread_right(me, c).start()

        @pl.when(has_l)
        def _():
            spread_left(me, c).start()

    def pass_on(c, d):
        @pl.when(me - d >= 0)
        def _():
            j = me - d
            spread_right(j, c).wait_recv()

            @pl.when(has_r)
            def _():
                spread_right(j, c).start()

        @pl.when(me + d < nt)
        def _():
            j = me + d
            spread_left(j, c).wait_recv()

            @pl.when(has_l)
            def _():
                spread_left(j, c).start()

    def relay(c, t):
        j_up, j_down = nt - 1 - t, t

        @pl.when(has_l & (me < j_up))
        def _():
            sum_right(j_up, c, tx.at[j_up, c]).wait_recv()
            tx[j_up, c] = (part[j_up, c].astype(F32) + from_left[j_up, c].astype(F32)).astype(BF16)
            sum_right(j_up, c, tx.at[j_up, c]).start()

        @pl.when(has_r & (me > j_down))
        def _():
            sum_left(j_down, c, tx.at[j_down, c]).wait_recv()
            tx[j_down, c] = (
                part[j_down, c].astype(F32) + from_right[j_down, c].astype(F32)
            ).astype(BF16)
            sum_left(j_down, c, tx.at[j_down, c]).start()

    def own_rows(c):
        acc[...] = part[me, c].astype(F32)

        @pl.when(has_l)
        def _():
            sum_right(me, c, tx.at[me, c]).wait_recv()
            acc[...] += from_left[me, c].astype(F32)

        @pl.when(has_r)
        def _():
            sum_left(me, c, tx.at[me, c]).wait_recv()
            acc[...] += from_right[me, c].astype(F32)

        total = acc[...]
        if kind == "fwd":
            total = total + extra_ref[c]
            all_ref[me, c] = normed(total, gain_ref[...]).astype(BF16)
            own_ref[c] = total
        elif kind == "last":
            own_ref[c] = total + extra_ref[c]
        else:
            if extra:
                total = total + extra_ref[c]
            base = base_ref[c]
            scale = lax.rsqrt(jnp.mean(base * base, axis=-1, keepdims=True) + EPS)
            unit = base * scale
            grad_unit = total * gain_ref[...]
            below = scale * (grad_unit - unit * jnp.mean(grad_unit * unit, axis=-1, keepdims=True))
            result = below + skip_ref[c]
            if has_gather:
                all_ref[me, c] = result.astype(BF16)
            own_ref[c] = result
            gg = jnp.sum(total * unit, axis=0, keepdims=True)
            if c == 0:
                gg_ref[...] = gg
            else:
                gg_ref[...] += gg
        if kind in ("fwd", "bwd"):
            offer(c)

    if kind == "start":
        for c in range(chunks):
            all_ref[me, c] = normed(x_ref[c].astype(F32), gain_ref[...]).astype(BF16)
            offer(c)
        for c in range(chunks):
            for d in range(1, nt):
                pass_on(c, d)
    else:

        @pl.when(jnp.logical_not(has_l))
        def _():
            for c in range(chunks):
                for j in range(nt - 1, 0, -1):
                    sum_right(j, c, part.at[j, c]).start()

        @pl.when(jnp.logical_not(has_r))
        def _():
            for c in range(chunks):
                for j in range(nt - 1):
                    sum_left(j, c, part.at[j, c]).start()

        if kind == "last":
            for c in range(chunks):
                all_ref[me, c] = og_ref[c]
            for c in range(chunks):
                offer(c)
        for c in range(chunks + (1 if has_gather and kind != "last" else 0)):
            for t in range(nt - 1):
                if c < chunks:
                    relay(c, t)
                if kind == "last":
                    pass_on(c, t + 1)
                elif has_gather and c >= 1:
                    pass_on(c - 1, t + 1)
            if c < chunks:
                own_rows(c)

    for c in range(chunks):
        for j in range(nt):
            if has_sum:

                @pl.when(me < j)
                def _():
                    sum_right(j, c, tx.at[j, c]).wait_send()

                @pl.when(me > j)
                def _():
                    sum_left(j, c, tx.at[j, c]).wait_send()

            if has_gather:

                @pl.when(has_r & (j <= me))
                def _():
                    spread_right(j, c).wait_send()

                @pl.when(has_l & (j >= me))
                def _():
                    spread_left(j, c).wait_send()


def line_exchange(kind, args, rows, width, collective_id, extra=False, chunks=2):
    nt = lax.axis_size("tensor")
    has_sum = kind != "start"
    has_gather = kind != "end"
    piece = rows // chunks
    split = []
    for item in args:
        if item.shape[0] == nt * rows:
            split.append(item.reshape(nt, chunks, piece, width))
        elif item.shape[0] == rows:
            split.append(item.reshape(chunks, piece, width))
        else:
            split.append(item)
    outs = []
    if has_sum:
        outs.append(jax.ShapeDtypeStruct((chunks, piece, width), F32))
    if kind in ("bwd", "end"):
        outs.append(jax.ShapeDtypeStruct((1, width), F32))
    if has_gather:
        outs.append(jax.ShapeDtypeStruct((nt, chunks, piece, width), BF16))
    scratch = []
    sems = pltpu.SemaphoreType.DMA((nt, chunks))
    if has_sum:
        buf = pltpu.VMEM((nt, chunks, piece, width), BF16)
        scratch += [buf, buf, buf, pltpu.VMEM((piece, width), F32), sems, sems, sems]
    if has_gather:
        scratch += [sems, sems, sems]
    results = pl.pallas_call(
        functools.partial(line_kernel, kind, nt, chunks, extra),
        out_shape=outs,
        in_specs=[VMEM_SPEC] * len(split),
        out_specs=[VMEM_SPEC] * len(outs),
        scratch_shapes=scratch,
        compiler_params=pltpu.CompilerParams(
            collective_id=collective_id, has_side_effects=True, vmem_limit_bytes=VMEM_LIMIT
        ),
        cost_estimate=pl.CostEstimate(
            flops=10 * nt * rows * width, bytes_accessed=100 * rows * width * nt, transcendentals=0
        ),
        name="line_" + kind,
    )(*split)
    results = list(results)
    if has_sum:
        results[0] = results[0].reshape(rows, width)
    if has_gather:
        results[-1] = results[-1].reshape(nt * rows, width)
    return results


def span_mask(starts_ref, row_at, rows, cols, spans):
    row = row_at + lax.broadcasted_iota(jnp.int32, (rows, cols), 0)
    col = lax.broadcasted_iota(jnp.int32, (rows, cols), 1)
    seen = col <= row
    for k in range(spans):
        begin = starts_ref[0, k]
        seen = seen | (
            (row >= begin) & (row < begin + PIC) & (col >= begin) & (col < begin + PIC)
        )
    return seen


def key_extent(row_at, seq_len, spans):
    segment = seq_len // spans
    return (row_at // segment + 1) * segment


def attend_kernel(heads, spans, block, starts_ref, a_ref, w_ref, qkv_ref, o_ref, lse_ref, out_ref):
    seq_len = a_ref.shape[0]
    wide = heads * HEAD
    factor = HEAD ** (-0.5)
    qkv_ref[...] = dot(a_ref[...], w_ref[:, : 3 * wide]).astype(BF16)
    for at in range(0, seq_len, block):
        reach = key_extent(at, seq_len, spans)
        seen = span_mask(starts_ref, at, block, reach, spans)
        for h in range(heads):
            q = qkv_ref[at : at + block, h * HEAD : (h + 1) * HEAD]
            k = qkv_ref[:reach, wide + h * HEAD : wide + (h + 1) * HEAD]
            v = qkv_ref[:reach, 2 * wide + h * HEAD : 2 * wide + (h + 1) * HEAD]
            s = jnp.where(seen, dot_nt(q, k) * factor, -1e30)
            top = jnp.max(s, axis=-1, keepdims=True)
            e = jnp.exp(s - top)
            total = jnp.sum(e, axis=-1, keepdims=True)
            probs = (e * (1.0 / total)).astype(BF16)
            o_ref[at : at + block, h * HEAD : (h + 1) * HEAD] = dot(probs, v).astype(BF16)
            lse_ref[at : at + block, h : h + 1] = top + jnp.log(total)
    out_ref[...] = dot_nt(o_ref[...], w_ref[:, 3 * wide :]).astype(BF16)


def attend_forward(starts, a_all, w_attn, heads):
    seq_len, width = a_all.shape
    wide = heads * HEAD
    spans = starts.shape[1]
    return pl.pallas_call(
        functools.partial(attend_kernel, heads, spans, PIC),
        out_shape=[
            jax.ShapeDtypeStruct((seq_len, 3 * wide), BF16),
            jax.ShapeDtypeStruct((seq_len, wide), BF16),
            jax.ShapeDtypeStruct((seq_len, heads), F32),
            jax.ShapeDtypeStruct((seq_len, width), BF16),
        ],
        in_specs=[pl.BlockSpec(memory_space=pltpu.SMEM), VMEM_SPEC, VMEM_SPEC],
        out_specs=[VMEM_SPEC] * 4,
        compiler_params=pltpu.CompilerParams(vmem_limit_bytes=VMEM_LIMIT),
        cost_estimate=pl.CostEstimate(
            flops=8 * seq_len * width * wide + 4 * heads * seq_len * seq_len * HEAD,
            bytes_accessed=6 * seq_len * width,
            transcendentals=heads * seq_len * seq_len,
        ),
        name="attend_forward",
    )(starts, a_all, w_attn)


def attend_back_kernel(
    heads, spans, block, starts_ref, g_ref, w_ref, a_ref, qkv_ref, o_ref, lse_ref,
    ga_ref, gw_ref, go_scr, gq_scr, gk_acc, gv_acc,
):
    seq_len = a_ref.shape[0]
    wide = heads * HEAD
    factor = HEAD ** (-0.5)
    go_scr[...] = dot(g_ref[...], w_ref[:, 3 * wide :]).astype(BF16)
    gw_ref[:, 3 * wide :] = dot_tn(g_ref[...], o_ref[...]).astype(BF16)
    gk_acc[...] = jnp.zeros_like(gk_acc)
    gv_acc[...] = jnp.zeros_like(gv_acc)
    for at in range(0, seq_len, block):
        reach = key_extent(at, seq_len, spans)
        seen = span_mask(starts_ref, at, block, reach, spans)
        for h in range(heads):
            own = slice(h * HEAD, (h + 1) * HEAD)
            q = qkv_ref[at : at + block, own]
            k = qkv_ref[:reach, wide + h * HEAD : wide + (h + 1) * HEAD]
            v = qkv_ref[:reach, 2 * wide + h * HEAD : 2 * wide + (h + 1) * HEAD]
            go = go_scr[at : at + block, own]
            s = jnp.where(seen, dot_nt(q, k) * factor, -1e30)
            probs = jnp.exp(s - lse_ref[at : at + block, h : h + 1])
            gp = dot_nt(go, v)
            inner = jnp.sum(probs * gp, axis=-1, keepdims=True)
            gs = (probs * (gp - inner)).astype(BF16)
            gq_scr[at : at + block, own] = (dot(gs, k) * factor).astype(BF16)
            gk_acc[:reach, own] += dot_tn(gs, q) * factor
            gv_acc[:reach, own] += dot_tn(probs.astype(BF16), go)
    gq_scr[:, wide : 2 * wide] = gk_acc[...].astype(BF16)
    gq_scr[:, 2 * wide :] = gv_acc[...].astype(BF16)
    gw_ref[:, : 3 * wide] = dot_tn(a_ref[...], gq_scr[...]).astype(BF16)
    ga_ref[...] = dot_nt(gq_scr[...], w_ref[:, : 3 * wide]).astype(BF16)


def attend_backward(starts, g_all, w_attn, a_all, qkv, o, lse, heads):
    seq_len, width = a_all.shape
    wide = heads * HEAD
    spans = starts.shape[1]
    return pl.pallas_call(
        functools.partial(attend_back_kernel, heads, spans, PIC),
        out_shape=[
            jax.ShapeDtypeStruct((seq_len, width), BF16),
            jax.ShapeDtypeStruct((width, 4 * wide), BF16),
        ],
        in_specs=[pl.BlockSpec(memory_space=pltpu.SMEM)] + [VMEM_SPEC] * 6,
        out_specs=[VMEM_SPEC] * 2,
        scratch_shapes=[
            pltpu.VMEM((seq_len, wide), BF16),
            pltpu.VMEM((seq_len, 3 * wide), BF16),
            pltpu.VMEM((seq_len, wide), F32),
            pltpu.VMEM((seq_len, wide), F32),
        ],
        compiler_params=pltpu.CompilerParams(vmem_limit_bytes=VMEM_LIMIT),
        cost_estimate=pl.CostEstimate(
            flops=16 * seq_len * width * wide + 10 * heads * seq_len * seq_len * HEAD,
            bytes_accessed=12 * seq_len * width,
            transcendentals=heads * seq_len * seq_len,
        ),
        name="attend_backward",
    )(starts, g_all, w_attn, a_all, qkv, o, lse)


def lane_column(values, at):
    lane = lax.broadcasted_iota(jnp.int32, values.shape, 1)
    return jnp.sum(jnp.where(lane == at, values, 0), axis=1, keepdims=True)


def two_parts(values):
    high = values.astype(BF16)
    return high, (values - high.astype(F32)).astype(BF16)


def experts_kernel(
    cap, b_ref, w_ref, rowpos_ref, pos_ref, router_ref, zterm_ref,
    x_ref, gu_ref, z_ref, wd_ref, f_ref, pick_scr, y_scr,
):
    e = pl.program_id(0)
    seq_len, width = b_ref.shape
    half = gu_ref.shape[2] // 2

    @pl.when(e == 0)
    def _():
        z = dot(b_ref[...], router_ref[...]) + zterm_ref[...]
        z_ref[...] = z
        hit = pos_ref[...] >= 0
        top = jnp.max(jnp.where(hit, z, -3e38), axis=1, keepdims=True)
        ez = jnp.where(hit, jnp.exp(jnp.where(hit, z - top, 0.0)), 0.0)
        wd_ref[...] = ez / jnp.sum(ez, axis=1, keepdims=True)

    w = w_ref[...].reshape(width, 3 * half)
    take = (
        lax.broadcasted_iota(jnp.int32, (cap, seq_len), 0) == rowpos_ref[0]
    ).astype(F32).astype(BF16)
    x = dot(take, b_ref[...]).astype(BF16)
    x_ref[0] = x
    gu = dot(x, w[:, : 2 * half])
    gu_ref[0] = gu.astype(BF16)
    g, u = gu[:, :half], gu[:, half:]
    h = (g * jax.nn.sigmoid(g) * u).astype(BF16)
    y = dot_nt(h, w[:, 2 * half :])
    y_scr[pl.ds(pl.multiple_of(e * cap, cap), cap), :] = y.astype(BF16)
    column = lane_column(pos_ref[...], e)
    weight = lane_column(wd_ref[...], e)
    put = jnp.where(
        lax.broadcasted_iota(jnp.int32, (seq_len, cap), 1) == column, weight, 0.0
    ).astype(BF16)
    pick_scr[:, pl.ds(pl.multiple_of(e * cap, cap), cap)] = put

    @pl.when(e == pl.num_programs(0) - 1)
    def _():
        f_ref[...] = dot(pick_scr[...], y_scr[...]).astype(BF16)


def whole(shape):
    return pl.BlockSpec(shape, lambda e: (0,) * len(shape))


def experts_forward(b_all, w_exp, rowpos, pos, router, zterm, cap):
    seq_len, width = b_all.shape
    shards_dp, count, rows, wide3 = w_exp.shape
    half = wide3 // 3
    return pl.pallas_call(
        functools.partial(experts_kernel, cap),
        grid=(count,),
        out_shape=[
            jax.ShapeDtypeStruct((count, cap, width), BF16),
            jax.ShapeDtypeStruct((count, cap, 2 * half), BF16),
            jax.ShapeDtypeStruct((seq_len, LANES), F32),
            jax.ShapeDtypeStruct((seq_len, LANES), F32),
            jax.ShapeDtypeStruct((seq_len, width), BF16),
        ],
        in_specs=[
            whole((seq_len, width)),
            pl.BlockSpec((shards_dp, 1, rows, wide3), lambda e: (0, e, 0, 0)),
            pl.BlockSpec((1, 1, seq_len), lambda e: (e, 0, 0)),
            whole((seq_len, LANES)),
            whole((width, LANES)),
            whole((seq_len, LANES)),
        ],
        out_specs=[
            pl.BlockSpec((1, cap, width), lambda e: (e, 0, 0)),
            pl.BlockSpec((1, cap, 2 * half), lambda e: (e, 0, 0)),
            whole((seq_len, LANES)),
            whole((seq_len, LANES)),
            whole((seq_len, width)),
        ],
        scratch_shapes=[
            pltpu.VMEM((seq_len, count * cap), BF16),
            pltpu.VMEM((count * cap, width), BF16),
        ],
        compiler_params=pltpu.CompilerParams(vmem_limit_bytes=VMEM_LIMIT),
        cost_estimate=pl.CostEstimate(
            flops=count * (4 * cap * seq_len * width + 6 * cap * width * half),
            bytes_accessed=2 * count * width * wide3,
            transcendentals=0,
        ),
        name="experts_forward",
    )(b_all, w_exp, rowpos, pos, router, zterm)


def experts_back_kernel(
    cap, g_ref, w_ref, x_ref, gu_ref, rowpos_ref, pos_ref, wd_ref, gwown_ref, gprev_ref, rt_ref,
    gw_ref, gz_ref, gb_ref, pick_scr, gx_scr, gg_scr,
):
    e = pl.program_id(0)
    seq_len, width = g_ref.shape
    shards_dp, _, rows, wide3 = w_ref.shape
    half = wide3 // 3
    w = w_ref[...].reshape(width, wide3)
    take = (
        lax.broadcasted_iota(jnp.int32, (cap, seq_len), 0) == rowpos_ref[0]
    ).astype(F32).astype(BF16)
    w_high, w_low = two_parts(wd_ref[...])
    weight = lane_column(dot(take, w_high) + dot(take, w_low), e)
    gf = dot(take, g_ref[...])
    gh = dot(gf.astype(BF16), w[:, 2 * half :])
    gu = gu_ref[0].astype(F32)
    g, u = gu[:, :half], gu[:, half:]
    sig = jax.nn.sigmoid(g)
    h = (g * sig * u).astype(BF16)
    slot_grad = jnp.sum(h.astype(F32) * gh, axis=1, keepdims=True)
    gh = gh * weight
    gg = gh * u * sig * (1.0 + g * (1.0 - sig))
    gup = gh * g * sig
    both = jnp.concatenate([gg.astype(BF16), gup.astype(BF16)], axis=1)
    gy = (gf * weight).astype(BF16)
    gw_ref[:, 0, :, : 2 * half] = dot_tn(x_ref[0], both).astype(BF16).reshape(
        shards_dp, rows, 2 * half
    )
    gw_ref[:, 0, :, 2 * half :] = dot_tn(gy, h).astype(BF16).reshape(shards_dp, rows, half)
    here = pl.ds(pl.multiple_of(e * cap, cap), cap)
    gx_scr[here, :] = dot_nt(both, w[:, : 2 * half]).astype(BF16)
    s_high, s_low = two_parts(slot_grad)
    lane = lax.broadcasted_iota(jnp.int32, (cap, LANES), 1)
    gg_scr[here, :LANES] = jnp.where(lane == e, s_high.astype(F32), 0.0).astype(BF16)
    gg_scr[here, LANES:] = jnp.where(lane == e, s_low.astype(F32), 0.0).astype(BF16)
    column = lane_column(pos_ref[...], e)
    pick_scr[:, here] = (
        lax.broadcasted_iota(jnp.int32, (seq_len, cap), 1) == column
    ).astype(F32).astype(BF16)

    @pl.when(e == pl.num_programs(0) - 1)
    def _():
        slots = dot(pick_scr[...], gg_scr[...])
        gw = slots[:, :LANES] + slots[:, LANES:] + gwown_ref[...]
        wd = wd_ref[...]
        gz = wd * (gw - jnp.sum(wd * gw, axis=1, keepdims=True)) + gprev_ref[...]
        gz_ref[...] = gz
        z_high, z_low = two_parts(gz)
        gb = dot(pick_scr[...], gx_scr[...]) + dot(z_high, rt_ref[...]) + dot(z_low, rt_ref[...])
        gb_ref[...] = gb.astype(BF16)


def experts_backward(g_all, w_exp, x, gu, rowpos, pos, wd, gw_own, grad_prev, router_t, cap):
    seq_len, width = g_all.shape
    shards_dp, count, rows, wide3 = w_exp.shape
    half = wide3 // 3
    weight_spec = pl.BlockSpec((shards_dp, 1, rows, wide3), lambda e: (0, e, 0, 0))
    return pl.pallas_call(
        functools.partial(experts_back_kernel, cap),
        grid=(count,),
        out_shape=[
            jax.ShapeDtypeStruct(w_exp.shape, BF16),
            jax.ShapeDtypeStruct((seq_len, LANES), F32),
            jax.ShapeDtypeStruct((seq_len, width), BF16),
        ],
        in_specs=[
            whole((seq_len, width)),
            weight_spec,
            pl.BlockSpec((1, cap, width), lambda e: (e, 0, 0)),
            pl.BlockSpec((1, cap, 2 * half), lambda e: (e, 0, 0)),
            pl.BlockSpec((1, 1, seq_len), lambda e: (e, 0, 0)),
            whole((seq_len, LANES)),
            whole((seq_len, LANES)),
            whole((seq_len, LANES)),
            whole((seq_len, LANES)),
            whole((LANES, width)),
        ],
        out_specs=[weight_spec, whole((seq_len, LANES)), whole((seq_len, width))],
        scratch_shapes=[
            pltpu.VMEM((seq_len, count * cap), BF16),
            pltpu.VMEM((count * cap, width), BF16),
            pltpu.VMEM((count * cap, 2 * LANES), BF16),
        ],
        compiler_params=pltpu.CompilerParams(vmem_limit_bytes=VMEM_LIMIT),
        cost_estimate=pl.CostEstimate(
            flops=count * (4 * cap * seq_len * width + 12 * cap * width * half),
            bytes_accessed=4 * count * width * wide3,
            transcendentals=0,
        ),
        name="experts_backward",
    )(g_all, w_exp, x, gu, rowpos, pos, wd, gw_own, grad_prev, router_t)


def lanes(values):
    return jnp.pad(values, ((0, 0), (0, LANES - values.shape[1])))


def slot_table(route_ids):
    tokens = route_ids.shape[0]
    codes = jnp.arange(LANES, dtype=jnp.int32)
    hit = jnp.any(route_ids[:, :, None] == codes[None, None, :], axis=1)
    place = jnp.arange(tokens, dtype=jnp.int32)
    before = (place[None, :] < place[:, None]).astype(BF16)
    slots = dot(before, hit.astype(BF16)).astype(jnp.int32)
    return jnp.where(hit, slots, -1)


def shards(
    hidden_in,
    prev_logits,
    routes,
    span_starts,
    attn_norm,
    qkv_weight,
    out_weight,
    moe_norm,
    router,
    gate_mix,
    const_vec,
    const_mix,
    up_weight,
    down_weight,
    out_grad,
):
    layers = qkv_weight.shape[0]
    own, width = hidden_in.shape
    nt = lax.axis_size("tensor")
    ndp = lax.axis_size("dp")
    seq_len = own * nt
    offset = lax.axis_index("tensor") * own
    cap = seq_len // 4
    heads = qkv_weight.shape[3] // HEAD
    wide = heads * HEAD
    half = up_weight.shape[4]
    rows = qkv_weight.shape[1]
    cols = attn_norm.shape[1]
    consts = const_vec.shape[1]

    packed = jnp.concatenate(
        [attn_norm.T, moe_norm.T]
        + [router[l] for l in range(layers)]
        + [const_vec.reshape(-1, cols).T]
        + [const_mix[l, j] for l in range(layers) for j in range(consts)],
        axis=1,
    )
    small = everyone(lanes(packed), False, 0).reshape(width, LANES)
    at = 0
    fields = {}
    for name, size in (
        ("attn", layers),
        ("moe", layers),
        ("router", layers * NEXP),
        ("cvec", layers * consts),
        ("cmix", layers * consts * 2),
    ):
        fields[name] = (at, size)
        at += size

    def field(name, l, per):
        begin = fields[name][0] + l * per
        return small[:, begin : begin + per]

    attn_w, exp_w = [], []
    for l in range(layers):
        local = jnp.concatenate(
            [qkv_weight[l].reshape(rows, 3 * wide), out_weight[l].T], axis=1
        )
        attn_w.append(lax.all_gather(local, "dp", axis=0, tiled=False).reshape(width, 4 * wide))
        local = jnp.concatenate(
            [
                up_weight[l].reshape(EXPERTS, rows, 2 * half),
                jnp.swapaxes(down_weight[l], 1, 2),
            ],
            axis=2,
        )
        exp_w.append(lax.all_gather(local, "dp", axis=0, tiled=False))

    pos = [slot_table(routes[l]) for l in range(layers)]
    rowpos = [p[:, :EXPERTS].T[:, None, :] for p in pos]

    hidden = hidden_in.astype(F32)
    gain = field("attn", 0, 1).astype(F32).T
    (a_all,) = line_exchange("start", [hidden_in, gain], own, width, 1)
    z_prev = lanes(prev_logits)
    next_id = 2
    stored = []
    for l in range(layers):
        mix = jnp.pad(gate_mix[l].astype(F32), ((0, LANES - NEXP), (0, LANES - NEXP)))
        zterm = jnp.dot(z_prev, mix, precision=HIGH)
        qkv, o, lse, partial = attend_forward(span_starts, a_all, attn_w[l], heads)
        gain = field("moe", l, 1).astype(F32).T
        mid, b_all = line_exchange("fwd", [partial, hidden, gain], own, width, next_id)
        router_l = lanes(field("router", l, NEXP))
        x, gu, z, wd, partial = experts_forward(
            b_all, exp_w[l], rowpos[l], pos[l], router_l, zterm, cap
        )
        b_own = lax.dynamic_slice_in_dim(b_all, offset, own, 0)
        cmix = field("cmix", l, 2 * consts)
        cvec = field("cvec", l, consts).astype(F32).T
        logit = dot(b_own, cmix)
        alpha = jax.nn.softmax(logit.reshape(own, consts, 2), axis=2)
        gates = lax.dynamic_slice_in_dim(wd, offset, own, 0)
        copy_gate = gates[:, EXPERTS + 1 : EXPERTS + 2]
        const_gate = gates[:, EXPERTS + 2 : EXPERTS + 2 + consts]
        keep = copy_gate + jnp.sum(const_gate * alpha[:, :, 0], axis=1, keepdims=True)
        inject = const_gate * alpha[:, :, 1]
        side = keep * b_own.astype(F32)
        for j in range(consts):
            side = side + inject[:, j : j + 1] * cvec[j : j + 1]
        stored.append(
            dict(
                hidden=hidden, a_all=a_all, qkv=qkv, o=o, lse=lse, mid=mid, b_all=b_all,
                b_own=b_own, x=x, gu=gu, wd=wd, z_prev=z_prev, alpha=alpha,
                const_gate=const_gate, keep=keep, inject=inject, cvec=cvec, cmix=cmix, mix=mix,
                router=router_l,
            )
        )
        if l + 1 < layers:
            gain = field("attn", l + 1, 1).astype(F32).T
            hidden, a_all = line_exchange("fwd", [partial, mid + side, gain], own, width, next_id + 1)
        else:
            hidden, g_all = line_exchange(
                "last", [partial, mid + side, out_grad], own, width, next_id + 1
            )
        z_prev = z
        next_id += 2
    hidden_out = hidden

    grad = out_grad.astype(F32)
    grad_prev = jnp.zeros((seq_len, LANES), F32)
    attn_grads, exp_grads = [None] * layers, [None] * layers
    gains_a, gains_m = [None] * layers, [None] * layers
    routers, cvecs, cmixes, mixes = ([None] * layers for _ in range(4))
    for l in reversed(range(layers)):
        s = stored[l]
        b_own = s["b_own"].astype(F32)
        bg = jnp.sum(b_own * grad, axis=1, keepdims=True)
        cg = jnp.concatenate(
            [jnp.sum(grad * s["cvec"][j : j + 1], axis=1, keepdims=True) for j in range(consts)],
            axis=1,
        )
        alpha = s["alpha"]
        gw_const = alpha[:, :, 0] * bg + alpha[:, :, 1] * cg
        gw_own = jnp.pad(
            jnp.concatenate([bg, gw_const], axis=1),
            ((0, 0), (EXPERTS + 1, LANES - EXPERTS - 2 - consts)),
        )
        gw_own = lax.dynamic_update_slice_in_dim(
            jnp.zeros((seq_len, LANES), F32), gw_own, offset, 0
        )
        ga = s["const_gate"][:, :, None] * jnp.stack([jnp.broadcast_to(bg, cg.shape), cg], axis=2)
        gt = alpha * (ga - jnp.sum(alpha * ga, axis=2, keepdims=True))
        gt = gt.reshape(own, 2 * consts)
        own_part = s["keep"] * grad
        cmix_f = s["cmix"].astype(F32).T
        for j in range(2 * consts):
            own_part = own_part + gt[:, j : j + 1] * cmix_f[j : j + 1]
        cmixes[l] = lax.dot_general(b_own, gt, (((0,), (0,)), ((), ())), precision=HIGH)
        cvecs[l] = lax.dot_general(grad, s["inject"], (((0,), (0,)), ((), ())), precision=HIGH)

        gw_exp, gz, partial = experts_backward(
            g_all, exp_w[l], s["x"], s["gu"], rowpos[l], pos[l], s["wd"], gw_own, grad_prev,
            s["router"].T, cap,
        )
        exp_grads[l] = lax.psum_scatter(gw_exp, "dp", scatter_dimension=0, tiled=False)
        z_high, z_low = two_parts(gz)
        routers[l] = (dot_tn(s["b_all"], z_high) + dot_tn(s["b_all"], z_low))[:, :NEXP]
        mixes[l] = lax.dot_general(
            s["z_prev"], gz, (((0,), (0,)), ((), ())), precision=HIGH
        )[:NEXP, :NEXP]
        if l > 0:
            grad_prev = lax.dot_general(gz, s["mix"], (((1,), (1,)), ((), ())), precision=HIGH)
        gain = field("moe", l, 1).astype(F32).T
        grad_mid, gains_m[l], g_all = line_exchange(
            "bwd", [partial, own_part, s["mid"], grad, gain], own, width, next_id, extra=True
        )
        partial, gw_attn = attend_backward(
            span_starts, g_all, attn_w[l], s["a_all"], s["qkv"], s["o"], s["lse"], heads
        )
        attn_grads[l] = lax.psum_scatter(
            gw_attn.reshape(ndp, rows, 4 * wide), "dp", scatter_dimension=0, tiled=False
        )
        gain = field("attn", l, 1).astype(F32).T
        if l > 0:
            grad, gains_a[l], g_all = line_exchange(
                "bwd", [partial, s["hidden"], grad_mid, gain], own, width, next_id + 1
            )
        else:
            grad, gains_a[l] = line_exchange(
                "end", [partial, s["hidden"], grad_mid, gain], own, width, next_id + 1
            )
        next_id += 2

    sums = jnp.concatenate(
        [item.T for item in gains_a]
        + [item.T for item in gains_m]
        + routers
        + cvecs
        + cmixes,
        axis=1,
    )
    sums = lanes(sums).reshape(ndp * nt, cols, LANES)
    flat = jnp.stack(mixes).reshape(-1)
    mix_rows = -(-flat.shape[0] // LANES)
    flat = jnp.pad(flat, (0, mix_rows * LANES - flat.shape[0])).reshape(1, mix_rows, LANES)
    flat = jnp.broadcast_to(flat, (ndp * nt, mix_rows, LANES))
    total = everyone(jnp.concatenate([sums, flat], axis=1), True, next_id)
    mix_total = total[cols:].reshape(-1)[: layers * NEXP * NEXP].reshape(layers, NEXP, NEXP)
    total = total[:cols]

    def back(name):
        begin, size = fields[name]
        return total[:, begin : begin + size]

    router_grad = jnp.swapaxes(back("router").reshape(cols, layers, NEXP), 0, 1)
    cmix_grad = jnp.transpose(back("cmix").reshape(cols, layers, consts, 2), (1, 2, 0, 3))
    cvec_grad = back("cvec").T.reshape(layers, consts, cols)
    qkv_grad = jnp.stack(
        [item[:, : 3 * wide].reshape(rows, 3, wide) for item in attn_grads]
    ).astype(F32)
    outw_grad = jnp.stack([item[:, 3 * wide :].T for item in attn_grads]).astype(F32)
    up_grad = jnp.stack(
        [item[:, :, : 2 * half].reshape(EXPERTS, rows, 2, half) for item in exp_grads]
    ).astype(F32)
    down_grad = jnp.stack(
        [jnp.swapaxes(item[:, :, 2 * half :], 1, 2) for item in exp_grads]
    ).astype(F32)
    return (
        hidden_out,
        grad,
        back("attn").T,
        qkv_grad,
        outw_grad,
        back("moe").T,
        router_grad,
        mix_total,
        cvec_grad,
        cmix_grad,
        up_grad,
        down_grad,
    )


def solution(mesh):
    return jax.shard_map(
        shards,
        mesh=mesh,
        in_specs=(
            P(("dp", "tensor"), None),
            P("dp", None),
            P(None, "dp", None),
            P("dp", None),
            P(None, ("dp", "tensor")),
            P(None, "dp", None, "tensor"),
            P(None, "tensor", "dp"),
            P(None, ("dp", "tensor")),
            P(None, ("dp", "tensor"), None),
            P(),
            P(None, None, ("dp", "tensor")),
            P(None, None, ("dp", "tensor"), None),
            P(None, None, "dp", None, "tensor"),
            P(None, None, "tensor", "dp"),
            P(("dp", "tensor"), None),
        ),
        out_specs=(
            P(("dp", "tensor"), None),
            P(("dp", "tensor"), None),
            P(None, ("dp", "tensor")),
            P(None, "dp", None, "tensor"),
            P(None, "tensor", "dp"),
            P(None, ("dp", "tensor")),
            P(None, ("dp", "tensor"), None),
            P(),
            P(None, None, ("dp", "tensor")),
            P(None, None, ("dp", "tensor"), None),
            P(None, None, "dp", None, "tensor"),
            P(None, None, "tensor", "dp"),
        ),
        check_vma=False,
    )
```

```python
import functools

import jax
import jax.numpy as jnp
from jax import lax
from jax.experimental import pallas as pl
from jax.experimental.pallas import tpu as pltpu
from jax.sharding import PartitionSpec as P

HEAD = 64
EXPERTS = 8
NEXP = 12
TOPK = 2
PIC = 256
LANES = 128

EPS = 1e-06
HIGH = lax.Precision.HIGHEST
MESH = pl.DeviceIdType.MESH
F32 = jnp.float32
BF16 = jnp.bfloat16
VMEM_SPEC = pl.BlockSpec(memory_space=pltpu.VMEM)
AHEAD = 2
VMEM_LIMIT = 60 * 1024 * 1024


def dot(a, b):
    return jnp.dot(a, b, preferred_element_type=F32)


def dot_nt(a, b):
    return lax.dot_general(a, b, (((1,), (1,)), ((), ())), preferred_element_type=F32)


def dot_tn(a, b):
    return lax.dot_general(a, b, (((0,), (0,)), ((), ())), preferred_element_type=F32)


def greet_all(count, me, place):
    barrier = pltpu.get_barrier_semaphore()

    def greet(step, carry):
        other = lax.rem(me + step, count)
        pl.semaphore_signal(barrier, inc=1, device_id=place(other), device_id_type=MESH)
        return carry

    lax.fori_loop(1, count, greet, 0)
    pl.semaphore_wait(barrier, count - 1)


def swap_all(count, me, place, source, land, send_sems, recv_sems):
    def copy(other, slot):
        return pltpu.make_async_remote_copy(
            src_ref=source(other),
            dst_ref=land.at[slot],
            send_sem=send_sems.at[other],
            recv_sem=recv_sems.at[slot],
            device_id=place(other),
            device_id_type=MESH,
        )

    def start():
        def send(step, carry):
            other = lax.rem(me + step, count)
            copy(other, me).start()
            return carry

        lax.fori_loop(1, count, send, 0)

    def finish():
        def wait(step, carry):
            other = lax.rem(me + count - step, count)
            copy(other, other).wait()
            return carry

        lax.fori_loop(1, count, wait, 0)

    return start, finish


def closing_kernel(ndp, inner, *refs):
    small_ref, first_ref, second_ref, out_ref, first_out, second_out = refs[:6]
    land, first_land, second_land = refs[6:9]
    sems = refs[9:]
    count = ndp * inner
    row, col = lax.axis_index("dp"), lax.axis_index("tensor")
    me = row * inner + col

    def anywhere(other):
        return (lax.div(other, inner), lax.rem(other, inner))

    def along(other):
        return (other, col)

    greet_all(count, me, anywhere)
    moves = [
        (swap_all(count, me, anywhere, lambda o: small_ref.at[o], land, *sems[0:2])),
        (swap_all(ndp, row, along, lambda o: first_ref.at[o], first_land, *sems[2:4])),
        (swap_all(ndp, row, along, lambda o: second_ref.at[o], second_land, *sems[4:6])),
    ]
    for start, _ in moves:
        start()
    land[me] = small_ref[me]
    first_land[row] = first_ref[row]
    second_land[row] = second_ref[row]
    for _, finish in moves:
        finish()
    out_ref[...] = jnp.sum(land[...], axis=0)
    first_out[...] = jnp.sum(first_land[...].astype(F32), axis=0)
    second_out[...] = jnp.sum(second_land[...].astype(F32), axis=0)


def closing(small, first, second, collective_id):
    inner, ndp = lax.axis_size("tensor"), lax.axis_size("dp")
    pair = [pltpu.SemaphoreType.DMA((ndp * inner,))] * 2
    return pl.pallas_call(
        functools.partial(closing_kernel, ndp, inner),
        out_shape=[
            jax.ShapeDtypeStruct(small.shape[1:], F32),
            jax.ShapeDtypeStruct(first.shape[1:], F32),
            jax.ShapeDtypeStruct(second.shape[1:], F32),
        ],
        in_specs=[VMEM_SPEC] * 3,
        out_specs=[VMEM_SPEC] * 3,
        scratch_shapes=[
            pltpu.VMEM(small.shape, F32),
            pltpu.VMEM(first.shape, BF16),
            pltpu.VMEM(second.shape, BF16),
        ]
        + pair
        + [pltpu.SemaphoreType.DMA((ndp,))] * 4,
        compiler_params=pltpu.CompilerParams(
            collective_id=collective_id, has_side_effects=True, vmem_limit_bytes=VMEM_LIMIT
        ),
        name="closing",
    )(small, first, second)


def normed(values, gain):
    return values * lax.rsqrt(jnp.mean(values * values, axis=-1, keepdims=True) + EPS) * gain


def line_kernel(kind, nt, chunks, lag, extra, *refs):
    refs = list(refs)
    has_sum = kind != "start"
    has_gather = kind != "end"
    part = refs.pop(0) if has_sum else None
    if kind == "start":
        x_ref, small_ref = refs.pop(0), refs.pop(0)
    elif kind == "fwd":
        extra_ref, gain_ref = refs.pop(0), refs.pop(0)
    elif kind == "last":
        extra_ref, og_ref = refs.pop(0), refs.pop(0)
    else:
        extra_ref = refs.pop(0) if extra else None
        base_ref, skip_ref, gain_ref = refs.pop(0), refs.pop(0), refs.pop(0)
    own_ref = refs.pop(0) if has_sum else None
    gg_ref = refs.pop(0) if kind in ("bwd", "end") else None
    all_ref = refs.pop(0) if has_gather else None
    land_ref = refs.pop(0) if kind == "start" else None
    if has_sum:
        from_left, from_right, tx, acc, rs_send, rl_sem, rr_sem = refs[:7]
        refs = refs[7:]
    if has_gather:
        ag_right, ag_left, ag_recv = refs[:3]
        refs = refs[3:]

    me = lax.axis_index("tensor")
    has_l, has_r = me > 0, me < nt - 1
    left, right = jnp.maximum(me - 1, 0), jnp.minimum(me + 1, nt - 1)

    if kind == "start":
        count = lax.axis_size("dp") * nt
        me_all = lax.axis_index("dp") * nt + me

        def place(other):
            return (lax.div(other, nt), lax.rem(other, nt))

        greet_all(count, me_all, place)
        small_start, small_finish = swap_all(
            count, me_all, place, lambda other: small_ref, land_ref, *refs[:2]
        )
        small_start()
        land_ref[me_all] = small_ref[...]
    else:
        barrier = pltpu.get_barrier_semaphore()

        @pl.when(has_l)
        def _():
            pl.semaphore_signal(barrier, inc=1, device_id={"tensor": left}, device_id_type=MESH)

        @pl.when(has_r)
        def _():
            pl.semaphore_signal(barrier, inc=1, device_id={"tensor": right}, device_id_type=MESH)

        pl.semaphore_wait(barrier, has_l.astype(jnp.int32) + has_r.astype(jnp.int32))

    def copy(src, dst, send_sem, recv_sem, to):
        return pltpu.make_async_remote_copy(
            src_ref=src,
            dst_ref=dst,
            send_sem=send_sem,
            recv_sem=recv_sem,
            device_id={"tensor": to},
            device_id_type=MESH,
        )

    def sum_right(j, c, src):
        return copy(src, from_left.at[j, c], rs_send.at[j, c], rl_sem.at[j, c], right)

    def sum_left(j, c, src):
        return copy(src, from_right.at[j, c], rs_send.at[j, c], rr_sem.at[j, c], left)

    def spread_right(j, c):
        block = all_ref.at[j, c]
        return copy(block, block, ag_right.at[j, c], ag_recv.at[j, c], right)

    def spread_left(j, c):
        block = all_ref.at[j, c]
        return copy(block, block, ag_left.at[j, c], ag_recv.at[j, c], left)

    def offer(c):
        @pl.when(has_r)
        def _():
            spread_right(me, c).start()

        @pl.when(has_l)
        def _():
            spread_left(me, c).start()

    def pass_on(c, d):
        @pl.when(me - d >= 0)
        def _():
            j = me - d
            spread_right(j, c).wait_recv()

            @pl.when(has_r)
            def _():
                spread_right(j, c).start()

        @pl.when(me + d < nt)
        def _():
            j = me + d
            spread_left(j, c).wait_recv()

            @pl.when(has_l)
            def _():
                spread_left(j, c).start()

    hops = nt - 1

    count = hops * chunks

    def relay(step):
        k = jnp.clip(step - lag * me, 0, count - 1)
        c, j = lax.div(k, hops), hops - lax.rem(k, hops)

        @pl.when(has_l & (step >= lag * me) & (step - lag * me < count) & (me < j))
        def _():
            sum_right(j, c, tx.at[j, c]).wait_recv()
            tx[j, c] = (part[j, c].astype(F32) + from_left[j, c].astype(F32)).astype(BF16)
            sum_right(j, c, tx.at[j, c]).start()

        far = lag * (hops - me)
        k_down = jnp.clip(step - far, 0, count - 1)
        c_down, j_down = lax.div(k_down, hops), lax.rem(k_down, hops)

        @pl.when(has_r & (step >= far) & (step - far < count) & (me > j_down))
        def _():
            sum_left(j_down, c_down, tx.at[j_down, c_down]).wait_recv()
            tx[j_down, c_down] = (
                part[j_down, c_down].astype(F32) + from_right[j_down, c_down].astype(F32)
            ).astype(BF16)
            sum_left(j_down, c_down, tx.at[j_down, c_down]).start()

    def push(first, last):
        ks = range(min(first, count), min(last, count))

        @pl.when(jnp.logical_not(has_l))
        def _():
            for k in ks:
                j, c = hops - k % hops, k // hops
                sum_right(j, c, part.at[j, c]).start()

        @pl.when(jnp.logical_not(has_r))
        def _():
            for k in ks:
                j, c = k % hops, k // hops
                sum_left(j, c, part.at[j, c]).start()

    def own_rows(c):
        acc[...] = part[me, c].astype(F32)

        @pl.when(has_l)
        def _():
            sum_right(me, c, tx.at[me, c]).wait_recv()
            acc[...] += from_left[me, c].astype(F32)

        @pl.when(has_r)
        def _():
            sum_left(me, c, tx.at[me, c]).wait_recv()
            acc[...] += from_right[me, c].astype(F32)

        total = acc[...]
        if kind == "fwd":
            total = total + extra_ref[c]
            all_ref[me, c] = normed(total, gain_ref[...]).astype(BF16)
            own_ref[c] = total
        elif kind == "last":
            own_ref[c] = total + extra_ref[c]
        else:
            if extra:
                total = total + extra_ref[c]
            base = base_ref[c]
            scale = lax.rsqrt(jnp.mean(base * base, axis=-1, keepdims=True) + EPS)
            unit = base * scale
            grad_unit = total * gain_ref[...]
            below = scale * (grad_unit - unit * jnp.mean(grad_unit * unit, axis=-1, keepdims=True))
            result = below + skip_ref[c]
            if has_gather:
                all_ref[me, c] = result.astype(BF16)
            own_ref[c] = result
            gg = jnp.sum(total * unit, axis=0, keepdims=True)
            if c == 0:
                gg_ref[...] = gg
            else:
                gg_ref[...] += gg
        if kind in ("fwd", "bwd"):
            offer(c)

    if kind == "start":
        for c in range(chunks):
            all_ref[me, c] = x_ref[c]
            offer(c)
        for c in range(chunks):
            for d in range(1, nt):
                pass_on(c, d)
        small_finish()
    else:

        push(0, AHEAD)
        if kind == "last":
            for c in range(chunks):
                all_ref[me, c] = og_ref[c]
            for c in range(chunks):
                offer(c)
        delay = 0 if kind == "last" else hops * lag
        spreads = {}
        for c in range(chunks if has_gather else 0):
            for d in range(1, nt):
                spreads.setdefault(delay + hops * c + lag * d, []).append((c, d))
        final = max([hops * (chunks - 1 + lag)] + list(spreads))
        for step in range(1, final + 1):
            push(step + AHEAD - 1, step + AHEAD)
            relay(step)
            for c, d in spreads.get(step, ()):
                pass_on(c, d)
            if step % hops == 0 and 0 <= step // hops - lag < chunks:
                own_rows(step // hops - lag)

    for c in range(chunks):
        for j in range(nt):
            if has_sum:

                @pl.when(me < j)
                def _():
                    sum_right(j, c, tx.at[j, c]).wait_send()

                @pl.when(me > j)
                def _():
                    sum_left(j, c, tx.at[j, c]).wait_send()

            if has_gather:

                @pl.when(has_r & (j <= me))
                def _():
                    spread_right(j, c).wait_send()

                @pl.when(has_l & (j >= me))
                def _():
                    spread_left(j, c).wait_send()


def line_exchange(kind, args, rows, width, collective_id, extra=False, chunks=2, lag=2):
    nt = lax.axis_size("tensor")
    has_sum = kind != "start"
    has_gather = kind != "end"
    piece = rows // chunks
    split = []
    for item in args:
        if item.shape[0] == nt * rows:
            split.append(item.reshape(nt, chunks, piece, width))
        elif item.shape[0] == rows:
            split.append(item.reshape(chunks, piece, width))
        else:
            split.append(item)
    outs = []
    if has_sum:
        outs.append(jax.ShapeDtypeStruct((chunks, piece, width), F32))
    if kind in ("bwd", "end"):
        outs.append(jax.ShapeDtypeStruct((1, width), F32))
    if has_gather:
        outs.append(jax.ShapeDtypeStruct((nt, chunks, piece, width), BF16))
    if kind == "start":
        count = lax.axis_size("dp") * nt
        outs.append(jax.ShapeDtypeStruct((count,) + args[1].shape, args[1].dtype))
    scratch = []
    sems = pltpu.SemaphoreType.DMA((nt, chunks))
    if has_sum:
        buf = pltpu.VMEM((nt, chunks, piece, width), BF16)
        scratch += [buf, buf, buf, pltpu.VMEM((piece, width), F32), sems, sems, sems]
    if has_gather:
        scratch += [sems, sems, sems]
    if kind == "start":
        scratch += [pltpu.SemaphoreType.DMA((count,))] * 2
    results = pl.pallas_call(
        functools.partial(line_kernel, kind, nt, chunks, lag, extra),
        out_shape=outs,
        in_specs=[VMEM_SPEC] * len(split),
        out_specs=[VMEM_SPEC] * len(outs),
        scratch_shapes=scratch,
        compiler_params=pltpu.CompilerParams(
            collective_id=collective_id, has_side_effects=True, vmem_limit_bytes=VMEM_LIMIT
        ),
        cost_estimate=pl.CostEstimate(
            flops=10 * nt * rows * width, bytes_accessed=100 * rows * width * nt, transcendentals=0
        ),
        name="line_" + kind,
    )(*split)
    results = list(results)
    if has_sum:
        results[0] = results[0].reshape(rows, width)
    if has_gather:
        at = 0 if kind == "start" else -1
        results[at] = results[at].reshape(nt * rows, width)
    return results


def span_mask(starts_ref, row_at, rows, cols, spans):
    row = row_at + lax.broadcasted_iota(jnp.int32, (rows, cols), 0)
    col = lax.broadcasted_iota(jnp.int32, (rows, cols), 1)
    seen = col <= row
    for k in range(spans):
        begin = starts_ref[0, k]
        seen = seen | (
            (row >= begin) & (row < begin + PIC) & (col >= begin) & (col < begin + PIC)
        )
    return seen


def key_extent(row_at, seq_len, spans):
    segment = seq_len // spans
    return (row_at // segment + 1) * segment


def attend_kernel(heads, spans, block, raw, starts_ref, a_ref, w_ref, *refs):
    if raw:
        gain_ref, qkv_ref, o_ref, lse_ref, out_ref, normed_ref = refs
        normed_ref[...] = normed(a_ref[...].astype(F32), gain_ref[...]).astype(BF16)
        a_ref = normed_ref
    else:
        qkv_ref, o_ref, lse_ref, out_ref = refs
    seq_len = a_ref.shape[0]
    wide = heads * HEAD
    factor = HEAD ** (-0.5)
    qkv_ref[...] = dot(a_ref[...], w_ref[:, : 3 * wide]).astype(BF16)
    for at in range(0, seq_len, block):
        reach = key_extent(at, seq_len, spans)
        seen = span_mask(starts_ref, at, block, reach, spans)
        for h in range(heads):
            q = qkv_ref[at : at + block, h * HEAD : (h + 1) * HEAD]
            k = qkv_ref[:reach, wide + h * HEAD : wide + (h + 1) * HEAD]
            v = qkv_ref[:reach, 2 * wide + h * HEAD : 2 * wide + (h + 1) * HEAD]
            s = jnp.where(seen, dot_nt(q, k) * factor, -1e30)
            top = jnp.max(s, axis=-1, keepdims=True)
            e = jnp.exp(s - top)
            total = jnp.sum(e, axis=-1, keepdims=True)
            probs = (e * (1.0 / total)).astype(BF16)
            o_ref[at : at + block, h * HEAD : (h + 1) * HEAD] = dot(probs, v).astype(BF16)
            lse_ref[at : at + block, h : h + 1] = top + jnp.log(total)
    out_ref[...] = dot_nt(o_ref[...], w_ref[:, 3 * wide :]).astype(BF16)


def attend_forward(starts, a_all, w_attn, heads, gain=None):
    seq_len, width = a_all.shape
    wide = heads * HEAD
    spans = starts.shape[1]
    raw = gain is not None
    return pl.pallas_call(
        functools.partial(attend_kernel, heads, spans, PIC, raw),
        out_shape=[
            jax.ShapeDtypeStruct((seq_len, 3 * wide), BF16),
            jax.ShapeDtypeStruct((seq_len, wide), BF16),
            jax.ShapeDtypeStruct((seq_len, heads), F32),
            jax.ShapeDtypeStruct((seq_len, width), BF16),
        ]
        + [jax.ShapeDtypeStruct((seq_len, width), BF16)] * raw,
        in_specs=[pl.BlockSpec(memory_space=pltpu.SMEM)] + [VMEM_SPEC] * (2 + raw),
        out_specs=[VMEM_SPEC] * (4 + raw),
        compiler_params=pltpu.CompilerParams(vmem_limit_bytes=VMEM_LIMIT),
        cost_estimate=pl.CostEstimate(
            flops=8 * seq_len * width * wide + 4 * heads * seq_len * seq_len * HEAD,
            bytes_accessed=6 * seq_len * width,
            transcendentals=heads * seq_len * seq_len,
        ),
        name="attend_forward",
    )(starts, a_all, w_attn, *([gain] if raw else []))


def attend_back_kernel(
    heads, spans, block, starts_ref, g_ref, w_ref, a_ref, qkv_ref, o_ref, lse_ref,
    ga_ref, gw_ref, go_scr, gq_scr, gk_acc, gv_acc,
):
    seq_len = a_ref.shape[0]
    wide = heads * HEAD
    factor = HEAD ** (-0.5)
    go_scr[...] = dot(g_ref[...], w_ref[:, 3 * wide :]).astype(BF16)
    gw_ref[:, 3 * wide :] = dot_tn(g_ref[...], o_ref[...]).astype(BF16)
    gk_acc[...] = jnp.zeros_like(gk_acc)
    gv_acc[...] = jnp.zeros_like(gv_acc)
    for at in range(0, seq_len, block):
        reach = key_extent(at, seq_len, spans)
        seen = span_mask(starts_ref, at, block, reach, spans)
        for h in range(heads):
            own = slice(h * HEAD, (h + 1) * HEAD)
            q = qkv_ref[at : at + block, own]
            k = qkv_ref[:reach, wide + h * HEAD : wide + (h + 1) * HEAD]
            v = qkv_ref[:reach, 2 * wide + h * HEAD : 2 * wide + (h + 1) * HEAD]
            go = go_scr[at : at + block, own]
            s = jnp.where(seen, dot_nt(q, k) * factor, -1e30)
            probs = jnp.exp(s - lse_ref[at : at + block, h : h + 1])
            gp = dot_nt(go, v)
            inner = jnp.sum(probs * gp, axis=-1, keepdims=True)
            gs = (probs * (gp - inner)).astype(BF16)
            gq_scr[at : at + block, own] = (dot(gs, k) * factor).astype(BF16)
            gk_acc[:reach, own] += dot_tn(gs, q) * factor
            gv_acc[:reach, own] += dot_tn(probs.astype(BF16), go)
    gq_scr[:, wide : 2 * wide] = gk_acc[...].astype(BF16)
    gq_scr[:, 2 * wide :] = gv_acc[...].astype(BF16)
    gw_ref[:, : 3 * wide] = dot_tn(a_ref[...], gq_scr[...]).astype(BF16)
    ga_ref[...] = dot_nt(gq_scr[...], w_ref[:, : 3 * wide]).astype(BF16)


def attend_backward(starts, g_all, w_attn, a_all, qkv, o, lse, heads):
    seq_len, width = a_all.shape
    wide = heads * HEAD
    spans = starts.shape[1]
    return pl.pallas_call(
        functools.partial(attend_back_kernel, heads, spans, PIC),
        out_shape=[
            jax.ShapeDtypeStruct((seq_len, width), BF16),
            jax.ShapeDtypeStruct((width, 4 * wide), BF16),
        ],
        in_specs=[pl.BlockSpec(memory_space=pltpu.SMEM)] + [VMEM_SPEC] * 6,
        out_specs=[VMEM_SPEC] * 2,
        scratch_shapes=[
            pltpu.VMEM((seq_len, wide), BF16),
            pltpu.VMEM((seq_len, 3 * wide), BF16),
            pltpu.VMEM((seq_len, wide), F32),
            pltpu.VMEM((seq_len, wide), F32),
        ],
        compiler_params=pltpu.CompilerParams(vmem_limit_bytes=VMEM_LIMIT),
        cost_estimate=pl.CostEstimate(
            flops=16 * seq_len * width * wide + 10 * heads * seq_len * seq_len * HEAD,
            bytes_accessed=12 * seq_len * width,
            transcendentals=heads * seq_len * seq_len,
        ),
        name="attend_backward",
    )(starts, g_all, w_attn, a_all, qkv, o, lse)


def lane_column(values, at):
    lane = lax.broadcasted_iota(jnp.int32, values.shape, 1)
    return jnp.sum(jnp.where(lane == at, values, 0), axis=1, keepdims=True)


def two_parts(values):
    high = values.astype(BF16)
    return high, (values - high.astype(F32)).astype(BF16)


def experts_kernel(
    cap, b_ref, w_ref, rowpos_ref, pos_ref, router_ref, zterm_ref,
    x_ref, gu_ref, z_ref, wd_ref, f_ref, pick_scr, y_scr,
):
    e = pl.program_id(0)
    seq_len, width = b_ref.shape
    half = gu_ref.shape[2] // 2

    @pl.when(e == 0)
    def _():
        z = dot(b_ref[...], router_ref[...]) + zterm_ref[...]
        z_ref[...] = z
        hit = pos_ref[...] >= 0
        top = jnp.max(jnp.where(hit, z, -3e38), axis=1, keepdims=True)
        ez = jnp.where(hit, jnp.exp(jnp.where(hit, z - top, 0.0)), 0.0)
        wd_ref[...] = ez / jnp.sum(ez, axis=1, keepdims=True)

    w = w_ref[...].reshape(width, 3 * half)
    take = (
        lax.broadcasted_iota(jnp.int32, (cap, seq_len), 0) == rowpos_ref[0]
    ).astype(F32).astype(BF16)
    x = dot(take, b_ref[...]).astype(BF16)
    x_ref[0] = x
    gu = dot(x, w[:, : 2 * half])
    gu_ref[0] = gu.astype(BF16)
    g, u = gu[:, :half], gu[:, half:]
    h = (g * jax.nn.sigmoid(g) * u).astype(BF16)
    y = dot_nt(h, w[:, 2 * half :])
    y_scr[pl.ds(pl.multiple_of(e * cap, cap), cap), :] = y.astype(BF16)
    column = lane_column(pos_ref[...], e)
    weight = lane_column(wd_ref[...], e)
    put = jnp.where(
        lax.broadcasted_iota(jnp.int32, (seq_len, cap), 1) == column, weight, 0.0
    ).astype(BF16)
    pick_scr[:, pl.ds(pl.multiple_of(e * cap, cap), cap)] = put

    @pl.when(e == pl.num_programs(0) - 1)
    def _():
        f_ref[...] = dot(pick_scr[...], y_scr[...]).astype(BF16)


def whole(shape):
    return pl.BlockSpec(shape, lambda e: (0,) * len(shape))


def experts_forward(b_all, w_exp, rowpos, pos, router, zterm, cap):
    seq_len, width = b_all.shape
    shards_dp, count, rows, wide3 = w_exp.shape
    half = wide3 // 3
    return pl.pallas_call(
        functools.partial(experts_kernel, cap),
        grid=(count,),
        out_shape=[
            jax.ShapeDtypeStruct((count, cap, width), BF16),
            jax.ShapeDtypeStruct((count, cap, 2 * half), BF16),
            jax.ShapeDtypeStruct((seq_len, LANES), F32),
            jax.ShapeDtypeStruct((seq_len, LANES), F32),
            jax.ShapeDtypeStruct((seq_len, width), BF16),
        ],
        in_specs=[
            whole((seq_len, width)),
            pl.BlockSpec((shards_dp, 1, rows, wide3), lambda e: (0, e, 0, 0)),
            pl.BlockSpec((1, 1, seq_len), lambda e: (e, 0, 0)),
            whole((seq_len, LANES)),
            whole((width, LANES)),
            whole((seq_len, LANES)),
        ],
        out_specs=[
            pl.BlockSpec((1, cap, width), lambda e: (e, 0, 0)),
            pl.BlockSpec((1, cap, 2 * half), lambda e: (e, 0, 0)),
            whole((seq_len, LANES)),
            whole((seq_len, LANES)),
            whole((seq_len, width)),
        ],
        scratch_shapes=[
            pltpu.VMEM((seq_len, count * cap), BF16),
            pltpu.VMEM((count * cap, width), BF16),
        ],
        compiler_params=pltpu.CompilerParams(vmem_limit_bytes=VMEM_LIMIT),
        cost_estimate=pl.CostEstimate(
            flops=count * (4 * cap * seq_len * width + 6 * cap * width * half),
            bytes_accessed=2 * count * width * wide3,
            transcendentals=0,
        ),
        name="experts_forward",
    )(b_all, w_exp, rowpos, pos, router, zterm)


def experts_back_kernel(
    cap, g_ref, w_ref, x_ref, gu_ref, rowpos_ref, pos_ref, wd_ref, gwown_ref, gprev_ref, rt_ref,
    gw_ref, gz_ref, gb_ref, pick_scr, gx_scr, gg_scr,
):
    e = pl.program_id(0)
    seq_len, width = g_ref.shape
    shards_dp, _, rows, wide3 = w_ref.shape
    half = wide3 // 3
    w = w_ref[...].reshape(width, wide3)
    take = (
        lax.broadcasted_iota(jnp.int32, (cap, seq_len), 0) == rowpos_ref[0]
    ).astype(F32).astype(BF16)
    w_high, w_low = two_parts(wd_ref[...])
    weight = lane_column(dot(take, w_high) + dot(take, w_low), e)
    gf = dot(take, g_ref[...])
    gh = dot(gf.astype(BF16), w[:, 2 * half :])
    gu = gu_ref[0].astype(F32)
    g, u = gu[:, :half], gu[:, half:]
    sig = jax.nn.sigmoid(g)
    h = (g * sig * u).astype(BF16)
    slot_grad = jnp.sum(h.astype(F32) * gh, axis=1, keepdims=True)
    gh = gh * weight
    gg = gh * u * sig * (1.0 + g * (1.0 - sig))
    gup = gh * g * sig
    both = jnp.concatenate([gg.astype(BF16), gup.astype(BF16)], axis=1)
    gy = (gf * weight).astype(BF16)
    gw_ref[:, 0, :, : 2 * half] = dot_tn(x_ref[0], both).astype(BF16).reshape(
        shards_dp, rows, 2 * half
    )
    gw_ref[:, 0, :, 2 * half :] = dot_tn(gy, h).astype(BF16).reshape(shards_dp, rows, half)
    here = pl.ds(pl.multiple_of(e * cap, cap), cap)
    gx_scr[here, :] = dot_nt(both, w[:, : 2 * half]).astype(BF16)
    s_high, s_low = two_parts(slot_grad)
    lane = lax.broadcasted_iota(jnp.int32, (cap, LANES), 1)
    gg_scr[here, :LANES] = jnp.where(lane == e, s_high.astype(F32), 0.0).astype(BF16)
    gg_scr[here, LANES:] = jnp.where(lane == e, s_low.astype(F32), 0.0).astype(BF16)
    column = lane_column(pos_ref[...], e)
    pick_scr[:, here] = (
        lax.broadcasted_iota(jnp.int32, (seq_len, cap), 1) == column
    ).astype(F32).astype(BF16)

    @pl.when(e == pl.num_programs(0) - 1)
    def _():
        slots = dot(pick_scr[...], gg_scr[...])
        gw = slots[:, :LANES] + slots[:, LANES:] + gwown_ref[...]
        wd = wd_ref[...]
        gz = wd * (gw - jnp.sum(wd * gw, axis=1, keepdims=True)) + gprev_ref[...]
        gz_ref[...] = gz
        z_high, z_low = two_parts(gz)
        gb = dot(pick_scr[...], gx_scr[...]) + dot(z_high, rt_ref[...]) + dot(z_low, rt_ref[...])
        gb_ref[...] = gb.astype(BF16)


def experts_backward(g_all, w_exp, x, gu, rowpos, pos, wd, gw_own, grad_prev, router_t, cap):
    seq_len, width = g_all.shape
    shards_dp, count, rows, wide3 = w_exp.shape
    half = wide3 // 3
    weight_spec = pl.BlockSpec((shards_dp, 1, rows, wide3), lambda e: (0, e, 0, 0))
    return pl.pallas_call(
        functools.partial(experts_back_kernel, cap),
        grid=(count,),
        out_shape=[
            jax.ShapeDtypeStruct(w_exp.shape, BF16),
            jax.ShapeDtypeStruct((seq_len, LANES), F32),
            jax.ShapeDtypeStruct((seq_len, width), BF16),
        ],
        in_specs=[
            whole((seq_len, width)),
            weight_spec,
            pl.BlockSpec((1, cap, width), lambda e: (e, 0, 0)),
            pl.BlockSpec((1, cap, 2 * half), lambda e: (e, 0, 0)),
            pl.BlockSpec((1, 1, seq_len), lambda e: (e, 0, 0)),
            whole((seq_len, LANES)),
            whole((seq_len, LANES)),
            whole((seq_len, LANES)),
            whole((seq_len, LANES)),
            whole((LANES, width)),
        ],
        out_specs=[weight_spec, whole((seq_len, LANES)), whole((seq_len, width))],
        scratch_shapes=[
            pltpu.VMEM((seq_len, count * cap), BF16),
            pltpu.VMEM((count * cap, width), BF16),
            pltpu.VMEM((count * cap, 2 * LANES), BF16),
        ],
        compiler_params=pltpu.CompilerParams(vmem_limit_bytes=VMEM_LIMIT),
        cost_estimate=pl.CostEstimate(
            flops=count * (4 * cap * seq_len * width + 12 * cap * width * half),
            bytes_accessed=4 * count * width * wide3,
            transcendentals=0,
        ),
        name="experts_backward",
    )(g_all, w_exp, x, gu, rowpos, pos, wd, gw_own, grad_prev, router_t)


def lanes(values):
    return jnp.pad(values, ((0, 0), (0, LANES - values.shape[1])))


def slot_table(route_ids):
    tokens = route_ids.shape[0]
    codes = jnp.arange(LANES, dtype=jnp.int32)
    hit = jnp.any(route_ids[:, :, None] == codes[None, None, :], axis=1)
    place = jnp.arange(tokens, dtype=jnp.int32)
    before = (place[None, :] < place[:, None]).astype(BF16)
    slots = dot(before, hit.astype(BF16)).astype(jnp.int32)
    return jnp.where(hit, slots, -1)


def shards(
    hidden_in,
    prev_logits,
    routes,
    span_starts,
    attn_norm,
    qkv_weight,
    out_weight,
    moe_norm,
    router,
    gate_mix,
    const_vec,
    const_mix,
    up_weight,
    down_weight,
    out_grad,
):
    layers = qkv_weight.shape[0]
    own, width = hidden_in.shape
    nt = lax.axis_size("tensor")
    ndp = lax.axis_size("dp")
    seq_len = own * nt
    offset = lax.axis_index("tensor") * own
    cap = seq_len // 4
    heads = qkv_weight.shape[3] // HEAD
    wide = heads * HEAD
    half = up_weight.shape[4]
    rows = qkv_weight.shape[1]
    cols = attn_norm.shape[1]
    consts = const_vec.shape[1]

    packed = jnp.concatenate(
        [attn_norm.T, moe_norm.T]
        + [router[l] for l in range(layers)]
        + [const_vec.reshape(-1, cols).T]
        + [const_mix[l, j] for l in range(layers) for j in range(consts)],
        axis=1,
    )
    hidden = hidden_in.astype(F32)
    x_all, small = line_exchange("start", [hidden_in, lanes(packed)], own, width, 0)
    small = small.reshape(width, LANES)
    at = 0
    fields = {}
    for name, size in (
        ("attn", layers),
        ("moe", layers),
        ("router", layers * NEXP),
        ("cvec", layers * consts),
        ("cmix", layers * consts * 2),
    ):
        fields[name] = (at, size)
        at += size

    def field(name, l, per):
        begin = fields[name][0] + l * per
        return small[:, begin : begin + per]

    attn_w, exp_w = [], []
    for l in range(layers):
        local = jnp.concatenate(
            [qkv_weight[l].reshape(rows, 3 * wide), out_weight[l].T], axis=1
        )
        attn_w.append(lax.all_gather(local, "dp", axis=0, tiled=False).reshape(width, 4 * wide))
        local = jnp.concatenate(
            [
                up_weight[l].reshape(EXPERTS, rows, 2 * half),
                jnp.swapaxes(down_weight[l], 1, 2),
            ],
            axis=2,
        )
        exp_w.append(lax.all_gather(local, "dp", axis=0, tiled=False))

    pos = [slot_table(routes[l]) for l in range(layers)]
    rowpos = [p[:, :EXPERTS].T[:, None, :] for p in pos]

    a_all = None
    z_prev = lanes(prev_logits)
    next_id = 2
    stored = []
    for l in range(layers):
        mix = jnp.pad(gate_mix[l].astype(F32), ((0, LANES - NEXP), (0, LANES - NEXP)))
        zterm = jnp.dot(z_prev, mix, precision=HIGH)
        if l == 0:
            gain = field("attn", 0, 1).astype(F32).T
            qkv, o, lse, partial, a_all = attend_forward(
                span_starts, x_all, attn_w[l], heads, gain
            )
        else:
            qkv, o, lse, partial = attend_forward(span_starts, a_all, attn_w[l], heads)
        gain = field("moe", l, 1).astype(F32).T
        mid, b_all = line_exchange("fwd", [partial, hidden, gain], own, width, next_id)
        router_l = lanes(field("router", l, NEXP))
        x, gu, z, wd, partial = experts_forward(
            b_all, exp_w[l], rowpos[l], pos[l], router_l, zterm, cap
        )
        b_own = lax.dynamic_slice_in_dim(b_all, offset, own, 0)
        cmix = field("cmix", l, 2 * consts)
        cvec = field("cvec", l, consts).astype(F32).T
        logit = dot(b_own, cmix)
        alpha = jax.nn.softmax(logit.reshape(own, consts, 2), axis=2)
        gates = lax.dynamic_slice_in_dim(wd, offset, own, 0)
        copy_gate = gates[:, EXPERTS + 1 : EXPERTS + 2]
        const_gate = gates[:, EXPERTS + 2 : EXPERTS + 2 + consts]
        keep = copy_gate + jnp.sum(const_gate * alpha[:, :, 0], axis=1, keepdims=True)
        inject = const_gate * alpha[:, :, 1]
        side = keep * b_own.astype(F32)
        for j in range(consts):
            side = side + inject[:, j : j + 1] * cvec[j : j + 1]
        stored.append(
            dict(
                hidden=hidden, a_all=a_all, qkv=qkv, o=o, lse=lse, mid=mid, b_all=b_all,
                b_own=b_own, x=x, gu=gu, wd=wd, z_prev=z_prev, alpha=alpha,
                const_gate=const_gate, keep=keep, inject=inject, cvec=cvec, cmix=cmix, mix=mix,
                router=router_l,
            )
        )
        if l + 1 < layers:
            gain = field("attn", l + 1, 1).astype(F32).T
            hidden, a_all = line_exchange("fwd", [partial, mid + side, gain], own, width, next_id + 1)
        else:
            hidden, g_all = line_exchange(
                "last", [partial, mid + side, out_grad], own, width, next_id + 1
            )
        z_prev = z
        next_id += 2
    hidden_out = hidden

    grad = out_grad.astype(F32)
    grad_prev = jnp.zeros((seq_len, LANES), F32)
    attn_grads, exp_grads = [None] * layers, [None] * layers
    gains_a, gains_m = [None] * layers, [None] * layers
    routers, cvecs, cmixes, mixes = ([None] * layers for _ in range(4))
    for l in reversed(range(layers)):
        s = stored[l]
        b_own = s["b_own"].astype(F32)
        bg = jnp.sum(b_own * grad, axis=1, keepdims=True)
        cg = jnp.concatenate(
            [jnp.sum(grad * s["cvec"][j : j + 1], axis=1, keepdims=True) for j in range(consts)],
            axis=1,
        )
        alpha = s["alpha"]
        gw_const = alpha[:, :, 0] * bg + alpha[:, :, 1] * cg
        gw_own = jnp.pad(
            jnp.concatenate([bg, gw_const], axis=1),
            ((0, 0), (EXPERTS + 1, LANES - EXPERTS - 2 - consts)),
        )
        gw_own = lax.dynamic_update_slice_in_dim(
            jnp.zeros((seq_len, LANES), F32), gw_own, offset, 0
        )
        ga = s["const_gate"][:, :, None] * jnp.stack([jnp.broadcast_to(bg, cg.shape), cg], axis=2)
        gt = alpha * (ga - jnp.sum(alpha * ga, axis=2, keepdims=True))
        gt = gt.reshape(own, 2 * consts)
        own_part = s["keep"] * grad
        cmix_f = s["cmix"].astype(F32).T
        for j in range(2 * consts):
            own_part = own_part + gt[:, j : j + 1] * cmix_f[j : j + 1]
        cmixes[l] = lax.dot_general(b_own, gt, (((0,), (0,)), ((), ())), precision=HIGH)
        cvecs[l] = lax.dot_general(grad, s["inject"], (((0,), (0,)), ((), ())), precision=HIGH)

        gw_exp, gz, partial = experts_backward(
            g_all, exp_w[l], s["x"], s["gu"], rowpos[l], pos[l], s["wd"], gw_own, grad_prev,
            s["router"].T, cap,
        )
        exp_grads[l] = lax.psum_scatter(gw_exp, "dp", scatter_dimension=0, tiled=False)
        if l + 1 < layers:
            partial, exp_grads[l + 1] = lax.optimization_barrier((partial, exp_grads[l + 1]))
        z_high, z_low = two_parts(gz)
        routers[l] = (dot_tn(s["b_all"], z_high) + dot_tn(s["b_all"], z_low))[:, :NEXP]
        mixes[l] = lax.dot_general(
            s["z_prev"], gz, (((0,), (0,)), ((), ())), precision=HIGH
        )[:NEXP, :NEXP]
        if l > 0:
            grad_prev = lax.dot_general(gz, s["mix"], (((1,), (1,)), ((), ())), precision=HIGH)
        gain = field("moe", l, 1).astype(F32).T
        grad_mid, gains_m[l], g_all = line_exchange(
            "bwd", [partial, own_part, s["mid"], grad, gain], own, width, next_id, extra=True
        )
        partial, gw_attn = attend_backward(
            span_starts, g_all, attn_w[l], s["a_all"], s["qkv"], s["o"], s["lse"], heads
        )
        attn_grads[l] = gw_attn.reshape(ndp, rows, 4 * wide)
        gain = field("attn", l, 1).astype(F32).T
        if l > 0:
            grad, gains_a[l], g_all = line_exchange(
                "bwd", [partial, s["hidden"], grad_mid, gain], own, width, next_id + 1
            )
        else:
            grad, gains_a[l] = line_exchange(
                "end", [partial, s["hidden"], grad_mid, gain], own, width, next_id + 1
            )
        next_id += 2

    sums = jnp.concatenate(
        [item.T for item in gains_a]
        + [item.T for item in gains_m]
        + routers
        + cvecs
        + cmixes,
        axis=1,
    )
    sums = lanes(sums).reshape(ndp * nt, cols, LANES)
    flat = jnp.stack(mixes).reshape(-1)
    mix_rows = -(-flat.shape[0] // LANES)
    flat = jnp.pad(flat, (0, mix_rows * LANES - flat.shape[0])).reshape(1, mix_rows, LANES)
    flat = jnp.broadcast_to(flat, (ndp * nt, mix_rows, LANES))
    total, *attn_grads = closing(jnp.concatenate([sums, flat], axis=1), *attn_grads, next_id)
    mix_total = total[cols:].reshape(-1)[: layers * NEXP * NEXP].reshape(layers, NEXP, NEXP)
    total = total[:cols]

    def back(name):
        begin, size = fields[name]
        return total[:, begin : begin + size]

    router_grad = jnp.swapaxes(back("router").reshape(cols, layers, NEXP), 0, 1)
    cmix_grad = jnp.transpose(back("cmix").reshape(cols, layers, consts, 2), (1, 2, 0, 3))
    cvec_grad = back("cvec").T.reshape(layers, consts, cols)
    qkv_grad = jnp.stack(
        [item[:, : 3 * wide].reshape(rows, 3, wide) for item in attn_grads]
    )
    outw_grad = jnp.stack([item[:, 3 * wide :].T for item in attn_grads])
    up_grad = jnp.stack(
        [item[:, :, : 2 * half].reshape(EXPERTS, rows, 2, half) for item in exp_grads]
    ).astype(F32)
    down_grad = jnp.stack(
        [jnp.swapaxes(item[:, :, 2 * half :], 1, 2) for item in exp_grads]
    ).astype(F32)
    return (
        hidden_out,
        grad,
        back("attn").T,
        qkv_grad,
        outw_grad,
        back("moe").T,
        router_grad,
        mix_total,
        cvec_grad,
        cmix_grad,
        up_grad,
        down_grad,
    )


def solution(mesh):
    return jax.shard_map(
        shards,
        mesh=mesh,
        in_specs=(
            P(("dp", "tensor"), None),
            P("dp", None),
            P(None, "dp", None),
            P("dp", None),
            P(None, ("dp", "tensor")),
            P(None, "dp", None, "tensor"),
            P(None, "tensor", "dp"),
            P(None, ("dp", "tensor")),
            P(None, ("dp", "tensor"), None),
            P(),
            P(None, None, ("dp", "tensor")),
            P(None, None, ("dp", "tensor"), None),
            P(None, None, "dp", None, "tensor"),
            P(None, None, "tensor", "dp"),
            P(("dp", "tensor"), None),
        ),
        out_specs=(
            P(("dp", "tensor"), None),
            P(("dp", "tensor"), None),
            P(None, ("dp", "tensor")),
            P(None, "dp", None, "tensor"),
            P(None, "tensor", "dp"),
            P(None, ("dp", "tensor")),
            P(None, ("dp", "tensor"), None),
            P(),
            P(None, None, ("dp", "tensor")),
            P(None, None, ("dp", "tensor"), None),
            P(None, None, "dp", None, "tensor"),
            P(None, None, "tensor", "dp"),
        ),
        check_vma=False,
    )
```

```python
import functools

import jax
import jax.numpy as jnp
from jax import lax
from jax.experimental import pallas as pl
from jax.experimental.pallas import tpu as pltpu
from jax.sharding import PartitionSpec as P

HEAD = 64
EXPERTS = 8
NEXP = 12
TOPK = 2
PIC = 256
LANES = 128

EPS = 1e-06
HIGH = lax.Precision.HIGHEST
MESH = pl.DeviceIdType.MESH
F32 = jnp.float32
BF16 = jnp.bfloat16
VMEM_SPEC = pl.BlockSpec(memory_space=pltpu.VMEM)
AHEAD = 2
PIECES = 16
LAG = 2
MIX_STEP = 16
VMEM_LIMIT = 60 * 1024 * 1024


def dot(a, b):
    return jnp.dot(a, b, preferred_element_type=F32)


def dot_nt(a, b):
    return lax.dot_general(a, b, (((1,), (1,)), ((), ())), preferred_element_type=F32)


def dot_tn(a, b):
    return lax.dot_general(a, b, (((0,), (0,)), ((), ())), preferred_element_type=F32)


def layout(layers, consts):
    at, begin = {}, 0
    for name, size in (
        ("attn", layers),
        ("moe", layers),
        ("router", layers * NEXP),
        ("cvec", layers * consts),
        ("cmix", layers * consts * 2),
    ):
        at[name] = begin
        begin += size
    return at


def shift(values, lanes_up):
    return pltpu.roll(values, lanes_up % LANES, 1)


def greet_all(count, me, place):
    barrier = pltpu.get_barrier_semaphore()

    def greet(step, carry):
        other = lax.rem(me + step, count)
        pl.semaphore_signal(barrier, inc=1, device_id=place(other), device_id_type=MESH)
        return carry

    lax.fori_loop(1, count, greet, 0)
    pl.semaphore_wait(barrier, count - 1)


def swap_all(count, me, place, source, land, send_sems, recv_sems):
    def copy(other, slot):
        return pltpu.make_async_remote_copy(
            src_ref=source(other),
            dst_ref=land.at[slot],
            send_sem=send_sems.at[other],
            recv_sem=recv_sems.at[slot],
            device_id=place(other),
            device_id_type=MESH,
        )

    def start():
        def send(step, carry):
            other = lax.rem(me + step, count)
            copy(other, me).start()
            return carry

        lax.fori_loop(1, count, send, 0)

    def finish():
        def wait(step, carry):
            other = lax.rem(me + count - step, count)
            copy(other, other).wait()
            return carry

        lax.fori_loop(1, count, wait, 0)

    return start, finish


def closing_kernel(ndp, inner, layers, consts, wide, *refs):
    small_ref, proj_refs = refs[0], refs[1 : 1 + layers]
    refs = refs[1 + layers :]
    attn_out, moe_out, router_out, mix_out, cvec_out, cmix_out, qkv_out, outw_out = refs[:8]
    land, proj_lands = refs[8], refs[9 : 9 + layers]
    square, tall = refs[9 + layers : 11 + layers]
    sems = refs[11 + layers :]
    count = ndp * inner
    row, col = lax.axis_index("dp"), lax.axis_index("tensor")
    me = row * inner + col
    cols = attn_out.shape[1]
    rows = qkv_out.shape[1]

    def anywhere(other):
        return (lax.div(other, inner), lax.rem(other, inner))

    def along(other):
        return (other, col)

    def piece(ref):
        return lambda other: ref.at[other]

    greet_all(count, me, anywhere)
    moves = [
        swap_all(ndp, row, along, piece(ref), to, *sems[2 + 2 * l : 4 + 2 * l])
        for l, (ref, to) in enumerate(zip(proj_refs, proj_lands))
    ] + [swap_all(count, me, anywhere, piece(small_ref), land, *sems[0:2])]
    for start, _ in moves:
        start()
    land[me] = small_ref[me]
    for ref, to in zip(proj_refs, proj_lands):
        to[row] = ref[row]
    square[...] = jnp.zeros_like(square)
    tall[...] = jnp.zeros_like(tall)
    for l in range(layers):
        moves[l][1]()
        total = jnp.sum(proj_lands[l][...].astype(F32), axis=0)
        for part in range(3):
            qkv_out[l, :, part, :] = total[:, part * wide : (part + 1) * wide]
        tall[:rows, :wide] = total[:, 3 * wide :]
        outw_out[l] = tall[...].T[:wide, :rows]
    moves[layers][1]()
    total = jnp.sum(land[...], axis=0)
    square[:cols, :] = total[:cols]
    turned = square[...].T
    at = layout(layers, consts)
    attn_out[...] = turned[at["attn"] : at["attn"] + layers, :cols]
    moe_out[...] = turned[at["moe"] : at["moe"] + layers, :cols]
    for l in range(layers):
        begin = at["router"] + l * NEXP
        router_out[l] = total[:cols, begin : begin + NEXP]
        mix_out[l] = total[cols : cols + NEXP, l * MIX_STEP : l * MIX_STEP + NEXP]
        begin = at["cvec"] + l * consts
        cvec_out[l] = turned[begin : begin + consts, :cols]
        begin = at["cmix"] + l * 2 * consts
        for j in range(consts):
            for k in range(2):
                lane = begin + k * consts + j
                cmix_out[l, j, :, k : k + 1] = total[:cols, lane : lane + 1]


def closing(small, projections, consts, cols, collective_id):
    inner, ndp = lax.axis_size("tensor"), lax.axis_size("dp")
    layers = len(projections)
    rows, packed = projections[0].shape[1:]
    wide = packed // 4
    pair = [pltpu.SemaphoreType.DMA((ndp * inner,))] * 2
    shapes = [
        (layers, cols), (layers, cols), (layers, cols, NEXP), (layers, NEXP, NEXP),
        (layers, consts, cols), (layers, consts, cols, 2),
        (layers, rows, 3, wide), (layers, wide, rows),
    ]
    return pl.pallas_call(
        functools.partial(closing_kernel, ndp, inner, layers, consts, wide),
        out_shape=[jax.ShapeDtypeStruct(shape, F32) for shape in shapes],
        in_specs=[VMEM_SPEC] * (1 + layers),
        out_specs=[VMEM_SPEC] * len(shapes),
        scratch_shapes=[pltpu.VMEM(small.shape, F32)]
        + [pltpu.VMEM(item.shape, BF16) for item in projections]
        + [
            pltpu.VMEM((-(-cols // LANES) * LANES, LANES), F32),
            pltpu.VMEM((-(-rows // LANES) * LANES, -(-wide // LANES) * LANES), F32),
        ]
        + pair
        + [pltpu.SemaphoreType.DMA((ndp,))] * (2 * layers),
        compiler_params=pltpu.CompilerParams(
            collective_id=collective_id, has_side_effects=True, vmem_limit_bytes=VMEM_LIMIT
        ),
        name="closing",
    )(small, *projections)


def join_kernel(back, gain_row, nt, pieces, lag, *refs):
    if back:
        part, base_ref, skip_ref, rows_ref, result_ref, gg_ref = refs[:6]
    else:
        part, base_ref, rows_ref, total_ref, normed_ref = refs[:5]
    refs = refs[6 if back else 5 :]
    inbox, half, across, full, out_sem, in_sem, cross_out, cross_in, full_out, full_in = refs
    me = lax.axis_index("tensor")
    is_end = (me == 0) | (me == nt - 1)
    buddy = jnp.where(me < 2, 1 - me, 5 - me)
    cross = 3 - me

    barrier = pltpu.get_barrier_semaphore()
    pl.semaphore_signal(barrier, inc=1, device_id={"tensor": buddy}, device_id_type=MESH)

    @pl.when(jnp.logical_not(is_end))
    def _():
        pl.semaphore_signal(barrier, inc=1, device_id={"tensor": cross}, device_id_type=MESH)

    pl.semaphore_wait(barrier, 2 - is_end.astype(jnp.int32))

    def copy(src, dst, send_sem, recv_sem, to):
        return pltpu.make_async_remote_copy(
            src_ref=src,
            dst_ref=dst,
            send_sem=send_sem,
            recv_sem=recv_sem,
            device_id={"tensor": to},
            device_id_type=MESH,
        )

    def inward(n):
        return copy(part.at[n], inbox.at[n], out_sem.at[n], in_sem.at[n], buddy)

    def over(n):
        return copy(half.at[n], across.at[n], cross_out.at[n], cross_in.at[n], cross)

    def outward(n):
        return copy(full.at[n], full.at[n], full_out.at[n], full_in.at[n], buddy)

    gain = rows_ref[gain_row : gain_row + 1, :]
    if back:
        gg_ref[...] = jnp.zeros_like(gg_ref)

    def settle(n):
        total = full[n].astype(F32)
        base = base_ref[n].astype(F32)
        if back:
            scale = lax.rsqrt(jnp.mean(base * base, axis=-1, keepdims=True) + EPS)
            unit = base * scale
            grad_unit = total * gain
            below = scale * (grad_unit - unit * jnp.mean(grad_unit * unit, axis=-1, keepdims=True))
            result_ref[n] = (below + skip_ref[n].astype(F32)).astype(BF16)

            @pl.when(lax.div(n, pieces // nt) == me)
            def _():
                gg_ref[...] += jnp.sum(total * unit, axis=0, keepdims=True)
        else:
            total = total + base
            total_ref[n] = total.astype(BF16)
            normed_ref[n] = normed(total, gain).astype(BF16)

    @pl.when(is_end)
    def _():
        for n in range(pieces):
            inward(n).start()

        def take(n, carry):
            outward(n).wait_recv()
            settle(n)
            return carry

        lax.fori_loop(0, pieces, take, 0)
        for n in range(pieces):
            inward(n).wait_send()

    @pl.when(jnp.logical_not(is_end))
    def _():
        def step(at, carry):
            @pl.when(at < pieces)
            def _():
                inward(at).wait_recv()
                half[at] = (part[at].astype(F32) + inbox[at].astype(F32)).astype(BF16)
                over(at).start()

            @pl.when(at >= lag)
            def _():
                n = at - lag
                over(n).wait_recv()
                full[n] = (half[n].astype(F32) + across[n].astype(F32)).astype(BF16)
                outward(n).start()
                settle(n)

            return carry

        lax.fori_loop(0, pieces + lag, step, 0)
        for n in range(pieces):
            over(n).wait_send()
            outward(n).wait_send()


def join(back, part, others, rows, gain_row, collective_id, pieces=PIECES, lag=LAG):
    nt = lax.axis_size("tensor")
    seq_len, width = part.shape
    cut = (pieces, seq_len // pieces, width)
    outs = [jax.ShapeDtypeStruct(cut, BF16)]
    outs.append(jax.ShapeDtypeStruct((1, width) if back else cut, F32 if back else BF16))
    sems = pltpu.SemaphoreType.DMA((pieces,))
    results = pl.pallas_call(
        functools.partial(join_kernel, back, gain_row, nt, pieces, lag),
        out_shape=outs,
        in_specs=[VMEM_SPEC] * (2 + len(others)),
        out_specs=[VMEM_SPEC] * 2,
        scratch_shapes=[pltpu.VMEM(cut, BF16)] * 4 + [sems] * 6,
        compiler_params=pltpu.CompilerParams(
            collective_id=collective_id, has_side_effects=True, vmem_limit_bytes=VMEM_LIMIT
        ),
        cost_estimate=pl.CostEstimate(
            flops=10 * seq_len * width, bytes_accessed=100 * seq_len * width, transcendentals=0
        ),
        name="join_back" if back else "join",
    )(part.reshape(cut), *[item.reshape(cut) for item in others], rows)
    return results[0].reshape(seq_len, width), (
        results[1] if back else results[1].reshape(seq_len, width)
    )


def normed(values, gain):
    return values * lax.rsqrt(jnp.mean(values * values, axis=-1, keepdims=True) + EPS) * gain


def line_kernel(kind, nt, chunks, lag, extra, *refs):
    refs = list(refs)
    has_sum = kind != "start"
    has_gather = kind != "end"
    part = refs.pop(0) if has_sum else None
    if kind == "start":
        x_ref, small_ref = refs.pop(0), refs.pop(0)
    elif kind == "fwd":
        extra_ref, gain_ref = refs.pop(0), refs.pop(0)
    elif kind == "last":
        extra_ref, og_ref = refs.pop(0), refs.pop(0)
    else:
        extra_ref = refs.pop(0) if extra else None
        base_ref, skip_ref, rows_ref = refs.pop(0), refs.pop(0), refs.pop(0)
    own_ref = refs.pop(0) if has_sum else None
    gg_ref = refs.pop(0) if kind in ("bwd", "end") else None
    all_ref = refs.pop(0) if has_gather else None
    land_ref = refs.pop(0) if kind == "start" else None
    if has_sum:
        from_left, from_right, tx, acc, rs_send, rl_sem, rr_sem = refs[:7]
        refs = refs[7:]
    if has_gather:
        ag_right, ag_left, ag_recv = refs[:3]
        refs = refs[3:]

    me = lax.axis_index("tensor")
    has_l, has_r = me > 0, me < nt - 1
    left, right = jnp.maximum(me - 1, 0), jnp.minimum(me + 1, nt - 1)

    if kind == "start":
        count = lax.axis_size("dp") * nt
        me_all = lax.axis_index("dp") * nt + me

        def place(other):
            return (lax.div(other, nt), lax.rem(other, nt))

        greet_all(count, me_all, place)
        small_start, small_finish = swap_all(
            count, me_all, place, lambda other: small_ref, land_ref, *refs[:2]
        )
        small_start()
        land_ref[me_all] = small_ref[...]
    else:
        barrier = pltpu.get_barrier_semaphore()

        @pl.when(has_l)
        def _():
            pl.semaphore_signal(barrier, inc=1, device_id={"tensor": left}, device_id_type=MESH)

        @pl.when(has_r)
        def _():
            pl.semaphore_signal(barrier, inc=1, device_id={"tensor": right}, device_id_type=MESH)

        pl.semaphore_wait(barrier, has_l.astype(jnp.int32) + has_r.astype(jnp.int32))

    def copy(src, dst, send_sem, recv_sem, to):
        return pltpu.make_async_remote_copy(
            src_ref=src,
            dst_ref=dst,
            send_sem=send_sem,
            recv_sem=recv_sem,
            device_id={"tensor": to},
            device_id_type=MESH,
        )

    def sum_right(j, c, src):
        return copy(src, from_left.at[j, c], rs_send.at[j, c], rl_sem.at[j, c], right)

    def sum_left(j, c, src):
        return copy(src, from_right.at[j, c], rs_send.at[j, c], rr_sem.at[j, c], left)

    def spread_right(j, c):
        block = all_ref.at[j, c]
        return copy(block, block, ag_right.at[j, c], ag_recv.at[j, c], right)

    def spread_left(j, c):
        block = all_ref.at[j, c]
        return copy(block, block, ag_left.at[j, c], ag_recv.at[j, c], left)

    def offer(c):
        @pl.when(has_r)
        def _():
            spread_right(me, c).start()

        @pl.when(has_l)
        def _():
            spread_left(me, c).start()

    def pass_on(c, d):
        @pl.when(me - d >= 0)
        def _():
            j = me - d
            spread_right(j, c).wait_recv()

            @pl.when(has_r)
            def _():
                spread_right(j, c).start()

        @pl.when(me + d < nt)
        def _():
            j = me + d
            spread_left(j, c).wait_recv()

            @pl.when(has_l)
            def _():
                spread_left(j, c).start()

    hops = nt - 1

    count = hops * chunks

    def relay(step):
        k = jnp.clip(step - lag * me, 0, count - 1)
        c, j = lax.div(k, hops), hops - lax.rem(k, hops)

        @pl.when(has_l & (step >= lag * me) & (step - lag * me < count) & (me < j))
        def _():
            sum_right(j, c, tx.at[j, c]).wait_recv()
            tx[j, c] = (part[j, c].astype(F32) + from_left[j, c].astype(F32)).astype(BF16)
            sum_right(j, c, tx.at[j, c]).start()

        far = lag * (hops - me)
        k_down = jnp.clip(step - far, 0, count - 1)
        c_down, j_down = lax.div(k_down, hops), lax.rem(k_down, hops)

        @pl.when(has_r & (step >= far) & (step - far < count) & (me > j_down))
        def _():
            sum_left(j_down, c_down, tx.at[j_down, c_down]).wait_recv()
            tx[j_down, c_down] = (
                part[j_down, c_down].astype(F32) + from_right[j_down, c_down].astype(F32)
            ).astype(BF16)
            sum_left(j_down, c_down, tx.at[j_down, c_down]).start()

    def push(first, last):
        ks = range(min(first, count), min(last, count))

        @pl.when(jnp.logical_not(has_l))
        def _():
            for k in ks:
                j, c = hops - k % hops, k // hops
                sum_right(j, c, part.at[j, c]).start()

        @pl.when(jnp.logical_not(has_r))
        def _():
            for k in ks:
                j, c = k % hops, k // hops
                sum_left(j, c, part.at[j, c]).start()

    def own_rows(c):
        acc[...] = part[me, c].astype(F32)

        @pl.when(has_l)
        def _():
            sum_right(me, c, tx.at[me, c]).wait_recv()
            acc[...] += from_left[me, c].astype(F32)

        @pl.when(has_r)
        def _():
            sum_left(me, c, tx.at[me, c]).wait_recv()
            acc[...] += from_right[me, c].astype(F32)

        total = acc[...]
        if kind == "fwd":
            total = total + extra_ref[c]
            all_ref[me, c] = normed(total, gain_ref[...]).astype(BF16)
            own_ref[c] = total
        elif kind == "last":
            own_ref[c] = total + extra_ref[c]
        else:
            if extra:
                total = total + extra_ref[c]
            base = base_ref[c].astype(F32)
            scale = lax.rsqrt(jnp.mean(base * base, axis=-1, keepdims=True) + EPS)
            unit = base * scale
            grad_unit = total * rows_ref[0:1, :]
            below = scale * (grad_unit - unit * jnp.mean(grad_unit * unit, axis=-1, keepdims=True))
            result = below + skip_ref[c].astype(F32)
            if has_gather:
                all_ref[me, c] = result.astype(BF16)
            own_ref[c] = result
            gg = jnp.sum(total * unit, axis=0, keepdims=True)
            if c == 0:
                gg_ref[...] = gg
            else:
                gg_ref[...] += gg
        if kind in ("fwd", "bwd"):
            offer(c)

    if kind == "start":
        for c in range(chunks):
            all_ref[me, c] = x_ref[c]
            offer(c)
        for c in range(chunks):
            for d in range(1, nt):
                pass_on(c, d)
        small_finish()
    else:

        push(0, AHEAD)
        if kind == "last":
            for c in range(chunks):
                all_ref[me, c] = og_ref[c]
            for c in range(chunks):
                offer(c)
        delay = 0 if kind == "last" else hops * lag
        spreads = {}
        for c in range(chunks if has_gather else 0):
            for d in range(1, nt):
                spreads.setdefault(delay + hops * c + lag * d, []).append((c, d))
        final = max([hops * (chunks - 1 + lag)] + list(spreads))
        for step in range(1, final + 1):
            push(step + AHEAD - 1, step + AHEAD)
            relay(step)
            for c, d in spreads.get(step, ()):
                pass_on(c, d)
            if step % hops == 0 and 0 <= step // hops - lag < chunks:
                own_rows(step // hops - lag)

    for c in range(chunks):
        for j in range(nt):
            if has_sum:

                @pl.when(me < j)
                def _():
                    sum_right(j, c, tx.at[j, c]).wait_send()

                @pl.when(me > j)
                def _():
                    sum_left(j, c, tx.at[j, c]).wait_send()

            if has_gather:

                @pl.when(has_r & (j <= me))
                def _():
                    spread_right(j, c).wait_send()

                @pl.when(has_l & (j >= me))
                def _():
                    spread_left(j, c).wait_send()


def line_exchange(kind, args, rows, width, collective_id, extra=False, chunks=2, lag=2):
    nt = lax.axis_size("tensor")
    has_sum = kind != "start"
    has_gather = kind != "end"
    piece = rows // chunks
    split = []
    for item in args:
        if item.shape[0] == nt * rows:
            split.append(item.reshape(nt, chunks, piece, width))
        elif item.shape[0] == rows:
            split.append(item.reshape(chunks, piece, width))
        else:
            split.append(item)
    outs = []
    if has_sum:
        outs.append(jax.ShapeDtypeStruct((chunks, piece, width), F32))
    if kind in ("bwd", "end"):
        outs.append(jax.ShapeDtypeStruct((1, width), F32))
    if has_gather:
        outs.append(jax.ShapeDtypeStruct((nt, chunks, piece, width), BF16))
    if kind == "start":
        count = lax.axis_size("dp") * nt
        outs.append(jax.ShapeDtypeStruct((count,) + args[1].shape, args[1].dtype))
    scratch = []
    sems = pltpu.SemaphoreType.DMA((nt, chunks))
    if has_sum:
        buf = pltpu.VMEM((nt, chunks, piece, width), BF16)
        scratch += [buf, buf, buf, pltpu.VMEM((piece, width), F32), sems, sems, sems]
    if has_gather:
        scratch += [sems, sems, sems]
    if kind == "start":
        scratch += [pltpu.SemaphoreType.DMA((count,))] * 2
    results = pl.pallas_call(
        functools.partial(line_kernel, kind, nt, chunks, lag, extra),
        out_shape=outs,
        in_specs=[VMEM_SPEC] * len(split),
        out_specs=[VMEM_SPEC] * len(outs),
        scratch_shapes=scratch,
        compiler_params=pltpu.CompilerParams(
            collective_id=collective_id, has_side_effects=True, vmem_limit_bytes=VMEM_LIMIT
        ),
        cost_estimate=pl.CostEstimate(
            flops=10 * nt * rows * width, bytes_accessed=100 * rows * width * nt, transcendentals=0
        ),
        name="line_" + kind,
    )(*split)
    results = list(results)
    if has_sum:
        results[0] = results[0].reshape(rows, width)
    if has_gather:
        at = 0 if kind == "start" else -1
        results[at] = results[at].reshape(nt * rows, width)
    return results


def span_mask(starts_ref, row_at, rows, cols, spans):
    row = row_at + lax.broadcasted_iota(jnp.int32, (rows, cols), 0)
    col = lax.broadcasted_iota(jnp.int32, (rows, cols), 1)
    seen = col <= row
    for k in range(spans):
        begin = starts_ref[0, k]
        seen = seen | (
            (row >= begin) & (row < begin + PIC) & (col >= begin) & (col < begin + PIC)
        )
    return seen


def key_extent(row_at, seq_len, spans):
    segment = seq_len // spans
    return (row_at // segment + 1) * segment


def attend_kernel(heads, spans, block, raw, starts_ref, a_ref, w_ref, *refs):
    if raw:
        gain_ref, qkv_ref, o_ref, lse_ref, out_ref, normed_ref = refs
        normed_ref[...] = normed(a_ref[...].astype(F32), gain_ref[0:1, :]).astype(BF16)
        a_ref = normed_ref
    else:
        qkv_ref, o_ref, lse_ref, out_ref = refs
    seq_len = a_ref.shape[0]
    wide = heads * HEAD
    factor = HEAD ** (-0.5)
    qkv_ref[...] = dot(a_ref[...], w_ref[:, : 3 * wide]).astype(BF16)
    for at in range(0, seq_len, block):
        reach = key_extent(at, seq_len, spans)
        seen = span_mask(starts_ref, at, block, reach, spans)
        for h in range(heads):
            q = qkv_ref[at : at + block, h * HEAD : (h + 1) * HEAD]
            k = qkv_ref[:reach, wide + h * HEAD : wide + (h + 1) * HEAD]
            v = qkv_ref[:reach, 2 * wide + h * HEAD : 2 * wide + (h + 1) * HEAD]
            s = jnp.where(seen, dot_nt(q, k) * factor, -1e30)
            top = jnp.max(s, axis=-1, keepdims=True)
            e = jnp.exp(s - top)
            total = jnp.sum(e, axis=-1, keepdims=True)
            probs = (e * (1.0 / total)).astype(BF16)
            o_ref[at : at + block, h * HEAD : (h + 1) * HEAD] = dot(probs, v).astype(BF16)
            lse_ref[at : at + block, h : h + 1] = top + jnp.log(total)
    out_ref[...] = dot_nt(o_ref[...], w_ref[:, 3 * wide :]).astype(BF16)


def attend_forward(starts, a_all, w_attn, heads, gain=None):
    seq_len, width = a_all.shape
    wide = heads * HEAD
    spans = starts.shape[1]
    raw = gain is not None
    return pl.pallas_call(
        functools.partial(attend_kernel, heads, spans, PIC, raw),
        out_shape=[
            jax.ShapeDtypeStruct((seq_len, 3 * wide), BF16),
            jax.ShapeDtypeStruct((seq_len, wide), BF16),
            jax.ShapeDtypeStruct((seq_len, heads), F32),
            jax.ShapeDtypeStruct((seq_len, width), BF16),
        ]
        + [jax.ShapeDtypeStruct((seq_len, width), BF16)] * raw,
        in_specs=[pl.BlockSpec(memory_space=pltpu.SMEM)] + [VMEM_SPEC] * (2 + raw),
        out_specs=[VMEM_SPEC] * (4 + raw),
        compiler_params=pltpu.CompilerParams(vmem_limit_bytes=VMEM_LIMIT),
        cost_estimate=pl.CostEstimate(
            flops=8 * seq_len * width * wide + 4 * heads * seq_len * seq_len * HEAD,
            bytes_accessed=6 * seq_len * width,
            transcendentals=heads * seq_len * seq_len,
        ),
        name="attend_forward",
    )(starts, a_all, w_attn, *([gain] if raw else []))


def attend_back_kernel(
    heads, spans, block, starts_ref, g_ref, w_ref, a_ref, qkv_ref, o_ref, lse_ref,
    ga_ref, gw_ref, go_scr, gq_scr, gk_acc, gv_acc,
):
    seq_len = a_ref.shape[0]
    wide = heads * HEAD
    factor = HEAD ** (-0.5)
    go_scr[...] = dot(g_ref[...], w_ref[:, 3 * wide :]).astype(BF16)
    gw_ref[:, 3 * wide :] = dot_tn(g_ref[...], o_ref[...]).astype(BF16)
    gk_acc[...] = jnp.zeros_like(gk_acc)
    gv_acc[...] = jnp.zeros_like(gv_acc)
    for at in range(0, seq_len, block):
        reach = key_extent(at, seq_len, spans)
        seen = span_mask(starts_ref, at, block, reach, spans)
        for h in range(heads):
            own = slice(h * HEAD, (h + 1) * HEAD)
            q = qkv_ref[at : at + block, own]
            k = qkv_ref[:reach, wide + h * HEAD : wide + (h + 1) * HEAD]
            v = qkv_ref[:reach, 2 * wide + h * HEAD : 2 * wide + (h + 1) * HEAD]
            go = go_scr[at : at + block, own]
            s = jnp.where(seen, dot_nt(q, k) * factor, -1e30)
            probs = jnp.exp(s - lse_ref[at : at + block, h : h + 1])
            gp = dot_nt(go, v)
            inner = jnp.sum(probs * gp, axis=-1, keepdims=True)
            gs = (probs * (gp - inner)).astype(BF16)
            gq_scr[at : at + block, own] = (dot(gs, k) * factor).astype(BF16)
            gk_acc[:reach, own] += dot_tn(gs, q) * factor
            gv_acc[:reach, own] += dot_tn(probs.astype(BF16), go)
    gq_scr[:, wide : 2 * wide] = gk_acc[...].astype(BF16)
    gq_scr[:, 2 * wide :] = gv_acc[...].astype(BF16)
    gw_ref[:, : 3 * wide] = dot_tn(a_ref[...], gq_scr[...]).astype(BF16)
    ga_ref[...] = dot_nt(gq_scr[...], w_ref[:, : 3 * wide]).astype(BF16)


def attend_backward(starts, g_all, w_attn, a_all, qkv, o, lse, heads):
    seq_len, width = a_all.shape
    wide = heads * HEAD
    spans = starts.shape[1]
    return pl.pallas_call(
        functools.partial(attend_back_kernel, heads, spans, PIC),
        out_shape=[
            jax.ShapeDtypeStruct((seq_len, width), BF16),
            jax.ShapeDtypeStruct((width, 4 * wide), BF16),
        ],
        in_specs=[pl.BlockSpec(memory_space=pltpu.SMEM)] + [VMEM_SPEC] * 6,
        out_specs=[VMEM_SPEC] * 2,
        scratch_shapes=[
            pltpu.VMEM((seq_len, wide), BF16),
            pltpu.VMEM((seq_len, 3 * wide), BF16),
            pltpu.VMEM((seq_len, wide), F32),
            pltpu.VMEM((seq_len, wide), F32),
        ],
        compiler_params=pltpu.CompilerParams(vmem_limit_bytes=VMEM_LIMIT),
        cost_estimate=pl.CostEstimate(
            flops=16 * seq_len * width * wide + 10 * heads * seq_len * seq_len * HEAD,
            bytes_accessed=12 * seq_len * width,
            transcendentals=heads * seq_len * seq_len,
        ),
        name="attend_backward",
    )(starts, g_all, w_attn, a_all, qkv, o, lse)


def lane_column(values, at):
    lane = lax.broadcasted_iota(jnp.int32, values.shape, 1)
    return jnp.sum(jnp.where(lane == at, values, 0), axis=1, keepdims=True)


def two_parts(values):
    high = values.astype(BF16)
    return high, (values - high.astype(F32)).astype(BF16)


def const_parts(product, wd, layer, at, consts):
    first = EXPERTS + 2
    zero = shift(product, first - at["cmix"] - layer * 2 * consts)
    one = shift(product, first - at["cmix"] - layer * 2 * consts - consts)
    lane = lax.broadcasted_iota(jnp.int32, product.shape, 1)
    here = (lane >= first) & (lane < first + consts)
    gap = jnp.where(here, one - zero, 0.0)
    alpha0 = 1.0 / (1.0 + jnp.exp(gap))
    alpha1 = 1.0 / (1.0 + jnp.exp(-gap))
    gate = jnp.where(here, wd, 0.0)
    keep = jnp.sum(gate * alpha0 + jnp.where(lane == EXPERTS + 1, wd, 0.0), axis=1, keepdims=True)
    return lane, here, alpha0, alpha1, gate, keep


def experts_kernel(
    cap, layer, at, consts, b_ref, w_ref, rowpos_ref, pos_ref, small_ref, rows_ref, mix_ref, zprev_ref,
    mid_ref, x_ref, gu_ref, z_ref, wd_ref, f_ref, extra_ref, pick_scr, y_scr,
):
    e = pl.program_id(0)
    seq_len, width = b_ref.shape
    half = gu_ref.shape[2] // 2

    @pl.when(e == 0)
    def _():
        product = dot(b_ref[...], small_ref[...])
        lane = lax.broadcasted_iota(jnp.int32, product.shape, 1)
        p_high, p_low = two_parts(zprev_ref[...])
        z = (
            jnp.where(lane < NEXP, shift(product, -at["router"] - layer * NEXP), 0.0)
            + dot(p_high, mix_ref[...])
            + dot(p_low, mix_ref[...])
        )
        z_ref[...] = z
        hit = pos_ref[...] >= 0
        top = jnp.max(jnp.where(hit, z, -3e38), axis=1, keepdims=True)
        ez = jnp.where(hit, jnp.exp(jnp.where(hit, z - top, 0.0)), 0.0)
        wd = ez / jnp.sum(ez, axis=1, keepdims=True)
        wd_ref[...] = wd
        _, _, _, alpha1, gate, keep = const_parts(product, wd, layer, at, consts)
        extra = mid_ref[...].astype(F32) + keep * b_ref[...].astype(F32)
        for j in range(consts):
            row = at["cvec"] + layer * consts + j
            extra = extra + lane_column(gate * alpha1, EXPERTS + 2 + j) * rows_ref[row : row + 1, :]
        extra_ref[...] = extra.astype(BF16)

    w = w_ref[...].reshape(width, 3 * half)
    take = (
        lax.broadcasted_iota(jnp.int32, (cap, seq_len), 0) == rowpos_ref[0]
    ).astype(F32).astype(BF16)
    x = dot(take, b_ref[...]).astype(BF16)
    x_ref[0] = x
    gu = dot(x, w[:, : 2 * half])
    gu_ref[0] = gu.astype(BF16)
    g, u = gu[:, :half], gu[:, half:]
    h = (g * jax.nn.sigmoid(g) * u).astype(BF16)
    y = dot_nt(h, w[:, 2 * half :])
    y_scr[pl.ds(pl.multiple_of(e * cap, cap), cap), :] = y.astype(BF16)
    column = lane_column(pos_ref[...], e)
    weight = lane_column(wd_ref[...], e)
    put = jnp.where(
        lax.broadcasted_iota(jnp.int32, (seq_len, cap), 1) == column, weight, 0.0
    ).astype(BF16)
    pick_scr[:, pl.ds(pl.multiple_of(e * cap, cap), cap)] = put

    @pl.when(e == pl.num_programs(0) - 1)
    def _():
        f_ref[...] = dot(pick_scr[...], y_scr[...]).astype(BF16)


def whole(shape):
    return pl.BlockSpec(shape, lambda e: (0,) * len(shape))


def experts_forward(
    layer, at, consts, b_all, w_exp, rowpos, pos, small, rows_t, mix, z_prev, mid, cap
):
    seq_len, width = b_all.shape
    shards_dp, count, rows, wide3 = w_exp.shape
    half = wide3 // 3
    return pl.pallas_call(
        functools.partial(experts_kernel, cap, layer, at, consts),
        grid=(count,),
        out_shape=[
            jax.ShapeDtypeStruct((count, cap, width), BF16),
            jax.ShapeDtypeStruct((count, cap, 2 * half), BF16),
            jax.ShapeDtypeStruct((seq_len, LANES), F32),
            jax.ShapeDtypeStruct((seq_len, LANES), F32),
            jax.ShapeDtypeStruct((seq_len, width), BF16),
            jax.ShapeDtypeStruct((seq_len, width), BF16),
        ],
        in_specs=[
            whole((seq_len, width)),
            pl.BlockSpec((shards_dp, 1, rows, wide3), lambda e: (0, e, 0, 0)),
            pl.BlockSpec((1, 1, seq_len), lambda e: (e, 0, 0)),
            whole((seq_len, LANES)),
            whole((width, LANES)),
            whole(rows_t.shape),
            whole((LANES, LANES)),
            whole((seq_len, LANES)),
            whole((seq_len, width)),
        ],
        out_specs=[
            pl.BlockSpec((1, cap, width), lambda e: (e, 0, 0)),
            pl.BlockSpec((1, cap, 2 * half), lambda e: (e, 0, 0)),
            whole((seq_len, LANES)),
            whole((seq_len, LANES)),
            whole((seq_len, width)),
            whole((seq_len, width)),
        ],
        scratch_shapes=[
            pltpu.VMEM((seq_len, count * cap), BF16),
            pltpu.VMEM((count * cap, width), BF16),
        ],
        compiler_params=pltpu.CompilerParams(vmem_limit_bytes=VMEM_LIMIT),
        cost_estimate=pl.CostEstimate(
            flops=count * (4 * cap * seq_len * width + 6 * cap * width * half),
            bytes_accessed=2 * count * width * wide3,
            transcendentals=0,
        ),
        name="experts_forward",
    )(b_all, w_exp, rowpos, pos, small, rows_t, mix, z_prev, mid)


def experts_back_kernel(
    cap, layer, at, consts, own, offset_ref, g_ref, w_ref, x_ref, gu_ref, rowpos_ref, pos_ref, wd_ref,
    b_ref, small_ref, rows_ref, mix_ref, zprev_ref, gprev_ref, sums_ref, mixes_ref,
    gw_ref, below_ref, gb_ref, sums_out, mixes_out, pick_scr, gx_scr, gg_scr, gb_scr, zs_scr,
):
    e = pl.program_id(0)
    seq_len, width = g_ref.shape
    shards_dp, _, rows, wide3 = w_ref.shape
    half = wide3 // 3
    w = w_ref[...].reshape(width, wide3)
    take = (
        lax.broadcasted_iota(jnp.int32, (cap, seq_len), 0) == rowpos_ref[0]
    ).astype(F32).astype(BF16)
    w_high, w_low = two_parts(wd_ref[...])
    weight = lane_column(dot(take, w_high) + dot(take, w_low), e)
    gf = dot(take, g_ref[...])
    gh = dot(gf.astype(BF16), w[:, 2 * half :])
    gu = gu_ref[0].astype(F32)
    g, u = gu[:, :half], gu[:, half:]
    sig = jax.nn.sigmoid(g)
    h = (g * sig * u).astype(BF16)
    slot_grad = jnp.sum(h.astype(F32) * gh, axis=1, keepdims=True)
    gh = gh * weight
    gg = gh * u * sig * (1.0 + g * (1.0 - sig))
    gup = gh * g * sig
    both = jnp.concatenate([gg.astype(BF16), gup.astype(BF16)], axis=1)
    gy = (gf * weight).astype(BF16)
    gw_ref[:, 0, :, : 2 * half] = dot_tn(x_ref[0], both).astype(BF16).reshape(
        shards_dp, rows, 2 * half
    )
    gw_ref[:, 0, :, 2 * half :] = dot_tn(gy, h).astype(BF16).reshape(shards_dp, rows, half)
    here = pl.ds(pl.multiple_of(e * cap, cap), cap)
    gx_scr[here, :] = dot_nt(both, w[:, : 2 * half]).astype(BF16)
    s_high, s_low = two_parts(slot_grad)
    lane = lax.broadcasted_iota(jnp.int32, (cap, LANES), 1)
    gg_scr[here, :LANES] = jnp.where(lane == e, s_high.astype(F32), 0.0).astype(BF16)
    gg_scr[here, LANES:] = jnp.where(lane == e, s_low.astype(F32), 0.0).astype(BF16)
    column = lane_column(pos_ref[...], e)
    pick_scr[:, here] = (
        lax.broadcasted_iota(jnp.int32, (seq_len, cap), 1) == column
    ).astype(F32).astype(BF16)

    @pl.when(e == pl.num_programs(0) - 1)
    def _():
        mine = pl.ds(pl.multiple_of(offset_ref[0], own), own)
        b_own, g_own = b_ref[mine, :], g_ref[mine, :].astype(F32)
        wd_own = wd_ref[mine, :]
        lane, here_own, alpha0, alpha1, gate, keep = const_parts(
            dot(b_own, small_ref[...]), wd_own, layer, at, consts
        )
        b_dot = jnp.sum(b_own.astype(F32) * g_own, axis=1, keepdims=True)
        c_dot = jnp.zeros_like(wd_own)
        for j in range(consts):
            row = at["cvec"] + layer * consts + j
            one = jnp.sum(g_own * rows_ref[row : row + 1, :], axis=1, keepdims=True)
            c_dot = jnp.where(lane == EXPERTS + 2 + j, one, c_dot)
        gw_own = jnp.where(here_own, alpha0 * b_dot + alpha1 * c_dot, 0.0)
        gw_own = jnp.where(lane == EXPERTS + 1, b_dot, gw_own)
        inner = gate * (alpha0 * b_dot + alpha1 * c_dot)
        gt0 = alpha0 * (gate * b_dot - inner)
        gt1 = alpha1 * (gate * c_dot - inner)

        slots = dot(pick_scr[...], gg_scr[...])
        zs_scr[...] = slots[:, :LANES] + slots[:, LANES:]
        zs_scr[mine, :] += gw_own
        gw = zs_scr[...]
        wd = wd_ref[...]
        gz = wd * (gw - jnp.sum(wd * gw, axis=1, keepdims=True)) + gprev_ref[...]
        z_high, z_low = two_parts(gz)
        below_ref[...] = dot_nt(z_high, mix_ref[...]) + dot_nt(z_low, mix_ref[...])
        p_high, p_low = two_parts(zprev_ref[...])
        mixes_out[...] = mixes_ref[...] + shift(
            dot_tn(p_high, z_high) + dot_tn(p_high, z_low) + dot_tn(p_low, z_high), layer * MIX_STEP
        )
        zs_scr[...] = shift(gz, at["router"] + layer * NEXP)
        up = at["cmix"] + layer * 2 * consts - EXPERTS - 2
        zs_scr[mine, :] += shift(gt0, up) + shift(gt1, up + consts)
        z_high, z_low = two_parts(zs_scr[...])
        gb_scr[...] = (
            dot(pick_scr[...], gx_scr[...])
            + dot_nt(z_high, small_ref[...])
            + dot_nt(z_low, small_ref[...])
        )
        gb_scr[mine, :] += keep * g_own
        gb_ref[...] = gb_scr[...].astype(BF16)
        i_high, i_low = two_parts(
            shift(gate * alpha1, at["cvec"] + layer * consts - EXPERTS - 2)
        )
        g_low = g_ref[mine, :]
        sums_out[...] = (
            sums_ref[...]
            + dot_tn(b_ref[...], z_high)
            + dot_tn(b_ref[...], z_low)
            + dot_tn(g_low, i_high)
            + dot_tn(g_low, i_low)
        )


def experts_backward(
    layer, at, consts, own, offset, g_all, w_exp, x, gu, rowpos, pos, wd, b_all, small, rows_t, mix,
    z_prev, grad_prev, sums, mixes, cap,
):
    seq_len, width = g_all.shape
    shards_dp, count, rows, wide3 = w_exp.shape
    half = wide3 // 3
    weight_spec = pl.BlockSpec((shards_dp, 1, rows, wide3), lambda e: (0, e, 0, 0))
    return pl.pallas_call(
        functools.partial(experts_back_kernel, cap, layer, at, consts, own),
        grid=(count,),
        out_shape=[
            jax.ShapeDtypeStruct(w_exp.shape, BF16),
            jax.ShapeDtypeStruct((seq_len, LANES), F32),
            jax.ShapeDtypeStruct((seq_len, width), BF16),
            jax.ShapeDtypeStruct((width, LANES), F32),
            jax.ShapeDtypeStruct((LANES, LANES), F32),
        ],
        in_specs=[
            pl.BlockSpec(memory_space=pltpu.SMEM),
            whole((seq_len, width)),
            weight_spec,
            pl.BlockSpec((1, cap, width), lambda e: (e, 0, 0)),
            pl.BlockSpec((1, cap, 2 * half), lambda e: (e, 0, 0)),
            pl.BlockSpec((1, 1, seq_len), lambda e: (e, 0, 0)),
            whole((seq_len, LANES)),
            whole((seq_len, LANES)),
            whole((seq_len, width)),
            whole((width, LANES)),
            whole(rows_t.shape),
            whole((LANES, LANES)),
            whole((seq_len, LANES)),
            whole((seq_len, LANES)),
            whole((width, LANES)),
            whole((LANES, LANES)),
        ],
        out_specs=[
            weight_spec,
            whole((seq_len, LANES)),
            whole((seq_len, width)),
            whole((width, LANES)),
            whole((LANES, LANES)),
        ],
        scratch_shapes=[
            pltpu.VMEM((seq_len, count * cap), BF16),
            pltpu.VMEM((count * cap, width), BF16),
            pltpu.VMEM((count * cap, 2 * LANES), BF16),
            pltpu.VMEM((seq_len, width), F32),
            pltpu.VMEM((seq_len, LANES), F32),
        ],
        compiler_params=pltpu.CompilerParams(vmem_limit_bytes=VMEM_LIMIT),
        cost_estimate=pl.CostEstimate(
            flops=count * (4 * cap * seq_len * width + 12 * cap * width * half),
            bytes_accessed=4 * count * width * wide3,
            transcendentals=0,
        ),
        name="experts_backward",
    )(
        offset, g_all, w_exp, x, gu, rowpos, pos, wd, b_all, small, rows_t, mix, z_prev, grad_prev,
        sums, mixes,
    )


def unpack_kernel(half, *refs):
    *in_refs, up_ref, down_ref, tall = refs
    rows = up_ref.shape[2]
    tall[...] = jnp.zeros_like(tall)
    for l, ref in enumerate(in_refs):
        values = ref[0].astype(F32)
        for part in range(2):
            up_ref[l, 0, :, part, :] = values[:, part * half : (part + 1) * half]
        tall[:rows, :] = values[:, 2 * half :]
        down_ref[l, 0] = tall[...].T[:, :rows]


def unpack(items):
    count, rows, wide3 = items[0].shape
    half = wide3 // 3
    layers = len(items)
    return pl.pallas_call(
        functools.partial(unpack_kernel, half),
        grid=(count,),
        out_shape=[
            jax.ShapeDtypeStruct((layers, count, rows, 2, half), F32),
            jax.ShapeDtypeStruct((layers, count, half, rows), F32),
        ],
        in_specs=[pl.BlockSpec((1, rows, wide3), lambda e: (e, 0, 0))] * layers,
        out_specs=[
            pl.BlockSpec((layers, 1, rows, 2, half), lambda e: (0, e, 0, 0, 0)),
            pl.BlockSpec((layers, 1, half, rows), lambda e: (0, e, 0, 0)),
        ],
        scratch_shapes=[pltpu.VMEM((-(-rows // LANES) * LANES, half), F32)],
        compiler_params=pltpu.CompilerParams(vmem_limit_bytes=VMEM_LIMIT),
        name="unpack",
    )(*items)


def lanes(values):
    return jnp.pad(values, ((0, 0), (0, LANES - values.shape[1])))


def slot_table(route_ids):
    tokens = route_ids.shape[0]
    codes = jnp.arange(LANES, dtype=jnp.int32)
    hit = jnp.any(route_ids[:, :, None] == codes[None, None, :], axis=1)
    place = jnp.arange(tokens, dtype=jnp.int32)
    before = (place[None, :] < place[:, None]).astype(BF16)
    slots = dot(before, hit.astype(BF16)).astype(jnp.int32)
    return jnp.where(hit, slots, -1)


def shards(
    hidden_in,
    prev_logits,
    routes,
    span_starts,
    attn_norm,
    qkv_weight,
    out_weight,
    moe_norm,
    router,
    gate_mix,
    const_vec,
    const_mix,
    up_weight,
    down_weight,
    out_grad,
):
    layers = qkv_weight.shape[0]
    own, width = hidden_in.shape
    nt = lax.axis_size("tensor")
    ndp = lax.axis_size("dp")
    seq_len = own * nt
    offset = lax.axis_index("tensor") * own
    cap = seq_len // 4
    heads = qkv_weight.shape[3] // HEAD
    wide = heads * HEAD
    half = up_weight.shape[4]
    rows = qkv_weight.shape[1]
    cols = attn_norm.shape[1]
    consts = const_vec.shape[1]

    at = layout(layers, consts)
    packed = jnp.concatenate(
        [attn_norm.T, moe_norm.T]
        + [router[l] for l in range(layers)]
        + [const_vec.reshape(-1, cols).T]
        + [const_mix[l, :, :, k].T for l in range(layers) for k in range(2)],
        axis=1,
    )
    x_all, small = line_exchange("start", [hidden_in, lanes(packed)], own, width, 0)
    small = small.reshape(width, LANES)
    rows_t = small[:, :48].T.astype(F32)

    attn_w, exp_w = [], []
    for l in range(layers):
        local = jnp.concatenate(
            [qkv_weight[l].reshape(rows, 3 * wide), out_weight[l].T], axis=1
        )
        attn_w.append(lax.all_gather(local, "dp", axis=0, tiled=False).reshape(width, 4 * wide))
        local = jnp.concatenate(
            [
                up_weight[l].reshape(EXPERTS, rows, 2 * half),
                jnp.swapaxes(down_weight[l], 1, 2),
            ],
            axis=2,
        )
        exp_w.append(lax.all_gather(local, "dp", axis=0, tiled=False))

    pos = [slot_table(routes[l]) for l in range(layers)]
    rowpos = [p[:, :EXPERTS].T[:, None, :] for p in pos]

    z_prev = lanes(prev_logits)
    hidden, a_all = x_all, None
    grad_all = out_grad
    next_id = 1
    stored = []
    for l in range(layers):
        mix = jnp.pad(gate_mix[l], ((0, LANES - NEXP), (0, LANES - NEXP)))
        if l == 0:
            qkv, o, lse, partial, a_all = attend_forward(
                span_starts, x_all, attn_w[l], heads, rows_t
            )
        else:
            qkv, o, lse, partial = attend_forward(span_starts, a_all, attn_w[l], heads)
        if l == layers - 1:
            partial, grad_all = lax.optimization_barrier((partial, grad_all))
            grad_all = lax.all_gather(grad_all, "tensor", axis=0, tiled=True)
        mid, b_all = join(False, partial, [hidden], rows_t, at["moe"] + l, next_id)
        x, gu, z, wd, partial, extra = experts_forward(
            l, at, consts, b_all, exp_w[l], rowpos[l], pos[l], small, rows_t, mix, z_prev, mid, cap
        )
        stored.append(
            dict(
                hidden=hidden, a_all=a_all, qkv=qkv, o=o, lse=lse, mid=mid, b_all=b_all, x=x, gu=gu,
                wd=wd, z_prev=z_prev, mix=mix,
            )
        )
        if l + 1 < layers:
            hidden, a_all = join(False, partial, [extra], rows_t, at["attn"] + l + 1, next_id + 1)
        else:
            hidden_out = lax.psum_scatter(partial, "tensor", scatter_dimension=0, tiled=True)
            extra = lax.dynamic_slice_in_dim(extra, offset, own, 0)
        z_prev = z
        next_id += 2

    below = jnp.zeros((seq_len, LANES), F32)
    sums = jnp.zeros((width, LANES), F32)
    mixes = jnp.zeros((LANES, LANES), F32)
    attn_grads, exp_grads = [None] * layers, [None] * layers
    gains_a, gains_m = [None] * layers, [None] * layers
    for l in reversed(range(layers)):
        s = stored[l]
        gw_exp, below, partial, sums, mixes = experts_backward(
            l, at, consts, own, offset.reshape(1), grad_all, exp_w[l], s["x"], s["gu"], rowpos[l],
            pos[l], s["wd"], s["b_all"], small, rows_t, s["mix"], s["z_prev"], below, sums, mixes, cap,
        )
        exp_grads[l] = lax.psum_scatter(gw_exp, "dp", scatter_dimension=0, tiled=False)
        if l + 1 < layers:
            partial, exp_grads[l + 1] = lax.optimization_barrier((partial, exp_grads[l + 1]))
        else:
            partial, hidden_out = lax.optimization_barrier((partial, hidden_out))
        grad_mid, gains_m[l] = join(
            True, partial, [s["mid"], grad_all], rows_t, at["moe"] + l, next_id
        )
        partial, gw_attn = attend_backward(
            span_starts, grad_mid, attn_w[l], s["a_all"], s["qkv"], s["o"], s["lse"], heads
        )
        attn_grads[l] = gw_attn.reshape(ndp, rows, 4 * wide)
        if l > 0:
            grad_all, gains_a[l] = join(
                True, partial, [s["hidden"], grad_mid], rows_t, at["attn"] + l, next_id + 1
            )
        else:
            skip = lax.dynamic_slice_in_dim(grad_mid, offset, own, 0)
            grad, gains_a[l] = line_exchange(
                "end", [partial, hidden_in, skip, rows_t], own, width, next_id + 1
            )
        next_id += 2
    hidden_out = hidden_out.astype(F32) + extra.astype(F32)

    gains = jnp.concatenate(gains_a + gains_m, axis=0)
    sums = sums + jnp.pad(gains, ((0, LANES - 2 * layers), (0, 0))).T
    sums = jnp.concatenate(
        [
            sums.reshape(ndp * nt, cols, LANES),
            jnp.broadcast_to(mixes[None, :MIX_STEP], (ndp * nt, MIX_STEP, LANES)),
        ],
        axis=1,
    )
    attn_g, moe_g, router_g, mix_g, cvec_g, cmix_g, qkv_g, outw_g = closing(
        sums, attn_grads, consts, cols, next_id
    )
    up_grad, down_grad = unpack(exp_grads)
    return (
        hidden_out,
        grad,
        attn_g,
        qkv_g,
        outw_g,
        moe_g,
        router_g,
        mix_g,
        cvec_g,
        cmix_g,
        up_grad,
        down_grad,
    )


def solution(mesh):
    return jax.shard_map(
        shards,
        mesh=mesh,
        in_specs=(
            P(("dp", "tensor"), None),
            P("dp", None),
            P(None, "dp", None),
            P("dp", None),
            P(None, ("dp", "tensor")),
            P(None, "dp", None, "tensor"),
            P(None, "tensor", "dp"),
            P(None, ("dp", "tensor")),
            P(None, ("dp", "tensor"), None),
            P(),
            P(None, None, ("dp", "tensor")),
            P(None, None, ("dp", "tensor"), None),
            P(None, None, "dp", None, "tensor"),
            P(None, None, "tensor", "dp"),
            P(("dp", "tensor"), None),
        ),
        out_specs=(
            P(("dp", "tensor"), None),
            P(("dp", "tensor"), None),
            P(None, ("dp", "tensor")),
            P(None, "dp", None, "tensor"),
            P(None, "tensor", "dp"),
            P(None, ("dp", "tensor")),
            P(None, ("dp", "tensor"), None),
            P(),
            P(None, None, ("dp", "tensor")),
            P(None, None, ("dp", "tensor"), None),
            P(None, None, "dp", None, "tensor"),
            P(None, None, "tensor", "dp"),
        ),
        check_vma=False,
    )
```

```python
import functools

import jax
import jax.numpy as jnp
from jax import lax
from jax.experimental import pallas as pl
from jax.experimental.pallas import tpu as pltpu
from jax.sharding import PartitionSpec as P

HEAD = 64
EXPERTS = 8
NEXP = 12
TOPK = 2
PIC = 256
LANES = 128

EPS = 1e-06
HIGH = lax.Precision.HIGHEST
MESH = pl.DeviceIdType.MESH
F32 = jnp.float32
BF16 = jnp.bfloat16
VMEM_SPEC = pl.BlockSpec(memory_space=pltpu.VMEM)
AHEAD = 2
PIECES = 16
LAG = 2
MIX_STEP = 16
VMEM_LIMIT = 60 * 1024 * 1024


def dot(a, b):
    return jnp.dot(a, b, preferred_element_type=F32)


def dot_nt(a, b):
    return lax.dot_general(a, b, (((1,), (1,)), ((), ())), preferred_element_type=F32)


def dot_tn(a, b):
    return lax.dot_general(a, b, (((0,), (0,)), ((), ())), preferred_element_type=F32)


def layout(layers, consts):
    at, begin = {}, 0
    for name, size in (
        ("attn", layers),
        ("moe", layers),
        ("router", layers * NEXP),
        ("cvec", layers * consts),
        ("cmix", layers * consts * 2),
    ):
        at[name] = begin
        begin += size
    return at


def shift(values, lanes_up):
    return pltpu.roll(values, lanes_up % LANES, 1)


def greet_all(count, me, place):
    barrier = pltpu.get_barrier_semaphore()

    def greet(step, carry):
        other = lax.rem(me + step, count)
        pl.semaphore_signal(barrier, inc=1, device_id=place(other), device_id_type=MESH)
        return carry

    lax.fori_loop(1, count, greet, 0)
    pl.semaphore_wait(barrier, count - 1)


def swap_all(count, me, place, source, land, send_sems, recv_sems):
    def copy(other, slot):
        return pltpu.make_async_remote_copy(
            src_ref=source(other),
            dst_ref=land.at[slot],
            send_sem=send_sems.at[other],
            recv_sem=recv_sems.at[slot],
            device_id=place(other),
            device_id_type=MESH,
        )

    def start():
        def send(step, carry):
            other = lax.rem(me + step, count)
            copy(other, me).start()
            return carry

        lax.fori_loop(1, count, send, 0)

    def finish():
        def wait(step, carry):
            other = lax.rem(me + count - step, count)
            copy(other, other).wait()
            return carry

        lax.fori_loop(1, count, wait, 0)

    return start, finish


def closing_kernel(ndp, inner, layers, consts, wide, *refs):
    small_ref, proj_ref, above_ref = refs[:3]
    attn_out, moe_out, router_out, mix_out, cvec_out, cmix_out, qkv_out, outw_out = refs[3:11]
    land, proj_land, square, tall = refs[11:15]
    sems = refs[15:]
    count = ndp * inner
    row, col = lax.axis_index("dp"), lax.axis_index("tensor")
    me = row * inner + col
    cols = attn_out.shape[1]
    rows = qkv_out.shape[2]

    def anywhere(other):
        return (lax.div(other, inner), lax.rem(other, inner))

    def along(other):
        return (other, col)

    def piece(ref):
        return lambda other: ref.at[other]

    greet_all(count, me, anywhere)
    moves = [
        swap_all(ndp, row, along, piece(proj_ref), proj_land, *sems[2:4]),
        swap_all(count, me, anywhere, piece(small_ref), land, *sems[0:2]),
    ]
    for start, _ in moves:
        start()
    land[me] = small_ref[me]
    proj_land[row] = proj_ref[row]
    square[...] = jnp.zeros_like(square)
    tall[...] = jnp.zeros_like(tall)

    def place(l, total):
        for part in range(3):
            qkv_out[l, part] = total[:, part * wide : (part + 1) * wide]
        tall[:rows, :wide] = total[:, 3 * wide :]
        outw_out[l] = tall[...].T[:wide, :rows]

    for l in range(1, layers):
        place(l, above_ref[l - 1].astype(F32))
    moves[0][1]()
    place(0, jnp.sum(proj_land[...].astype(F32), axis=0))
    moves[1][1]()
    total = jnp.sum(land[...], axis=0)
    square[:cols, :] = total[:cols]
    turned = square[...].T
    at = layout(layers, consts)
    attn_out[...] = turned[at["attn"] : at["attn"] + layers, :cols]
    moe_out[...] = turned[at["moe"] : at["moe"] + layers, :cols]
    for l in range(layers):
        begin = at["router"] + l * NEXP
        for e in range(NEXP):
            router_out[e, l : l + 1, :] = turned[begin + e : begin + e + 1, :cols]
            mix_out[e, l : l + 1, :] = total[
                cols + e : cols + e + 1, l * MIX_STEP : l * MIX_STEP + NEXP
            ]
        begin = at["cvec"] + l * consts
        cvec_out[l] = turned[begin : begin + consts, :cols]
        begin = at["cmix"] + l * 2 * consts
        for j in range(consts):
            for k in range(2):
                lane = begin + k * consts + j
                cmix_out[l, j, k : k + 1, :] = turned[lane : lane + 1, :cols]


def closing(small, projection, above, consts, layers, cols, collective_id):
    inner, ndp = lax.axis_size("tensor"), lax.axis_size("dp")
    rows, packed = projection.shape[1:]
    wide = packed // 4
    shapes = [
        (layers, cols), (layers, cols), (NEXP, layers, cols), (NEXP, layers, NEXP),
        (layers, consts, cols), (layers, consts, 2, cols),
        (layers, 3, rows, wide), (layers, wide, rows),
    ]
    return pl.pallas_call(
        functools.partial(closing_kernel, ndp, inner, layers, consts, wide),
        out_shape=[jax.ShapeDtypeStruct(shape, F32) for shape in shapes],
        in_specs=[VMEM_SPEC] * 3,
        out_specs=[VMEM_SPEC] * len(shapes),
        scratch_shapes=[
            pltpu.VMEM(small.shape, F32),
            pltpu.VMEM(projection.shape, BF16),
            pltpu.VMEM((-(-cols // LANES) * LANES, LANES), F32),
            pltpu.VMEM((-(-rows // LANES) * LANES, -(-wide // LANES) * LANES), F32),
        ]
        + [pltpu.SemaphoreType.DMA((ndp * inner,))] * 2
        + [pltpu.SemaphoreType.DMA((ndp,))] * 2,
        compiler_params=pltpu.CompilerParams(
            collective_id=collective_id, has_side_effects=True, vmem_limit_bytes=VMEM_LIMIT
        ),
        name="closing",
    )(small, projection, above)


def join_kernel(back, gain_row, nt, pieces, lag, *refs):
    if back:
        part, base_ref, skip_ref, rows_ref, result_ref, gg_ref = refs[:6]
    else:
        part, base_ref, rows_ref, total_ref, normed_ref = refs[:5]
    refs = refs[6 if back else 5 :]
    inbox, half, across, full, out_sem, in_sem, cross_out, cross_in, full_out, full_in = refs
    me = lax.axis_index("tensor")
    is_end = (me == 0) | (me == nt - 1)
    buddy = jnp.where(me < 2, 1 - me, 5 - me)
    cross = 3 - me

    barrier = pltpu.get_barrier_semaphore()
    pl.semaphore_signal(barrier, inc=1, device_id={"tensor": buddy}, device_id_type=MESH)

    @pl.when(jnp.logical_not(is_end))
    def _():
        pl.semaphore_signal(barrier, inc=1, device_id={"tensor": cross}, device_id_type=MESH)

    pl.semaphore_wait(barrier, 2 - is_end.astype(jnp.int32))

    def copy(src, dst, send_sem, recv_sem, to):
        return pltpu.make_async_remote_copy(
            src_ref=src,
            dst_ref=dst,
            send_sem=send_sem,
            recv_sem=recv_sem,
            device_id={"tensor": to},
            device_id_type=MESH,
        )

    def inward(n):
        return copy(part.at[n], inbox.at[n], out_sem.at[n], in_sem.at[n], buddy)

    def over(n):
        return copy(half.at[n], across.at[n], cross_out.at[n], cross_in.at[n], cross)

    def outward(n):
        return copy(full.at[n], full.at[n], full_out.at[n], full_in.at[n], buddy)

    gain = rows_ref[gain_row : gain_row + 1, :]
    if back:
        gg_ref[...] = jnp.zeros_like(gg_ref)

    def settle(n):
        total = full[n].astype(F32)
        base = base_ref[n].astype(F32)
        if back:
            scale = lax.rsqrt(jnp.mean(base * base, axis=-1, keepdims=True) + EPS)
            unit = base * scale
            grad_unit = total * gain
            below = scale * (grad_unit - unit * jnp.mean(grad_unit * unit, axis=-1, keepdims=True))
            result_ref[n] = (below + skip_ref[n].astype(F32)).astype(BF16)

            @pl.when(lax.div(n, pieces // nt) == me)
            def _():
                gg_ref[...] += jnp.sum(total * unit, axis=0, keepdims=True)
        else:
            total = total + base
            total_ref[n] = total.astype(BF16)
            normed_ref[n] = normed(total, gain).astype(BF16)

    @pl.when(is_end)
    def _():
        for n in range(pieces):
            inward(n).start()

        def take(n, carry):
            outward(n).wait_recv()
            settle(n)
            return carry

        lax.fori_loop(0, pieces, take, 0)
        for n in range(pieces):
            inward(n).wait_send()

    @pl.when(jnp.logical_not(is_end))
    def _():
        def step(at, carry):
            @pl.when(at < pieces)
            def _():
                inward(at).wait_recv()
                half[at] = (part[at].astype(F32) + inbox[at].astype(F32)).astype(BF16)
                over(at).start()

            @pl.when(at >= lag)
            def _():
                n = at - lag
                over(n).wait_recv()
                full[n] = (half[n].astype(F32) + across[n].astype(F32)).astype(BF16)
                outward(n).start()
                settle(n)

            return carry

        lax.fori_loop(0, pieces + lag, step, 0)
        for n in range(pieces):
            over(n).wait_send()
            outward(n).wait_send()


def join(back, part, others, rows, gain_row, collective_id, pieces=PIECES, lag=LAG):
    nt = lax.axis_size("tensor")
    seq_len, width = part.shape
    cut = (pieces, seq_len // pieces, width)
    outs = [jax.ShapeDtypeStruct(cut, BF16)]
    outs.append(jax.ShapeDtypeStruct((1, width) if back else cut, F32 if back else BF16))
    sems = pltpu.SemaphoreType.DMA((pieces,))
    results = pl.pallas_call(
        functools.partial(join_kernel, back, gain_row, nt, pieces, lag),
        out_shape=outs,
        in_specs=[VMEM_SPEC] * (2 + len(others)),
        out_specs=[VMEM_SPEC] * 2,
        scratch_shapes=[pltpu.VMEM(cut, BF16)] * 4 + [sems] * 6,
        compiler_params=pltpu.CompilerParams(
            collective_id=collective_id, has_side_effects=True, vmem_limit_bytes=VMEM_LIMIT
        ),
        cost_estimate=pl.CostEstimate(
            flops=10 * seq_len * width, bytes_accessed=100 * seq_len * width, transcendentals=0
        ),
        name="join_back" if back else "join",
    )(part.reshape(cut), *[item.reshape(cut) for item in others], rows)
    return results[0].reshape(seq_len, width), (
        results[1] if back else results[1].reshape(seq_len, width)
    )


def normed(values, gain):
    return values * lax.rsqrt(jnp.mean(values * values, axis=-1, keepdims=True) + EPS) * gain


def line_kernel(kind, nt, chunks, lag, extra, *refs):
    refs = list(refs)
    has_sum = kind != "start"
    has_gather = kind != "end"
    part = refs.pop(0) if has_sum else None
    if kind == "start":
        x_ref, small_ref = refs.pop(0), refs.pop(0)
    elif kind == "fwd":
        extra_ref, gain_ref = refs.pop(0), refs.pop(0)
    elif kind == "last":
        extra_ref, og_ref = refs.pop(0), refs.pop(0)
    else:
        extra_ref = refs.pop(0) if extra else None
        base_ref, skip_ref, rows_ref = refs.pop(0), refs.pop(0), refs.pop(0)
    own_ref = refs.pop(0) if has_sum else None
    gg_ref = refs.pop(0) if kind in ("bwd", "end") else None
    all_ref = refs.pop(0) if has_gather else None
    land_ref = refs.pop(0) if kind == "start" else None
    if has_sum:
        from_left, from_right, tx, acc, rs_send, rl_sem, rr_sem = refs[:7]
        refs = refs[7:]
    if has_gather:
        ag_right, ag_left, ag_recv = refs[:3]
        refs = refs[3:]

    me = lax.axis_index("tensor")
    has_l, has_r = me > 0, me < nt - 1
    left, right = jnp.maximum(me - 1, 0), jnp.minimum(me + 1, nt - 1)

    if kind == "start":
        count = lax.axis_size("dp") * nt
        me_all = lax.axis_index("dp") * nt + me

        def place(other):
            return (lax.div(other, nt), lax.rem(other, nt))

        greet_all(count, me_all, place)
        small_start, small_finish = swap_all(
            count, me_all, place, lambda other: small_ref, land_ref, *refs[:2]
        )
        small_start()
        land_ref[me_all] = small_ref[...]
    else:
        barrier = pltpu.get_barrier_semaphore()

        @pl.when(has_l)
        def _():
            pl.semaphore_signal(barrier, inc=1, device_id={"tensor": left}, device_id_type=MESH)

        @pl.when(has_r)
        def _():
            pl.semaphore_signal(barrier, inc=1, device_id={"tensor": right}, device_id_type=MESH)

        pl.semaphore_wait(barrier, has_l.astype(jnp.int32) + has_r.astype(jnp.int32))

    def copy(src, dst, send_sem, recv_sem, to):
        return pltpu.make_async_remote_copy(
            src_ref=src,
            dst_ref=dst,
            send_sem=send_sem,
            recv_sem=recv_sem,
            device_id={"tensor": to},
            device_id_type=MESH,
        )

    def sum_right(j, c, src):
        return copy(src, from_left.at[j, c], rs_send.at[j, c], rl_sem.at[j, c], right)

    def sum_left(j, c, src):
        return copy(src, from_right.at[j, c], rs_send.at[j, c], rr_sem.at[j, c], left)

    def spread_right(j, c):
        block = all_ref.at[j, c]
        return copy(block, block, ag_right.at[j, c], ag_recv.at[j, c], right)

    def spread_left(j, c):
        block = all_ref.at[j, c]
        return copy(block, block, ag_left.at[j, c], ag_recv.at[j, c], left)

    def offer(c):
        @pl.when(has_r)
        def _():
            spread_right(me, c).start()

        @pl.when(has_l)
        def _():
            spread_left(me, c).start()

    def pass_on(c, d):
        @pl.when(me - d >= 0)
        def _():
            j = me - d
            spread_right(j, c).wait_recv()

            @pl.when(has_r)
            def _():
                spread_right(j, c).start()

        @pl.when(me + d < nt)
        def _():
            j = me + d
            spread_left(j, c).wait_recv()

            @pl.when(has_l)
            def _():
                spread_left(j, c).start()

    hops = nt - 1

    count = hops * chunks

    def relay(step):
        k = jnp.clip(step - lag * me, 0, count - 1)
        c, j = lax.div(k, hops), hops - lax.rem(k, hops)

        @pl.when(has_l & (step >= lag * me) & (step - lag * me < count) & (me < j))
        def _():
            sum_right(j, c, tx.at[j, c]).wait_recv()
            tx[j, c] = (part[j, c].astype(F32) + from_left[j, c].astype(F32)).astype(BF16)
            sum_right(j, c, tx.at[j, c]).start()

        far = lag * (hops - me)
        k_down = jnp.clip(step - far, 0, count - 1)
        c_down, j_down = lax.div(k_down, hops), lax.rem(k_down, hops)

        @pl.when(has_r & (step >= far) & (step - far < count) & (me > j_down))
        def _():
            sum_left(j_down, c_down, tx.at[j_down, c_down]).wait_recv()
            tx[j_down, c_down] = (
                part[j_down, c_down].astype(F32) + from_right[j_down, c_down].astype(F32)
            ).astype(BF16)
            sum_left(j_down, c_down, tx.at[j_down, c_down]).start()

    def push(first, last):
        ks = range(min(first, count), min(last, count))

        @pl.when(jnp.logical_not(has_l))
        def _():
            for k in ks:
                j, c = hops - k % hops, k // hops
                sum_right(j, c, part.at[j, c]).start()

        @pl.when(jnp.logical_not(has_r))
        def _():
            for k in ks:
                j, c = k % hops, k // hops
                sum_left(j, c, part.at[j, c]).start()

    def own_rows(c):
        acc[...] = part[me, c].astype(F32)

        @pl.when(has_l)
        def _():
            sum_right(me, c, tx.at[me, c]).wait_recv()
            acc[...] += from_left[me, c].astype(F32)

        @pl.when(has_r)
        def _():
            sum_left(me, c, tx.at[me, c]).wait_recv()
            acc[...] += from_right[me, c].astype(F32)

        total = acc[...]
        if kind == "fwd":
            total = total + extra_ref[c]
            all_ref[me, c] = normed(total, gain_ref[...]).astype(BF16)
            own_ref[c] = total
        elif kind == "last":
            own_ref[c] = total + extra_ref[c]
        else:
            if extra:
                total = total + extra_ref[c]
            base = base_ref[c].astype(F32)
            scale = lax.rsqrt(jnp.mean(base * base, axis=-1, keepdims=True) + EPS)
            unit = base * scale
            grad_unit = total * rows_ref[0:1, :]
            below = scale * (grad_unit - unit * jnp.mean(grad_unit * unit, axis=-1, keepdims=True))
            result = below + skip_ref[c].astype(F32)
            if has_gather:
                all_ref[me, c] = result.astype(BF16)
            own_ref[c] = result
            gg = jnp.sum(total * unit, axis=0, keepdims=True)
            if c == 0:
                gg_ref[...] = gg
            else:
                gg_ref[...] += gg
        if kind in ("fwd", "bwd"):
            offer(c)

    if kind == "start":
        for c in range(chunks):
            all_ref[me, c] = x_ref[c]
            offer(c)
        for c in range(chunks):
            for d in range(1, nt):
                pass_on(c, d)
        small_finish()
    else:

        push(0, AHEAD)
        if kind == "last":
            for c in range(chunks):
                all_ref[me, c] = og_ref[c]
            for c in range(chunks):
                offer(c)
        delay = 0 if kind == "last" else hops * lag
        spreads = {}
        for c in range(chunks if has_gather else 0):
            for d in range(1, nt):
                spreads.setdefault(delay + hops * c + lag * d, []).append((c, d))
        final = max([hops * (chunks - 1 + lag)] + list(spreads))
        for step in range(1, final + 1):
            push(step + AHEAD - 1, step + AHEAD)
            relay(step)
            for c, d in spreads.get(step, ()):
                pass_on(c, d)
            if step % hops == 0 and 0 <= step // hops - lag < chunks:
                own_rows(step // hops - lag)

    for c in range(chunks):
        for j in range(nt):
            if has_sum:

                @pl.when(me < j)
                def _():
                    sum_right(j, c, tx.at[j, c]).wait_send()

                @pl.when(me > j)
                def _():
                    sum_left(j, c, tx.at[j, c]).wait_send()

            if has_gather:

                @pl.when(has_r & (j <= me))
                def _():
                    spread_right(j, c).wait_send()

                @pl.when(has_l & (j >= me))
                def _():
                    spread_left(j, c).wait_send()


def line_exchange(kind, args, rows, width, collective_id, extra=False, chunks=2, lag=2):
    nt = lax.axis_size("tensor")
    has_sum = kind != "start"
    has_gather = kind != "end"
    piece = rows // chunks
    split = []
    for item in args:
        if item.shape[0] == nt * rows:
            split.append(item.reshape(nt, chunks, piece, width))
        elif item.shape[0] == rows:
            split.append(item.reshape(chunks, piece, width))
        else:
            split.append(item)
    outs = []
    if has_sum:
        outs.append(jax.ShapeDtypeStruct((chunks, piece, width), F32))
    if kind in ("bwd", "end"):
        outs.append(jax.ShapeDtypeStruct((1, width), F32))
    if has_gather:
        outs.append(jax.ShapeDtypeStruct((nt, chunks, piece, width), BF16))
    if kind == "start":
        count = lax.axis_size("dp") * nt
        outs.append(jax.ShapeDtypeStruct((count,) + args[1].shape, args[1].dtype))
    scratch = []
    sems = pltpu.SemaphoreType.DMA((nt, chunks))
    if has_sum:
        buf = pltpu.VMEM((nt, chunks, piece, width), BF16)
        scratch += [buf, buf, buf, pltpu.VMEM((piece, width), F32), sems, sems, sems]
    if has_gather:
        scratch += [sems, sems, sems]
    if kind == "start":
        scratch += [pltpu.SemaphoreType.DMA((count,))] * 2
    results = pl.pallas_call(
        functools.partial(line_kernel, kind, nt, chunks, lag, extra),
        out_shape=outs,
        in_specs=[VMEM_SPEC] * len(split),
        out_specs=[VMEM_SPEC] * len(outs),
        scratch_shapes=scratch,
        compiler_params=pltpu.CompilerParams(
            collective_id=collective_id, has_side_effects=True, vmem_limit_bytes=VMEM_LIMIT
        ),
        cost_estimate=pl.CostEstimate(
            flops=10 * nt * rows * width, bytes_accessed=100 * rows * width * nt, transcendentals=0
        ),
        name="line_" + kind,
    )(*split)
    results = list(results)
    if has_sum:
        results[0] = results[0].reshape(rows, width)
    if has_gather:
        at = 0 if kind == "start" else -1
        results[at] = results[at].reshape(nt * rows, width)
    return results


def span_mask(starts_ref, row_at, rows, cols, spans):
    row = row_at + lax.broadcasted_iota(jnp.int32, (rows, cols), 0)
    col = lax.broadcasted_iota(jnp.int32, (rows, cols), 1)
    seen = col <= row
    for k in range(spans):
        begin = starts_ref[0, k]
        seen = seen | (
            (row >= begin) & (row < begin + PIC) & (col >= begin) & (col < begin + PIC)
        )
    return seen


def key_extent(row_at, seq_len, spans):
    segment = seq_len // spans
    return (row_at // segment + 1) * segment


def attend_kernel(heads, spans, block, raw, starts_ref, a_ref, w_ref, *refs):
    if raw:
        gain_ref, qkv_ref, o_ref, lse_ref, out_ref, normed_ref = refs
        normed_ref[...] = normed(a_ref[...].astype(F32), gain_ref[0:1, :]).astype(BF16)
        a_ref = normed_ref
    else:
        qkv_ref, o_ref, lse_ref, out_ref = refs
    seq_len = a_ref.shape[0]
    wide = heads * HEAD
    factor = HEAD ** (-0.5)
    qkv_ref[...] = dot(a_ref[...], w_ref[:, : 3 * wide]).astype(BF16)
    for at in range(0, seq_len, block):
        reach = key_extent(at, seq_len, spans)
        seen = span_mask(starts_ref, at, block, reach, spans)
        for h in range(heads):
            q = qkv_ref[at : at + block, h * HEAD : (h + 1) * HEAD]
            k = qkv_ref[:reach, wide + h * HEAD : wide + (h + 1) * HEAD]
            v = qkv_ref[:reach, 2 * wide + h * HEAD : 2 * wide + (h + 1) * HEAD]
            s = jnp.where(seen, dot_nt(q, k) * factor, -1e30)
            top = jnp.max(s, axis=-1, keepdims=True)
            e = jnp.exp(s - top)
            total = jnp.sum(e, axis=-1, keepdims=True)
            probs = (e * (1.0 / total)).astype(BF16)
            o_ref[at : at + block, h * HEAD : (h + 1) * HEAD] = dot(probs, v).astype(BF16)
            lse_ref[at : at + block, h : h + 1] = top + jnp.log(total)
    out_ref[...] = dot_nt(o_ref[...], w_ref[:, 3 * wide :]).astype(BF16)


def attend_forward(starts, a_all, w_attn, heads, gain=None):
    seq_len, width = a_all.shape
    wide = heads * HEAD
    spans = starts.shape[1]
    raw = gain is not None
    return pl.pallas_call(
        functools.partial(attend_kernel, heads, spans, PIC, raw),
        out_shape=[
            jax.ShapeDtypeStruct((seq_len, 3 * wide), BF16),
            jax.ShapeDtypeStruct((seq_len, wide), BF16),
            jax.ShapeDtypeStruct((seq_len, heads), F32),
            jax.ShapeDtypeStruct((seq_len, width), BF16),
        ]
        + [jax.ShapeDtypeStruct((seq_len, width), BF16)] * raw,
        in_specs=[pl.BlockSpec(memory_space=pltpu.SMEM)] + [VMEM_SPEC] * (2 + raw),
        out_specs=[VMEM_SPEC] * (4 + raw),
        compiler_params=pltpu.CompilerParams(vmem_limit_bytes=VMEM_LIMIT),
        cost_estimate=pl.CostEstimate(
            flops=8 * seq_len * width * wide + 4 * heads * seq_len * seq_len * HEAD,
            bytes_accessed=6 * seq_len * width,
            transcendentals=heads * seq_len * seq_len,
        ),
        name="attend_forward",
    )(starts, a_all, w_attn, *([gain] if raw else []))


def attend_back_kernel(
    heads, spans, block, starts_ref, g_ref, w_ref, a_ref, qkv_ref, o_ref, lse_ref,
    ga_ref, gw_ref, go_scr, gq_scr, gk_acc, gv_acc,
):
    seq_len = a_ref.shape[0]
    wide = heads * HEAD
    factor = HEAD ** (-0.5)
    go_scr[...] = dot(g_ref[...], w_ref[:, 3 * wide :]).astype(BF16)
    gw_ref[:, 3 * wide :] = dot_tn(g_ref[...], o_ref[...]).astype(BF16)
    gk_acc[...] = jnp.zeros_like(gk_acc)
    gv_acc[...] = jnp.zeros_like(gv_acc)
    for at in range(0, seq_len, block):
        reach = key_extent(at, seq_len, spans)
        seen = span_mask(starts_ref, at, block, reach, spans)
        for h in range(heads):
            own = slice(h * HEAD, (h + 1) * HEAD)
            q = qkv_ref[at : at + block, own]
            k = qkv_ref[:reach, wide + h * HEAD : wide + (h + 1) * HEAD]
            v = qkv_ref[:reach, 2 * wide + h * HEAD : 2 * wide + (h + 1) * HEAD]
            go = go_scr[at : at + block, own]
            s = jnp.where(seen, dot_nt(q, k) * factor, -1e30)
            probs = jnp.exp(s - lse_ref[at : at + block, h : h + 1])
            gp = dot_nt(go, v)
            inner = jnp.sum(probs * gp, axis=-1, keepdims=True)
            gs = (probs * (gp - inner)).astype(BF16)
            gq_scr[at : at + block, own] = (dot(gs, k) * factor).astype(BF16)
            gk_acc[:reach, own] += dot_tn(gs, q) * factor
            gv_acc[:reach, own] += dot_tn(probs.astype(BF16), go)
    gq_scr[:, wide : 2 * wide] = gk_acc[...].astype(BF16)
    gq_scr[:, 2 * wide :] = gv_acc[...].astype(BF16)
    gw_ref[:, : 3 * wide] = dot_tn(a_ref[...], gq_scr[...]).astype(BF16)
    ga_ref[...] = dot_nt(gq_scr[...], w_ref[:, : 3 * wide]).astype(BF16)


def attend_backward(starts, g_all, w_attn, a_all, qkv, o, lse, heads):
    seq_len, width = a_all.shape
    wide = heads * HEAD
    spans = starts.shape[1]
    return pl.pallas_call(
        functools.partial(attend_back_kernel, heads, spans, PIC),
        out_shape=[
            jax.ShapeDtypeStruct((seq_len, width), BF16),
            jax.ShapeDtypeStruct((width, 4 * wide), BF16),
        ],
        in_specs=[pl.BlockSpec(memory_space=pltpu.SMEM)] + [VMEM_SPEC] * 6,
        out_specs=[VMEM_SPEC] * 2,
        scratch_shapes=[
            pltpu.VMEM((seq_len, wide), BF16),
            pltpu.VMEM((seq_len, 3 * wide), BF16),
            pltpu.VMEM((seq_len, wide), F32),
            pltpu.VMEM((seq_len, wide), F32),
        ],
        compiler_params=pltpu.CompilerParams(vmem_limit_bytes=VMEM_LIMIT),
        cost_estimate=pl.CostEstimate(
            flops=16 * seq_len * width * wide + 10 * heads * seq_len * seq_len * HEAD,
            bytes_accessed=12 * seq_len * width,
            transcendentals=heads * seq_len * seq_len,
        ),
        name="attend_backward",
    )(starts, g_all, w_attn, a_all, qkv, o, lse)


def lane_column(values, at):
    lane = lax.broadcasted_iota(jnp.int32, values.shape, 1)
    return jnp.sum(jnp.where(lane == at, values, 0), axis=1, keepdims=True)


def two_parts(values):
    high = values.astype(BF16)
    return high, (values - high.astype(F32)).astype(BF16)


def const_parts(product, wd, layer, at, consts):
    first = EXPERTS + 2
    zero = shift(product, first - at["cmix"] - layer * 2 * consts)
    one = shift(product, first - at["cmix"] - layer * 2 * consts - consts)
    lane = lax.broadcasted_iota(jnp.int32, product.shape, 1)
    here = (lane >= first) & (lane < first + consts)
    gap = jnp.where(here, one - zero, 0.0)
    alpha0 = 1.0 / (1.0 + jnp.exp(gap))
    alpha1 = 1.0 / (1.0 + jnp.exp(-gap))
    gate = jnp.where(here, wd, 0.0)
    keep = jnp.sum(gate * alpha0 + jnp.where(lane == EXPERTS + 1, wd, 0.0), axis=1, keepdims=True)
    return lane, here, alpha0, alpha1, gate, keep


def experts_kernel(
    cap, layer, at, consts, b_ref, w_ref, rowpos_ref, pos_ref, small_ref, rows_ref, mix_ref, zprev_ref,
    mid_ref, x_ref, gu_ref, z_ref, wd_ref, f_ref, extra_ref, pick_scr, y_scr,
):
    e = pl.program_id(0)
    seq_len, width = b_ref.shape
    half = gu_ref.shape[2] // 2

    @pl.when(e == 0)
    def _():
        product = dot(b_ref[...], small_ref[...])
        lane = lax.broadcasted_iota(jnp.int32, product.shape, 1)
        p_high, p_low = two_parts(zprev_ref[...])
        z = (
            jnp.where(lane < NEXP, shift(product, -at["router"] - layer * NEXP), 0.0)
            + dot(p_high, mix_ref[...])
            + dot(p_low, mix_ref[...])
        )
        z_ref[...] = z
        hit = pos_ref[...] >= 0
        top = jnp.max(jnp.where(hit, z, -3e38), axis=1, keepdims=True)
        ez = jnp.where(hit, jnp.exp(jnp.where(hit, z - top, 0.0)), 0.0)
        wd = ez / jnp.sum(ez, axis=1, keepdims=True)
        wd_ref[...] = wd
        _, _, _, alpha1, gate, keep = const_parts(product, wd, layer, at, consts)
        extra = mid_ref[...].astype(F32) + keep * b_ref[...].astype(F32)
        for j in range(consts):
            row = at["cvec"] + layer * consts + j
            extra = extra + lane_column(gate * alpha1, EXPERTS + 2 + j) * rows_ref[row : row + 1, :]
        extra_ref[...] = extra.astype(BF16)

    w = w_ref[...].reshape(width, 3 * half)
    take = (
        lax.broadcasted_iota(jnp.int32, (cap, seq_len), 0) == rowpos_ref[0]
    ).astype(F32).astype(BF16)
    x = dot(take, b_ref[...]).astype(BF16)
    x_ref[0] = x
    gu = dot(x, w[:, : 2 * half])
    gu_ref[0] = gu.astype(BF16)
    g, u = gu[:, :half], gu[:, half:]
    h = (g * jax.nn.sigmoid(g) * u).astype(BF16)
    y = dot_nt(h, w[:, 2 * half :])
    y_scr[pl.ds(pl.multiple_of(e * cap, cap), cap), :] = y.astype(BF16)
    column = lane_column(pos_ref[...], e)
    weight = lane_column(wd_ref[...], e)
    put = jnp.where(
        lax.broadcasted_iota(jnp.int32, (seq_len, cap), 1) == column, weight, 0.0
    ).astype(BF16)
    pick_scr[:, pl.ds(pl.multiple_of(e * cap, cap), cap)] = put

    @pl.when(e == pl.num_programs(0) - 1)
    def _():
        f_ref[...] = dot(pick_scr[...], y_scr[...]).astype(BF16)


def whole(shape):
    return pl.BlockSpec(shape, lambda e: (0,) * len(shape))


def experts_forward(
    layer, at, consts, b_all, w_exp, rowpos, pos, small, rows_t, mix, z_prev, mid, cap
):
    seq_len, width = b_all.shape
    shards_dp, count, rows, wide3 = w_exp.shape
    half = wide3 // 3
    return pl.pallas_call(
        functools.partial(experts_kernel, cap, layer, at, consts),
        grid=(count,),
        out_shape=[
            jax.ShapeDtypeStruct((count, cap, width), BF16),
            jax.ShapeDtypeStruct((count, cap, 2 * half), BF16),
            jax.ShapeDtypeStruct((seq_len, LANES), F32),
            jax.ShapeDtypeStruct((seq_len, LANES), F32),
            jax.ShapeDtypeStruct((seq_len, width), BF16),
            jax.ShapeDtypeStruct((seq_len, width), BF16),
        ],
        in_specs=[
            whole((seq_len, width)),
            pl.BlockSpec((shards_dp, 1, rows, wide3), lambda e: (0, e, 0, 0)),
            pl.BlockSpec((1, 1, seq_len), lambda e: (e, 0, 0)),
            whole((seq_len, LANES)),
            whole((width, LANES)),
            whole(rows_t.shape),
            whole((LANES, LANES)),
            whole((seq_len, LANES)),
            whole((seq_len, width)),
        ],
        out_specs=[
            pl.BlockSpec((1, cap, width), lambda e: (e, 0, 0)),
            pl.BlockSpec((1, cap, 2 * half), lambda e: (e, 0, 0)),
            whole((seq_len, LANES)),
            whole((seq_len, LANES)),
            whole((seq_len, width)),
            whole((seq_len, width)),
        ],
        scratch_shapes=[
            pltpu.VMEM((seq_len, count * cap), BF16),
            pltpu.VMEM((count * cap, width), BF16),
        ],
        compiler_params=pltpu.CompilerParams(vmem_limit_bytes=VMEM_LIMIT),
        cost_estimate=pl.CostEstimate(
            flops=count * (4 * cap * seq_len * width + 6 * cap * width * half),
            bytes_accessed=2 * count * width * wide3,
            transcendentals=0,
        ),
        name="experts_forward",
    )(b_all, w_exp, rowpos, pos, small, rows_t, mix, z_prev, mid)


def experts_back_kernel(
    cap, layer, at, consts, own, g_ref, w_ref, x_ref, gu_ref, rowpos_ref, pos_ref, wd_ref,
    b_ref, small_ref, rows_ref, mix_ref, zprev_ref, gprev_ref, sums_ref, mixes_ref,
    gw_ref, below_ref, gb_ref, sums_out, mixes_out, pick_scr, gx_scr, gg_scr, gb_scr, zs_scr,
    halves, inbox, out_sems, in_sems,
):
    e = pl.program_id(0)
    last = pl.num_programs(0) - 1
    me = lax.axis_index("dp")
    parity = lax.rem(me, 2)
    partner = me + 1 - 2 * parity

    def to_partner(expert):
        return pltpu.make_async_remote_copy(
            src_ref=halves.at[lax.rem(expert, 2), 1 - parity],
            dst_ref=inbox.at[expert],
            send_sem=out_sems.at[expert],
            recv_sem=in_sems.at[expert],
            device_id={"dp": partner},
            device_id_type=MESH,
        )

    @pl.when(e == 0)
    def _():
        barrier = pltpu.get_barrier_semaphore()
        pl.semaphore_signal(barrier, inc=1, device_id={"dp": partner}, device_id_type=MESH)
        pl.semaphore_wait(barrier, 1)

    @pl.when(e < last)
    def _():
        one_expert_back(
            cap, e, g_ref, w_ref, x_ref, gu_ref, rowpos_ref, pos_ref, wd_ref, pick_scr, gx_scr, gg_scr,
            halves,
        )
        to_partner(e).start()

    @pl.when(e > 0)
    def _():
        before = e - 1
        to_partner(before).wait()
        gw_ref[:, 0] = (
            halves[lax.rem(before, 2), parity].astype(F32) + inbox[before].astype(F32)
        ).astype(BF16)

    @pl.when(e == last)
    def _():
        tokens_back(
            layer, at, consts, own, g_ref, wd_ref, b_ref, small_ref, rows_ref, mix_ref, zprev_ref,
            gprev_ref, sums_ref, mixes_ref, below_ref, gb_ref, sums_out, mixes_out, pick_scr, gx_scr,
            gg_scr, gb_scr, zs_scr,
        )


def one_expert_back(
    cap, e, g_ref, w_ref, x_ref, gu_ref, rowpos_ref, pos_ref, wd_ref, pick_scr, gx_scr, gg_scr, halves,
):
    seq_len, width = g_ref.shape
    shards_dp, _, rows, wide3 = w_ref.shape
    half = wide3 // 3
    slot = lax.rem(e, 2)
    w = w_ref[...].reshape(width, wide3)
    take = (
        lax.broadcasted_iota(jnp.int32, (cap, seq_len), 0) == rowpos_ref[0]
    ).astype(F32).astype(BF16)
    w_high, w_low = two_parts(wd_ref[...])
    weight = lane_column(dot(take, w_high) + dot(take, w_low), e)
    gf = dot(take, g_ref[...])
    gh = dot(gf.astype(BF16), w[:, 2 * half :])
    gu = gu_ref[0].astype(F32)
    g, u = gu[:, :half], gu[:, half:]
    sig = jax.nn.sigmoid(g)
    h = (g * sig * u).astype(BF16)
    slot_grad = jnp.sum(h.astype(F32) * gh, axis=1, keepdims=True)
    gh = gh * weight
    gg = gh * u * sig * (1.0 + g * (1.0 - sig))
    gup = gh * g * sig
    both = jnp.concatenate([gg.astype(BF16), gup.astype(BF16)], axis=1)
    gy = (gf * weight).astype(BF16)
    gw_in = dot_tn(x_ref[0], both).astype(BF16)
    gw_down = dot_tn(gy, h).astype(BF16)
    for shard in range(shards_dp):
        own_rows = slice(shard * rows, (shard + 1) * rows)
        halves[slot, shard % 2, shard // 2, :, : 2 * half] = gw_in[own_rows]
        halves[slot, shard % 2, shard // 2, :, 2 * half :] = gw_down[own_rows]
    here = pl.ds(pl.multiple_of(e * cap, cap), cap)
    gx_scr[here, :] = dot_nt(both, w[:, : 2 * half]).astype(BF16)
    s_high, s_low = two_parts(slot_grad)
    lane = lax.broadcasted_iota(jnp.int32, (cap, LANES), 1)
    gg_scr[here, :LANES] = jnp.where(lane == e, s_high.astype(F32), 0.0).astype(BF16)
    gg_scr[here, LANES:] = jnp.where(lane == e, s_low.astype(F32), 0.0).astype(BF16)
    column = lane_column(pos_ref[...], e)
    pick_scr[:, here] = (
        lax.broadcasted_iota(jnp.int32, (seq_len, cap), 1) == column
    ).astype(F32).astype(BF16)


def tokens_back(
    layer, at, consts, own, g_ref, wd_ref, b_ref, small_ref, rows_ref, mix_ref, zprev_ref, gprev_ref,
    sums_ref, mixes_ref, below_ref, gb_ref, sums_out, mixes_out, pick_scr, gx_scr, gg_scr, gb_scr, zs_scr,
):
    mine = pl.ds(pl.multiple_of(lax.axis_index("tensor") * own, own), own)
    b_own, g_own = b_ref[mine, :], g_ref[mine, :].astype(F32)
    wd_own = wd_ref[mine, :]
    lane, here_own, alpha0, alpha1, gate, keep = const_parts(
        dot(b_own, small_ref[...]), wd_own, layer, at, consts
    )
    b_dot = jnp.sum(b_own.astype(F32) * g_own, axis=1, keepdims=True)
    c_dot = jnp.zeros_like(wd_own)
    for j in range(consts):
        row = at["cvec"] + layer * consts + j
        one = jnp.sum(g_own * rows_ref[row : row + 1, :], axis=1, keepdims=True)
        c_dot = jnp.where(lane == EXPERTS + 2 + j, one, c_dot)
    gw_own = jnp.where(here_own, alpha0 * b_dot + alpha1 * c_dot, 0.0)
    gw_own = jnp.where(lane == EXPERTS + 1, b_dot, gw_own)
    inner = gate * (alpha0 * b_dot + alpha1 * c_dot)
    gt0 = alpha0 * (gate * b_dot - inner)
    gt1 = alpha1 * (gate * c_dot - inner)

    slots = dot(pick_scr[...], gg_scr[...])
    zs_scr[...] = slots[:, :LANES] + slots[:, LANES:]
    zs_scr[mine, :] += gw_own
    gw = zs_scr[...]
    wd = wd_ref[...]
    gz = wd * (gw - jnp.sum(wd * gw, axis=1, keepdims=True)) + gprev_ref[...]
    z_high, z_low = two_parts(gz)
    below_ref[...] = dot_nt(z_high, mix_ref[...]) + dot_nt(z_low, mix_ref[...])
    p_high, p_low = two_parts(zprev_ref[...])
    mixes_out[...] = mixes_ref[...] + shift(
        dot_tn(p_high, z_high) + dot_tn(p_high, z_low) + dot_tn(p_low, z_high), layer * MIX_STEP
    )
    zs_scr[...] = shift(gz, at["router"] + layer * NEXP)
    up = at["cmix"] + layer * 2 * consts - EXPERTS - 2
    zs_scr[mine, :] += shift(gt0, up) + shift(gt1, up + consts)
    z_high, z_low = two_parts(zs_scr[...])
    gb_scr[...] = (
        dot(pick_scr[...], gx_scr[...])
        + dot_nt(z_high, small_ref[...])
        + dot_nt(z_low, small_ref[...])
    )
    gb_scr[mine, :] += keep * g_own
    gb_ref[...] = gb_scr[...].astype(BF16)
    i_high, i_low = two_parts(
        shift(gate * alpha1, at["cvec"] + layer * consts - EXPERTS - 2)
    )
    g_low = g_ref[mine, :]
    sums_out[...] = (
        sums_ref[...]
        + dot_tn(b_ref[...], z_high)
        + dot_tn(b_ref[...], z_low)
        + dot_tn(g_low, i_high)
        + dot_tn(g_low, i_low)
    )


def experts_backward(
    collective_id, layer, at, consts, own, g_all, w_exp, x, gu, rowpos, pos, wd, b_all, small, rows_t, mix,
    z_prev, grad_prev, sums, mixes, cap,
):
    seq_len, width = g_all.shape
    shards_dp, count, rows, wide3 = w_exp.shape
    half = wide3 // 3
    weight_spec = pl.BlockSpec(
        (shards_dp, 1, rows, wide3), lambda e: (0, jnp.minimum(e, count - 1), 0, 0)
    )
    half_shape = (shards_dp // 2, 1, rows, wide3)
    return pl.pallas_call(
        functools.partial(experts_back_kernel, cap, layer, at, consts, own),
        grid=(count + 1,),
        out_shape=[
            jax.ShapeDtypeStruct((shards_dp // 2,) + w_exp.shape[1:], BF16),
            jax.ShapeDtypeStruct((seq_len, LANES), F32),
            jax.ShapeDtypeStruct((seq_len, width), BF16),
            jax.ShapeDtypeStruct((width, LANES), F32),
            jax.ShapeDtypeStruct((LANES, LANES), F32),
        ],
        in_specs=[
            whole((seq_len, width)),
            weight_spec,
            pl.BlockSpec((1, cap, width), lambda e: (jnp.minimum(e, count - 1), 0, 0)),
            pl.BlockSpec((1, cap, 2 * half), lambda e: (jnp.minimum(e, count - 1), 0, 0)),
            pl.BlockSpec((1, 1, seq_len), lambda e: (jnp.minimum(e, count - 1), 0, 0)),
            whole((seq_len, LANES)),
            whole((seq_len, LANES)),
            whole((seq_len, width)),
            whole((width, LANES)),
            whole(rows_t.shape),
            whole((LANES, LANES)),
            whole((seq_len, LANES)),
            whole((seq_len, LANES)),
            whole((width, LANES)),
            whole((LANES, LANES)),
        ],
        out_specs=[
            pl.BlockSpec(half_shape, lambda e: (0, jnp.maximum(e - 1, 0), 0, 0)),
            whole((seq_len, LANES)),
            whole((seq_len, width)),
            whole((width, LANES)),
            whole((LANES, LANES)),
        ],
        scratch_shapes=[
            pltpu.VMEM((seq_len, count * cap), BF16),
            pltpu.VMEM((count * cap, width), BF16),
            pltpu.VMEM((count * cap, 2 * LANES), BF16),
            pltpu.VMEM((seq_len, width), F32),
            pltpu.VMEM((seq_len, LANES), F32),
            pltpu.VMEM((2, 2, shards_dp // 2, rows, wide3), BF16),
            pltpu.VMEM((count, shards_dp // 2, rows, wide3), BF16),
            pltpu.SemaphoreType.DMA((count,)),
            pltpu.SemaphoreType.DMA((count,)),
        ],
        compiler_params=pltpu.CompilerParams(
            collective_id=collective_id, has_side_effects=True, vmem_limit_bytes=VMEM_LIMIT
        ),
        cost_estimate=pl.CostEstimate(
            flops=count * (4 * cap * seq_len * width + 12 * cap * width * half),
            bytes_accessed=4 * count * width * wide3,
            transcendentals=0,
        ),
        name="experts_backward",
    )(
        g_all, w_exp, x, gu, rowpos, pos, wd, b_all, small, rows_t, mix, z_prev, grad_prev,
        sums, mixes,
    )


def unpack_kernel(half, *refs):
    *in_refs, up_ref, down_ref = refs
    for l, ref in enumerate(in_refs):
        values = ref[0].astype(F32)
        for part in range(2):
            up_ref[l, 0, :, part, :] = values[:, part * half : (part + 1) * half]
        down_ref[l, 0] = values[:, 2 * half :]


def unpack(items):
    count, rows, wide3 = items[0].shape
    half = wide3 // 3
    layers = len(items)
    return pl.pallas_call(
        functools.partial(unpack_kernel, half),
        grid=(count,),
        out_shape=[
            jax.ShapeDtypeStruct((layers, count, rows, 2, half), F32),
            jax.ShapeDtypeStruct((layers, count, rows, half), F32),
        ],
        in_specs=[pl.BlockSpec((1, rows, wide3), lambda e: (e, 0, 0))] * layers,
        out_specs=[
            pl.BlockSpec((layers, 1, rows, 2, half), lambda e: (0, e, 0, 0, 0)),
            pl.BlockSpec((layers, 1, rows, half), lambda e: (0, e, 0, 0)),
        ],
        compiler_params=pltpu.CompilerParams(vmem_limit_bytes=VMEM_LIMIT),
        name="unpack",
    )(*items)


def lanes(values):
    return jnp.pad(values, ((0, 0), (0, LANES - values.shape[1])))


def slot_table(route_ids):
    tokens = route_ids.shape[0]
    codes = jnp.arange(LANES, dtype=jnp.int32)
    hit = jnp.any(route_ids[:, :, None] == codes[None, None, :], axis=1)
    place = jnp.arange(tokens, dtype=jnp.int32)
    before = (place[None, :] < place[:, None]).astype(BF16)
    slots = dot(before, hit.astype(BF16)).astype(jnp.int32)
    return jnp.where(hit, slots, -1)


def shards(
    hidden_in,
    prev_logits,
    routes,
    span_starts,
    attn_norm,
    qkv_weight,
    out_weight,
    moe_norm,
    router,
    gate_mix,
    const_vec,
    const_mix,
    up_weight,
    down_weight,
    out_grad,
):
    layers = qkv_weight.shape[0]
    own, width = hidden_in.shape
    nt = lax.axis_size("tensor")
    ndp = lax.axis_size("dp")
    seq_len = own * nt
    offset = lax.axis_index("tensor") * own
    cap = seq_len // 4
    heads = qkv_weight.shape[3] // HEAD
    wide = heads * HEAD
    half = up_weight.shape[4]
    rows = qkv_weight.shape[1]
    cols = attn_norm.shape[1]
    consts = const_vec.shape[1]

    at = layout(layers, consts)
    packed = jnp.concatenate(
        [attn_norm.T, moe_norm.T]
        + [router[l] for l in range(layers)]
        + [const_vec.reshape(-1, cols).T]
        + [const_mix[l, :, :, k].T for l in range(layers) for k in range(2)],
        axis=1,
    )
    x_all, small = line_exchange("start", [hidden_in, lanes(packed)], own, width, 0)
    small = small.reshape(width, LANES)
    rows_t = small[:, :48].T.astype(F32)

    attn_w, exp_w = [], []
    for l in range(layers):
        local = jnp.concatenate(
            [qkv_weight[l].reshape(rows, 3 * wide), out_weight[l].T], axis=1
        )
        attn_w.append(lax.all_gather(local, "dp", axis=0, tiled=False).reshape(width, 4 * wide))
        local = jnp.concatenate(
            [
                up_weight[l].reshape(EXPERTS, rows, 2 * half),
                jnp.swapaxes(down_weight[l], 1, 2),
            ],
            axis=2,
        )
        exp_w.append(lax.all_gather(local, "dp", axis=0, tiled=False))

    pos = [slot_table(routes[l]) for l in range(layers)]
    rowpos = [p[:, :EXPERTS].T[:, None, :] for p in pos]

    z_prev = lanes(prev_logits)
    hidden, a_all = x_all, None
    grad_all = out_grad
    next_id = 1
    stored = []
    for l in range(layers):
        mix = jnp.pad(gate_mix[l], ((0, LANES - NEXP), (0, LANES - NEXP)))
        if l == 0:
            qkv, o, lse, partial, a_all = attend_forward(
                span_starts, x_all, attn_w[l], heads, rows_t
            )
        else:
            qkv, o, lse, partial = attend_forward(span_starts, a_all, attn_w[l], heads)
        if l == layers - 1:
            partial, grad_all = lax.optimization_barrier((partial, grad_all))
            grad_all = lax.all_gather(grad_all, "tensor", axis=0, tiled=True)
        mid, b_all = join(False, partial, [hidden], rows_t, at["moe"] + l, next_id)
        x, gu, z, wd, partial, extra = experts_forward(
            l, at, consts, b_all, exp_w[l], rowpos[l], pos[l], small, rows_t, mix, z_prev, mid, cap
        )
        stored.append(
            dict(
                hidden=hidden, a_all=a_all, qkv=qkv, o=o, lse=lse, mid=mid, b_all=b_all, x=x, gu=gu,
                wd=wd, z_prev=z_prev, mix=mix,
            )
        )
        if l + 1 < layers:
            hidden, a_all = join(False, partial, [extra], rows_t, at["attn"] + l + 1, next_id + 1)
        else:
            hidden_out = lax.psum_scatter(partial, "tensor", scatter_dimension=0, tiled=True)
            extra = lax.dynamic_slice_in_dim(extra, offset, own, 0)
        z_prev = z
        next_id += 2

    below = jnp.zeros((seq_len, LANES), F32)
    sums = jnp.zeros((width, LANES), F32)
    mixes = jnp.zeros((LANES, LANES), F32)
    attn_grads, exp_grads = [None] * layers, [None] * layers
    gains_a, gains_m = [None] * layers, [None] * layers
    for l in reversed(range(layers)):
        s = stored[l]
        gw_exp, below, partial, sums, mixes = experts_backward(
            next_id + 2, l, at, consts, own, grad_all, exp_w[l], s["x"], s["gu"], rowpos[l],
            pos[l], s["wd"], s["b_all"], small, rows_t, s["mix"], s["z_prev"], below, sums, mixes, cap,
        )
        exp_grads[l] = sum_over_pairs(gw_exp)
        if l + 1 < layers:
            partial, exp_grads[l + 1] = lax.optimization_barrier((partial, exp_grads[l + 1]))
        else:
            partial, hidden_out = lax.optimization_barrier((partial, hidden_out))
        grad_mid, gains_m[l] = join(
            True, partial, [s["mid"], grad_all], rows_t, at["moe"] + l, next_id
        )
        partial, gw_attn = attend_backward(
            span_starts, grad_mid, attn_w[l], s["a_all"], s["qkv"], s["o"], s["lse"], heads
        )
        attn_grads[l] = gw_attn.reshape(ndp, rows, 4 * wide)
        if l > 0:
            attn_grads[l] = lax.psum_scatter(attn_grads[l], "dp", scatter_dimension=0, tiled=False)
            grad_all, gains_a[l] = join(
                True, partial, [s["hidden"], grad_mid], rows_t, at["attn"] + l, next_id + 1
            )
        else:
            partial, attn_grads[1:] = lax.optimization_barrier((partial, attn_grads[1:]))
            skip = lax.dynamic_slice_in_dim(grad_mid, offset, own, 0)
            grad, gains_a[l] = line_exchange(
                "end", [partial, hidden_in, skip, rows_t], own, width, next_id + 1
            )
        next_id += 3
    hidden_out = hidden_out.astype(F32) + extra.astype(F32)

    gains = jnp.concatenate(gains_a + gains_m, axis=0)
    sums = sums + jnp.pad(gains, ((0, LANES - 2 * layers), (0, 0))).T
    sums = jnp.concatenate(
        [
            sums.reshape(ndp * nt, cols, LANES),
            jnp.broadcast_to(mixes[None, :MIX_STEP], (ndp * nt, MIX_STEP, LANES)),
        ],
        axis=1,
    )
    attn_g, moe_g, router_g, mix_g, cvec_g, cmix_g, qkv_g, outw_g = closing(
        sums, attn_grads[0], jnp.stack(attn_grads[1:]), consts, layers, cols, next_id
    )
    up_grad, down_grad = unpack(exp_grads)
    qkv_g = jnp.swapaxes(qkv_g, 1, 2)
    router_g = jnp.transpose(router_g, (1, 2, 0))
    mix_g = jnp.swapaxes(mix_g, 0, 1)
    cmix_g = jnp.swapaxes(cmix_g, 2, 3)
    down_grad = jnp.swapaxes(down_grad, 2, 3)
    return (
        hidden_out,
        grad,
        attn_g,
        qkv_g,
        outw_g,
        moe_g,
        router_g,
        mix_g,
        cvec_g,
        cmix_g,
        up_grad,
        down_grad,
    )


def sum_over_pairs(values):
    members = lax.axis_size("dp")
    groups = [list(range(parity, members, 2)) for parity in range(2)]
    return lax.psum_scatter(
        values, "dp", scatter_dimension=0, axis_index_groups=groups, tiled=False
    )


def solution(mesh):
    return jax.shard_map(
        shards,
        mesh=mesh,
        in_specs=(
            P(("dp", "tensor"), None),
            P("dp", None),
            P(None, "dp", None),
            P("dp", None),
            P(None, ("dp", "tensor")),
            P(None, "dp", None, "tensor"),
            P(None, "tensor", "dp"),
            P(None, ("dp", "tensor")),
            P(None, ("dp", "tensor"), None),
            P(),
            P(None, None, ("dp", "tensor")),
            P(None, None, ("dp", "tensor"), None),
            P(None, None, "dp", None, "tensor"),
            P(None, None, "tensor", "dp"),
            P(("dp", "tensor"), None),
        ),
        out_specs=(
            P(("dp", "tensor"), None),
            P(("dp", "tensor"), None),
            P(None, ("dp", "tensor")),
            P(None, "dp", None, "tensor"),
            P(None, "tensor", "dp"),
            P(None, ("dp", "tensor")),
            P(None, ("dp", "tensor"), None),
            P(),
            P(None, None, ("dp", "tensor")),
            P(None, None, ("dp", "tensor"), None),
            P(None, None, "dp", None, "tensor"),
            P(None, None, "tensor", "dp"),
        ),
        check_vma=False,
    )
```

```python
import functools

import jax
import jax.numpy as jnp
from jax import lax
from jax.experimental import pallas as pl
from jax.experimental.pallas import tpu as pltpu
from jax.sharding import PartitionSpec as P

HEAD = 64
EXPERTS = 8
NEXP = 12
TOPK = 2
PIC = 256
LANES = 128

EPS = 1e-06
HIGH = lax.Precision.HIGHEST
MESH = pl.DeviceIdType.MESH
F32 = jnp.float32
BF16 = jnp.bfloat16
VMEM_SPEC = pl.BlockSpec(memory_space=pltpu.VMEM)
AHEAD = 2
PIECES = 32
LAG = 4
APART = 16000
MIX_STEP = 16
VMEM_LIMIT = 60 * 1024 * 1024


def dot(a, b):
    return jnp.dot(a, b, preferred_element_type=F32)


def dot_nt(a, b):
    return lax.dot_general(a, b, (((1,), (1,)), ((), ())), preferred_element_type=F32)


def dot_tn(a, b):
    return lax.dot_general(a, b, (((0,), (0,)), ((), ())), preferred_element_type=F32)


def layout(layers, consts):
    at, begin = {}, 0
    for name, size in (
        ("attn", layers),
        ("moe", layers),
        ("router", layers * NEXP),
        ("cvec", layers * consts),
        ("cmix", layers * consts * 2),
    ):
        at[name] = begin
        begin += size
    return at


def shift(values, lanes_up):
    return pltpu.roll(values, lanes_up % LANES, 1)


def greet_all(count, me, place):
    barrier = pltpu.get_barrier_semaphore()

    def greet(step, carry):
        other = lax.rem(me + step, count)
        pl.semaphore_signal(barrier, inc=1, device_id=place(other), device_id_type=MESH)
        return carry

    lax.fori_loop(1, count, greet, 0)
    pl.semaphore_wait(barrier, count - 1)


def swap_all(count, me, place, source, land, send_sems, recv_sems):
    def copy(other, slot):
        return pltpu.make_async_remote_copy(
            src_ref=source(other),
            dst_ref=land.at[slot],
            send_sem=send_sems.at[other],
            recv_sem=recv_sems.at[slot],
            device_id=place(other),
            device_id_type=MESH,
        )

    def start():
        def send(step, carry):
            other = lax.rem(me + step, count)
            copy(other, me).start()
            return carry

        lax.fori_loop(1, count, send, 0)

    def finish():
        def wait(step, carry):
            other = lax.rem(me + count - step, count)
            copy(other, other).wait()
            return carry

        lax.fori_loop(1, count, wait, 0)

    return start, finish


def closing_kernel(ndp, inner, layers, consts, wide, *refs):
    small_ref, proj_ref, above_ref = refs[:3]
    attn_out, moe_out, router_out, mix_out, cvec_out, cmix_out, qkv_out, outw_out = refs[3:11]
    land, proj_land, square, tall = refs[11:15]
    sems = refs[15:]
    count = ndp * inner
    row, col = lax.axis_index("dp"), lax.axis_index("tensor")
    me = row * inner + col
    cols = attn_out.shape[1]
    rows = qkv_out.shape[2]

    def anywhere(other):
        return (lax.div(other, inner), lax.rem(other, inner))

    def along(other):
        return (other, col)

    def piece(ref):
        return lambda other: ref.at[other]

    greet_all(count, me, anywhere)
    moves = [
        swap_all(ndp, row, along, piece(proj_ref), proj_land, *sems[2:4]),
        swap_all(count, me, anywhere, piece(small_ref), land, *sems[0:2]),
    ]
    for start, _ in moves:
        start()
    land[me] = small_ref[me]
    proj_land[row] = proj_ref[row]
    square[...] = jnp.zeros_like(square)
    tall[...] = jnp.zeros_like(tall)

    def place(l, total):
        for part in range(3):
            qkv_out[l, part] = total[:, part * wide : (part + 1) * wide]
        tall[:rows, :wide] = total[:, 3 * wide :]
        outw_out[l] = tall[...].T[:wide, :rows]

    for l in range(1, layers):
        place(l, above_ref[l - 1].astype(F32))
    moves[0][1]()
    place(0, jnp.sum(proj_land[...].astype(F32), axis=0))
    moves[1][1]()
    total = jnp.sum(land[...], axis=0)
    square[:cols, :] = total[:cols]
    turned = square[...].T
    at = layout(layers, consts)
    attn_out[...] = turned[at["attn"] : at["attn"] + layers, :cols]
    moe_out[...] = turned[at["moe"] : at["moe"] + layers, :cols]
    for l in range(layers):
        begin = at["router"] + l * NEXP
        for e in range(NEXP):
            router_out[e, l : l + 1, :] = turned[begin + e : begin + e + 1, :cols]
            mix_out[e, l : l + 1, :] = total[
                cols + e : cols + e + 1, l * MIX_STEP : l * MIX_STEP + NEXP
            ]
        begin = at["cvec"] + l * consts
        cvec_out[l] = turned[begin : begin + consts, :cols]
        begin = at["cmix"] + l * 2 * consts
        for j in range(consts):
            for k in range(2):
                lane = begin + k * consts + j
                cmix_out[l, j, k : k + 1, :] = turned[lane : lane + 1, :cols]


def closing(small, projection, above, consts, layers, cols, collective_id):
    inner, ndp = lax.axis_size("tensor"), lax.axis_size("dp")
    rows, packed = projection.shape[1:]
    wide = packed // 4
    shapes = [
        (layers, cols), (layers, cols), (NEXP, layers, cols), (NEXP, layers, NEXP),
        (layers, consts, cols), (layers, consts, 2, cols),
        (layers, 3, rows, wide), (layers, wide, rows),
    ]
    return pl.pallas_call(
        functools.partial(closing_kernel, ndp, inner, layers, consts, wide),
        out_shape=[jax.ShapeDtypeStruct(shape, F32) for shape in shapes],
        in_specs=[VMEM_SPEC] * 3,
        out_specs=[VMEM_SPEC] * len(shapes),
        scratch_shapes=[
            pltpu.VMEM(small.shape, F32),
            pltpu.VMEM(projection.shape, BF16),
            pltpu.VMEM((-(-cols // LANES) * LANES, LANES), F32),
            pltpu.VMEM((-(-rows // LANES) * LANES, -(-wide // LANES) * LANES), F32),
        ]
        + [pltpu.SemaphoreType.DMA((ndp * inner,))] * 2
        + [pltpu.SemaphoreType.DMA((ndp,))] * 2,
        compiler_params=pltpu.CompilerParams(
            collective_id=collective_id, has_side_effects=True, vmem_limit_bytes=VMEM_LIMIT
        ),
        name="closing",
    )(small, projection, above)


def join_kernel(back, gain_row, nt, pieces, lag, wait, *refs):
    if back:
        part, base_ref, skip_ref, rows_ref, result_ref, gg_ref = refs[:6]
    else:
        part, base_ref, rows_ref, total_ref, normed_ref = refs[:5]
    refs = refs[6 if back else 5 :]
    inbox, half, across, full, out_sem, in_sem, cross_out, cross_in, full_out, full_in = refs
    me = lax.axis_index("tensor")
    is_end = (me == 0) | (me == nt - 1)
    buddy = jnp.where(me < 2, 1 - me, 5 - me)
    cross = 3 - me

    if wait:
        @pl.when(lax.rem(lax.axis_index("dp"), 2) == 1)
        def _():
            pl.delay(wait)

    barrier = pltpu.get_barrier_semaphore()
    pl.semaphore_signal(barrier, inc=1, device_id={"tensor": buddy}, device_id_type=MESH)

    @pl.when(jnp.logical_not(is_end))
    def _():
        pl.semaphore_signal(barrier, inc=1, device_id={"tensor": cross}, device_id_type=MESH)

    pl.semaphore_wait(barrier, 2 - is_end.astype(jnp.int32))

    def copy(src, dst, send_sem, recv_sem, to):
        return pltpu.make_async_remote_copy(
            src_ref=src,
            dst_ref=dst,
            send_sem=send_sem,
            recv_sem=recv_sem,
            device_id={"tensor": to},
            device_id_type=MESH,
        )

    def inward(n):
        return copy(part.at[n], inbox.at[n], out_sem.at[n], in_sem.at[n], buddy)

    def over(n):
        return copy(half.at[n], across.at[n], cross_out.at[n], cross_in.at[n], cross)

    def outward(n):
        return copy(full.at[n], full.at[n], full_out.at[n], full_in.at[n], buddy)

    gain = rows_ref[gain_row : gain_row + 1, :]
    if back:
        gg_ref[...] = jnp.zeros_like(gg_ref)

    def settle(n):
        total = full[n].astype(F32)
        base = base_ref[n].astype(F32)
        if back:
            scale = lax.rsqrt(jnp.mean(base * base, axis=-1, keepdims=True) + EPS)
            unit = base * scale
            grad_unit = total * gain
            below = scale * (grad_unit - unit * jnp.mean(grad_unit * unit, axis=-1, keepdims=True))
            result_ref[n] = (below + skip_ref[n].astype(F32)).astype(BF16)

            @pl.when(lax.div(n, pieces // nt) == me)
            def _():
                gg_ref[...] += jnp.sum(total * unit, axis=0, keepdims=True)
        else:
            total = total + base
            total_ref[n] = total.astype(BF16)
            normed_ref[n] = normed(total, gain).astype(BF16)

    @pl.when(is_end)
    def _():
        for n in range(pieces):
            inward(n).start()

        def take(n, carry):
            outward(n).wait_recv()
            settle(n)
            return carry

        lax.fori_loop(0, pieces, take, 0)
        for n in range(pieces):
            inward(n).wait_send()

    @pl.when(jnp.logical_not(is_end))
    def _():
        def step(at, carry):
            @pl.when(at < pieces)
            def _():
                inward(at).wait_recv()
                half[at] = (part[at].astype(F32) + inbox[at].astype(F32)).astype(BF16)
                over(at).start()

            @pl.when(at >= lag)
            def _():
                n = at - lag
                over(n).wait_recv()
                full[n] = (half[n].astype(F32) + across[n].astype(F32)).astype(BF16)
                outward(n).start()
                settle(n)

            return carry

        lax.fori_loop(0, pieces + lag, step, 0)
        for n in range(pieces):
            over(n).wait_send()
            outward(n).wait_send()


def join(back, part, others, rows, gain_row, collective_id, wait=0, pieces=PIECES, lag=LAG):
    nt = lax.axis_size("tensor")
    seq_len, width = part.shape
    cut = (pieces, seq_len // pieces, width)
    outs = [jax.ShapeDtypeStruct(cut, BF16)]
    outs.append(jax.ShapeDtypeStruct((1, width) if back else cut, F32 if back else BF16))
    sems = pltpu.SemaphoreType.DMA((pieces,))
    results = pl.pallas_call(
        functools.partial(join_kernel, back, gain_row, nt, pieces, lag, wait),
        out_shape=outs,
        in_specs=[VMEM_SPEC] * (2 + len(others)),
        out_specs=[VMEM_SPEC] * 2,
        scratch_shapes=[pltpu.VMEM(cut, BF16)] * 4 + [sems] * 6,
        compiler_params=pltpu.CompilerParams(
            collective_id=collective_id, has_side_effects=True, vmem_limit_bytes=VMEM_LIMIT
        ),
        cost_estimate=pl.CostEstimate(
            flops=10 * seq_len * width, bytes_accessed=100 * seq_len * width, transcendentals=0
        ),
        name="join_back" if back else "join",
    )(part.reshape(cut), *[item.reshape(cut) for item in others], rows)
    return results[0].reshape(seq_len, width), (
        results[1] if back else results[1].reshape(seq_len, width)
    )


def normed(values, gain):
    return values * lax.rsqrt(jnp.mean(values * values, axis=-1, keepdims=True) + EPS) * gain


def line_kernel(kind, nt, chunks, lag, extra, *refs):
    refs = list(refs)
    has_sum = kind != "start"
    has_gather = kind != "end"
    part = refs.pop(0) if has_sum else None
    if kind == "start":
        x_ref, small_ref = refs.pop(0), refs.pop(0)
        proj_refs = [refs.pop(0) for _ in range(extra)]
    elif kind == "fwd":
        extra_ref, gain_ref = refs.pop(0), refs.pop(0)
    elif kind == "last":
        extra_ref, og_ref = refs.pop(0), refs.pop(0)
    else:
        extra_ref = refs.pop(0) if extra else None
        base_ref, skip_ref, rows_ref = refs.pop(0), refs.pop(0), refs.pop(0)
    own_ref = refs.pop(0) if has_sum else None
    gg_ref = refs.pop(0) if kind in ("bwd", "end") else None
    all_ref = refs.pop(0) if has_gather else None
    if kind == "start":
        land_ref = refs.pop(0)
        proj_lands = [refs.pop(0) for _ in range(extra)]
    if has_sum:
        from_left, from_right, tx, acc, rs_send, rl_sem, rr_sem = refs[:7]
        refs = refs[7:]
    if has_gather:
        ag_right, ag_left, ag_recv = refs[:3]
        refs = refs[3:]

    me = lax.axis_index("tensor")
    has_l, has_r = me > 0, me < nt - 1
    left, right = jnp.maximum(me - 1, 0), jnp.minimum(me + 1, nt - 1)

    if kind == "start":
        count = lax.axis_size("dp") * nt
        me_all = lax.axis_index("dp") * nt + me

        def place(other):
            return (lax.div(other, nt), lax.rem(other, nt))

        greet_all(count, me_all, place)
        small_start, small_finish = swap_all(
            count, me_all, place, lambda other: small_ref, land_ref, *refs[:2]
        )
        row = lax.axis_index("dp")
        members = lax.axis_size("dp")
        proj_moves = [
            swap_all(
                members, row, lambda other: (other, me), lambda other, ref=ref: ref, to,
                *refs[2 + 2 * n : 4 + 2 * n],
            )
            for n, (ref, to) in enumerate(zip(proj_refs, proj_lands))
        ]
        small_start()
        for start, _ in proj_moves:
            start()
        land_ref[me_all] = small_ref[...]
        for ref, to in zip(proj_refs, proj_lands):
            to[row] = ref[...]
    else:
        barrier = pltpu.get_barrier_semaphore()

        @pl.when(has_l)
        def _():
            pl.semaphore_signal(barrier, inc=1, device_id={"tensor": left}, device_id_type=MESH)

        @pl.when(has_r)
        def _():
            pl.semaphore_signal(barrier, inc=1, device_id={"tensor": right}, device_id_type=MESH)

        pl.semaphore_wait(barrier, has_l.astype(jnp.int32) + has_r.astype(jnp.int32))

    def copy(src, dst, send_sem, recv_sem, to):
        return pltpu.make_async_remote_copy(
            src_ref=src,
            dst_ref=dst,
            send_sem=send_sem,
            recv_sem=recv_sem,
            device_id={"tensor": to},
            device_id_type=MESH,
        )

    def sum_right(j, c, src):
        return copy(src, from_left.at[j, c], rs_send.at[j, c], rl_sem.at[j, c], right)

    def sum_left(j, c, src):
        return copy(src, from_right.at[j, c], rs_send.at[j, c], rr_sem.at[j, c], left)

    def spread_right(j, c):
        block = all_ref.at[j, c]
        return copy(block, block, ag_right.at[j, c], ag_recv.at[j, c], right)

    def spread_left(j, c):
        block = all_ref.at[j, c]
        return copy(block, block, ag_left.at[j, c], ag_recv.at[j, c], left)

    def offer(c):
        @pl.when(has_r)
        def _():
            spread_right(me, c).start()

        @pl.when(has_l)
        def _():
            spread_left(me, c).start()

    def pass_on(c, d):
        @pl.when(me - d >= 0)
        def _():
            j = me - d
            spread_right(j, c).wait_recv()

            @pl.when(has_r)
            def _():
                spread_right(j, c).start()

        @pl.when(me + d < nt)
        def _():
            j = me + d
            spread_left(j, c).wait_recv()

            @pl.when(has_l)
            def _():
                spread_left(j, c).start()

    hops = nt - 1

    count = hops * chunks

    def relay(step):
        k = jnp.clip(step - lag * me, 0, count - 1)
        c, j = lax.div(k, hops), hops - lax.rem(k, hops)

        @pl.when(has_l & (step >= lag * me) & (step - lag * me < count) & (me < j))
        def _():
            sum_right(j, c, tx.at[j, c]).wait_recv()
            tx[j, c] = (part[j, c].astype(F32) + from_left[j, c].astype(F32)).astype(BF16)
            sum_right(j, c, tx.at[j, c]).start()

        far = lag * (hops - me)
        k_down = jnp.clip(step - far, 0, count - 1)
        c_down, j_down = lax.div(k_down, hops), lax.rem(k_down, hops)

        @pl.when(has_r & (step >= far) & (step - far < count) & (me > j_down))
        def _():
            sum_left(j_down, c_down, tx.at[j_down, c_down]).wait_recv()
            tx[j_down, c_down] = (
                part[j_down, c_down].astype(F32) + from_right[j_down, c_down].astype(F32)
            ).astype(BF16)
            sum_left(j_down, c_down, tx.at[j_down, c_down]).start()

    def push(first, last):
        ks = range(min(first, count), min(last, count))

        @pl.when(jnp.logical_not(has_l))
        def _():
            for k in ks:
                j, c = hops - k % hops, k // hops
                sum_right(j, c, part.at[j, c]).start()

        @pl.when(jnp.logical_not(has_r))
        def _():
            for k in ks:
                j, c = k % hops, k // hops
                sum_left(j, c, part.at[j, c]).start()

    def own_rows(c):
        acc[...] = part[me, c].astype(F32)

        @pl.when(has_l)
        def _():
            sum_right(me, c, tx.at[me, c]).wait_recv()
            acc[...] += from_left[me, c].astype(F32)

        @pl.when(has_r)
        def _():
            sum_left(me, c, tx.at[me, c]).wait_recv()
            acc[...] += from_right[me, c].astype(F32)

        total = acc[...]
        if kind == "fwd":
            total = total + extra_ref[c]
            all_ref[me, c] = normed(total, gain_ref[...]).astype(BF16)
            own_ref[c] = total
        elif kind == "last":
            own_ref[c] = total + extra_ref[c]
        else:
            if extra:
                total = total + extra_ref[c]
            base = base_ref[c].astype(F32)
            scale = lax.rsqrt(jnp.mean(base * base, axis=-1, keepdims=True) + EPS)
            unit = base * scale
            grad_unit = total * rows_ref[0:1, :]
            below = scale * (grad_unit - unit * jnp.mean(grad_unit * unit, axis=-1, keepdims=True))
            result = below + skip_ref[c].astype(F32)
            if has_gather:
                all_ref[me, c] = result.astype(BF16)
            own_ref[c] = result
            gg = jnp.sum(total * unit, axis=0, keepdims=True)
            if c == 0:
                gg_ref[...] = gg
            else:
                gg_ref[...] += gg
        if kind in ("fwd", "bwd"):
            offer(c)

    if kind == "start":
        for c in range(chunks):
            all_ref[me, c] = x_ref[c]
            offer(c)
        for c in range(chunks):
            for d in range(1, nt):
                pass_on(c, d)
        small_finish()
        for _, finish in proj_moves:
            finish()
    else:

        push(0, AHEAD)
        if kind == "last":
            for c in range(chunks):
                all_ref[me, c] = og_ref[c]
            for c in range(chunks):
                offer(c)
        delay = 0 if kind == "last" else hops * lag
        spreads = {}
        for c in range(chunks if has_gather else 0):
            for d in range(1, nt):
                spreads.setdefault(delay + hops * c + lag * d, []).append((c, d))
        final = max([hops * (chunks - 1 + lag)] + list(spreads))
        for step in range(1, final + 1):
            push(step + AHEAD - 1, step + AHEAD)
            relay(step)
            for c, d in spreads.get(step, ()):
                pass_on(c, d)
            if step % hops == 0 and 0 <= step // hops - lag < chunks:
                own_rows(step // hops - lag)

    for c in range(chunks):
        for j in range(nt):
            if has_sum:

                @pl.when(me < j)
                def _():
                    sum_right(j, c, tx.at[j, c]).wait_send()

                @pl.when(me > j)
                def _():
                    sum_left(j, c, tx.at[j, c]).wait_send()

            if has_gather:

                @pl.when(has_r & (j <= me))
                def _():
                    spread_right(j, c).wait_send()

                @pl.when(has_l & (j >= me))
                def _():
                    spread_left(j, c).wait_send()


def line_exchange(kind, args, rows, width, collective_id, extra=False, chunks=2, lag=2):
    nt = lax.axis_size("tensor")
    has_sum = kind != "start"
    has_gather = kind != "end"
    piece = rows // chunks
    split = []
    for item in args:
        if item.shape[1] != width or kind == "start" and split:
            split.append(item)
        elif item.shape[0] == nt * rows:
            split.append(item.reshape(nt, chunks, piece, width))
        elif item.shape[0] == rows:
            split.append(item.reshape(chunks, piece, width))
        else:
            split.append(item)
    outs = []
    if has_sum:
        outs.append(jax.ShapeDtypeStruct((chunks, piece, width), F32))
    if kind in ("bwd", "end"):
        outs.append(jax.ShapeDtypeStruct((1, width), F32))
    if has_gather:
        outs.append(jax.ShapeDtypeStruct((nt, chunks, piece, width), BF16))
    if kind == "start":
        count = lax.axis_size("dp") * nt
        outs.append(jax.ShapeDtypeStruct((count,) + args[1].shape, args[1].dtype))
        members = lax.axis_size("dp")
        for item in args[2:]:
            outs.append(jax.ShapeDtypeStruct((members,) + item.shape, item.dtype))
    scratch = []
    sems = pltpu.SemaphoreType.DMA((nt, chunks))
    if has_sum:
        buf = pltpu.VMEM((nt, chunks, piece, width), BF16)
        scratch += [buf, buf, buf, pltpu.VMEM((piece, width), F32), sems, sems, sems]
    if has_gather:
        scratch += [sems, sems, sems]
    if kind == "start":
        scratch += [pltpu.SemaphoreType.DMA((count,))] * 2
        scratch += [pltpu.SemaphoreType.DMA((members,))] * (2 * extra)
    results = pl.pallas_call(
        functools.partial(line_kernel, kind, nt, chunks, lag, extra),
        out_shape=outs,
        in_specs=[VMEM_SPEC] * len(split),
        out_specs=[VMEM_SPEC] * len(outs),
        scratch_shapes=scratch,
        compiler_params=pltpu.CompilerParams(
            collective_id=collective_id, has_side_effects=True, vmem_limit_bytes=VMEM_LIMIT
        ),
        cost_estimate=pl.CostEstimate(
            flops=10 * nt * rows * width, bytes_accessed=100 * rows * width * nt, transcendentals=0
        ),
        name="line_" + kind,
    )(*split)
    results = list(results)
    if has_sum:
        results[0] = results[0].reshape(rows, width)
    if has_gather:
        at = 0 if kind == "start" else -1
        results[at] = results[at].reshape(nt * rows, width)
    return results


def span_mask(starts_ref, row_at, rows, cols, spans):
    row = row_at + lax.broadcasted_iota(jnp.int32, (rows, cols), 0)
    col = lax.broadcasted_iota(jnp.int32, (rows, cols), 1)
    seen = col <= row
    for k in range(spans):
        begin = starts_ref[0, k]
        seen = seen | (
            (row >= begin) & (row < begin + PIC) & (col >= begin) & (col < begin + PIC)
        )
    return seen


def key_extent(row_at, seq_len, spans):
    segment = seq_len // spans
    return (row_at // segment + 1) * segment


def attend_kernel(heads, spans, block, raw, starts_ref, a_ref, w_ref, *refs):
    if raw:
        gain_ref, qkv_ref, o_ref, lse_ref, out_ref, normed_ref = refs
        normed_ref[...] = normed(a_ref[...].astype(F32), gain_ref[0:1, :]).astype(BF16)
        a_ref = normed_ref
    else:
        qkv_ref, o_ref, lse_ref, out_ref = refs
    seq_len = a_ref.shape[0]
    wide = heads * HEAD
    factor = HEAD ** (-0.5)
    qkv_ref[...] = dot(a_ref[...], w_ref[:, : 3 * wide]).astype(BF16)
    for at in range(0, seq_len, block):
        reach = key_extent(at, seq_len, spans)
        seen = span_mask(starts_ref, at, block, reach, spans)
        for h in range(heads):
            q = qkv_ref[at : at + block, h * HEAD : (h + 1) * HEAD]
            k = qkv_ref[:reach, wide + h * HEAD : wide + (h + 1) * HEAD]
            v = qkv_ref[:reach, 2 * wide + h * HEAD : 2 * wide + (h + 1) * HEAD]
            s = jnp.where(seen, dot_nt(q, k) * factor, -1e30)
            top = jnp.max(s, axis=-1, keepdims=True)
            e = jnp.exp(s - top)
            total = jnp.sum(e, axis=-1, keepdims=True)
            probs = (e * (1.0 / total)).astype(BF16)
            o_ref[at : at + block, h * HEAD : (h + 1) * HEAD] = dot(probs, v).astype(BF16)
            lse_ref[at : at + block, h : h + 1] = top + jnp.log(total)
    out_ref[...] = dot_nt(o_ref[...], w_ref[:, 3 * wide :]).astype(BF16)


def attend_forward(starts, a_all, w_attn, heads, gain=None):
    seq_len, width = a_all.shape
    wide = heads * HEAD
    spans = starts.shape[1]
    raw = gain is not None
    return pl.pallas_call(
        functools.partial(attend_kernel, heads, spans, PIC, raw),
        out_shape=[
            jax.ShapeDtypeStruct((seq_len, 3 * wide), BF16),
            jax.ShapeDtypeStruct((seq_len, wide), BF16),
            jax.ShapeDtypeStruct((seq_len, heads), F32),
            jax.ShapeDtypeStruct((seq_len, width), BF16),
        ]
        + [jax.ShapeDtypeStruct((seq_len, width), BF16)] * raw,
        in_specs=[pl.BlockSpec(memory_space=pltpu.SMEM)] + [VMEM_SPEC] * (2 + raw),
        out_specs=[VMEM_SPEC] * (4 + raw),
        compiler_params=pltpu.CompilerParams(vmem_limit_bytes=VMEM_LIMIT),
        cost_estimate=pl.CostEstimate(
            flops=8 * seq_len * width * wide + 4 * heads * seq_len * seq_len * HEAD,
            bytes_accessed=6 * seq_len * width,
            transcendentals=heads * seq_len * seq_len,
        ),
        name="attend_forward",
    )(starts, a_all, w_attn, *([gain] if raw else []))


def attend_back_kernel(
    heads, spans, block, starts_ref, g_ref, w_ref, a_ref, qkv_ref, o_ref, lse_ref,
    ga_ref, gw_ref, go_scr, gq_scr, gk_acc, gv_acc,
):
    seq_len = a_ref.shape[0]
    wide = heads * HEAD
    factor = HEAD ** (-0.5)
    go_scr[...] = dot(g_ref[...], w_ref[:, 3 * wide :]).astype(BF16)
    gw_ref[:, 3 * wide :] = dot_tn(g_ref[...], o_ref[...]).astype(BF16)
    gk_acc[...] = jnp.zeros_like(gk_acc)
    gv_acc[...] = jnp.zeros_like(gv_acc)
    for at in range(0, seq_len, block):
        reach = key_extent(at, seq_len, spans)
        seen = span_mask(starts_ref, at, block, reach, spans)
        for h in range(heads):
            own = slice(h * HEAD, (h + 1) * HEAD)
            q = qkv_ref[at : at + block, own]
            k = qkv_ref[:reach, wide + h * HEAD : wide + (h + 1) * HEAD]
            v = qkv_ref[:reach, 2 * wide + h * HEAD : 2 * wide + (h + 1) * HEAD]
            go = go_scr[at : at + block, own]
            s = jnp.where(seen, dot_nt(q, k) * factor, -1e30)
            probs = jnp.exp(s - lse_ref[at : at + block, h : h + 1])
            gp = dot_nt(go, v)
            inner = jnp.sum(probs * gp, axis=-1, keepdims=True)
            gs = (probs * (gp - inner)).astype(BF16)
            gq_scr[at : at + block, own] = (dot(gs, k) * factor).astype(BF16)
            gk_acc[:reach, own] += dot_tn(gs, q) * factor
            gv_acc[:reach, own] += dot_tn(probs.astype(BF16), go)
    gq_scr[:, wide : 2 * wide] = gk_acc[...].astype(BF16)
    gq_scr[:, 2 * wide :] = gv_acc[...].astype(BF16)
    gw_ref[:, : 3 * wide] = dot_tn(a_ref[...], gq_scr[...]).astype(BF16)
    ga_ref[...] = dot_nt(gq_scr[...], w_ref[:, : 3 * wide]).astype(BF16)


def attend_backward(starts, g_all, w_attn, a_all, qkv, o, lse, heads):
    seq_len, width = a_all.shape
    wide = heads * HEAD
    spans = starts.shape[1]
    return pl.pallas_call(
        functools.partial(attend_back_kernel, heads, spans, PIC),
        out_shape=[
            jax.ShapeDtypeStruct((seq_len, width), BF16),
            jax.ShapeDtypeStruct((width, 4 * wide), BF16),
        ],
        in_specs=[pl.BlockSpec(memory_space=pltpu.SMEM)] + [VMEM_SPEC] * 6,
        out_specs=[VMEM_SPEC] * 2,
        scratch_shapes=[
            pltpu.VMEM((seq_len, wide), BF16),
            pltpu.VMEM((seq_len, 3 * wide), BF16),
            pltpu.VMEM((seq_len, wide), F32),
            pltpu.VMEM((seq_len, wide), F32),
        ],
        compiler_params=pltpu.CompilerParams(vmem_limit_bytes=VMEM_LIMIT),
        cost_estimate=pl.CostEstimate(
            flops=16 * seq_len * width * wide + 10 * heads * seq_len * seq_len * HEAD,
            bytes_accessed=12 * seq_len * width,
            transcendentals=heads * seq_len * seq_len,
        ),
        name="attend_backward",
    )(starts, g_all, w_attn, a_all, qkv, o, lse)


def lane_column(values, at):
    lane = lax.broadcasted_iota(jnp.int32, values.shape, 1)
    return jnp.sum(jnp.where(lane == at, values, 0), axis=1, keepdims=True)


def two_parts(values):
    high = values.astype(BF16)
    return high, (values - high.astype(F32)).astype(BF16)


def const_parts(product, wd, layer, at, consts):
    first = EXPERTS + 2
    zero = shift(product, first - at["cmix"] - layer * 2 * consts)
    one = shift(product, first - at["cmix"] - layer * 2 * consts - consts)
    lane = lax.broadcasted_iota(jnp.int32, product.shape, 1)
    here = (lane >= first) & (lane < first + consts)
    gap = jnp.where(here, one - zero, 0.0)
    alpha0 = 1.0 / (1.0 + jnp.exp(gap))
    alpha1 = 1.0 / (1.0 + jnp.exp(-gap))
    gate = jnp.where(here, wd, 0.0)
    keep = jnp.sum(gate * alpha0 + jnp.where(lane == EXPERTS + 1, wd, 0.0), axis=1, keepdims=True)
    return lane, here, alpha0, alpha1, gate, keep


def experts_kernel(
    cap, layer, at, consts, b_ref, w_ref, rowpos_ref, pos_ref, small_ref, rows_ref, mix_ref, zprev_ref,
    mid_ref, x_ref, gu_ref, z_ref, wd_ref, f_ref, extra_ref, pick_scr, y_scr,
):
    e = pl.program_id(0)
    seq_len, width = b_ref.shape
    half = gu_ref.shape[2] // 2

    @pl.when(e == 0)
    def _():
        product = dot(b_ref[...], small_ref[...])
        lane = lax.broadcasted_iota(jnp.int32, product.shape, 1)
        p_high, p_low = two_parts(zprev_ref[...])
        z = (
            jnp.where(lane < NEXP, shift(product, -at["router"] - layer * NEXP), 0.0)
            + dot(p_high, mix_ref[...])
            + dot(p_low, mix_ref[...])
        )
        z_ref[...] = z
        hit = pos_ref[...] >= 0
        top = jnp.max(jnp.where(hit, z, -3e38), axis=1, keepdims=True)
        ez = jnp.where(hit, jnp.exp(jnp.where(hit, z - top, 0.0)), 0.0)
        wd = ez / jnp.sum(ez, axis=1, keepdims=True)
        wd_ref[...] = wd
        _, _, _, alpha1, gate, keep = const_parts(product, wd, layer, at, consts)
        extra = mid_ref[...].astype(F32) + keep * b_ref[...].astype(F32)
        for j in range(consts):
            row = at["cvec"] + layer * consts + j
            extra = extra + lane_column(gate * alpha1, EXPERTS + 2 + j) * rows_ref[row : row + 1, :]
        extra_ref[...] = extra.astype(BF16)

    w = w_ref[...].reshape(width, 3 * half)
    take = (
        lax.broadcasted_iota(jnp.int32, (cap, seq_len), 0) == rowpos_ref[0]
    ).astype(F32).astype(BF16)
    x = dot(take, b_ref[...]).astype(BF16)
    x_ref[0] = x
    gu = dot(x, w[:, : 2 * half])
    gu_ref[0] = gu.astype(BF16)
    g, u = gu[:, :half], gu[:, half:]
    h = (g * jax.nn.sigmoid(g) * u).astype(BF16)
    y = dot_nt(h, w[:, 2 * half :])
    y_scr[pl.ds(pl.multiple_of(e * cap, cap), cap), :] = y.astype(BF16)
    column = lane_column(pos_ref[...], e)
    weight = lane_column(wd_ref[...], e)
    put = jnp.where(
        lax.broadcasted_iota(jnp.int32, (seq_len, cap), 1) == column, weight, 0.0
    ).astype(BF16)
    pick_scr[:, pl.ds(pl.multiple_of(e * cap, cap), cap)] = put

    @pl.when(e == pl.num_programs(0) - 1)
    def _():
        f_ref[...] = dot(pick_scr[...], y_scr[...]).astype(BF16)


def whole(shape):
    return pl.BlockSpec(shape, lambda e: (0,) * len(shape))


def experts_forward(
    layer, at, consts, b_all, w_exp, rowpos, pos, small, rows_t, mix, z_prev, mid, cap
):
    seq_len, width = b_all.shape
    shards_dp, count, rows, wide3 = w_exp.shape
    half = wide3 // 3
    return pl.pallas_call(
        functools.partial(experts_kernel, cap, layer, at, consts),
        grid=(count,),
        out_shape=[
            jax.ShapeDtypeStruct((count, cap, width), BF16),
            jax.ShapeDtypeStruct((count, cap, 2 * half), BF16),
            jax.ShapeDtypeStruct((seq_len, LANES), F32),
            jax.ShapeDtypeStruct((seq_len, LANES), F32),
            jax.ShapeDtypeStruct((seq_len, width), BF16),
            jax.ShapeDtypeStruct((seq_len, width), BF16),
        ],
        in_specs=[
            whole((seq_len, width)),
            pl.BlockSpec((shards_dp, 1, rows, wide3), lambda e: (0, e, 0, 0)),
            pl.BlockSpec((1, 1, seq_len), lambda e: (e, 0, 0)),
            whole((seq_len, LANES)),
            whole((width, LANES)),
            whole(rows_t.shape),
            whole((LANES, LANES)),
            whole((seq_len, LANES)),
            whole((seq_len, width)),
        ],
        out_specs=[
            pl.BlockSpec((1, cap, width), lambda e: (e, 0, 0)),
            pl.BlockSpec((1, cap, 2 * half), lambda e: (e, 0, 0)),
            whole((seq_len, LANES)),
            whole((seq_len, LANES)),
            whole((seq_len, width)),
            whole((seq_len, width)),
        ],
        scratch_shapes=[
            pltpu.VMEM((seq_len, count * cap), BF16),
            pltpu.VMEM((count * cap, width), BF16),
        ],
        compiler_params=pltpu.CompilerParams(vmem_limit_bytes=VMEM_LIMIT),
        cost_estimate=pl.CostEstimate(
            flops=count * (4 * cap * seq_len * width + 6 * cap * width * half),
            bytes_accessed=2 * count * width * wide3,
            transcendentals=0,
        ),
        name="experts_forward",
    )(b_all, w_exp, rowpos, pos, small, rows_t, mix, z_prev, mid)


def experts_back_kernel(
    cap, layer, at, consts, own, g_ref, w_ref, x_ref, gu_ref, rowpos_ref, pos_ref, wd_ref,
    b_ref, small_ref, rows_ref, mix_ref, zprev_ref, gprev_ref, sums_ref, mixes_ref,
    gw_ref, below_ref, gb_ref, sums_out, mixes_out, pick_scr, gx_scr, gg_scr, gb_scr, zs_scr,
    halves, inbox, out_sems, in_sems,
):
    e = pl.program_id(0)
    last = pl.num_programs(0) - 1
    me = lax.axis_index("dp")
    parity = lax.rem(me, 2)
    partner = me + 1 - 2 * parity

    def to_partner(expert):
        return pltpu.make_async_remote_copy(
            src_ref=halves.at[lax.rem(expert, 2), 1 - parity],
            dst_ref=inbox.at[expert],
            send_sem=out_sems.at[expert],
            recv_sem=in_sems.at[expert],
            device_id={"dp": partner},
            device_id_type=MESH,
        )

    @pl.when(e == 0)
    def _():
        barrier = pltpu.get_barrier_semaphore()
        pl.semaphore_signal(barrier, inc=1, device_id={"dp": partner}, device_id_type=MESH)
        pl.semaphore_wait(barrier, 1)

    @pl.when(e < last)
    def _():
        one_expert_back(
            cap, e, g_ref, w_ref, x_ref, gu_ref, rowpos_ref, pos_ref, wd_ref, pick_scr, gx_scr, gg_scr,
            halves,
        )
        to_partner(e).start()

    @pl.when(e > 0)
    def _():
        before = e - 1
        to_partner(before).wait()
        gw_ref[:, 0] = (
            halves[lax.rem(before, 2), parity].astype(F32) + inbox[before].astype(F32)
        ).astype(BF16)

    @pl.when(e == last)
    def _():
        tokens_back(
            layer, at, consts, own, g_ref, wd_ref, b_ref, small_ref, rows_ref, mix_ref, zprev_ref,
            gprev_ref, sums_ref, mixes_ref, below_ref, gb_ref, sums_out, mixes_out, pick_scr, gx_scr,
            gg_scr, gb_scr, zs_scr,
        )


def one_expert_back(
    cap, e, g_ref, w_ref, x_ref, gu_ref, rowpos_ref, pos_ref, wd_ref, pick_scr, gx_scr, gg_scr, halves,
):
    seq_len, width = g_ref.shape
    shards_dp, _, rows, wide3 = w_ref.shape
    half = wide3 // 3
    slot = lax.rem(e, 2)
    w = w_ref[...].reshape(width, wide3)
    take = (
        lax.broadcasted_iota(jnp.int32, (cap, seq_len), 0) == rowpos_ref[0]
    ).astype(F32).astype(BF16)
    w_high, w_low = two_parts(wd_ref[...])
    weight = lane_column(dot(take, w_high) + dot(take, w_low), e)
    gf = dot(take, g_ref[...])
    gh = dot(gf.astype(BF16), w[:, 2 * half :])
    gu = gu_ref[0].astype(F32)
    g, u = gu[:, :half], gu[:, half:]
    sig = jax.nn.sigmoid(g)
    h = (g * sig * u).astype(BF16)
    slot_grad = jnp.sum(h.astype(F32) * gh, axis=1, keepdims=True)
    gh = gh * weight
    gg = gh * u * sig * (1.0 + g * (1.0 - sig))
    gup = gh * g * sig
    both = jnp.concatenate([gg.astype(BF16), gup.astype(BF16)], axis=1)
    gy = (gf * weight).astype(BF16)
    gw_in = dot_tn(x_ref[0], both).astype(BF16)
    gw_down = dot_tn(gy, h).astype(BF16)
    for shard in range(shards_dp):
        own_rows = slice(shard * rows, (shard + 1) * rows)
        halves[slot, shard % 2, shard // 2, :, : 2 * half] = gw_in[own_rows]
        halves[slot, shard % 2, shard // 2, :, 2 * half :] = gw_down[own_rows]
    here = pl.ds(pl.multiple_of(e * cap, cap), cap)
    gx_scr[here, :] = dot_nt(both, w[:, : 2 * half]).astype(BF16)
    s_high, s_low = two_parts(slot_grad)
    lane = lax.broadcasted_iota(jnp.int32, (cap, LANES), 1)
    gg_scr[here, :LANES] = jnp.where(lane == e, s_high.astype(F32), 0.0).astype(BF16)
    gg_scr[here, LANES:] = jnp.where(lane == e, s_low.astype(F32), 0.0).astype(BF16)
    column = lane_column(pos_ref[...], e)
    pick_scr[:, here] = (
        lax.broadcasted_iota(jnp.int32, (seq_len, cap), 1) == column
    ).astype(F32).astype(BF16)


def tokens_back(
    layer, at, consts, own, g_ref, wd_ref, b_ref, small_ref, rows_ref, mix_ref, zprev_ref, gprev_ref,
    sums_ref, mixes_ref, below_ref, gb_ref, sums_out, mixes_out, pick_scr, gx_scr, gg_scr, gb_scr, zs_scr,
):
    mine = pl.ds(pl.multiple_of(lax.axis_index("tensor") * own, own), own)
    b_own, g_own = b_ref[mine, :], g_ref[mine, :].astype(F32)
    wd_own = wd_ref[mine, :]
    lane, here_own, alpha0, alpha1, gate, keep = const_parts(
        dot(b_own, small_ref[...]), wd_own, layer, at, consts
    )
    b_dot = jnp.sum(b_own.astype(F32) * g_own, axis=1, keepdims=True)
    c_dot = jnp.zeros_like(wd_own)
    for j in range(consts):
        row = at["cvec"] + layer * consts + j
        one = jnp.sum(g_own * rows_ref[row : row + 1, :], axis=1, keepdims=True)
        c_dot = jnp.where(lane == EXPERTS + 2 + j, one, c_dot)
    gw_own = jnp.where(here_own, alpha0 * b_dot + alpha1 * c_dot, 0.0)
    gw_own = jnp.where(lane == EXPERTS + 1, b_dot, gw_own)
    inner = gate * (alpha0 * b_dot + alpha1 * c_dot)
    gt0 = alpha0 * (gate * b_dot - inner)
    gt1 = alpha1 * (gate * c_dot - inner)

    slots = dot(pick_scr[...], gg_scr[...])
    zs_scr[...] = slots[:, :LANES] + slots[:, LANES:]
    zs_scr[mine, :] += gw_own
    gw = zs_scr[...]
    wd = wd_ref[...]
    gz = wd * (gw - jnp.sum(wd * gw, axis=1, keepdims=True)) + gprev_ref[...]
    z_high, z_low = two_parts(gz)
    below_ref[...] = dot_nt(z_high, mix_ref[...]) + dot_nt(z_low, mix_ref[...])
    p_high, p_low = two_parts(zprev_ref[...])
    mixes_out[...] = mixes_ref[...] + shift(
        dot_tn(p_high, z_high) + dot_tn(p_high, z_low) + dot_tn(p_low, z_high), layer * MIX_STEP
    )
    zs_scr[...] = shift(gz, at["router"] + layer * NEXP)
    up = at["cmix"] + layer * 2 * consts - EXPERTS - 2
    zs_scr[mine, :] += shift(gt0, up) + shift(gt1, up + consts)
    z_high, z_low = two_parts(zs_scr[...])
    gb_scr[...] = (
        dot(pick_scr[...], gx_scr[...])
        + dot_nt(z_high, small_ref[...])
        + dot_nt(z_low, small_ref[...])
    )
    gb_scr[mine, :] += keep * g_own
    gb_ref[...] = gb_scr[...].astype(BF16)
    i_high, i_low = two_parts(
        shift(gate * alpha1, at["cvec"] + layer * consts - EXPERTS - 2)
    )
    g_low = g_ref[mine, :]
    sums_out[...] = (
        sums_ref[...]
        + dot_tn(b_ref[...], z_high)
        + dot_tn(b_ref[...], z_low)
        + dot_tn(g_low, i_high)
        + dot_tn(g_low, i_low)
    )


def experts_backward(
    collective_id, layer, at, consts, own, g_all, w_exp, x, gu, rowpos, pos, wd, b_all, small, rows_t, mix,
    z_prev, grad_prev, sums, mixes, cap,
):
    seq_len, width = g_all.shape
    shards_dp, count, rows, wide3 = w_exp.shape
    half = wide3 // 3
    weight_spec = pl.BlockSpec(
        (shards_dp, 1, rows, wide3), lambda e: (0, jnp.minimum(e, count - 1), 0, 0)
    )
    half_shape = (shards_dp // 2, 1, rows, wide3)
    return pl.pallas_call(
        functools.partial(experts_back_kernel, cap, layer, at, consts, own),
        grid=(count + 1,),
        out_shape=[
            jax.ShapeDtypeStruct((shards_dp // 2,) + w_exp.shape[1:], BF16),
            jax.ShapeDtypeStruct((seq_len, LANES), F32),
            jax.ShapeDtypeStruct((seq_len, width), BF16),
            jax.ShapeDtypeStruct((width, LANES), F32),
            jax.ShapeDtypeStruct((LANES, LANES), F32),
        ],
        in_specs=[
            whole((seq_len, width)),
            weight_spec,
            pl.BlockSpec((1, cap, width), lambda e: (jnp.minimum(e, count - 1), 0, 0)),
            pl.BlockSpec((1, cap, 2 * half), lambda e: (jnp.minimum(e, count - 1), 0, 0)),
            pl.BlockSpec((1, 1, seq_len), lambda e: (jnp.minimum(e, count - 1), 0, 0)),
            whole((seq_len, LANES)),
            whole((seq_len, LANES)),
            whole((seq_len, width)),
            whole((width, LANES)),
            whole(rows_t.shape),
            whole((LANES, LANES)),
            whole((seq_len, LANES)),
            whole((seq_len, LANES)),
            whole((width, LANES)),
            whole((LANES, LANES)),
        ],
        out_specs=[
            pl.BlockSpec(half_shape, lambda e: (0, jnp.maximum(e - 1, 0), 0, 0)),
            whole((seq_len, LANES)),
            whole((seq_len, width)),
            whole((width, LANES)),
            whole((LANES, LANES)),
        ],
        scratch_shapes=[
            pltpu.VMEM((seq_len, count * cap), BF16),
            pltpu.VMEM((count * cap, width), BF16),
            pltpu.VMEM((count * cap, 2 * LANES), BF16),
            pltpu.VMEM((seq_len, width), F32),
            pltpu.VMEM((seq_len, LANES), F32),
            pltpu.VMEM((2, 2, shards_dp // 2, rows, wide3), BF16),
            pltpu.VMEM((count, shards_dp // 2, rows, wide3), BF16),
            pltpu.SemaphoreType.DMA((count,)),
            pltpu.SemaphoreType.DMA((count,)),
        ],
        compiler_params=pltpu.CompilerParams(
            collective_id=collective_id, has_side_effects=True, vmem_limit_bytes=VMEM_LIMIT
        ),
        cost_estimate=pl.CostEstimate(
            flops=count * (4 * cap * seq_len * width + 12 * cap * width * half),
            bytes_accessed=4 * count * width * wide3,
            transcendentals=0,
        ),
        name="experts_backward",
    )(
        g_all, w_exp, x, gu, rowpos, pos, wd, b_all, small, rows_t, mix, z_prev, grad_prev,
        sums, mixes,
    )


def unpack_kernel(half, *refs):
    *in_refs, up_ref, down_ref = refs
    for l, ref in enumerate(in_refs):
        values = ref[0].astype(F32)
        for part in range(2):
            up_ref[l, 0, :, part, :] = values[:, part * half : (part + 1) * half]
        down_ref[l, 0] = values[:, 2 * half :]


def unpack(items):
    count, rows, wide3 = items[0].shape
    half = wide3 // 3
    layers = len(items)
    return pl.pallas_call(
        functools.partial(unpack_kernel, half),
        grid=(count,),
        out_shape=[
            jax.ShapeDtypeStruct((layers, count, rows, 2, half), F32),
            jax.ShapeDtypeStruct((layers, count, rows, half), F32),
        ],
        in_specs=[pl.BlockSpec((1, rows, wide3), lambda e: (e, 0, 0))] * layers,
        out_specs=[
            pl.BlockSpec((layers, 1, rows, 2, half), lambda e: (0, e, 0, 0, 0)),
            pl.BlockSpec((layers, 1, rows, half), lambda e: (0, e, 0, 0)),
        ],
        compiler_params=pltpu.CompilerParams(vmem_limit_bytes=VMEM_LIMIT),
        name="unpack",
    )(*items)


def lanes(values):
    return jnp.pad(values, ((0, 0), (0, LANES - values.shape[1])))


def slot_table(route_ids):
    tokens = route_ids.shape[0]
    codes = jnp.arange(LANES, dtype=jnp.int32)
    hit = jnp.any(route_ids[:, :, None] == codes[None, None, :], axis=1)
    place = jnp.arange(tokens, dtype=jnp.int32)
    before = (place[None, :] < place[:, None]).astype(BF16)
    slots = dot(before, hit.astype(BF16)).astype(jnp.int32)
    return jnp.where(hit, slots, -1)


def shards(
    hidden_in,
    prev_logits,
    routes,
    span_starts,
    attn_norm,
    qkv_weight,
    out_weight,
    moe_norm,
    router,
    gate_mix,
    const_vec,
    const_mix,
    up_weight,
    down_weight,
    out_grad,
):
    layers = qkv_weight.shape[0]
    own, width = hidden_in.shape
    nt = lax.axis_size("tensor")
    ndp = lax.axis_size("dp")
    seq_len = own * nt
    offset = lax.axis_index("tensor") * own
    cap = seq_len // 4
    heads = qkv_weight.shape[3] // HEAD
    wide = heads * HEAD
    half = up_weight.shape[4]
    rows = qkv_weight.shape[1]
    cols = attn_norm.shape[1]
    consts = const_vec.shape[1]

    at = layout(layers, consts)
    packed = jnp.concatenate(
        [attn_norm.T, moe_norm.T]
        + [router[l] for l in range(layers)]
        + [const_vec.reshape(-1, cols).T]
        + [const_mix[l, :, :, k].T for l in range(layers) for k in range(2)],
        axis=1,
    )
    exp_local = [
        jnp.concatenate(
            [up_weight[l].reshape(EXPERTS, rows, 2 * half), jnp.swapaxes(down_weight[l], 1, 2)], axis=2
        )
        for l in range(layers)
    ]
    attn_local = [
        jnp.concatenate([qkv_weight[l].reshape(rows, 3 * wide), out_weight[l].T], axis=1)
        for l in range(layers)
    ]
    exp_w = [lax.all_gather(item, "dp", axis=0, tiled=False) for item in exp_local]
    x_all, small, *attn_w = line_exchange(
        "start", [hidden_in, lanes(packed)] + attn_local, own, width, 0, extra=layers
    )
    attn_w = [item.reshape(width, 4 * wide) for item in attn_w]
    small = small.reshape(width, LANES)
    rows_t = small[:, :48].T.astype(F32)

    pos = [slot_table(routes[l]) for l in range(layers)]
    rowpos = [p[:, :EXPERTS].T[:, None, :] for p in pos]

    z_prev = lanes(prev_logits)
    hidden, a_all = x_all, None
    grad_all = out_grad
    next_id = 1
    stored = []
    for l in range(layers):
        mix = jnp.pad(gate_mix[l], ((0, LANES - NEXP), (0, LANES - NEXP)))
        if l == 0:
            qkv, o, lse, partial, a_all = attend_forward(
                span_starts, x_all, attn_w[l], heads, rows_t
            )
        else:
            qkv, o, lse, partial = attend_forward(span_starts, a_all, attn_w[l], heads)
        if l == layers - 1:
            partial, grad_all = lax.optimization_barrier((partial, grad_all))
            grad_all = lax.all_gather(grad_all, "tensor", axis=0, tiled=True)
        mid, b_all = join(
            False, partial, [hidden], rows_t, at["moe"] + l, next_id, APART if l == 0 else 0
        )
        x, gu, z, wd, partial, extra = experts_forward(
            l, at, consts, b_all, exp_w[l], rowpos[l], pos[l], small, rows_t, mix, z_prev, mid, cap
        )
        stored.append(
            dict(
                hidden=hidden, a_all=a_all, qkv=qkv, o=o, lse=lse, mid=mid, b_all=b_all, x=x, gu=gu,
                wd=wd, z_prev=z_prev, mix=mix,
            )
        )
        if l + 1 < layers:
            hidden, a_all = join(False, partial, [extra], rows_t, at["attn"] + l + 1, next_id + 1)
        else:
            hidden_out = lax.psum_scatter(partial, "tensor", scatter_dimension=0, tiled=True)
            extra = lax.dynamic_slice_in_dim(extra, offset, own, 0)
        z_prev = z
        next_id += 2

    below = jnp.zeros((seq_len, LANES), F32)
    sums = jnp.zeros((width, LANES), F32)
    mixes = jnp.zeros((LANES, LANES), F32)
    attn_grads, exp_grads = [None] * layers, [None] * layers
    gains_a, gains_m = [None] * layers, [None] * layers
    for l in reversed(range(layers)):
        s = stored[l]
        gw_exp, below, partial, sums, mixes = experts_backward(
            next_id + 2, l, at, consts, own, grad_all, exp_w[l], s["x"], s["gu"], rowpos[l],
            pos[l], s["wd"], s["b_all"], small, rows_t, s["mix"], s["z_prev"], below, sums, mixes, cap,
        )
        exp_grads[l] = sum_over_pairs(gw_exp)
        if l + 1 < layers:
            partial, exp_grads[l + 1] = lax.optimization_barrier((partial, exp_grads[l + 1]))
        else:
            partial, hidden_out = lax.optimization_barrier((partial, hidden_out))
        grad_mid, gains_m[l] = join(
            True, partial, [s["mid"], grad_all], rows_t, at["moe"] + l, next_id, APART
        )
        partial, gw_attn = attend_backward(
            span_starts, grad_mid, attn_w[l], s["a_all"], s["qkv"], s["o"], s["lse"], heads
        )
        attn_grads[l] = gw_attn.reshape(ndp, rows, 4 * wide)
        if l > 0:
            attn_grads[l] = lax.psum_scatter(attn_grads[l], "dp", scatter_dimension=0, tiled=False)
            grad_all, gains_a[l] = join(
                True, partial, [s["hidden"], grad_mid], rows_t, at["attn"] + l, next_id + 1
            )
        else:
            partial, attn_grads[1:] = lax.optimization_barrier((partial, attn_grads[1:]))
            skip = lax.dynamic_slice_in_dim(grad_mid, offset, own, 0)
            grad, gains_a[l] = line_exchange(
                "end", [partial, hidden_in, skip, rows_t], own, width, next_id + 1
            )
        next_id += 3
    hidden_out = hidden_out.astype(F32) + extra.astype(F32)

    gains = jnp.concatenate(gains_a + gains_m, axis=0)
    sums = sums + jnp.pad(gains, ((0, LANES - 2 * layers), (0, 0))).T
    sums = jnp.concatenate(
        [
            sums.reshape(ndp * nt, cols, LANES),
            jnp.broadcast_to(mixes[None, :MIX_STEP], (ndp * nt, MIX_STEP, LANES)),
        ],
        axis=1,
    )
    attn_g, moe_g, router_g, mix_g, cvec_g, cmix_g, qkv_g, outw_g = closing(
        sums, attn_grads[0], jnp.stack(attn_grads[1:]), consts, layers, cols, next_id
    )
    up_grad, down_grad = unpack(exp_grads)
    qkv_g = jnp.swapaxes(qkv_g, 1, 2)
    router_g = jnp.transpose(router_g, (1, 2, 0))
    mix_g = jnp.swapaxes(mix_g, 0, 1)
    cmix_g = jnp.swapaxes(cmix_g, 2, 3)
    down_grad = jnp.swapaxes(down_grad, 2, 3)
    return (
        hidden_out,
        grad,
        attn_g,
        qkv_g,
        outw_g,
        moe_g,
        router_g,
        mix_g,
        cvec_g,
        cmix_g,
        up_grad,
        down_grad,
    )


def sum_over_pairs(values):
    members = lax.axis_size("dp")
    groups = [list(range(parity, members, 2)) for parity in range(2)]
    return lax.psum_scatter(
        values, "dp", scatter_dimension=0, axis_index_groups=groups, tiled=False
    )


def solution(mesh):
    return jax.shard_map(
        shards,
        mesh=mesh,
        in_specs=(
            P(("dp", "tensor"), None),
            P("dp", None),
            P(None, "dp", None),
            P("dp", None),
            P(None, ("dp", "tensor")),
            P(None, "dp", None, "tensor"),
            P(None, "tensor", "dp"),
            P(None, ("dp", "tensor")),
            P(None, ("dp", "tensor"), None),
            P(),
            P(None, None, ("dp", "tensor")),
            P(None, None, ("dp", "tensor"), None),
            P(None, None, "dp", None, "tensor"),
            P(None, None, "tensor", "dp"),
            P(("dp", "tensor"), None),
        ),
        out_specs=(
            P(("dp", "tensor"), None),
            P(("dp", "tensor"), None),
            P(None, ("dp", "tensor")),
            P(None, "dp", None, "tensor"),
            P(None, "tensor", "dp"),
            P(None, ("dp", "tensor")),
            P(None, ("dp", "tensor"), None),
            P(),
            P(None, None, ("dp", "tensor")),
            P(None, None, ("dp", "tensor"), None),
            P(None, None, "dp", None, "tensor"),
            P(None, None, "tensor", "dp"),
        ),
        check_vma=False,
    )
```

```python
import functools

import jax
import jax.numpy as jnp
from jax import lax
from jax.experimental import pallas as pl
from jax.experimental.pallas import tpu as pltpu
from jax.sharding import PartitionSpec as P

HEAD = 64
EXPERTS = 8
NEXP = 12
TOPK = 2
PIC = 256
LANES = 128

EPS = 1e-06
HIGH = lax.Precision.HIGHEST
MESH = pl.DeviceIdType.MESH
F32 = jnp.float32
BF16 = jnp.bfloat16
VMEM_SPEC = pl.BlockSpec(memory_space=pltpu.VMEM)
AHEAD = 2
PIECES = 32
LAG = 4
MIX_STEP = 16
VMEM_LIMIT = 60 * 1024 * 1024


def dot(a, b):
    return jnp.dot(a, b, preferred_element_type=F32)


def dot_nt(a, b):
    return lax.dot_general(a, b, (((1,), (1,)), ((), ())), preferred_element_type=F32)


def dot_tn(a, b):
    return lax.dot_general(a, b, (((0,), (0,)), ((), ())), preferred_element_type=F32)


def layout(layers, consts):
    at, begin = {}, 0
    for name, size in (
        ("attn", layers),
        ("moe", layers),
        ("router", layers * NEXP),
        ("cvec", layers * consts),
        ("cmix", layers * consts * 2),
    ):
        at[name] = begin
        begin += size
    return at


def shift(values, lanes_up):
    return pltpu.roll(values, lanes_up % LANES, 1)


def greet_all(count, me, place):
    barrier = pltpu.get_barrier_semaphore()

    def greet(step, carry):
        other = lax.rem(me + step, count)
        pl.semaphore_signal(barrier, inc=1, device_id=place(other), device_id_type=MESH)
        return carry

    lax.fori_loop(1, count, greet, 0)
    pl.semaphore_wait(barrier, count - 1)


def swap_all(count, me, place, source, land, send_sems, recv_sems):
    def copy(other, slot):
        return pltpu.make_async_remote_copy(
            src_ref=source(other),
            dst_ref=land.at[slot],
            send_sem=send_sems.at[other],
            recv_sem=recv_sems.at[slot],
            device_id=place(other),
            device_id_type=MESH,
        )

    def start():
        def send(step, carry):
            other = lax.rem(me + step, count)
            copy(other, me).start()
            return carry

        lax.fori_loop(1, count, send, 0)

    def finish():
        def wait(step, carry):
            other = lax.rem(me + count - step, count)
            copy(other, other).wait()
            return carry

        lax.fori_loop(1, count, wait, 0)

    return start, finish


def closing_kernel(ndp, inner, layers, consts, wide, *refs):
    small_ref, first_ref, above_ref = refs[:3]
    attn_out, moe_out, router_out, mix_out, cvec_out, cmix_out, qkv_out, outw_out = refs[3:11]
    land, square, tall = refs[11:14]
    sems = refs[14:]
    count = ndp * inner
    row, col = lax.axis_index("dp"), lax.axis_index("tensor")
    me = row * inner + col
    cols = attn_out.shape[1]
    rows = qkv_out.shape[2]

    def anywhere(other):
        return (lax.div(other, inner), lax.rem(other, inner))

    greet_all(count, me, anywhere)
    start, finish = swap_all(count, me, anywhere, lambda other: small_ref.at[other], land, *sems)
    start()
    land[me] = small_ref[me]
    square[...] = jnp.zeros_like(square)
    tall[...] = jnp.zeros_like(tall)

    def place(l, total):
        for part in range(3):
            qkv_out[l, part] = total[:, part * wide : (part + 1) * wide]
        tall[:rows, :wide] = total[:, 3 * wide :]
        outw_out[l] = tall[...].T[:wide, :rows]

    for l in range(1, layers):
        place(l, above_ref[l - 1].astype(F32))
    place(0, first_ref[...])
    finish()
    total = jnp.sum(land[...], axis=0)
    square[:cols, :] = total[:cols]
    turned = square[...].T
    at = layout(layers, consts)
    attn_out[...] = turned[at["attn"] : at["attn"] + layers, :cols]
    moe_out[...] = turned[at["moe"] : at["moe"] + layers, :cols]
    for l in range(layers):
        begin = at["router"] + l * NEXP
        for e in range(NEXP):
            router_out[e, l : l + 1, :] = turned[begin + e : begin + e + 1, :cols]
            mix_out[e, l : l + 1, :] = total[
                cols + e : cols + e + 1, l * MIX_STEP : l * MIX_STEP + NEXP
            ]
        begin = at["cvec"] + l * consts
        cvec_out[l] = turned[begin : begin + consts, :cols]
        begin = at["cmix"] + l * 2 * consts
        for j in range(consts):
            for k in range(2):
                lane = begin + k * consts + j
                cmix_out[l, j, k : k + 1, :] = turned[lane : lane + 1, :cols]


def closing(small, projection, above, consts, layers, cols, collective_id):
    inner, ndp = lax.axis_size("tensor"), lax.axis_size("dp")
    rows, packed = projection.shape
    wide = packed // 4
    shapes = [
        (layers, cols), (layers, cols), (NEXP, layers, cols), (NEXP, layers, NEXP),
        (layers, consts, cols), (layers, consts, 2, cols),
        (layers, 3, rows, wide), (layers, wide, rows),
    ]
    return pl.pallas_call(
        functools.partial(closing_kernel, ndp, inner, layers, consts, wide),
        out_shape=[jax.ShapeDtypeStruct(shape, F32) for shape in shapes],
        in_specs=[VMEM_SPEC] * 3,
        out_specs=[VMEM_SPEC] * len(shapes),
        scratch_shapes=[
            pltpu.VMEM(small.shape, F32),
            pltpu.VMEM((-(-cols // LANES) * LANES, LANES), F32),
            pltpu.VMEM((-(-rows // LANES) * LANES, -(-wide // LANES) * LANES), F32),
        ]
        + [pltpu.SemaphoreType.DMA((ndp * inner,))] * 2,
        compiler_params=pltpu.CompilerParams(
            collective_id=collective_id, has_side_effects=True, vmem_limit_bytes=VMEM_LIMIT
        ),
        name="closing",
    )(small, projection, above)


def join_kernel(back, gain_row, nt, pieces, lag, *refs):
    if back:
        part, base_ref, skip_ref, rows_ref, result_ref, gg_ref = refs[:6]
    else:
        part, base_ref, rows_ref, total_ref, normed_ref = refs[:5]
    refs = refs[6 if back else 5 :]
    inbox, half, across, full, out_sem, in_sem, cross_out, cross_in, full_out, full_in = refs
    me = lax.axis_index("tensor")
    is_end = (me == 0) | (me == nt - 1)
    buddy = jnp.where(me < 2, 1 - me, 5 - me)
    cross = 3 - me

    barrier = pltpu.get_barrier_semaphore()
    pl.semaphore_signal(barrier, inc=1, device_id={"tensor": buddy}, device_id_type=MESH)

    @pl.when(jnp.logical_not(is_end))
    def _():
        pl.semaphore_signal(barrier, inc=1, device_id={"tensor": cross}, device_id_type=MESH)

    pl.semaphore_wait(barrier, 2 - is_end.astype(jnp.int32))

    def copy(src, dst, send_sem, recv_sem, to):
        return pltpu.make_async_remote_copy(
            src_ref=src,
            dst_ref=dst,
            send_sem=send_sem,
            recv_sem=recv_sem,
            device_id={"tensor": to},
            device_id_type=MESH,
        )

    def inward(n):
        return copy(part.at[n], inbox.at[n], out_sem.at[n], in_sem.at[n], buddy)

    def over(n):
        return copy(half.at[n], across.at[n], cross_out.at[n], cross_in.at[n], cross)

    def outward(n):
        return copy(full.at[n], full.at[n], full_out.at[n], full_in.at[n], buddy)

    gain = rows_ref[gain_row : gain_row + 1, :]
    if back:
        gg_ref[...] = jnp.zeros_like(gg_ref)

    def settle(n):
        total = full[n].astype(F32)
        base = base_ref[n].astype(F32)
        if back:
            scale = lax.rsqrt(jnp.mean(base * base, axis=-1, keepdims=True) + EPS)
            unit = base * scale
            grad_unit = total * gain
            below = scale * (grad_unit - unit * jnp.mean(grad_unit * unit, axis=-1, keepdims=True))
            result_ref[n] = (below + skip_ref[n].astype(F32)).astype(BF16)

            @pl.when(lax.div(n, pieces // nt) == me)
            def _():
                gg_ref[...] += jnp.sum(total * unit, axis=0, keepdims=True)
        else:
            total = total + base
            total_ref[n] = total.astype(BF16)
            normed_ref[n] = normed(total, gain).astype(BF16)

    @pl.when(is_end)
    def _():
        for n in range(pieces):
            inward(n).start()

        def take(n, carry):
            outward(n).wait_recv()
            settle(n)
            return carry

        lax.fori_loop(0, pieces, take, 0)
        for n in range(pieces):
            inward(n).wait_send()

    @pl.when(jnp.logical_not(is_end))
    def _():
        def step(at, carry):
            @pl.when(at < pieces)
            def _():
                inward(at).wait_recv()
                half[at] = (part[at].astype(F32) + inbox[at].astype(F32)).astype(BF16)
                over(at).start()

            @pl.when(at >= lag)
            def _():
                n = at - lag
                over(n).wait_recv()
                full[n] = (half[n].astype(F32) + across[n].astype(F32)).astype(BF16)
                outward(n).start()
                settle(n)

            return carry

        lax.fori_loop(0, pieces + lag, step, 0)
        for n in range(pieces):
            over(n).wait_send()
            outward(n).wait_send()


def join(back, part, others, rows, gain_row, collective_id, pieces=PIECES, lag=LAG):
    nt = lax.axis_size("tensor")
    seq_len, width = part.shape
    cut = (pieces, seq_len // pieces, width)
    outs = [jax.ShapeDtypeStruct(cut, BF16)]
    outs.append(jax.ShapeDtypeStruct((1, width) if back else cut, F32 if back else BF16))
    sems = pltpu.SemaphoreType.DMA((pieces,))
    results = pl.pallas_call(
        functools.partial(join_kernel, back, gain_row, nt, pieces, lag),
        out_shape=outs,
        in_specs=[VMEM_SPEC] * (2 + len(others)),
        out_specs=[VMEM_SPEC] * 2,
        scratch_shapes=[pltpu.VMEM(cut, BF16)] * 4 + [sems] * 6,
        compiler_params=pltpu.CompilerParams(
            collective_id=collective_id, has_side_effects=True, vmem_limit_bytes=VMEM_LIMIT
        ),
        cost_estimate=pl.CostEstimate(
            flops=10 * seq_len * width, bytes_accessed=100 * seq_len * width, transcendentals=0
        ),
        name="join_back" if back else "join",
    )(part.reshape(cut), *[item.reshape(cut) for item in others], rows)
    return results[0].reshape(seq_len, width), (
        results[1] if back else results[1].reshape(seq_len, width)
    )


def normed(values, gain):
    return values * lax.rsqrt(jnp.mean(values * values, axis=-1, keepdims=True) + EPS) * gain


def line_kernel(kind, nt, chunks, lag, extra, *refs):
    refs = list(refs)
    has_sum = kind != "start"
    has_gather = kind != "end"
    part = refs.pop(0) if has_sum else None
    if kind == "start":
        x_ref, small_ref = refs.pop(0), refs.pop(0)
    elif kind == "fwd":
        extra_ref, gain_ref = refs.pop(0), refs.pop(0)
    elif kind == "last":
        extra_ref, og_ref = refs.pop(0), refs.pop(0)
    else:
        extra_ref = refs.pop(0) if extra else None
        base_ref, skip_ref, rows_ref = refs.pop(0), refs.pop(0), refs.pop(0)
        proj_ref = refs.pop(0)
    own_ref = refs.pop(0) if has_sum else None
    gg_ref = refs.pop(0) if kind in ("bwd", "end") else None
    proj_out = refs.pop(0) if kind == "end" else None
    all_ref = refs.pop(0) if has_gather else None
    land_ref = refs.pop(0) if kind == "start" else None
    if has_sum:
        from_left, from_right, tx, acc, rs_send, rl_sem, rr_sem = refs[:7]
        proj_land, proj_send, proj_recv = refs[7:10]
        refs = refs[10:]
    if has_gather:
        ag_right, ag_left, ag_recv = refs[:3]
        refs = refs[3:]

    me = lax.axis_index("tensor")
    has_l, has_r = me > 0, me < nt - 1
    left, right = jnp.maximum(me - 1, 0), jnp.minimum(me + 1, nt - 1)

    if kind == "start":
        count = lax.axis_size("dp") * nt
        me_all = lax.axis_index("dp") * nt + me

        def place(other):
            return (lax.div(other, nt), lax.rem(other, nt))

        greet_all(count, me_all, place)
        small_start, small_finish = swap_all(
            count, me_all, place, lambda other: small_ref, land_ref, *refs[:2]
        )
        small_start()
        land_ref[me_all] = small_ref[...]
    else:
        barrier = pltpu.get_barrier_semaphore()
        members, row = lax.axis_size("dp"), lax.axis_index("dp")

        @pl.when(has_l)
        def _():
            pl.semaphore_signal(barrier, inc=1, device_id={"tensor": left}, device_id_type=MESH)

        @pl.when(has_r)
        def _():
            pl.semaphore_signal(barrier, inc=1, device_id={"tensor": right}, device_id_type=MESH)

        def greet(step, carry):
            other = lax.rem(row + step, members)
            pl.semaphore_signal(barrier, inc=1, device_id={"dp": other}, device_id_type=MESH)
            return carry

        lax.fori_loop(1, members, greet, 0)
        pl.semaphore_wait(
            barrier, members - 1 + has_l.astype(jnp.int32) + has_r.astype(jnp.int32)
        )
        proj_start, proj_finish = swap_all(
            members, row, lambda other: (other, me), lambda other: proj_ref.at[other], proj_land,
            proj_send, proj_recv,
        )

    def copy(src, dst, send_sem, recv_sem, to):
        return pltpu.make_async_remote_copy(
            src_ref=src,
            dst_ref=dst,
            send_sem=send_sem,
            recv_sem=recv_sem,
            device_id={"tensor": to},
            device_id_type=MESH,
        )

    def sum_right(j, c, src):
        return copy(src, from_left.at[j, c], rs_send.at[j, c], rl_sem.at[j, c], right)

    def sum_left(j, c, src):
        return copy(src, from_right.at[j, c], rs_send.at[j, c], rr_sem.at[j, c], left)

    def spread_right(j, c):
        block = all_ref.at[j, c]
        return copy(block, block, ag_right.at[j, c], ag_recv.at[j, c], right)

    def spread_left(j, c):
        block = all_ref.at[j, c]
        return copy(block, block, ag_left.at[j, c], ag_recv.at[j, c], left)

    def offer(c):
        @pl.when(has_r)
        def _():
            spread_right(me, c).start()

        @pl.when(has_l)
        def _():
            spread_left(me, c).start()

    def pass_on(c, d):
        @pl.when(me - d >= 0)
        def _():
            j = me - d
            spread_right(j, c).wait_recv()

            @pl.when(has_r)
            def _():
                spread_right(j, c).start()

        @pl.when(me + d < nt)
        def _():
            j = me + d
            spread_left(j, c).wait_recv()

            @pl.when(has_l)
            def _():
                spread_left(j, c).start()

    hops = nt - 1

    count = hops * chunks

    def relay(step):
        k = jnp.clip(step - lag * me, 0, count - 1)
        c, j = lax.div(k, hops), hops - lax.rem(k, hops)

        @pl.when(has_l & (step >= lag * me) & (step - lag * me < count) & (me < j))
        def _():
            sum_right(j, c, tx.at[j, c]).wait_recv()
            tx[j, c] = (part[j, c].astype(F32) + from_left[j, c].astype(F32)).astype(BF16)
            sum_right(j, c, tx.at[j, c]).start()

        far = lag * (hops - me)
        k_down = jnp.clip(step - far, 0, count - 1)
        c_down, j_down = lax.div(k_down, hops), lax.rem(k_down, hops)

        @pl.when(has_r & (step >= far) & (step - far < count) & (me > j_down))
        def _():
            sum_left(j_down, c_down, tx.at[j_down, c_down]).wait_recv()
            tx[j_down, c_down] = (
                part[j_down, c_down].astype(F32) + from_right[j_down, c_down].astype(F32)
            ).astype(BF16)
            sum_left(j_down, c_down, tx.at[j_down, c_down]).start()

    def push(first, last):
        ks = range(min(first, count), min(last, count))

        @pl.when(jnp.logical_not(has_l))
        def _():
            for k in ks:
                j, c = hops - k % hops, k // hops
                sum_right(j, c, part.at[j, c]).start()

        @pl.when(jnp.logical_not(has_r))
        def _():
            for k in ks:
                j, c = k % hops, k // hops
                sum_left(j, c, part.at[j, c]).start()

    def own_rows(c):
        acc[...] = part[me, c].astype(F32)

        @pl.when(has_l)
        def _():
            sum_right(me, c, tx.at[me, c]).wait_recv()
            acc[...] += from_left[me, c].astype(F32)

        @pl.when(has_r)
        def _():
            sum_left(me, c, tx.at[me, c]).wait_recv()
            acc[...] += from_right[me, c].astype(F32)

        total = acc[...]
        if kind == "fwd":
            total = total + extra_ref[c]
            all_ref[me, c] = normed(total, gain_ref[...]).astype(BF16)
            own_ref[c] = total
        elif kind == "last":
            own_ref[c] = total + extra_ref[c]
        else:
            if extra:
                total = total + extra_ref[c]
            base = base_ref[c].astype(F32)
            scale = lax.rsqrt(jnp.mean(base * base, axis=-1, keepdims=True) + EPS)
            unit = base * scale
            grad_unit = total * rows_ref[0:1, :]
            below = scale * (grad_unit - unit * jnp.mean(grad_unit * unit, axis=-1, keepdims=True))
            result = below + skip_ref[me, c].astype(F32)
            if has_gather:
                all_ref[me, c] = result.astype(BF16)
            own_ref[c] = result
            gg = jnp.sum(total * unit, axis=0, keepdims=True)
            if c == 0:
                gg_ref[...] = gg
            else:
                gg_ref[...] += gg
        if kind in ("fwd", "bwd"):
            offer(c)

    if kind == "start":
        for c in range(chunks):
            all_ref[me, c] = x_ref[c]
            offer(c)
        for c in range(chunks):
            for d in range(1, nt):
                pass_on(c, d)
        small_finish()
    else:

        push(0, AHEAD)
        proj_start()
        proj_land[row] = proj_ref[row]
        if kind == "last":
            for c in range(chunks):
                all_ref[me, c] = og_ref[c]
            for c in range(chunks):
                offer(c)
        delay = 0 if kind == "last" else hops * lag
        spreads = {}
        for c in range(chunks if has_gather else 0):
            for d in range(1, nt):
                spreads.setdefault(delay + hops * c + lag * d, []).append((c, d))
        final = max([hops * (chunks - 1 + lag)] + list(spreads))
        for step in range(1, final + 1):
            push(step + AHEAD - 1, step + AHEAD)
            relay(step)
            for c, d in spreads.get(step, ()):
                pass_on(c, d)
            if step % hops == 0 and 0 <= step // hops - lag < chunks:
                own_rows(step // hops - lag)

    if kind == "end":
        proj_finish()
        proj_out[...] = jnp.sum(proj_land[...].astype(F32), axis=0)

    for c in range(chunks):
        for j in range(nt):
            if has_sum:

                @pl.when(me < j)
                def _():
                    sum_right(j, c, tx.at[j, c]).wait_send()

                @pl.when(me > j)
                def _():
                    sum_left(j, c, tx.at[j, c]).wait_send()

            if has_gather:

                @pl.when(has_r & (j <= me))
                def _():
                    spread_right(j, c).wait_send()

                @pl.when(has_l & (j >= me))
                def _():
                    spread_left(j, c).wait_send()


def line_exchange(kind, args, rows, width, collective_id, extra=False, chunks=2, lag=2):
    nt = lax.axis_size("tensor")
    has_sum = kind != "start"
    has_gather = kind != "end"
    piece = rows // chunks
    split = []
    for item in args:
        if item.shape[0] == nt * rows:
            split.append(item.reshape(nt, chunks, piece, width))
        elif item.shape[0] == rows:
            split.append(item.reshape(chunks, piece, width))
        else:
            split.append(item)
    outs = []
    if has_sum:
        outs.append(jax.ShapeDtypeStruct((chunks, piece, width), F32))
    if kind in ("bwd", "end"):
        outs.append(jax.ShapeDtypeStruct((1, width), F32))
        outs.append(jax.ShapeDtypeStruct(args[-1].shape[1:], F32))
    if has_gather:
        outs.append(jax.ShapeDtypeStruct((nt, chunks, piece, width), BF16))
    if kind == "start":
        count = lax.axis_size("dp") * nt
        outs.append(jax.ShapeDtypeStruct((count,) + args[1].shape, args[1].dtype))
    scratch = []
    sems = pltpu.SemaphoreType.DMA((nt, chunks))
    if has_sum:
        buf = pltpu.VMEM((nt, chunks, piece, width), BF16)
        scratch += [buf, buf, buf, pltpu.VMEM((piece, width), F32), sems, sems, sems]
        scratch.append(pltpu.VMEM(args[-1].shape, args[-1].dtype))
        scratch += [pltpu.SemaphoreType.DMA((lax.axis_size("dp"),))] * 2
    if has_gather:
        scratch += [sems, sems, sems]
    if kind == "start":
        scratch += [pltpu.SemaphoreType.DMA((count,))] * 2
    results = pl.pallas_call(
        functools.partial(line_kernel, kind, nt, chunks, lag, extra),
        out_shape=outs,
        in_specs=[VMEM_SPEC] * len(split),
        out_specs=[VMEM_SPEC] * len(outs),
        scratch_shapes=scratch,
        compiler_params=pltpu.CompilerParams(
            collective_id=collective_id, has_side_effects=True, vmem_limit_bytes=VMEM_LIMIT
        ),
        cost_estimate=pl.CostEstimate(
            flops=10 * nt * rows * width, bytes_accessed=100 * rows * width * nt, transcendentals=0
        ),
        name="line_" + kind,
    )(*split)
    results = list(results)
    if has_sum:
        results[0] = results[0].reshape(rows, width)
    if has_gather:
        at = 0 if kind == "start" else -1
        results[at] = results[at].reshape(nt * rows, width)
    return results


def span_mask(starts_ref, row_at, rows, cols, spans):
    row = row_at + lax.broadcasted_iota(jnp.int32, (rows, cols), 0)
    col = lax.broadcasted_iota(jnp.int32, (rows, cols), 1)
    seen = col <= row
    for k in range(spans):
        begin = starts_ref[0, k]
        seen = seen | (
            (row >= begin) & (row < begin + PIC) & (col >= begin) & (col < begin + PIC)
        )
    return seen


def key_extent(row_at, seq_len, spans):
    segment = seq_len // spans
    return (row_at // segment + 1) * segment


def attend_kernel(heads, spans, block, raw, starts_ref, a_ref, w_ref, *refs):
    if raw:
        gain_ref, qkv_ref, o_ref, lse_ref, out_ref, normed_ref = refs
        normed_ref[...] = normed(a_ref[...].astype(F32), gain_ref[0:1, :]).astype(BF16)
        a_ref = normed_ref
    else:
        qkv_ref, o_ref, lse_ref, out_ref = refs
    seq_len = a_ref.shape[0]
    wide = heads * HEAD
    factor = HEAD ** (-0.5)
    qkv_ref[...] = dot(a_ref[...], w_ref[:, : 3 * wide]).astype(BF16)
    for at in range(0, seq_len, block):
        reach = key_extent(at, seq_len, spans)
        seen = span_mask(starts_ref, at, block, reach, spans)
        for h in range(heads):
            q = qkv_ref[at : at + block, h * HEAD : (h + 1) * HEAD]
            k = qkv_ref[:reach, wide + h * HEAD : wide + (h + 1) * HEAD]
            v = qkv_ref[:reach, 2 * wide + h * HEAD : 2 * wide + (h + 1) * HEAD]
            s = jnp.where(seen, dot_nt(q, k) * factor, -1e30)
            top = jnp.max(s, axis=-1, keepdims=True)
            e = jnp.exp(s - top)
            total = jnp.sum(e, axis=-1, keepdims=True)
            probs = (e * (1.0 / total)).astype(BF16)
            o_ref[at : at + block, h * HEAD : (h + 1) * HEAD] = dot(probs, v).astype(BF16)
            lse_ref[at : at + block, h : h + 1] = top + jnp.log(total)
    out_ref[...] = dot_nt(o_ref[...], w_ref[:, 3 * wide :]).astype(BF16)


def attend_forward(starts, a_all, w_attn, heads, gain=None):
    seq_len, width = a_all.shape
    wide = heads * HEAD
    spans = starts.shape[1]
    raw = gain is not None
    return pl.pallas_call(
        functools.partial(attend_kernel, heads, spans, PIC, raw),
        out_shape=[
            jax.ShapeDtypeStruct((seq_len, 3 * wide), BF16),
            jax.ShapeDtypeStruct((seq_len, wide), BF16),
            jax.ShapeDtypeStruct((seq_len, heads), F32),
            jax.ShapeDtypeStruct((seq_len, width), BF16),
        ]
        + [jax.ShapeDtypeStruct((seq_len, width), BF16)] * raw,
        in_specs=[pl.BlockSpec(memory_space=pltpu.SMEM)] + [VMEM_SPEC] * (2 + raw),
        out_specs=[VMEM_SPEC] * (4 + raw),
        compiler_params=pltpu.CompilerParams(vmem_limit_bytes=VMEM_LIMIT),
        cost_estimate=pl.CostEstimate(
            flops=8 * seq_len * width * wide + 4 * heads * seq_len * seq_len * HEAD,
            bytes_accessed=6 * seq_len * width,
            transcendentals=heads * seq_len * seq_len,
        ),
        name="attend_forward",
    )(starts, a_all, w_attn, *([gain] if raw else []))


def attend_back_kernel(
    heads, spans, block, starts_ref, g_ref, w_ref, a_ref, qkv_ref, o_ref, lse_ref,
    ga_ref, gw_ref, go_scr, gq_scr, gk_acc, gv_acc,
):
    seq_len = a_ref.shape[0]
    wide = heads * HEAD
    factor = HEAD ** (-0.5)
    go_scr[...] = dot(g_ref[...], w_ref[:, 3 * wide :]).astype(BF16)
    gw_ref[:, 3 * wide :] = dot_tn(g_ref[...], o_ref[...]).astype(BF16)
    gk_acc[...] = jnp.zeros_like(gk_acc)
    gv_acc[...] = jnp.zeros_like(gv_acc)
    for at in range(0, seq_len, block):
        reach = key_extent(at, seq_len, spans)
        seen = span_mask(starts_ref, at, block, reach, spans)
        for h in range(heads):
            own = slice(h * HEAD, (h + 1) * HEAD)
            q = qkv_ref[at : at + block, own]
            k = qkv_ref[:reach, wide + h * HEAD : wide + (h + 1) * HEAD]
            v = qkv_ref[:reach, 2 * wide + h * HEAD : 2 * wide + (h + 1) * HEAD]
            go = go_scr[at : at + block, own]
            s = jnp.where(seen, dot_nt(q, k) * factor, -1e30)
            probs = jnp.exp(s - lse_ref[at : at + block, h : h + 1])
            gp = dot_nt(go, v)
            inner = jnp.sum(probs * gp, axis=-1, keepdims=True)
            gs = (probs * (gp - inner)).astype(BF16)
            gq_scr[at : at + block, own] = (dot(gs, k) * factor).astype(BF16)
            gk_acc[:reach, own] += dot_tn(gs, q) * factor
            gv_acc[:reach, own] += dot_tn(probs.astype(BF16), go)
    gq_scr[:, wide : 2 * wide] = gk_acc[...].astype(BF16)
    gq_scr[:, 2 * wide :] = gv_acc[...].astype(BF16)
    gw_ref[:, : 3 * wide] = dot_tn(a_ref[...], gq_scr[...]).astype(BF16)
    ga_ref[...] = dot_nt(gq_scr[...], w_ref[:, : 3 * wide]).astype(BF16)


def attend_backward(starts, g_all, w_attn, a_all, qkv, o, lse, heads):
    seq_len, width = a_all.shape
    wide = heads * HEAD
    spans = starts.shape[1]
    return pl.pallas_call(
        functools.partial(attend_back_kernel, heads, spans, PIC),
        out_shape=[
            jax.ShapeDtypeStruct((seq_len, width), BF16),
            jax.ShapeDtypeStruct((width, 4 * wide), BF16),
        ],
        in_specs=[pl.BlockSpec(memory_space=pltpu.SMEM)] + [VMEM_SPEC] * 6,
        out_specs=[VMEM_SPEC] * 2,
        scratch_shapes=[
            pltpu.VMEM((seq_len, wide), BF16),
            pltpu.VMEM((seq_len, 3 * wide), BF16),
            pltpu.VMEM((seq_len, wide), F32),
            pltpu.VMEM((seq_len, wide), F32),
        ],
        compiler_params=pltpu.CompilerParams(vmem_limit_bytes=VMEM_LIMIT),
        cost_estimate=pl.CostEstimate(
            flops=16 * seq_len * width * wide + 10 * heads * seq_len * seq_len * HEAD,
            bytes_accessed=12 * seq_len * width,
            transcendentals=heads * seq_len * seq_len,
        ),
        name="attend_backward",
    )(starts, g_all, w_attn, a_all, qkv, o, lse)


def lane_column(values, at):
    lane = lax.broadcasted_iota(jnp.int32, values.shape, 1)
    return jnp.sum(jnp.where(lane == at, values, 0), axis=1, keepdims=True)


def two_parts(values):
    high = values.astype(BF16)
    return high, (values - high.astype(F32)).astype(BF16)


def const_parts(product, wd, layer, at, consts):
    first = EXPERTS + 2
    zero = shift(product, first - at["cmix"] - layer * 2 * consts)
    one = shift(product, first - at["cmix"] - layer * 2 * consts - consts)
    lane = lax.broadcasted_iota(jnp.int32, product.shape, 1)
    here = (lane >= first) & (lane < first + consts)
    gap = jnp.where(here, one - zero, 0.0)
    alpha0 = 1.0 / (1.0 + jnp.exp(gap))
    alpha1 = 1.0 / (1.0 + jnp.exp(-gap))
    gate = jnp.where(here, wd, 0.0)
    keep = jnp.sum(gate * alpha0 + jnp.where(lane == EXPERTS + 1, wd, 0.0), axis=1, keepdims=True)
    return lane, here, alpha0, alpha1, gate, keep


def experts_kernel(
    cap, layer, at, consts, b_ref, w_ref, rowpos_ref, pos_ref, small_ref, rows_ref, mix_ref, zprev_ref,
    mid_ref, x_ref, gu_ref, z_ref, wd_ref, f_ref, extra_ref, pick_scr, y_scr,
):
    e = pl.program_id(0)
    seq_len, width = b_ref.shape
    half = gu_ref.shape[2] // 2

    @pl.when(e == 0)
    def _():
        product = dot(b_ref[...], small_ref[...])
        lane = lax.broadcasted_iota(jnp.int32, product.shape, 1)
        p_high, p_low = two_parts(zprev_ref[...])
        z = (
            jnp.where(lane < NEXP, shift(product, -at["router"] - layer * NEXP), 0.0)
            + dot(p_high, mix_ref[...])
            + dot(p_low, mix_ref[...])
        )
        z_ref[...] = z
        hit = pos_ref[...] >= 0
        top = jnp.max(jnp.where(hit, z, -3e38), axis=1, keepdims=True)
        ez = jnp.where(hit, jnp.exp(jnp.where(hit, z - top, 0.0)), 0.0)
        wd = ez / jnp.sum(ez, axis=1, keepdims=True)
        wd_ref[...] = wd
        _, _, _, alpha1, gate, keep = const_parts(product, wd, layer, at, consts)
        extra = mid_ref[...].astype(F32) + keep * b_ref[...].astype(F32)
        for j in range(consts):
            row = at["cvec"] + layer * consts + j
            extra = extra + lane_column(gate * alpha1, EXPERTS + 2 + j) * rows_ref[row : row + 1, :]
        extra_ref[...] = extra.astype(BF16)

    w = w_ref[...].reshape(width, 3 * half)
    take = (
        lax.broadcasted_iota(jnp.int32, (cap, seq_len), 0) == rowpos_ref[0]
    ).astype(F32).astype(BF16)
    x = dot(take, b_ref[...]).astype(BF16)
    x_ref[0] = x
    gu = dot(x, w[:, : 2 * half])
    gu_ref[0] = gu.astype(BF16)
    g, u = gu[:, :half], gu[:, half:]
    h = (g * jax.nn.sigmoid(g) * u).astype(BF16)
    y = dot_nt(h, w[:, 2 * half :])
    y_scr[pl.ds(pl.multiple_of(e * cap, cap), cap), :] = y.astype(BF16)
    column = lane_column(pos_ref[...], e)
    weight = lane_column(wd_ref[...], e)
    put = jnp.where(
        lax.broadcasted_iota(jnp.int32, (seq_len, cap), 1) == column, weight, 0.0
    ).astype(BF16)
    pick_scr[:, pl.ds(pl.multiple_of(e * cap, cap), cap)] = put

    @pl.when(e == pl.num_programs(0) - 1)
    def _():
        f_ref[...] = dot(pick_scr[...], y_scr[...]).astype(BF16)


def whole(shape):
    return pl.BlockSpec(shape, lambda e: (0,) * len(shape))


def experts_forward(
    layer, at, consts, b_all, w_exp, rowpos, pos, small, rows_t, mix, z_prev, mid, cap
):
    seq_len, width = b_all.shape
    shards_dp, count, rows, wide3 = w_exp.shape
    half = wide3 // 3
    return pl.pallas_call(
        functools.partial(experts_kernel, cap, layer, at, consts),
        grid=(count,),
        out_shape=[
            jax.ShapeDtypeStruct((count, cap, width), BF16),
            jax.ShapeDtypeStruct((count, cap, 2 * half), BF16),
            jax.ShapeDtypeStruct((seq_len, LANES), F32),
            jax.ShapeDtypeStruct((seq_len, LANES), F32),
            jax.ShapeDtypeStruct((seq_len, width), BF16),
            jax.ShapeDtypeStruct((seq_len, width), BF16),
        ],
        in_specs=[
            whole((seq_len, width)),
            pl.BlockSpec((shards_dp, 1, rows, wide3), lambda e: (0, e, 0, 0)),
            pl.BlockSpec((1, 1, seq_len), lambda e: (e, 0, 0)),
            whole((seq_len, LANES)),
            whole((width, LANES)),
            whole(rows_t.shape),
            whole((LANES, LANES)),
            whole((seq_len, LANES)),
            whole((seq_len, width)),
        ],
        out_specs=[
            pl.BlockSpec((1, cap, width), lambda e: (e, 0, 0)),
            pl.BlockSpec((1, cap, 2 * half), lambda e: (e, 0, 0)),
            whole((seq_len, LANES)),
            whole((seq_len, LANES)),
            whole((seq_len, width)),
            whole((seq_len, width)),
        ],
        scratch_shapes=[
            pltpu.VMEM((seq_len, count * cap), BF16),
            pltpu.VMEM((count * cap, width), BF16),
        ],
        compiler_params=pltpu.CompilerParams(vmem_limit_bytes=VMEM_LIMIT),
        cost_estimate=pl.CostEstimate(
            flops=count * (4 * cap * seq_len * width + 6 * cap * width * half),
            bytes_accessed=2 * count * width * wide3,
            transcendentals=0,
        ),
        name="experts_forward",
    )(b_all, w_exp, rowpos, pos, small, rows_t, mix, z_prev, mid)


def experts_back_kernel(
    cap, layer, at, consts, own, g_ref, w_ref, x_ref, gu_ref, rowpos_ref, pos_ref, wd_ref,
    b_ref, small_ref, rows_ref, mix_ref, zprev_ref, gprev_ref, sums_ref, mixes_ref,
    gw_ref, below_ref, gb_ref, sums_out, mixes_out, pick_scr, gx_scr, gg_scr, gb_scr, zs_scr,
    halves, inbox, out_sems, in_sems,
):
    e = pl.program_id(0)
    last = pl.num_programs(0) - 1
    me = lax.axis_index("dp")
    parity = lax.rem(me, 2)
    partner = me + 1 - 2 * parity

    def to_partner(expert):
        return pltpu.make_async_remote_copy(
            src_ref=halves.at[lax.rem(expert, 2), 1 - parity],
            dst_ref=inbox.at[expert],
            send_sem=out_sems.at[expert],
            recv_sem=in_sems.at[expert],
            device_id={"dp": partner},
            device_id_type=MESH,
        )

    @pl.when(e == 0)
    def _():
        barrier = pltpu.get_barrier_semaphore()
        pl.semaphore_signal(barrier, inc=1, device_id={"dp": partner}, device_id_type=MESH)
        pl.semaphore_wait(barrier, 1)

    @pl.when(e < last)
    def _():
        one_expert_back(
            cap, e, g_ref, w_ref, x_ref, gu_ref, rowpos_ref, pos_ref, wd_ref, pick_scr, gx_scr, gg_scr,
            halves,
        )
        to_partner(e).start()

    @pl.when(e > 0)
    def _():
        before = e - 1
        to_partner(before).wait()
        gw_ref[:, 0] = (
            halves[lax.rem(before, 2), parity].astype(F32) + inbox[before].astype(F32)
        ).astype(BF16)

    @pl.when(e == last)
    def _():
        tokens_back(
            layer, at, consts, own, g_ref, wd_ref, b_ref, small_ref, rows_ref, mix_ref, zprev_ref,
            gprev_ref, sums_ref, mixes_ref, below_ref, gb_ref, sums_out, mixes_out, pick_scr, gx_scr,
            gg_scr, gb_scr, zs_scr,
        )


def one_expert_back(
    cap, e, g_ref, w_ref, x_ref, gu_ref, rowpos_ref, pos_ref, wd_ref, pick_scr, gx_scr, gg_scr, halves,
):
    seq_len, width = g_ref.shape
    shards_dp, _, rows, wide3 = w_ref.shape
    half = wide3 // 3
    slot = lax.rem(e, 2)
    w = w_ref[...].reshape(width, wide3)
    take = (
        lax.broadcasted_iota(jnp.int32, (cap, seq_len), 0) == rowpos_ref[0]
    ).astype(F32).astype(BF16)
    w_high, w_low = two_parts(wd_ref[...])
    weight = lane_column(dot(take, w_high) + dot(take, w_low), e)
    gf = dot(take, g_ref[...])
    gh = dot(gf.astype(BF16), w[:, 2 * half :])
    gu = gu_ref[0].astype(F32)
    g, u = gu[:, :half], gu[:, half:]
    sig = jax.nn.sigmoid(g)
    h = (g * sig * u).astype(BF16)
    slot_grad = jnp.sum(h.astype(F32) * gh, axis=1, keepdims=True)
    gh = gh * weight
    gg = gh * u * sig * (1.0 + g * (1.0 - sig))
    gup = gh * g * sig
    both = jnp.concatenate([gg.astype(BF16), gup.astype(BF16)], axis=1)
    gy = (gf * weight).astype(BF16)
    gw_in = dot_tn(x_ref[0], both).astype(BF16)
    gw_down = dot_tn(gy, h).astype(BF16)
    for shard in range(shards_dp):
        own_rows = slice(shard * rows, (shard + 1) * rows)
        halves[slot, shard % 2, shard // 2, :, : 2 * half] = gw_in[own_rows]
        halves[slot, shard % 2, shard // 2, :, 2 * half :] = gw_down[own_rows]
    here = pl.ds(pl.multiple_of(e * cap, cap), cap)
    gx_scr[here, :] = dot_nt(both, w[:, : 2 * half]).astype(BF16)
    s_high, s_low = two_parts(slot_grad)
    lane = lax.broadcasted_iota(jnp.int32, (cap, LANES), 1)
    gg_scr[here, :LANES] = jnp.where(lane == e, s_high.astype(F32), 0.0).astype(BF16)
    gg_scr[here, LANES:] = jnp.where(lane == e, s_low.astype(F32), 0.0).astype(BF16)
    column = lane_column(pos_ref[...], e)
    pick_scr[:, here] = (
        lax.broadcasted_iota(jnp.int32, (seq_len, cap), 1) == column
    ).astype(F32).astype(BF16)


def tokens_back(
    layer, at, consts, own, g_ref, wd_ref, b_ref, small_ref, rows_ref, mix_ref, zprev_ref, gprev_ref,
    sums_ref, mixes_ref, below_ref, gb_ref, sums_out, mixes_out, pick_scr, gx_scr, gg_scr, gb_scr, zs_scr,
):
    mine = pl.ds(pl.multiple_of(lax.axis_index("tensor") * own, own), own)
    b_own, g_own = b_ref[mine, :], g_ref[mine, :].astype(F32)
    wd_own = wd_ref[mine, :]
    lane, here_own, alpha0, alpha1, gate, keep = const_parts(
        dot(b_own, small_ref[...]), wd_own, layer, at, consts
    )
    b_dot = jnp.sum(b_own.astype(F32) * g_own, axis=1, keepdims=True)
    c_dot = jnp.zeros_like(wd_own)
    for j in range(consts):
        row = at["cvec"] + layer * consts + j
        one = jnp.sum(g_own * rows_ref[row : row + 1, :], axis=1, keepdims=True)
        c_dot = jnp.where(lane == EXPERTS + 2 + j, one, c_dot)
    gw_own = jnp.where(here_own, alpha0 * b_dot + alpha1 * c_dot, 0.0)
    gw_own = jnp.where(lane == EXPERTS + 1, b_dot, gw_own)
    inner = gate * (alpha0 * b_dot + alpha1 * c_dot)
    gt0 = alpha0 * (gate * b_dot - inner)
    gt1 = alpha1 * (gate * c_dot - inner)

    slots = dot(pick_scr[...], gg_scr[...])
    zs_scr[...] = slots[:, :LANES] + slots[:, LANES:]
    zs_scr[mine, :] += gw_own
    gw = zs_scr[...]
    wd = wd_ref[...]
    gz = wd * (gw - jnp.sum(wd * gw, axis=1, keepdims=True)) + gprev_ref[...]
    z_high, z_low = two_parts(gz)
    below_ref[...] = dot_nt(z_high, mix_ref[...]) + dot_nt(z_low, mix_ref[...])
    p_high, p_low = two_parts(zprev_ref[...])
    mixes_out[...] = mixes_ref[...] + shift(
        dot_tn(p_high, z_high) + dot_tn(p_high, z_low) + dot_tn(p_low, z_high), layer * MIX_STEP
    )
    zs_scr[...] = shift(gz, at["router"] + layer * NEXP)
    up = at["cmix"] + layer * 2 * consts - EXPERTS - 2
    zs_scr[mine, :] += shift(gt0, up) + shift(gt1, up + consts)
    z_high, z_low = two_parts(zs_scr[...])
    gb_scr[...] = (
        dot(pick_scr[...], gx_scr[...])
        + dot_nt(z_high, small_ref[...])
        + dot_nt(z_low, small_ref[...])
    )
    gb_scr[mine, :] += keep * g_own
    gb_ref[...] = gb_scr[...].astype(BF16)
    i_high, i_low = two_parts(
        shift(gate * alpha1, at["cvec"] + layer * consts - EXPERTS - 2)
    )
    g_low = g_ref[mine, :]
    sums_out[...] = (
        sums_ref[...]
        + dot_tn(b_ref[...], z_high)
        + dot_tn(b_ref[...], z_low)
        + dot_tn(g_low, i_high)
        + dot_tn(g_low, i_low)
    )


def experts_backward(
    collective_id, layer, at, consts, own, g_all, w_exp, x, gu, rowpos, pos, wd, b_all, small, rows_t, mix,
    z_prev, grad_prev, sums, mixes, cap,
):
    seq_len, width = g_all.shape
    shards_dp, count, rows, wide3 = w_exp.shape
    half = wide3 // 3
    weight_spec = pl.BlockSpec(
        (shards_dp, 1, rows, wide3), lambda e: (0, jnp.minimum(e, count - 1), 0, 0)
    )
    half_shape = (shards_dp // 2, 1, rows, wide3)
    return pl.pallas_call(
        functools.partial(experts_back_kernel, cap, layer, at, consts, own),
        grid=(count + 1,),
        out_shape=[
            jax.ShapeDtypeStruct((shards_dp // 2,) + w_exp.shape[1:], BF16),
            jax.ShapeDtypeStruct((seq_len, LANES), F32),
            jax.ShapeDtypeStruct((seq_len, width), BF16),
            jax.ShapeDtypeStruct((width, LANES), F32),
            jax.ShapeDtypeStruct((LANES, LANES), F32),
        ],
        in_specs=[
            whole((seq_len, width)),
            weight_spec,
            pl.BlockSpec((1, cap, width), lambda e: (jnp.minimum(e, count - 1), 0, 0)),
            pl.BlockSpec((1, cap, 2 * half), lambda e: (jnp.minimum(e, count - 1), 0, 0)),
            pl.BlockSpec((1, 1, seq_len), lambda e: (jnp.minimum(e, count - 1), 0, 0)),
            whole((seq_len, LANES)),
            whole((seq_len, LANES)),
            whole((seq_len, width)),
            whole((width, LANES)),
            whole(rows_t.shape),
            whole((LANES, LANES)),
            whole((seq_len, LANES)),
            whole((seq_len, LANES)),
            whole((width, LANES)),
            whole((LANES, LANES)),
        ],
        out_specs=[
            pl.BlockSpec(half_shape, lambda e: (0, jnp.maximum(e - 1, 0), 0, 0)),
            whole((seq_len, LANES)),
            whole((seq_len, width)),
            whole((width, LANES)),
            whole((LANES, LANES)),
        ],
        scratch_shapes=[
            pltpu.VMEM((seq_len, count * cap), BF16),
            pltpu.VMEM((count * cap, width), BF16),
            pltpu.VMEM((count * cap, 2 * LANES), BF16),
            pltpu.VMEM((seq_len, width), F32),
            pltpu.VMEM((seq_len, LANES), F32),
            pltpu.VMEM((2, 2, shards_dp // 2, rows, wide3), BF16),
            pltpu.VMEM((count, shards_dp // 2, rows, wide3), BF16),
            pltpu.SemaphoreType.DMA((count,)),
            pltpu.SemaphoreType.DMA((count,)),
        ],
        compiler_params=pltpu.CompilerParams(
            collective_id=collective_id, has_side_effects=True, vmem_limit_bytes=VMEM_LIMIT
        ),
        cost_estimate=pl.CostEstimate(
            flops=count * (4 * cap * seq_len * width + 12 * cap * width * half),
            bytes_accessed=4 * count * width * wide3,
            transcendentals=0,
        ),
        name="experts_backward",
    )(
        g_all, w_exp, x, gu, rowpos, pos, wd, b_all, small, rows_t, mix, z_prev, grad_prev,
        sums, mixes,
    )


def unpack_kernel(half, *refs):
    *in_refs, up_ref, down_ref = refs
    for l, ref in enumerate(in_refs):
        values = ref[0].astype(F32)
        for part in range(2):
            up_ref[l, 0, :, part, :] = values[:, part * half : (part + 1) * half]
        down_ref[l, 0] = values[:, 2 * half :]


def unpack(items):
    count, rows, wide3 = items[0].shape
    half = wide3 // 3
    layers = len(items)
    return pl.pallas_call(
        functools.partial(unpack_kernel, half),
        grid=(count,),
        out_shape=[
            jax.ShapeDtypeStruct((layers, count, rows, 2, half), F32),
            jax.ShapeDtypeStruct((layers, count, rows, half), F32),
        ],
        in_specs=[pl.BlockSpec((1, rows, wide3), lambda e: (e, 0, 0))] * layers,
        out_specs=[
            pl.BlockSpec((layers, 1, rows, 2, half), lambda e: (0, e, 0, 0, 0)),
            pl.BlockSpec((layers, 1, rows, half), lambda e: (0, e, 0, 0)),
        ],
        compiler_params=pltpu.CompilerParams(vmem_limit_bytes=VMEM_LIMIT),
        name="unpack",
    )(*items)


def lanes(values):
    return jnp.pad(values, ((0, 0), (0, LANES - values.shape[1])))


def slot_table(route_ids):
    tokens = route_ids.shape[0]
    codes = jnp.arange(LANES, dtype=jnp.int32)
    hit = jnp.any(route_ids[:, :, None] == codes[None, None, :], axis=1)
    place = jnp.arange(tokens, dtype=jnp.int32)
    before = (place[None, :] < place[:, None]).astype(BF16)
    slots = dot(before, hit.astype(BF16)).astype(jnp.int32)
    return jnp.where(hit, slots, -1)


def shards(
    hidden_in,
    prev_logits,
    routes,
    span_starts,
    attn_norm,
    qkv_weight,
    out_weight,
    moe_norm,
    router,
    gate_mix,
    const_vec,
    const_mix,
    up_weight,
    down_weight,
    out_grad,
):
    layers = qkv_weight.shape[0]
    own, width = hidden_in.shape
    nt = lax.axis_size("tensor")
    ndp = lax.axis_size("dp")
    seq_len = own * nt
    offset = lax.axis_index("tensor") * own
    cap = seq_len // 4
    heads = qkv_weight.shape[3] // HEAD
    wide = heads * HEAD
    half = up_weight.shape[4]
    rows = qkv_weight.shape[1]
    cols = attn_norm.shape[1]
    consts = const_vec.shape[1]

    at = layout(layers, consts)
    packed = jnp.concatenate(
        [attn_norm.T, moe_norm.T]
        + [router[l] for l in range(layers)]
        + [const_vec.reshape(-1, cols).T]
        + [const_mix[l, :, :, k].T for l in range(layers) for k in range(2)],
        axis=1,
    )
    x_all, small = line_exchange("start", [hidden_in, lanes(packed)], own, width, 0)
    small = small.reshape(width, LANES)
    rows_t = small[:, :48].T.astype(F32)

    attn_w, exp_w = [], []
    for l in range(layers):
        local = jnp.concatenate(
            [qkv_weight[l].reshape(rows, 3 * wide), out_weight[l].T], axis=1
        )
        attn_w.append(lax.all_gather(local, "dp", axis=0, tiled=False).reshape(width, 4 * wide))
        local = jnp.concatenate(
            [
                up_weight[l].reshape(EXPERTS, rows, 2 * half),
                jnp.swapaxes(down_weight[l], 1, 2),
            ],
            axis=2,
        )
        exp_w.append(lax.all_gather(local, "dp", axis=0, tiled=False))

    pos = [slot_table(routes[l]) for l in range(layers)]
    rowpos = [p[:, :EXPERTS].T[:, None, :] for p in pos]

    z_prev = lanes(prev_logits)
    hidden, a_all = x_all, None
    grad_all = out_grad
    next_id = 1
    stored = []
    for l in range(layers):
        mix = jnp.pad(gate_mix[l], ((0, LANES - NEXP), (0, LANES - NEXP)))
        if l == 0:
            qkv, o, lse, partial, a_all = attend_forward(
                span_starts, x_all, attn_w[l], heads, rows_t
            )
        else:
            qkv, o, lse, partial = attend_forward(span_starts, a_all, attn_w[l], heads)
        if l == layers - 1:
            partial, grad_all = lax.optimization_barrier((partial, grad_all))
            grad_all = lax.all_gather(grad_all, "tensor", axis=0, tiled=True)
        mid, b_all = join(False, partial, [hidden], rows_t, at["moe"] + l, next_id)
        x, gu, z, wd, partial, extra = experts_forward(
            l, at, consts, b_all, exp_w[l], rowpos[l], pos[l], small, rows_t, mix, z_prev, mid, cap
        )
        stored.append(
            dict(
                hidden=hidden, a_all=a_all, qkv=qkv, o=o, lse=lse, mid=mid, b_all=b_all, x=x, gu=gu,
                wd=wd, z_prev=z_prev, mix=mix,
            )
        )
        if l + 1 < layers:
            hidden, a_all = join(False, partial, [extra], rows_t, at["attn"] + l + 1, next_id + 1)
        else:
            hidden_out = lax.psum_scatter(partial, "tensor", scatter_dimension=0, tiled=True)
            extra = lax.dynamic_slice_in_dim(extra, offset, own, 0)
        z_prev = z
        next_id += 2

    below = jnp.zeros((seq_len, LANES), F32)
    sums = jnp.zeros((width, LANES), F32)
    mixes = jnp.zeros((LANES, LANES), F32)
    attn_grads, exp_grads = [None] * layers, [None] * layers
    gains_a, gains_m = [None] * layers, [None] * layers
    for l in reversed(range(layers)):
        s = stored[l]
        gw_exp, below, partial, sums, mixes = experts_backward(
            next_id + 2, l, at, consts, own, grad_all, exp_w[l], s["x"], s["gu"], rowpos[l],
            pos[l], s["wd"], s["b_all"], small, rows_t, s["mix"], s["z_prev"], below, sums, mixes, cap,
        )
        exp_grads[l] = sum_over_pairs(gw_exp)
        if l + 1 < layers:
            partial, exp_grads[l + 1] = lax.optimization_barrier((partial, exp_grads[l + 1]))
        else:
            partial, hidden_out = lax.optimization_barrier((partial, hidden_out))
        grad_mid, gains_m[l] = join(
            True, partial, [s["mid"], grad_all], rows_t, at["moe"] + l, next_id
        )
        partial, gw_attn = attend_backward(
            span_starts, grad_mid, attn_w[l], s["a_all"], s["qkv"], s["o"], s["lse"], heads
        )
        attn_grads[l] = gw_attn.reshape(ndp, rows, 4 * wide)
        if l > 0:
            attn_grads[l] = lax.psum_scatter(attn_grads[l], "dp", scatter_dimension=0, tiled=False)
            grad_all, gains_a[l] = join(
                True, partial, [s["hidden"], grad_mid], rows_t, at["attn"] + l, next_id + 1
            )
        else:
            partial, attn_grads[1:] = lax.optimization_barrier((partial, attn_grads[1:]))
            grad, gains_a[l], attn_grads[l] = line_exchange(
                "end", [partial, hidden_in, grad_mid, rows_t, attn_grads[l]], own, width, next_id + 1
            )
        next_id += 3
    hidden_out = hidden_out.astype(F32) + extra.astype(F32)

    gains = jnp.concatenate(gains_a + gains_m, axis=0)
    sums = sums + jnp.pad(gains, ((0, LANES - 2 * layers), (0, 0))).T
    sums = jnp.concatenate(
        [
            sums.reshape(ndp * nt, cols, LANES),
            jnp.broadcast_to(mixes[None, :MIX_STEP], (ndp * nt, MIX_STEP, LANES)),
        ],
        axis=1,
    )
    attn_g, moe_g, router_g, mix_g, cvec_g, cmix_g, qkv_g, outw_g = closing(
        sums, attn_grads[0], jnp.stack(attn_grads[1:]), consts, layers, cols, next_id
    )
    up_grad, down_grad = unpack(exp_grads)
    qkv_g = jnp.swapaxes(qkv_g, 1, 2)
    router_g = jnp.transpose(router_g, (1, 2, 0))
    mix_g = jnp.swapaxes(mix_g, 0, 1)
    cmix_g = jnp.swapaxes(cmix_g, 2, 3)
    down_grad = jnp.swapaxes(down_grad, 2, 3)
    return (
        hidden_out,
        grad,
        attn_g,
        qkv_g,
        outw_g,
        moe_g,
        router_g,
        mix_g,
        cvec_g,
        cmix_g,
        up_grad,
        down_grad,
    )


def sum_over_pairs(values):
    members = lax.axis_size("dp")
    groups = [list(range(parity, members, 2)) for parity in range(2)]
    return lax.psum_scatter(
        values, "dp", scatter_dimension=0, axis_index_groups=groups, tiled=False
    )


def solution(mesh):
    return jax.shard_map(
        shards,
        mesh=mesh,
        in_specs=(
            P(("dp", "tensor"), None),
            P("dp", None),
            P(None, "dp", None),
            P("dp", None),
            P(None, ("dp", "tensor")),
            P(None, "dp", None, "tensor"),
            P(None, "tensor", "dp"),
            P(None, ("dp", "tensor")),
            P(None, ("dp", "tensor"), None),
            P(),
            P(None, None, ("dp", "tensor")),
            P(None, None, ("dp", "tensor"), None),
            P(None, None, "dp", None, "tensor"),
            P(None, None, "tensor", "dp"),
            P(("dp", "tensor"), None),
        ),
        out_specs=(
            P(("dp", "tensor"), None),
            P(("dp", "tensor"), None),
            P(None, ("dp", "tensor")),
            P(None, "dp", None, "tensor"),
            P(None, "tensor", "dp"),
            P(None, ("dp", "tensor")),
            P(None, ("dp", "tensor"), None),
            P(),
            P(None, None, ("dp", "tensor")),
            P(None, None, ("dp", "tensor"), None),
            P(None, None, "dp", None, "tensor"),
            P(None, None, "tensor", "dp"),
        ),
        check_vma=False,
    )
```

```python
import functools

import jax
import jax.numpy as jnp
from jax import lax
from jax.experimental import pallas as pl
from jax.experimental.pallas import tpu as pltpu
from jax.sharding import PartitionSpec as P

HEAD = 64
EXPERTS = 8
NEXP = 12
TOPK = 2
PIC = 256
LANES = 128

EPS = 1e-06
HIGH = lax.Precision.HIGHEST
MESH = pl.DeviceIdType.MESH
F32 = jnp.float32
BF16 = jnp.bfloat16
VMEM_SPEC = pl.BlockSpec(memory_space=pltpu.VMEM)
AHEAD = 2
PIECES = 32
LAG = 4
APART = 16000
MIX_STEP = 16
VMEM_LIMIT = 60 * 1024 * 1024


def dot(a, b):
    return jnp.dot(a, b, preferred_element_type=F32)


def dot_nt(a, b):
    return lax.dot_general(a, b, (((1,), (1,)), ((), ())), preferred_element_type=F32)


def dot_tn(a, b):
    return lax.dot_general(a, b, (((0,), (0,)), ((), ())), preferred_element_type=F32)


def layout(layers, consts):
    at, begin = {}, 0
    for name, size in (
        ("attn", layers),
        ("moe", layers),
        ("router", layers * NEXP),
        ("cvec", layers * consts),
        ("cmix", layers * consts * 2),
    ):
        at[name] = begin
        begin += size
    return at


def shift(values, lanes_up):
    return pltpu.roll(values, lanes_up % LANES, 1)


def greet_all(count, me, place):
    barrier = pltpu.get_barrier_semaphore()

    def greet(step, carry):
        other = lax.rem(me + step, count)
        pl.semaphore_signal(barrier, inc=1, device_id=place(other), device_id_type=MESH)
        return carry

    lax.fori_loop(1, count, greet, 0)
    pl.semaphore_wait(barrier, count - 1)


def swap_all(count, me, place, source, land, send_sems, recv_sems):
    def copy(other, slot):
        return pltpu.make_async_remote_copy(
            src_ref=source(other),
            dst_ref=land.at[slot],
            send_sem=send_sems.at[other],
            recv_sem=recv_sems.at[slot],
            device_id=place(other),
            device_id_type=MESH,
        )

    def start():
        def send(step, carry):
            other = lax.rem(me + step, count)
            copy(other, me).start()
            return carry

        lax.fori_loop(1, count, send, 0)

    def finish():
        def wait(step, carry):
            other = lax.rem(me + count - step, count)
            copy(other, other).wait()
            return carry

        lax.fori_loop(1, count, wait, 0)

    return start, finish


def closing_kernel(ndp, inner, layers, consts, wide, *refs):
    small_ref, first_ref, above_ref = refs[:3]
    attn_out, moe_out, router_out, mix_out, cvec_out, cmix_out, qkv_out, outw_out = refs[3:11]
    land, square, tall = refs[11:14]
    sems = refs[14:]
    count = ndp * inner
    row, col = lax.axis_index("dp"), lax.axis_index("tensor")
    me = row * inner + col
    cols = attn_out.shape[1]
    rows = qkv_out.shape[2]

    def anywhere(other):
        return (lax.div(other, inner), lax.rem(other, inner))

    greet_all(count, me, anywhere)
    start, finish = swap_all(count, me, anywhere, lambda other: small_ref.at[other], land, *sems)
    start()
    land[me] = small_ref[me]
    square[...] = jnp.zeros_like(square)
    tall[...] = jnp.zeros_like(tall)

    def place(l, total):
        for part in range(3):
            qkv_out[l, part] = total[:, part * wide : (part + 1) * wide]
        tall[:rows, :wide] = total[:, 3 * wide :]
        outw_out[l] = tall[...].T[:wide, :rows]

    for l in range(1, layers):
        place(l, above_ref[l - 1].astype(F32))
    place(0, first_ref[...])
    finish()
    total = jnp.sum(land[...].astype(F32), axis=0)
    square[:cols, :] = total[:cols]
    turned = square[...].T
    at = layout(layers, consts)
    attn_out[...] = turned[at["attn"] : at["attn"] + layers, :cols]
    moe_out[...] = turned[at["moe"] : at["moe"] + layers, :cols]
    for l in range(layers):
        begin = at["router"] + l * NEXP
        for e in range(NEXP):
            router_out[e, l : l + 1, :] = turned[begin + e : begin + e + 1, :cols]
            mix_out[e, l : l + 1, :] = total[
                cols + e : cols + e + 1, l * MIX_STEP : l * MIX_STEP + NEXP
            ]
        begin = at["cvec"] + l * consts
        cvec_out[l] = turned[begin : begin + consts, :cols]
        begin = at["cmix"] + l * 2 * consts
        for j in range(consts):
            for k in range(2):
                lane = begin + k * consts + j
                cmix_out[l, j, k : k + 1, :] = turned[lane : lane + 1, :cols]


def closing(small, projection, above, consts, layers, cols, collective_id):
    inner, ndp = lax.axis_size("tensor"), lax.axis_size("dp")
    rows, packed = projection.shape
    wide = packed // 4
    shapes = [
        (layers, cols), (layers, cols), (NEXP, layers, cols), (NEXP, layers, NEXP),
        (layers, consts, cols), (layers, consts, 2, cols),
        (layers, 3, rows, wide), (layers, wide, rows),
    ]
    return pl.pallas_call(
        functools.partial(closing_kernel, ndp, inner, layers, consts, wide),
        out_shape=[jax.ShapeDtypeStruct(shape, F32) for shape in shapes],
        in_specs=[VMEM_SPEC] * 3,
        out_specs=[VMEM_SPEC] * len(shapes),
        scratch_shapes=[
            pltpu.VMEM(small.shape, BF16),
            pltpu.VMEM((-(-cols // LANES) * LANES, LANES), F32),
            pltpu.VMEM((-(-rows // LANES) * LANES, -(-wide // LANES) * LANES), F32),
        ]
        + [pltpu.SemaphoreType.DMA((ndp * inner,))] * 2,
        compiler_params=pltpu.CompilerParams(
            collective_id=collective_id, has_side_effects=True, vmem_limit_bytes=VMEM_LIMIT
        ),
        name="closing",
    )(small, projection, above)


def join_kernel(back, gain_row, nt, pieces, lag, wait, *refs):
    if back:
        part, base_ref, skip_ref, rows_ref, result_ref, gg_ref = refs[:6]
    else:
        part, base_ref, rows_ref, total_ref, normed_ref = refs[:5]
    refs = refs[6 if back else 5 :]
    inbox, half, across, full, out_sem, in_sem, cross_out, cross_in, full_out, full_in = refs
    me = lax.axis_index("tensor")
    is_end = (me == 0) | (me == nt - 1)
    buddy = jnp.where(me < 2, 1 - me, 5 - me)
    cross = 3 - me

    if wait:
        @pl.when(lax.rem(lax.axis_index("dp"), 2) == 1)
        def _():
            pl.delay(wait)

    barrier = pltpu.get_barrier_semaphore()
    pl.semaphore_signal(barrier, inc=1, device_id={"tensor": buddy}, device_id_type=MESH)

    @pl.when(jnp.logical_not(is_end))
    def _():
        pl.semaphore_signal(barrier, inc=1, device_id={"tensor": cross}, device_id_type=MESH)

    pl.semaphore_wait(barrier, 2 - is_end.astype(jnp.int32))

    def copy(src, dst, send_sem, recv_sem, to):
        return pltpu.make_async_remote_copy(
            src_ref=src,
            dst_ref=dst,
            send_sem=send_sem,
            recv_sem=recv_sem,
            device_id={"tensor": to},
            device_id_type=MESH,
        )

    def inward(n):
        return copy(part.at[n], inbox.at[n], out_sem.at[n], in_sem.at[n], buddy)

    def over(n):
        return copy(half.at[n], across.at[n], cross_out.at[n], cross_in.at[n], cross)

    def outward(n):
        return copy(full.at[n], full.at[n], full_out.at[n], full_in.at[n], buddy)

    gain = rows_ref[gain_row : gain_row + 1, :]
    if back:
        gg_ref[...] = jnp.zeros_like(gg_ref)

    def settle(n):
        total = full[n].astype(F32)
        base = base_ref[n].astype(F32)
        if back:
            scale = lax.rsqrt(jnp.mean(base * base, axis=-1, keepdims=True) + EPS)
            unit = base * scale
            grad_unit = total * gain
            below = scale * (grad_unit - unit * jnp.mean(grad_unit * unit, axis=-1, keepdims=True))
            result_ref[n] = (below + skip_ref[n].astype(F32)).astype(BF16)

            @pl.when(lax.div(n, pieces // nt) == me)
            def _():
                gg_ref[...] += jnp.sum(total * unit, axis=0, keepdims=True)
        else:
            total = total + base
            total_ref[n] = total.astype(BF16)
            normed_ref[n] = normed(total, gain).astype(BF16)

    @pl.when(is_end)
    def _():
        for n in range(pieces):
            inward(n).start()

        def take(n, carry):
            outward(n).wait_recv()
            settle(n)
            return carry

        lax.fori_loop(0, pieces, take, 0)
        for n in range(pieces):
            inward(n).wait_send()

    @pl.when(jnp.logical_not(is_end))
    def _():
        def step(at, carry):
            @pl.when(at < pieces)
            def _():
                inward(at).wait_recv()
                half[at] = (part[at].astype(F32) + inbox[at].astype(F32)).astype(BF16)
                over(at).start()

            @pl.when(at >= lag)
            def _():
                n = at - lag
                over(n).wait_recv()
                full[n] = (half[n].astype(F32) + across[n].astype(F32)).astype(BF16)
                outward(n).start()
                settle(n)

            return carry

        lax.fori_loop(0, pieces + lag, step, 0)
        for n in range(pieces):
            over(n).wait_send()
            outward(n).wait_send()


def join(back, part, others, rows, gain_row, collective_id, wait=0, pieces=PIECES, lag=LAG):
    nt = lax.axis_size("tensor")
    seq_len, width = part.shape
    cut = (pieces, seq_len // pieces, width)
    outs = [jax.ShapeDtypeStruct(cut, BF16)]
    outs.append(jax.ShapeDtypeStruct((1, width) if back else cut, F32 if back else BF16))
    sems = pltpu.SemaphoreType.DMA((pieces,))
    results = pl.pallas_call(
        functools.partial(join_kernel, back, gain_row, nt, pieces, lag, wait),
        out_shape=outs,
        in_specs=[VMEM_SPEC] * (2 + len(others)),
        out_specs=[VMEM_SPEC] * 2,
        scratch_shapes=[pltpu.VMEM(cut, BF16)] * 4 + [sems] * 6,
        compiler_params=pltpu.CompilerParams(
            collective_id=collective_id, has_side_effects=True, vmem_limit_bytes=VMEM_LIMIT
        ),
        cost_estimate=pl.CostEstimate(
            flops=10 * seq_len * width, bytes_accessed=100 * seq_len * width, transcendentals=0
        ),
        name="join_back" if back else "join",
    )(part.reshape(cut), *[item.reshape(cut) for item in others], rows)
    return results[0].reshape(seq_len, width), (
        results[1] if back else results[1].reshape(seq_len, width)
    )


def normed(values, gain):
    return values * lax.rsqrt(jnp.mean(values * values, axis=-1, keepdims=True) + EPS) * gain


def line_kernel(kind, nt, chunks, lag, extra, *refs):
    refs = list(refs)
    has_sum = kind != "start"
    has_gather = kind != "end"
    part = refs.pop(0) if has_sum else None
    if kind == "start":
        x_ref, small_ref = refs.pop(0), refs.pop(0)
    elif kind == "fwd":
        extra_ref, gain_ref = refs.pop(0), refs.pop(0)
    elif kind == "last":
        extra_ref, og_ref = refs.pop(0), refs.pop(0)
    else:
        extra_ref = refs.pop(0) if extra else None
        base_ref, skip_ref, rows_ref = refs.pop(0), refs.pop(0), refs.pop(0)
        proj_ref = refs.pop(0)
    own_ref = refs.pop(0) if has_sum else None
    gg_ref = refs.pop(0) if kind in ("bwd", "end") else None
    proj_out = refs.pop(0) if kind == "end" else None
    all_ref = refs.pop(0) if has_gather else None
    land_ref = refs.pop(0) if kind == "start" else None
    if has_sum:
        from_left, from_right, tx, acc, rs_send, rl_sem, rr_sem = refs[:7]
        proj_land, proj_send, proj_recv = refs[7:10]
        refs = refs[10:]
    if has_gather:
        ag_right, ag_left, ag_recv = refs[:3]
        refs = refs[3:]

    me = lax.axis_index("tensor")
    has_l, has_r = me > 0, me < nt - 1
    left, right = jnp.maximum(me - 1, 0), jnp.minimum(me + 1, nt - 1)

    if kind == "start":
        count = lax.axis_size("dp") * nt
        me_all = lax.axis_index("dp") * nt + me

        def place(other):
            return (lax.div(other, nt), lax.rem(other, nt))

        greet_all(count, me_all, place)
        small_start, small_finish = swap_all(
            count, me_all, place, lambda other: small_ref, land_ref, *refs[:2]
        )
        small_start()
        land_ref[me_all] = small_ref[...]
    else:
        barrier = pltpu.get_barrier_semaphore()
        members, row = lax.axis_size("dp"), lax.axis_index("dp")

        @pl.when(has_l)
        def _():
            pl.semaphore_signal(barrier, inc=1, device_id={"tensor": left}, device_id_type=MESH)

        @pl.when(has_r)
        def _():
            pl.semaphore_signal(barrier, inc=1, device_id={"tensor": right}, device_id_type=MESH)

        def greet(step, carry):
            other = lax.rem(row + step, members)
            pl.semaphore_signal(barrier, inc=1, device_id={"dp": other}, device_id_type=MESH)
            return carry

        lax.fori_loop(1, members, greet, 0)
        pl.semaphore_wait(
            barrier, members - 1 + has_l.astype(jnp.int32) + has_r.astype(jnp.int32)
        )
        proj_start, proj_finish = swap_all(
            members, row, lambda other: (other, me), lambda other: proj_ref.at[other], proj_land,
            proj_send, proj_recv,
        )

    def copy(src, dst, send_sem, recv_sem, to):
        return pltpu.make_async_remote_copy(
            src_ref=src,
            dst_ref=dst,
            send_sem=send_sem,
            recv_sem=recv_sem,
            device_id={"tensor": to},
            device_id_type=MESH,
        )

    def sum_right(j, c, src):
        return copy(src, from_left.at[j, c], rs_send.at[j, c], rl_sem.at[j, c], right)

    def sum_left(j, c, src):
        return copy(src, from_right.at[j, c], rs_send.at[j, c], rr_sem.at[j, c], left)

    def spread_right(j, c):
        block = all_ref.at[j, c]
        return copy(block, block, ag_right.at[j, c], ag_recv.at[j, c], right)

    def spread_left(j, c):
        block = all_ref.at[j, c]
        return copy(block, block, ag_left.at[j, c], ag_recv.at[j, c], left)

    def offer(c):
        @pl.when(has_r)
        def _():
            spread_right(me, c).start()

        @pl.when(has_l)
        def _():
            spread_left(me, c).start()

    def pass_on(c, d):
        @pl.when(me - d >= 0)
        def _():
            j = me - d
            spread_right(j, c).wait_recv()

            @pl.when(has_r)
            def _():
                spread_right(j, c).start()

        @pl.when(me + d < nt)
        def _():
            j = me + d
            spread_left(j, c).wait_recv()

            @pl.when(has_l)
            def _():
                spread_left(j, c).start()

    hops = nt - 1

    count = hops * chunks

    def relay(step):
        k = jnp.clip(step - lag * me, 0, count - 1)
        c, j = lax.div(k, hops), hops - lax.rem(k, hops)

        @pl.when(has_l & (step >= lag * me) & (step - lag * me < count) & (me < j))
        def _():
            sum_right(j, c, tx.at[j, c]).wait_recv()
            tx[j, c] = (part[j, c].astype(F32) + from_left[j, c].astype(F32)).astype(BF16)
            sum_right(j, c, tx.at[j, c]).start()

        far = lag * (hops - me)
        k_down = jnp.clip(step - far, 0, count - 1)
        c_down, j_down = lax.div(k_down, hops), lax.rem(k_down, hops)

        @pl.when(has_r & (step >= far) & (step - far < count) & (me > j_down))
        def _():
            sum_left(j_down, c_down, tx.at[j_down, c_down]).wait_recv()
            tx[j_down, c_down] = (
                part[j_down, c_down].astype(F32) + from_right[j_down, c_down].astype(F32)
            ).astype(BF16)
            sum_left(j_down, c_down, tx.at[j_down, c_down]).start()

    def push(first, last):
        ks = range(min(first, count), min(last, count))

        @pl.when(jnp.logical_not(has_l))
        def _():
            for k in ks:
                j, c = hops - k % hops, k // hops
                sum_right(j, c, part.at[j, c]).start()

        @pl.when(jnp.logical_not(has_r))
        def _():
            for k in ks:
                j, c = k % hops, k // hops
                sum_left(j, c, part.at[j, c]).start()

    def own_rows(c):
        acc[...] = part[me, c].astype(F32)

        @pl.when(has_l)
        def _():
            sum_right(me, c, tx.at[me, c]).wait_recv()
            acc[...] += from_left[me, c].astype(F32)

        @pl.when(has_r)
        def _():
            sum_left(me, c, tx.at[me, c]).wait_recv()
            acc[...] += from_right[me, c].astype(F32)

        total = acc[...]
        if kind == "fwd":
            total = total + extra_ref[c]
            all_ref[me, c] = normed(total, gain_ref[...]).astype(BF16)
            own_ref[c] = total
        elif kind == "last":
            own_ref[c] = total + extra_ref[c]
        else:
            if extra:
                total = total + extra_ref[c]
            base = base_ref[c].astype(F32)
            scale = lax.rsqrt(jnp.mean(base * base, axis=-1, keepdims=True) + EPS)
            unit = base * scale
            grad_unit = total * rows_ref[0:1, :]
            below = scale * (grad_unit - unit * jnp.mean(grad_unit * unit, axis=-1, keepdims=True))
            result = below + skip_ref[me, c].astype(F32)
            if has_gather:
                all_ref[me, c] = result.astype(BF16)
            own_ref[c] = result
            gg = jnp.sum(total * unit, axis=0, keepdims=True)
            if c == 0:
                gg_ref[...] = gg
            else:
                gg_ref[...] += gg
        if kind in ("fwd", "bwd"):
            offer(c)

    if kind == "start":
        for c in range(chunks):
            all_ref[me, c] = x_ref[c]
            offer(c)
        for c in range(chunks):
            for d in range(1, nt):
                pass_on(c, d)
        small_finish()
    else:

        push(0, AHEAD)
        proj_start()
        proj_land[row] = proj_ref[row]
        if kind == "last":
            for c in range(chunks):
                all_ref[me, c] = og_ref[c]
            for c in range(chunks):
                offer(c)
        delay = 0 if kind == "last" else hops * lag
        spreads = {}
        for c in range(chunks if has_gather else 0):
            for d in range(1, nt):
                spreads.setdefault(delay + hops * c + lag * d, []).append((c, d))
        final = max([hops * (chunks - 1 + lag)] + list(spreads))
        for step in range(1, final + 1):
            push(step + AHEAD - 1, step + AHEAD)
            relay(step)
            for c, d in spreads.get(step, ()):
                pass_on(c, d)
            if step % hops == 0 and 0 <= step // hops - lag < chunks:
                own_rows(step // hops - lag)

    if kind == "end":
        proj_finish()
        proj_out[...] = jnp.sum(proj_land[...].astype(F32), axis=0)

    for c in range(chunks):
        for j in range(nt):
            if has_sum:

                @pl.when(me < j)
                def _():
                    sum_right(j, c, tx.at[j, c]).wait_send()

                @pl.when(me > j)
                def _():
                    sum_left(j, c, tx.at[j, c]).wait_send()

            if has_gather:

                @pl.when(has_r & (j <= me))
                def _():
                    spread_right(j, c).wait_send()

                @pl.when(has_l & (j >= me))
                def _():
                    spread_left(j, c).wait_send()


def line_exchange(kind, args, rows, width, collective_id, extra=False, chunks=2, lag=2):
    nt = lax.axis_size("tensor")
    has_sum = kind != "start"
    has_gather = kind != "end"
    piece = rows // chunks
    split = []
    for item in args:
        if item.shape[0] == nt * rows:
            split.append(item.reshape(nt, chunks, piece, width))
        elif item.shape[0] == rows:
            split.append(item.reshape(chunks, piece, width))
        else:
            split.append(item)
    outs = []
    if has_sum:
        outs.append(jax.ShapeDtypeStruct((chunks, piece, width), F32))
    if kind in ("bwd", "end"):
        outs.append(jax.ShapeDtypeStruct((1, width), F32))
        outs.append(jax.ShapeDtypeStruct(args[-1].shape[1:], F32))
    if has_gather:
        outs.append(jax.ShapeDtypeStruct((nt, chunks, piece, width), BF16))
    if kind == "start":
        count = lax.axis_size("dp") * nt
        outs.append(jax.ShapeDtypeStruct((count,) + args[1].shape, args[1].dtype))
    scratch = []
    sems = pltpu.SemaphoreType.DMA((nt, chunks))
    if has_sum:
        buf = pltpu.VMEM((nt, chunks, piece, width), BF16)
        scratch += [buf, buf, buf, pltpu.VMEM((piece, width), F32), sems, sems, sems]
        scratch.append(pltpu.VMEM(args[-1].shape, args[-1].dtype))
        scratch += [pltpu.SemaphoreType.DMA((lax.axis_size("dp"),))] * 2
    if has_gather:
        scratch += [sems, sems, sems]
    if kind == "start":
        scratch += [pltpu.SemaphoreType.DMA((count,))] * 2
    results = pl.pallas_call(
        functools.partial(line_kernel, kind, nt, chunks, lag, extra),
        out_shape=outs,
        in_specs=[VMEM_SPEC] * len(split),
        out_specs=[VMEM_SPEC] * len(outs),
        scratch_shapes=scratch,
        compiler_params=pltpu.CompilerParams(
            collective_id=collective_id, has_side_effects=True, vmem_limit_bytes=VMEM_LIMIT
        ),
        cost_estimate=pl.CostEstimate(
            flops=10 * nt * rows * width, bytes_accessed=100 * rows * width * nt, transcendentals=0
        ),
        name="line_" + kind,
    )(*split)
    results = list(results)
    if has_sum:
        results[0] = results[0].reshape(rows, width)
    if has_gather:
        at = 0 if kind == "start" else -1
        results[at] = results[at].reshape(nt * rows, width)
    return results


def span_mask(starts_ref, row_at, rows, cols, spans):
    row = row_at + lax.broadcasted_iota(jnp.int32, (rows, cols), 0)
    col = lax.broadcasted_iota(jnp.int32, (rows, cols), 1)
    seen = col <= row
    for k in range(spans):
        begin = starts_ref[0, k]
        seen = seen | (
            (row >= begin) & (row < begin + PIC) & (col >= begin) & (col < begin + PIC)
        )
    return seen


def key_extent(row_at, seq_len, spans):
    segment = seq_len // spans
    return (row_at // segment + 1) * segment


def attend_kernel(heads, spans, block, raw, starts_ref, a_ref, w_ref, *refs):
    if raw:
        gain_ref, qkv_ref, o_ref, lse_ref, out_ref, normed_ref = refs
        normed_ref[...] = normed(a_ref[...].astype(F32), gain_ref[0:1, :]).astype(BF16)
        a_ref = normed_ref
    else:
        qkv_ref, o_ref, lse_ref, out_ref = refs
    seq_len = a_ref.shape[0]
    wide = heads * HEAD
    factor = HEAD ** (-0.5)
    qkv_ref[...] = dot(a_ref[...], w_ref[:, : 3 * wide]).astype(BF16)
    for at in range(0, seq_len, block):
        reach = key_extent(at, seq_len, spans)
        seen = span_mask(starts_ref, at, block, reach, spans)
        for h in range(heads):
            q = qkv_ref[at : at + block, h * HEAD : (h + 1) * HEAD]
            k = qkv_ref[:reach, wide + h * HEAD : wide + (h + 1) * HEAD]
            v = qkv_ref[:reach, 2 * wide + h * HEAD : 2 * wide + (h + 1) * HEAD]
            s = jnp.where(seen, dot_nt(q, k) * factor, -1e30)
            top = jnp.max(s, axis=-1, keepdims=True)
            e = jnp.exp(s - top)
            total = jnp.sum(e, axis=-1, keepdims=True)
            probs = (e * (1.0 / total)).astype(BF16)
            o_ref[at : at + block, h * HEAD : (h + 1) * HEAD] = dot(probs, v).astype(BF16)
            lse_ref[at : at + block, h : h + 1] = top + jnp.log(total)
    out_ref[...] = dot_nt(o_ref[...], w_ref[:, 3 * wide :]).astype(BF16)


def attend_forward(starts, a_all, w_attn, heads, gain=None):
    seq_len, width = a_all.shape
    wide = heads * HEAD
    spans = starts.shape[1]
    raw = gain is not None
    return pl.pallas_call(
        functools.partial(attend_kernel, heads, spans, PIC, raw),
        out_shape=[
            jax.ShapeDtypeStruct((seq_len, 3 * wide), BF16),
            jax.ShapeDtypeStruct((seq_len, wide), BF16),
            jax.ShapeDtypeStruct((seq_len, heads), F32),
            jax.ShapeDtypeStruct((seq_len, width), BF16),
        ]
        + [jax.ShapeDtypeStruct((seq_len, width), BF16)] * raw,
        in_specs=[pl.BlockSpec(memory_space=pltpu.SMEM)] + [VMEM_SPEC] * (2 + raw),
        out_specs=[VMEM_SPEC] * (4 + raw),
        compiler_params=pltpu.CompilerParams(vmem_limit_bytes=VMEM_LIMIT),
        cost_estimate=pl.CostEstimate(
            flops=8 * seq_len * width * wide + 4 * heads * seq_len * seq_len * HEAD,
            bytes_accessed=6 * seq_len * width,
            transcendentals=heads * seq_len * seq_len,
        ),
        name="attend_forward",
    )(starts, a_all, w_attn, *([gain] if raw else []))


def attend_back_kernel(
    heads, spans, block, starts_ref, g_ref, w_ref, a_ref, qkv_ref, o_ref, lse_ref,
    ga_ref, gw_ref, go_scr, gq_scr, gk_acc, gv_acc,
):
    seq_len = a_ref.shape[0]
    wide = heads * HEAD
    factor = HEAD ** (-0.5)
    go_scr[...] = dot(g_ref[...], w_ref[:, 3 * wide :]).astype(BF16)
    gw_ref[:, 3 * wide :] = dot_tn(g_ref[...], o_ref[...]).astype(BF16)
    gk_acc[...] = jnp.zeros_like(gk_acc)
    gv_acc[...] = jnp.zeros_like(gv_acc)
    for at in range(0, seq_len, block):
        reach = key_extent(at, seq_len, spans)
        seen = span_mask(starts_ref, at, block, reach, spans)
        for h in range(heads):
            own = slice(h * HEAD, (h + 1) * HEAD)
            q = qkv_ref[at : at + block, own]
            k = qkv_ref[:reach, wide + h * HEAD : wide + (h + 1) * HEAD]
            v = qkv_ref[:reach, 2 * wide + h * HEAD : 2 * wide + (h + 1) * HEAD]
            go = go_scr[at : at + block, own]
            s = jnp.where(seen, dot_nt(q, k) * factor, -1e30)
            probs = jnp.exp(s - lse_ref[at : at + block, h : h + 1])
            gp = dot_nt(go, v)
            inner = jnp.sum(probs * gp, axis=-1, keepdims=True)
            gs = (probs * (gp - inner)).astype(BF16)
            gq_scr[at : at + block, own] = (dot(gs, k) * factor).astype(BF16)
            gk_acc[:reach, own] += dot_tn(gs, q) * factor
            gv_acc[:reach, own] += dot_tn(probs.astype(BF16), go)
    gq_scr[:, wide : 2 * wide] = gk_acc[...].astype(BF16)
    gq_scr[:, 2 * wide :] = gv_acc[...].astype(BF16)
    gw_ref[:, : 3 * wide] = dot_tn(a_ref[...], gq_scr[...]).astype(BF16)
    ga_ref[...] = dot_nt(gq_scr[...], w_ref[:, : 3 * wide]).astype(BF16)


def attend_backward(starts, g_all, w_attn, a_all, qkv, o, lse, heads):
    seq_len, width = a_all.shape
    wide = heads * HEAD
    spans = starts.shape[1]
    return pl.pallas_call(
        functools.partial(attend_back_kernel, heads, spans, PIC),
        out_shape=[
            jax.ShapeDtypeStruct((seq_len, width), BF16),
            jax.ShapeDtypeStruct((width, 4 * wide), BF16),
        ],
        in_specs=[pl.BlockSpec(memory_space=pltpu.SMEM)] + [VMEM_SPEC] * 6,
        out_specs=[VMEM_SPEC] * 2,
        scratch_shapes=[
            pltpu.VMEM((seq_len, wide), BF16),
            pltpu.VMEM((seq_len, 3 * wide), BF16),
            pltpu.VMEM((seq_len, wide), F32),
            pltpu.VMEM((seq_len, wide), F32),
        ],
        compiler_params=pltpu.CompilerParams(vmem_limit_bytes=VMEM_LIMIT),
        cost_estimate=pl.CostEstimate(
            flops=16 * seq_len * width * wide + 10 * heads * seq_len * seq_len * HEAD,
            bytes_accessed=12 * seq_len * width,
            transcendentals=heads * seq_len * seq_len,
        ),
        name="attend_backward",
    )(starts, g_all, w_attn, a_all, qkv, o, lse)


def lane_column(values, at):
    lane = lax.broadcasted_iota(jnp.int32, values.shape, 1)
    return jnp.sum(jnp.where(lane == at, values, 0), axis=1, keepdims=True)


def two_parts(values):
    high = values.astype(BF16)
    return high, (values - high.astype(F32)).astype(BF16)


def const_parts(product, wd, layer, at, consts):
    first = EXPERTS + 2
    zero = shift(product, first - at["cmix"] - layer * 2 * consts)
    one = shift(product, first - at["cmix"] - layer * 2 * consts - consts)
    lane = lax.broadcasted_iota(jnp.int32, product.shape, 1)
    here = (lane >= first) & (lane < first + consts)
    gap = jnp.where(here, one - zero, 0.0)
    alpha0 = 1.0 / (1.0 + jnp.exp(gap))
    alpha1 = 1.0 / (1.0 + jnp.exp(-gap))
    gate = jnp.where(here, wd, 0.0)
    keep = jnp.sum(gate * alpha0 + jnp.where(lane == EXPERTS + 1, wd, 0.0), axis=1, keepdims=True)
    return lane, here, alpha0, alpha1, gate, keep


def experts_kernel(
    cap, layer, at, consts, b_ref, w_ref, rowpos_ref, pos_ref, small_ref, rows_ref, mix_ref, zprev_ref,
    mid_ref, x_ref, gu_ref, z_ref, wd_ref, f_ref, extra_ref, pick_scr, y_scr,
):
    e = pl.program_id(0)
    seq_len, width = b_ref.shape
    half = gu_ref.shape[2] // 2

    @pl.when(e == 0)
    def _():
        product = dot(b_ref[...], small_ref[...])
        lane = lax.broadcasted_iota(jnp.int32, product.shape, 1)
        p_high, p_low = two_parts(zprev_ref[...])
        z = (
            jnp.where(lane < NEXP, shift(product, -at["router"] - layer * NEXP), 0.0)
            + dot(p_high, mix_ref[...])
            + dot(p_low, mix_ref[...])
        )
        z_ref[...] = z
        hit = pos_ref[...] >= 0
        top = jnp.max(jnp.where(hit, z, -3e38), axis=1, keepdims=True)
        ez = jnp.where(hit, jnp.exp(jnp.where(hit, z - top, 0.0)), 0.0)
        wd = ez / jnp.sum(ez, axis=1, keepdims=True)
        wd_ref[...] = wd
        _, _, _, alpha1, gate, keep = const_parts(product, wd, layer, at, consts)
        extra = mid_ref[...].astype(F32) + keep * b_ref[...].astype(F32)
        for j in range(consts):
            row = at["cvec"] + layer * consts + j
            extra = extra + lane_column(gate * alpha1, EXPERTS + 2 + j) * rows_ref[row : row + 1, :]
        extra_ref[...] = extra.astype(BF16)

    w = w_ref[...].reshape(width, 3 * half)
    take = (
        lax.broadcasted_iota(jnp.int32, (cap, seq_len), 0) == rowpos_ref[0]
    ).astype(F32).astype(BF16)
    x = dot(take, b_ref[...]).astype(BF16)
    x_ref[0] = x
    gu = dot(x, w[:, : 2 * half])
    gu_ref[0] = gu.astype(BF16)
    g, u = gu[:, :half], gu[:, half:]
    h = (g * jax.nn.sigmoid(g) * u).astype(BF16)
    y = dot_nt(h, w[:, 2 * half :])
    y_scr[pl.ds(pl.multiple_of(e * cap, cap), cap), :] = y.astype(BF16)
    column = lane_column(pos_ref[...], e)
    weight = lane_column(wd_ref[...], e)
    put = jnp.where(
        lax.broadcasted_iota(jnp.int32, (seq_len, cap), 1) == column, weight, 0.0
    ).astype(BF16)
    pick_scr[:, pl.ds(pl.multiple_of(e * cap, cap), cap)] = put

    @pl.when(e == pl.num_programs(0) - 1)
    def _():
        f_ref[...] = dot(pick_scr[...], y_scr[...]).astype(BF16)


def whole(shape):
    return pl.BlockSpec(shape, lambda e: (0,) * len(shape))


def experts_forward(
    layer, at, consts, b_all, w_exp, rowpos, pos, small, rows_t, mix, z_prev, mid, cap
):
    seq_len, width = b_all.shape
    shards_dp, count, rows, wide3 = w_exp.shape
    half = wide3 // 3
    return pl.pallas_call(
        functools.partial(experts_kernel, cap, layer, at, consts),
        grid=(count,),
        out_shape=[
            jax.ShapeDtypeStruct((count, cap, width), BF16),
            jax.ShapeDtypeStruct((count, cap, 2 * half), BF16),
            jax.ShapeDtypeStruct((seq_len, LANES), F32),
            jax.ShapeDtypeStruct((seq_len, LANES), F32),
            jax.ShapeDtypeStruct((seq_len, width), BF16),
            jax.ShapeDtypeStruct((seq_len, width), BF16),
        ],
        in_specs=[
            whole((seq_len, width)),
            pl.BlockSpec((shards_dp, 1, rows, wide3), lambda e: (0, e, 0, 0)),
            pl.BlockSpec((1, 1, seq_len), lambda e: (e, 0, 0)),
            whole((seq_len, LANES)),
            whole((width, LANES)),
            whole(rows_t.shape),
            whole((LANES, LANES)),
            whole((seq_len, LANES)),
            whole((seq_len, width)),
        ],
        out_specs=[
            pl.BlockSpec((1, cap, width), lambda e: (e, 0, 0)),
            pl.BlockSpec((1, cap, 2 * half), lambda e: (e, 0, 0)),
            whole((seq_len, LANES)),
            whole((seq_len, LANES)),
            whole((seq_len, width)),
            whole((seq_len, width)),
        ],
        scratch_shapes=[
            pltpu.VMEM((seq_len, count * cap), BF16),
            pltpu.VMEM((count * cap, width), BF16),
        ],
        compiler_params=pltpu.CompilerParams(vmem_limit_bytes=VMEM_LIMIT),
        cost_estimate=pl.CostEstimate(
            flops=count * (4 * cap * seq_len * width + 6 * cap * width * half),
            bytes_accessed=2 * count * width * wide3,
            transcendentals=0,
        ),
        name="experts_forward",
    )(b_all, w_exp, rowpos, pos, small, rows_t, mix, z_prev, mid)


def experts_back_kernel(
    cap, layer, at, consts, own, top, g_ref, w_ref, x_ref, gu_ref, rowpos_ref, pos_ref, wd_ref,
    b_ref, small_ref, rows_ref, mix_ref, zprev_ref, *refs,
):
    gprev_ref, sums_ref, mixes_ref = (None,) * 3 if top else refs[:3]
    (
        gw_ref, below_ref, gb_ref, sums_out, mixes_out, pick_scr, gx_scr, gg_scr, gb_scr, zs_scr,
        halves, inbox, out_sems, in_sems,
    ) = refs[0 if top else 3 :]
    e = pl.program_id(0)
    last = pl.num_programs(0) - 1
    me = lax.axis_index("dp")
    parity = lax.rem(me, 2)
    partner = me + 1 - 2 * parity

    def to_partner(expert):
        return pltpu.make_async_remote_copy(
            src_ref=halves.at[lax.rem(expert, 2), 1 - parity],
            dst_ref=inbox.at[expert],
            send_sem=out_sems.at[expert],
            recv_sem=in_sems.at[expert],
            device_id={"dp": partner},
            device_id_type=MESH,
        )

    @pl.when(e == 0)
    def _():
        barrier = pltpu.get_barrier_semaphore()
        pl.semaphore_signal(barrier, inc=1, device_id={"dp": partner}, device_id_type=MESH)
        pl.semaphore_wait(barrier, 1)

    @pl.when(e < last)
    def _():
        one_expert_back(
            cap, e, g_ref, w_ref, x_ref, gu_ref, rowpos_ref, pos_ref, wd_ref, pick_scr, gx_scr, gg_scr,
            halves,
        )
        to_partner(e).start()

    @pl.when(e > 0)
    def _():
        before = e - 1
        to_partner(before).wait()
        gw_ref[:, 0] = (
            halves[lax.rem(before, 2), parity].astype(F32) + inbox[before].astype(F32)
        ).astype(BF16)

    @pl.when(e == last)
    def _():
        tokens_back(
            layer, at, consts, own, g_ref, wd_ref, b_ref, small_ref, rows_ref, mix_ref, zprev_ref,
            gprev_ref, sums_ref, mixes_ref, below_ref, gb_ref, sums_out, mixes_out, pick_scr, gx_scr,
            gg_scr, gb_scr, zs_scr,
        )


def one_expert_back(
    cap, e, g_ref, w_ref, x_ref, gu_ref, rowpos_ref, pos_ref, wd_ref, pick_scr, gx_scr, gg_scr, halves,
):
    seq_len, width = g_ref.shape
    shards_dp, _, rows, wide3 = w_ref.shape
    half = wide3 // 3
    slot = lax.rem(e, 2)
    w = w_ref[...].reshape(width, wide3)
    take = (
        lax.broadcasted_iota(jnp.int32, (cap, seq_len), 0) == rowpos_ref[0]
    ).astype(F32).astype(BF16)
    w_high, w_low = two_parts(wd_ref[...])
    weight = lane_column(dot(take, w_high) + dot(take, w_low), e)
    gf = dot(take, g_ref[...])
    gh = dot(gf.astype(BF16), w[:, 2 * half :])
    gu = gu_ref[0].astype(F32)
    g, u = gu[:, :half], gu[:, half:]
    sig = jax.nn.sigmoid(g)
    h = (g * sig * u).astype(BF16)
    slot_grad = jnp.sum(h.astype(F32) * gh, axis=1, keepdims=True)
    gh = gh * weight
    gg = gh * u * sig * (1.0 + g * (1.0 - sig))
    gup = gh * g * sig
    both = jnp.concatenate([gg.astype(BF16), gup.astype(BF16)], axis=1)
    gy = (gf * weight).astype(BF16)
    gw_in = dot_tn(x_ref[0], both).astype(BF16)
    gw_down = dot_tn(gy, h).astype(BF16)
    for shard in range(shards_dp):
        own_rows = slice(shard * rows, (shard + 1) * rows)
        halves[slot, shard % 2, shard // 2, :, : 2 * half] = gw_in[own_rows]
        halves[slot, shard % 2, shard // 2, :, 2 * half :] = gw_down[own_rows]
    here = pl.ds(pl.multiple_of(e * cap, cap), cap)
    gx_scr[here, :] = dot_nt(both, w[:, : 2 * half]).astype(BF16)
    s_high, s_low = two_parts(slot_grad)
    lane = lax.broadcasted_iota(jnp.int32, (cap, LANES), 1)
    gg_scr[here, :LANES] = jnp.where(lane == e, s_high.astype(F32), 0.0).astype(BF16)
    gg_scr[here, LANES:] = jnp.where(lane == e, s_low.astype(F32), 0.0).astype(BF16)
    column = lane_column(pos_ref[...], e)
    pick_scr[:, here] = (
        lax.broadcasted_iota(jnp.int32, (seq_len, cap), 1) == column
    ).astype(F32).astype(BF16)


def tokens_back(
    layer, at, consts, own, g_ref, wd_ref, b_ref, small_ref, rows_ref, mix_ref, zprev_ref, gprev_ref,
    sums_ref, mixes_ref, below_ref, gb_ref, sums_out, mixes_out, pick_scr, gx_scr, gg_scr, gb_scr, zs_scr,
):
    mine = pl.ds(pl.multiple_of(lax.axis_index("tensor") * own, own), own)
    b_own, g_own = b_ref[mine, :], g_ref[mine, :].astype(F32)
    wd_own = wd_ref[mine, :]
    lane, here_own, alpha0, alpha1, gate, keep = const_parts(
        dot(b_own, small_ref[...]), wd_own, layer, at, consts
    )
    b_dot = jnp.sum(b_own.astype(F32) * g_own, axis=1, keepdims=True)
    c_dot = jnp.zeros_like(wd_own)
    for j in range(consts):
        row = at["cvec"] + layer * consts + j
        one = jnp.sum(g_own * rows_ref[row : row + 1, :], axis=1, keepdims=True)
        c_dot = jnp.where(lane == EXPERTS + 2 + j, one, c_dot)
    gw_own = jnp.where(here_own, alpha0 * b_dot + alpha1 * c_dot, 0.0)
    gw_own = jnp.where(lane == EXPERTS + 1, b_dot, gw_own)
    inner = gate * (alpha0 * b_dot + alpha1 * c_dot)
    gt0 = alpha0 * (gate * b_dot - inner)
    gt1 = alpha1 * (gate * c_dot - inner)

    slots = dot(pick_scr[...], gg_scr[...])
    zs_scr[...] = slots[:, :LANES] + slots[:, LANES:]
    zs_scr[mine, :] += gw_own
    gw = zs_scr[...]
    wd = wd_ref[...]
    gz = wd * (gw - jnp.sum(wd * gw, axis=1, keepdims=True))
    if gprev_ref is not None:
        gz = gz + gprev_ref[...]
    z_high, z_low = two_parts(gz)
    below_ref[...] = dot_nt(z_high, mix_ref[...]) + dot_nt(z_low, mix_ref[...])
    p_high, p_low = two_parts(zprev_ref[...])
    mixed = shift(
        dot_tn(p_high, z_high) + dot_tn(p_high, z_low) + dot_tn(p_low, z_high), layer * MIX_STEP
    )
    mixes_out[...] = mixed if mixes_ref is None else mixes_ref[...] + mixed
    zs_scr[...] = shift(gz, at["router"] + layer * NEXP)
    up = at["cmix"] + layer * 2 * consts - EXPERTS - 2
    zs_scr[mine, :] += shift(gt0, up) + shift(gt1, up + consts)
    z_high, z_low = two_parts(zs_scr[...])
    gb_scr[...] = (
        dot(pick_scr[...], gx_scr[...])
        + dot_nt(z_high, small_ref[...])
        + dot_nt(z_low, small_ref[...])
    )
    gb_scr[mine, :] += keep * g_own
    gb_ref[...] = gb_scr[...].astype(BF16)
    i_high, i_low = two_parts(
        shift(gate * alpha1, at["cvec"] + layer * consts - EXPERTS - 2)
    )
    g_low = g_ref[mine, :]
    sums_out[...] = (
        (0.0 if sums_ref is None else sums_ref[...])
        + dot_tn(b_ref[...], z_high)
        + dot_tn(b_ref[...], z_low)
        + dot_tn(g_low, i_high)
        + dot_tn(g_low, i_low)
    )


def experts_backward(
    collective_id, layer, at, consts, own, g_all, w_exp, x, gu, rowpos, pos, wd, b_all, small, rows_t, mix,
    z_prev, above, cap,
):
    seq_len, width = g_all.shape
    shards_dp, count, rows, wide3 = w_exp.shape
    half = wide3 // 3
    weight_spec = pl.BlockSpec(
        (shards_dp, 1, rows, wide3), lambda e: (0, jnp.minimum(e, count - 1), 0, 0)
    )
    half_shape = (shards_dp // 2, 1, rows, wide3)
    return pl.pallas_call(
        functools.partial(experts_back_kernel, cap, layer, at, consts, own, not above),
        grid=(count + 1,),
        out_shape=[
            jax.ShapeDtypeStruct((shards_dp // 2,) + w_exp.shape[1:], BF16),
            jax.ShapeDtypeStruct((seq_len, LANES), F32),
            jax.ShapeDtypeStruct((seq_len, width), BF16),
            jax.ShapeDtypeStruct((width, LANES), F32),
            jax.ShapeDtypeStruct((LANES, LANES), F32),
        ],
        in_specs=[
            whole((seq_len, width)),
            weight_spec,
            pl.BlockSpec((1, cap, width), lambda e: (jnp.minimum(e, count - 1), 0, 0)),
            pl.BlockSpec((1, cap, 2 * half), lambda e: (jnp.minimum(e, count - 1), 0, 0)),
            pl.BlockSpec((1, 1, seq_len), lambda e: (jnp.minimum(e, count - 1), 0, 0)),
            whole((seq_len, LANES)),
            whole((seq_len, LANES)),
            whole((seq_len, width)),
            whole((width, LANES)),
            whole(rows_t.shape),
            whole((LANES, LANES)),
            whole((seq_len, LANES)),
        ]
        + [whole(item.shape) for item in above],
        out_specs=[
            pl.BlockSpec(half_shape, lambda e: (0, jnp.maximum(e - 1, 0), 0, 0)),
            whole((seq_len, LANES)),
            whole((seq_len, width)),
            whole((width, LANES)),
            whole((LANES, LANES)),
        ],
        scratch_shapes=[
            pltpu.VMEM((seq_len, count * cap), BF16),
            pltpu.VMEM((count * cap, width), BF16),
            pltpu.VMEM((count * cap, 2 * LANES), BF16),
            pltpu.VMEM((seq_len, width), F32),
            pltpu.VMEM((seq_len, LANES), F32),
            pltpu.VMEM((2, 2, shards_dp // 2, rows, wide3), BF16),
            pltpu.VMEM((count, shards_dp // 2, rows, wide3), BF16),
            pltpu.SemaphoreType.DMA((count,)),
            pltpu.SemaphoreType.DMA((count,)),
        ],
        compiler_params=pltpu.CompilerParams(
            collective_id=collective_id, has_side_effects=True, vmem_limit_bytes=VMEM_LIMIT
        ),
        cost_estimate=pl.CostEstimate(
            flops=count * (4 * cap * seq_len * width + 12 * cap * width * half),
            bytes_accessed=4 * count * width * wide3,
            transcendentals=0,
        ),
        name="experts_backward",
    )(
        g_all, w_exp, x, gu, rowpos, pos, wd, b_all, small, rows_t, mix, z_prev,
        *above,
    )


def unpack_kernel(half, *refs):
    *in_refs, up_ref, down_ref = refs
    for l, ref in enumerate(in_refs):
        values = ref[0].astype(F32)
        for part in range(2):
            up_ref[l, 0, :, part, :] = values[:, part * half : (part + 1) * half]
        down_ref[l, 0] = values[:, 2 * half :]


def unpack(items):
    count, rows, wide3 = items[0].shape
    half = wide3 // 3
    layers = len(items)
    return pl.pallas_call(
        functools.partial(unpack_kernel, half),
        grid=(count,),
        out_shape=[
            jax.ShapeDtypeStruct((layers, count, rows, 2, half), F32),
            jax.ShapeDtypeStruct((layers, count, rows, half), F32),
        ],
        in_specs=[pl.BlockSpec((1, rows, wide3), lambda e: (e, 0, 0))] * layers,
        out_specs=[
            pl.BlockSpec((layers, 1, rows, 2, half), lambda e: (0, e, 0, 0, 0)),
            pl.BlockSpec((layers, 1, rows, half), lambda e: (0, e, 0, 0)),
        ],
        compiler_params=pltpu.CompilerParams(vmem_limit_bytes=VMEM_LIMIT),
        name="unpack",
    )(*items)


def lanes(values):
    return jnp.pad(values, ((0, 0), (0, LANES - values.shape[1])))


def slot_table(route_ids):
    tokens = route_ids.shape[0]
    codes = jnp.arange(LANES, dtype=jnp.int32)
    hit = jnp.any(route_ids[:, :, None] == codes[None, None, :], axis=1)
    place = jnp.arange(tokens, dtype=jnp.int32)
    before = (place[None, :] < place[:, None]).astype(BF16)
    slots = dot(before, hit.astype(BF16)).astype(jnp.int32)
    return jnp.where(hit, slots, -1)


def shards(
    hidden_in,
    prev_logits,
    routes,
    span_starts,
    attn_norm,
    qkv_weight,
    out_weight,
    moe_norm,
    router,
    gate_mix,
    const_vec,
    const_mix,
    up_weight,
    down_weight,
    out_grad,
):
    layers = qkv_weight.shape[0]
    own, width = hidden_in.shape
    nt = lax.axis_size("tensor")
    ndp = lax.axis_size("dp")
    seq_len = own * nt
    offset = lax.axis_index("tensor") * own
    cap = seq_len // 4
    heads = qkv_weight.shape[3] // HEAD
    wide = heads * HEAD
    half = up_weight.shape[4]
    rows = qkv_weight.shape[1]
    cols = attn_norm.shape[1]
    consts = const_vec.shape[1]

    at = layout(layers, consts)
    packed = jnp.concatenate(
        [attn_norm.T, moe_norm.T]
        + [router[l] for l in range(layers)]
        + [const_vec.reshape(-1, cols).T]
        + [const_mix[l, :, :, k].T for l in range(layers) for k in range(2)],
        axis=1,
    )
    x_all, small = line_exchange("start", [hidden_in, lanes(packed)], own, width, 0)
    small = small.reshape(width, LANES)
    rows_t = small[:, :48].T.astype(F32)

    attn_w, exp_w = [], []
    for l in range(layers):
        local = jnp.concatenate(
            [qkv_weight[l].reshape(rows, 3 * wide), out_weight[l].T], axis=1
        )
        attn_w.append(lax.all_gather(local, "dp", axis=0, tiled=False).reshape(width, 4 * wide))
        local = jnp.concatenate(
            [
                up_weight[l].reshape(EXPERTS, rows, 2 * half),
                jnp.swapaxes(down_weight[l], 1, 2),
            ],
            axis=2,
        )
        exp_w.append(lax.all_gather(local, "dp", axis=0, tiled=False))

    pos = [slot_table(routes[l]) for l in range(layers)]
    rowpos = [p[:, :EXPERTS].T[:, None, :] for p in pos]

    z_prev = lanes(prev_logits)
    hidden, a_all = x_all, None
    grad_all = out_grad
    next_id = 1
    stored = []
    for l in range(layers):
        mix = jnp.pad(gate_mix[l], ((0, LANES - NEXP), (0, LANES - NEXP)))
        if l == 0:
            qkv, o, lse, partial, a_all = attend_forward(
                span_starts, x_all, attn_w[l], heads, rows_t
            )
        else:
            qkv, o, lse, partial = attend_forward(span_starts, a_all, attn_w[l], heads)
        if l == layers - 1:
            partial, grad_all = lax.optimization_barrier((partial, grad_all))
            grad_all = lax.all_gather(grad_all, "tensor", axis=0, tiled=True)
        mid, b_all = join(False, partial, [hidden], rows_t, at["moe"] + l, next_id)
        x, gu, z, wd, partial, extra = experts_forward(
            l, at, consts, b_all, exp_w[l], rowpos[l], pos[l], small, rows_t, mix, z_prev, mid, cap
        )
        stored.append(
            dict(
                hidden=hidden, a_all=a_all, qkv=qkv, o=o, lse=lse, mid=mid, b_all=b_all, x=x, gu=gu,
                wd=wd, z_prev=z_prev, mix=mix,
            )
        )
        if l + 1 < layers:
            hidden, a_all = join(
                False, partial, [extra], rows_t, at["attn"] + l + 1, next_id + 1, APART
            )
        else:
            hidden_out = lax.psum_scatter(partial, "tensor", scatter_dimension=0, tiled=True)
            extra = lax.dynamic_slice_in_dim(extra, offset, own, 0)
        z_prev = z
        next_id += 2

    above = []
    attn_grads, exp_grads = [None] * layers, [None] * layers
    gains_a, gains_m = [None] * layers, [None] * layers
    for l in reversed(range(layers)):
        s = stored[l]
        gw_exp, below, partial, sums, mixes = experts_backward(
            next_id + 2, l, at, consts, own, grad_all, exp_w[l], s["x"], s["gu"], rowpos[l],
            pos[l], s["wd"], s["b_all"], small, rows_t, s["mix"], s["z_prev"], above, cap,
        )
        above = [below, sums, mixes]
        exp_grads[l] = sum_over_pairs(gw_exp)
        if l + 1 < layers:
            partial, exp_grads[l + 1] = lax.optimization_barrier((partial, exp_grads[l + 1]))
        else:
            partial, hidden_out = lax.optimization_barrier((partial, hidden_out))
        grad_mid, gains_m[l] = join(
            True, partial, [s["mid"], grad_all], rows_t, at["moe"] + l, next_id, APART if l > 0 else 0
        )
        partial, gw_attn = attend_backward(
            span_starts, grad_mid, attn_w[l], s["a_all"], s["qkv"], s["o"], s["lse"], heads
        )
        attn_grads[l] = gw_attn.reshape(ndp, rows, 4 * wide)
        if l > 0:
            attn_grads[l] = lax.psum_scatter(attn_grads[l], "dp", scatter_dimension=0, tiled=False)
            grad_all, gains_a[l] = join(
                True, partial, [s["hidden"], grad_mid], rows_t, at["attn"] + l, next_id + 1
            )
        else:
            partial, attn_grads[1:] = lax.optimization_barrier((partial, attn_grads[1:]))
            grad, gains_a[l], attn_grads[l] = line_exchange(
                "end", [partial, hidden_in, grad_mid, rows_t, attn_grads[l]], own, width, next_id + 1
            )
        next_id += 3
    hidden_out = hidden_out.astype(F32) + extra.astype(F32)

    gains = jnp.concatenate(gains_a + gains_m, axis=0)
    sums = sums + jnp.pad(gains, ((0, LANES - 2 * layers), (0, 0))).T
    sums = jnp.concatenate(
        [
            sums.reshape(ndp * nt, cols, LANES),
            jnp.broadcast_to(mixes[None, :MIX_STEP], (ndp * nt, MIX_STEP, LANES)),
        ],
        axis=1,
    )
    attn_g, moe_g, router_g, mix_g, cvec_g, cmix_g, qkv_g, outw_g = closing(
        sums.astype(BF16), attn_grads[0], jnp.stack(attn_grads[1:]), consts, layers, cols, next_id
    )
    up_grad, down_grad = unpack(exp_grads)
    qkv_g = jnp.swapaxes(qkv_g, 1, 2)
    router_g = jnp.transpose(router_g, (1, 2, 0))
    mix_g = jnp.swapaxes(mix_g, 0, 1)
    cmix_g = jnp.swapaxes(cmix_g, 2, 3)
    down_grad = jnp.swapaxes(down_grad, 2, 3)
    return (
        hidden_out,
        grad,
        attn_g,
        qkv_g,
        outw_g,
        moe_g,
        router_g,
        mix_g,
        cvec_g,
        cmix_g,
        up_grad,
        down_grad,
    )


def sum_over_pairs(values):
    members = lax.axis_size("dp")
    groups = [list(range(parity, members, 2)) for parity in range(2)]
    return lax.psum_scatter(
        values, "dp", scatter_dimension=0, axis_index_groups=groups, tiled=False
    )


def solution(mesh):
    return jax.shard_map(
        shards,
        mesh=mesh,
        in_specs=(
            P(("dp", "tensor"), None),
            P("dp", None),
            P(None, "dp", None),
            P("dp", None),
            P(None, ("dp", "tensor")),
            P(None, "dp", None, "tensor"),
            P(None, "tensor", "dp"),
            P(None, ("dp", "tensor")),
            P(None, ("dp", "tensor"), None),
            P(),
            P(None, None, ("dp", "tensor")),
            P(None, None, ("dp", "tensor"), None),
            P(None, None, "dp", None, "tensor"),
            P(None, None, "tensor", "dp"),
            P(("dp", "tensor"), None),
        ),
        out_specs=(
            P(("dp", "tensor"), None),
            P(("dp", "tensor"), None),
            P(None, ("dp", "tensor")),
            P(None, "dp", None, "tensor"),
            P(None, "tensor", "dp"),
            P(None, ("dp", "tensor")),
            P(None, ("dp", "tensor"), None),
            P(),
            P(None, None, ("dp", "tensor")),
            P(None, None, ("dp", "tensor"), None),
            P(None, None, "dp", None, "tensor"),
            P(None, None, "tensor", "dp"),
        ),
        check_vma=False,
    )
```

```python
import functools

import jax
import jax.numpy as jnp
from jax import lax
from jax.experimental import pallas as pl
from jax.experimental.pallas import tpu as pltpu
from jax.sharding import PartitionSpec as P

HEAD = 64
EXPERTS = 8
NEXP = 12
TOPK = 2
PIC = 256
LANES = 128

EPS = 1e-06
HIGH = lax.Precision.HIGHEST
MESH = pl.DeviceIdType.MESH
F32 = jnp.float32
BF16 = jnp.bfloat16
VMEM_SPEC = pl.BlockSpec(memory_space=pltpu.VMEM)
AHEAD = 2
PIECES = 32
LAG = 4
APART = 12000
MIX_STEP = 16
VMEM_LIMIT = 60 * 1024 * 1024


def dot(a, b):
    return jnp.dot(a, b, preferred_element_type=F32)


def dot_nt(a, b):
    return lax.dot_general(a, b, (((1,), (1,)), ((), ())), preferred_element_type=F32)


def dot_tn(a, b):
    return lax.dot_general(a, b, (((0,), (0,)), ((), ())), preferred_element_type=F32)


def layout(layers, consts):
    at, begin = {}, 0
    for name, size in (
        ("attn", layers),
        ("moe", layers),
        ("router", layers * NEXP),
        ("cvec", layers * consts),
        ("cmix", layers * consts * 2),
    ):
        at[name] = begin
        begin += size
    return at


def shift(values, lanes_up):
    return pltpu.roll(values, lanes_up % LANES, 1)


def greet_all(count, me, place):
    barrier = pltpu.get_barrier_semaphore()

    def greet(step, carry):
        other = lax.rem(me + step, count)
        pl.semaphore_signal(barrier, inc=1, device_id=place(other), device_id_type=MESH)
        return carry

    lax.fori_loop(1, count, greet, 0)
    pl.semaphore_wait(barrier, count - 1)


def swap_all(count, me, place, source, land, send_sems, recv_sems):
    def copy(other, slot):
        return pltpu.make_async_remote_copy(
            src_ref=source(other),
            dst_ref=land.at[slot],
            send_sem=send_sems.at[other],
            recv_sem=recv_sems.at[slot],
            device_id=place(other),
            device_id_type=MESH,
        )

    def start():
        def send(step, carry):
            other = lax.rem(me + step, count)
            copy(other, me).start()
            return carry

        lax.fori_loop(1, count, send, 0)

    def finish():
        def wait(step, carry):
            other = lax.rem(me + count - step, count)
            copy(other, other).wait()
            return carry

        lax.fori_loop(1, count, wait, 0)

    return start, finish


def closing_kernel(ndp, inner, layers, consts, wide, *refs):
    small_ref, first_ref, above_ref = refs[:3]
    attn_out, moe_out, router_out, mix_out, cvec_out, cmix_out, qkv_out, outw_out = refs[3:11]
    land, square, tall = refs[11:14]
    sems = refs[14:]
    count = ndp * inner
    row, col = lax.axis_index("dp"), lax.axis_index("tensor")
    me = row * inner + col
    cols = attn_out.shape[1]
    rows = qkv_out.shape[2]

    def anywhere(other):
        return (lax.div(other, inner), lax.rem(other, inner))

    greet_all(count, me, anywhere)
    start, finish = swap_all(count, me, anywhere, lambda other: small_ref.at[other], land, *sems)
    start()
    land[me] = small_ref[me]
    square[...] = jnp.zeros_like(square)
    tall[...] = jnp.zeros_like(tall)

    def place(l, total):
        for part in range(3):
            qkv_out[l, part] = total[:, part * wide : (part + 1) * wide]
        tall[:rows, :wide] = total[:, 3 * wide :]
        outw_out[l] = tall[...].T[:wide, :rows]

    for l in range(1, layers):
        place(l, above_ref[l - 1].astype(F32))
    place(0, first_ref[...])
    finish()
    total = jnp.sum(land[...].astype(F32), axis=0)
    square[:cols, :] = total[:cols]
    turned = square[...].T
    at = layout(layers, consts)
    attn_out[...] = turned[at["attn"] : at["attn"] + layers, :cols]
    moe_out[...] = turned[at["moe"] : at["moe"] + layers, :cols]
    for l in range(layers):
        begin = at["router"] + l * NEXP
        for e in range(NEXP):
            router_out[e, l : l + 1, :] = turned[begin + e : begin + e + 1, :cols]
            mix_out[e, l : l + 1, :] = total[
                cols + e : cols + e + 1, l * MIX_STEP : l * MIX_STEP + NEXP
            ]
        begin = at["cvec"] + l * consts
        cvec_out[l] = turned[begin : begin + consts, :cols]
        begin = at["cmix"] + l * 2 * consts
        for j in range(consts):
            for k in range(2):
                lane = begin + k * consts + j
                cmix_out[l, j, k : k + 1, :] = turned[lane : lane + 1, :cols]


def closing(small, projection, above, consts, layers, cols, collective_id):
    inner, ndp = lax.axis_size("tensor"), lax.axis_size("dp")
    rows, packed = projection.shape
    wide = packed // 4
    shapes = [
        (layers, cols), (layers, cols), (NEXP, layers, cols), (NEXP, layers, NEXP),
        (layers, consts, cols), (layers, consts, 2, cols),
        (layers, 3, rows, wide), (layers, wide, rows),
    ]
    return pl.pallas_call(
        functools.partial(closing_kernel, ndp, inner, layers, consts, wide),
        out_shape=[jax.ShapeDtypeStruct(shape, F32) for shape in shapes],
        in_specs=[VMEM_SPEC] * 3,
        out_specs=[VMEM_SPEC] * len(shapes),
        scratch_shapes=[
            pltpu.VMEM(small.shape, BF16),
            pltpu.VMEM((-(-cols // LANES) * LANES, LANES), F32),
            pltpu.VMEM((-(-rows // LANES) * LANES, -(-wide // LANES) * LANES), F32),
        ]
        + [pltpu.SemaphoreType.DMA((ndp * inner,))] * 2,
        compiler_params=pltpu.CompilerParams(
            collective_id=collective_id, has_side_effects=True, vmem_limit_bytes=VMEM_LIMIT
        ),
        name="closing",
    )(small, projection, above)


def join_kernel(back, gain_row, nt, pieces, lag, wait, *refs):
    if back:
        part, base_ref, skip_ref, rows_ref, result_ref, gg_ref = refs[:6]
    else:
        part, base_ref, rows_ref, total_ref, normed_ref = refs[:5]
    refs = refs[6 if back else 5 :]
    inbox, half, across, full, out_sem, in_sem, cross_out, cross_in, full_out, full_in = refs
    me = lax.axis_index("tensor")
    is_end = (me == 0) | (me == nt - 1)
    buddy = jnp.where(me < 2, 1 - me, 5 - me)
    cross = 3 - me

    if wait:
        @pl.when(lax.rem(lax.axis_index("dp"), 2) == 1)
        def _():
            pl.delay(wait)

    barrier = pltpu.get_barrier_semaphore()
    pl.semaphore_signal(barrier, inc=1, device_id={"tensor": buddy}, device_id_type=MESH)

    @pl.when(jnp.logical_not(is_end))
    def _():
        pl.semaphore_signal(barrier, inc=1, device_id={"tensor": cross}, device_id_type=MESH)

    pl.semaphore_wait(barrier, 2 - is_end.astype(jnp.int32))

    def copy(src, dst, send_sem, recv_sem, to):
        return pltpu.make_async_remote_copy(
            src_ref=src,
            dst_ref=dst,
            send_sem=send_sem,
            recv_sem=recv_sem,
            device_id={"tensor": to},
            device_id_type=MESH,
        )

    def inward(n):
        return copy(part.at[n], inbox.at[n], out_sem.at[n], in_sem.at[n], buddy)

    def over(n):
        return copy(half.at[n], across.at[n], cross_out.at[n], cross_in.at[n], cross)

    def outward(n):
        return copy(full.at[n], full.at[n], full_out.at[n], full_in.at[n], buddy)

    gain = rows_ref[gain_row : gain_row + 1, :]
    if back:
        gg_ref[...] = jnp.zeros_like(gg_ref)

    def settle(n):
        total = full[n].astype(F32)
        base = base_ref[n].astype(F32)
        if back:
            scale = lax.rsqrt(jnp.mean(base * base, axis=-1, keepdims=True) + EPS)
            unit = base * scale
            grad_unit = total * gain
            below = scale * (grad_unit - unit * jnp.mean(grad_unit * unit, axis=-1, keepdims=True))
            result_ref[n] = (below + skip_ref[n].astype(F32)).astype(BF16)

            @pl.when(lax.div(n, pieces // nt) == me)
            def _():
                gg_ref[...] += jnp.sum(total * unit, axis=0, keepdims=True)
        else:
            total = total + base
            total_ref[n] = total.astype(BF16)
            normed_ref[n] = normed(total, gain).astype(BF16)

    @pl.when(is_end)
    def _():
        for n in range(pieces):
            inward(n).start()

        def take(n, carry):
            outward(n).wait_recv()
            settle(n)
            return carry

        lax.fori_loop(0, pieces, take, 0)
        for n in range(pieces):
            inward(n).wait_send()

    @pl.when(jnp.logical_not(is_end))
    def _():
        def step(at, carry):
            @pl.when(at < pieces)
            def _():
                inward(at).wait_recv()
                half[at] = (part[at].astype(F32) + inbox[at].astype(F32)).astype(BF16)
                over(at).start()

            @pl.when(at >= lag)
            def _():
                n = at - lag
                over(n).wait_recv()
                full[n] = (half[n].astype(F32) + across[n].astype(F32)).astype(BF16)
                outward(n).start()
                settle(n)

            return carry

        lax.fori_loop(0, pieces + lag, step, 0)
        for n in range(pieces):
            over(n).wait_send()
            outward(n).wait_send()


def join(back, part, others, rows, gain_row, collective_id, wait=0, pieces=PIECES, lag=LAG):
    nt = lax.axis_size("tensor")
    seq_len, width = part.shape
    cut = (pieces, seq_len // pieces, width)
    outs = [jax.ShapeDtypeStruct(cut, BF16)]
    outs.append(jax.ShapeDtypeStruct((1, width) if back else cut, F32 if back else BF16))
    sems = pltpu.SemaphoreType.DMA((pieces,))
    results = pl.pallas_call(
        functools.partial(join_kernel, back, gain_row, nt, pieces, lag, wait),
        out_shape=outs,
        in_specs=[VMEM_SPEC] * (2 + len(others)),
        out_specs=[VMEM_SPEC] * 2,
        scratch_shapes=[pltpu.VMEM(cut, BF16)] * 4 + [sems] * 6,
        compiler_params=pltpu.CompilerParams(
            collective_id=collective_id, has_side_effects=True, vmem_limit_bytes=VMEM_LIMIT
        ),
        cost_estimate=pl.CostEstimate(
            flops=10 * seq_len * width, bytes_accessed=100 * seq_len * width, transcendentals=0
        ),
        name="join_back" if back else "join",
    )(part.reshape(cut), *[item.reshape(cut) for item in others], rows)
    return results[0].reshape(seq_len, width), (
        results[1] if back else results[1].reshape(seq_len, width)
    )


def normed(values, gain):
    return values * lax.rsqrt(jnp.mean(values * values, axis=-1, keepdims=True) + EPS) * gain


def line_kernel(kind, nt, chunks, lag, extra, *refs):
    refs = list(refs)
    has_sum = kind != "start"
    has_gather = kind != "end"
    part = refs.pop(0) if has_sum else None
    if kind == "start":
        x_ref, small_ref = refs.pop(0), refs.pop(0)
    elif kind == "fwd":
        extra_ref, gain_ref = refs.pop(0), refs.pop(0)
    elif kind == "last":
        extra_ref, og_ref = refs.pop(0), refs.pop(0)
    else:
        extra_ref = refs.pop(0) if extra else None
        base_ref, skip_ref, rows_ref = refs.pop(0), refs.pop(0), refs.pop(0)
        proj_ref = refs.pop(0)
    own_ref = refs.pop(0) if has_sum else None
    gg_ref = refs.pop(0) if kind in ("bwd", "end") else None
    proj_out = refs.pop(0) if kind == "end" else None
    all_ref = refs.pop(0) if has_gather else None
    land_ref = refs.pop(0) if kind == "start" else None
    if has_sum:
        from_left, from_right, tx, acc, rs_send, rl_sem, rr_sem = refs[:7]
        proj_land, proj_send, proj_recv = refs[7:10]
        refs = refs[10:]
    if has_gather:
        ag_right, ag_left, ag_recv = refs[:3]
        refs = refs[3:]

    me = lax.axis_index("tensor")
    has_l, has_r = me > 0, me < nt - 1
    left, right = jnp.maximum(me - 1, 0), jnp.minimum(me + 1, nt - 1)

    if kind == "start":
        count = lax.axis_size("dp") * nt
        me_all = lax.axis_index("dp") * nt + me

        def place(other):
            return (lax.div(other, nt), lax.rem(other, nt))

        greet_all(count, me_all, place)
        small_start, small_finish = swap_all(
            count, me_all, place, lambda other: small_ref, land_ref, *refs[:2]
        )
        small_start()
        land_ref[me_all] = small_ref[...]
    else:
        barrier = pltpu.get_barrier_semaphore()
        members, row = lax.axis_size("dp"), lax.axis_index("dp")

        @pl.when(has_l)
        def _():
            pl.semaphore_signal(barrier, inc=1, device_id={"tensor": left}, device_id_type=MESH)

        @pl.when(has_r)
        def _():
            pl.semaphore_signal(barrier, inc=1, device_id={"tensor": right}, device_id_type=MESH)

        def greet(step, carry):
            other = lax.rem(row + step, members)
            pl.semaphore_signal(barrier, inc=1, device_id={"dp": other}, device_id_type=MESH)
            return carry

        lax.fori_loop(1, members, greet, 0)
        pl.semaphore_wait(
            barrier, members - 1 + has_l.astype(jnp.int32) + has_r.astype(jnp.int32)
        )
        proj_start, proj_finish = swap_all(
            members, row, lambda other: (other, me), lambda other: proj_ref.at[other], proj_land,
            proj_send, proj_recv,
        )

    def copy(src, dst, send_sem, recv_sem, to):
        return pltpu.make_async_remote_copy(
            src_ref=src,
            dst_ref=dst,
            send_sem=send_sem,
            recv_sem=recv_sem,
            device_id={"tensor": to},
            device_id_type=MESH,
        )

    def sum_right(j, c, src):
        return copy(src, from_left.at[j, c], rs_send.at[j, c], rl_sem.at[j, c], right)

    def sum_left(j, c, src):
        return copy(src, from_right.at[j, c], rs_send.at[j, c], rr_sem.at[j, c], left)

    def spread_right(j, c):
        block = all_ref.at[j, c]
        return copy(block, block, ag_right.at[j, c], ag_recv.at[j, c], right)

    def spread_left(j, c):
        block = all_ref.at[j, c]
        return copy(block, block, ag_left.at[j, c], ag_recv.at[j, c], left)

    def offer(c):
        @pl.when(has_r)
        def _():
            spread_right(me, c).start()

        @pl.when(has_l)
        def _():
            spread_left(me, c).start()

    def pass_on(c, d):
        @pl.when(me - d >= 0)
        def _():
            j = me - d
            spread_right(j, c).wait_recv()

            @pl.when(has_r)
            def _():
                spread_right(j, c).start()

        @pl.when(me + d < nt)
        def _():
            j = me + d
            spread_left(j, c).wait_recv()

            @pl.when(has_l)
            def _():
                spread_left(j, c).start()

    hops = nt - 1

    count = hops * chunks

    def relay(step):
        k = jnp.clip(step - lag * me, 0, count - 1)
        c, j = lax.div(k, hops), hops - lax.rem(k, hops)

        @pl.when(has_l & (step >= lag * me) & (step - lag * me < count) & (me < j))
        def _():
            sum_right(j, c, tx.at[j, c]).wait_recv()
            tx[j, c] = (part[j, c].astype(F32) + from_left[j, c].astype(F32)).astype(BF16)
            sum_right(j, c, tx.at[j, c]).start()

        far = lag * (hops - me)
        k_down = jnp.clip(step - far, 0, count - 1)
        c_down, j_down = lax.div(k_down, hops), lax.rem(k_down, hops)

        @pl.when(has_r & (step >= far) & (step - far < count) & (me > j_down))
        def _():
            sum_left(j_down, c_down, tx.at[j_down, c_down]).wait_recv()
            tx[j_down, c_down] = (
                part[j_down, c_down].astype(F32) + from_right[j_down, c_down].astype(F32)
            ).astype(BF16)
            sum_left(j_down, c_down, tx.at[j_down, c_down]).start()

    def push(first, last):
        ks = range(min(first, count), min(last, count))

        @pl.when(jnp.logical_not(has_l))
        def _():
            for k in ks:
                j, c = hops - k % hops, k // hops
                sum_right(j, c, part.at[j, c]).start()

        @pl.when(jnp.logical_not(has_r))
        def _():
            for k in ks:
                j, c = k % hops, k // hops
                sum_left(j, c, part.at[j, c]).start()

    def own_rows(c):
        acc[...] = part[me, c].astype(F32)

        @pl.when(has_l)
        def _():
            sum_right(me, c, tx.at[me, c]).wait_recv()
            acc[...] += from_left[me, c].astype(F32)

        @pl.when(has_r)
        def _():
            sum_left(me, c, tx.at[me, c]).wait_recv()
            acc[...] += from_right[me, c].astype(F32)

        total = acc[...]
        if kind == "fwd":
            total = total + extra_ref[c]
            all_ref[me, c] = normed(total, gain_ref[...]).astype(BF16)
            own_ref[c] = total
        elif kind == "last":
            own_ref[c] = total + extra_ref[c]
        else:
            if extra:
                total = total + extra_ref[c]
            base = base_ref[c].astype(F32)
            scale = lax.rsqrt(jnp.mean(base * base, axis=-1, keepdims=True) + EPS)
            unit = base * scale
            grad_unit = total * rows_ref[0:1, :]
            below = scale * (grad_unit - unit * jnp.mean(grad_unit * unit, axis=-1, keepdims=True))
            result = below + skip_ref[me, c].astype(F32)
            if has_gather:
                all_ref[me, c] = result.astype(BF16)
            own_ref[c] = result
            gg = jnp.sum(total * unit, axis=0, keepdims=True)
            if c == 0:
                gg_ref[...] = gg
            else:
                gg_ref[...] += gg
        if kind in ("fwd", "bwd"):
            offer(c)

    if kind == "start":
        for c in range(chunks):
            all_ref[me, c] = x_ref[c]
            offer(c)
        for c in range(chunks):
            for d in range(1, nt):
                pass_on(c, d)
        small_finish()
    else:

        push(0, AHEAD)
        proj_start()
        proj_land[row] = proj_ref[row]
        if kind == "last":
            for c in range(chunks):
                all_ref[me, c] = og_ref[c]
            for c in range(chunks):
                offer(c)
        delay = 0 if kind == "last" else hops * lag
        spreads = {}
        for c in range(chunks if has_gather else 0):
            for d in range(1, nt):
                spreads.setdefault(delay + hops * c + lag * d, []).append((c, d))
        final = max([hops * (chunks - 1 + lag)] + list(spreads))
        for step in range(1, final + 1):
            push(step + AHEAD - 1, step + AHEAD)
            relay(step)
            for c, d in spreads.get(step, ()):
                pass_on(c, d)
            if step % hops == 0 and 0 <= step // hops - lag < chunks:
                own_rows(step // hops - lag)

    if kind == "end":
        proj_finish()
        proj_out[...] = jnp.sum(proj_land[...].astype(F32), axis=0)

    for c in range(chunks):
        for j in range(nt):
            if has_sum:

                @pl.when(me < j)
                def _():
                    sum_right(j, c, tx.at[j, c]).wait_send()

                @pl.when(me > j)
                def _():
                    sum_left(j, c, tx.at[j, c]).wait_send()

            if has_gather:

                @pl.when(has_r & (j <= me))
                def _():
                    spread_right(j, c).wait_send()

                @pl.when(has_l & (j >= me))
                def _():
                    spread_left(j, c).wait_send()


def line_exchange(kind, args, rows, width, collective_id, extra=False, chunks=2, lag=2):
    nt = lax.axis_size("tensor")
    has_sum = kind != "start"
    has_gather = kind != "end"
    piece = rows // chunks
    split = []
    for item in args:
        if item.shape[0] == nt * rows:
            split.append(item.reshape(nt, chunks, piece, width))
        elif item.shape[0] == rows:
            split.append(item.reshape(chunks, piece, width))
        else:
            split.append(item)
    outs = []
    if has_sum:
        outs.append(jax.ShapeDtypeStruct((chunks, piece, width), F32))
    if kind in ("bwd", "end"):
        outs.append(jax.ShapeDtypeStruct((1, width), F32))
        outs.append(jax.ShapeDtypeStruct(args[-1].shape[1:], F32))
    if has_gather:
        outs.append(jax.ShapeDtypeStruct((nt, chunks, piece, width), BF16))
    if kind == "start":
        count = lax.axis_size("dp") * nt
        outs.append(jax.ShapeDtypeStruct((count,) + args[1].shape, args[1].dtype))
    scratch = []
    sems = pltpu.SemaphoreType.DMA((nt, chunks))
    if has_sum:
        buf = pltpu.VMEM((nt, chunks, piece, width), BF16)
        scratch += [buf, buf, buf, pltpu.VMEM((piece, width), F32), sems, sems, sems]
        scratch.append(pltpu.VMEM(args[-1].shape, args[-1].dtype))
        scratch += [pltpu.SemaphoreType.DMA((lax.axis_size("dp"),))] * 2
    if has_gather:
        scratch += [sems, sems, sems]
    if kind == "start":
        scratch += [pltpu.SemaphoreType.DMA((count,))] * 2
    results = pl.pallas_call(
        functools.partial(line_kernel, kind, nt, chunks, lag, extra),
        out_shape=outs,
        in_specs=[VMEM_SPEC] * len(split),
        out_specs=[VMEM_SPEC] * len(outs),
        scratch_shapes=scratch,
        compiler_params=pltpu.CompilerParams(
            collective_id=collective_id, has_side_effects=True, vmem_limit_bytes=VMEM_LIMIT
        ),
        cost_estimate=pl.CostEstimate(
            flops=10 * nt * rows * width, bytes_accessed=100 * rows * width * nt, transcendentals=0
        ),
        name="line_" + kind,
    )(*split)
    results = list(results)
    if has_sum:
        results[0] = results[0].reshape(rows, width)
    if has_gather:
        at = 0 if kind == "start" else -1
        results[at] = results[at].reshape(nt * rows, width)
    return results


def span_mask(starts_ref, row_at, rows, cols, spans):
    row = row_at + lax.broadcasted_iota(jnp.int32, (rows, cols), 0)
    col = lax.broadcasted_iota(jnp.int32, (rows, cols), 1)
    seen = col <= row
    for k in range(spans):
        begin = starts_ref[0, k]
        seen = seen | (
            (row >= begin) & (row < begin + PIC) & (col >= begin) & (col < begin + PIC)
        )
    return seen


def key_extent(row_at, seq_len, spans):
    segment = seq_len // spans
    return (row_at // segment + 1) * segment


def attend_kernel(heads, spans, block, raw, starts_ref, a_ref, w_ref, *refs):
    if raw:
        gain_ref, qkv_ref, o_ref, lse_ref, out_ref, normed_ref = refs
        normed_ref[...] = normed(a_ref[...].astype(F32), gain_ref[0:1, :]).astype(BF16)
        a_ref = normed_ref
    else:
        qkv_ref, o_ref, lse_ref, out_ref = refs
    seq_len = a_ref.shape[0]
    wide = heads * HEAD
    factor = HEAD ** (-0.5)
    qkv_ref[...] = dot(a_ref[...], w_ref[:, : 3 * wide]).astype(BF16)
    for at in range(0, seq_len, block):
        reach = key_extent(at, seq_len, spans)
        seen = span_mask(starts_ref, at, block, reach, spans)
        for h in range(heads):
            q = qkv_ref[at : at + block, h * HEAD : (h + 1) * HEAD]
            k = qkv_ref[:reach, wide + h * HEAD : wide + (h + 1) * HEAD]
            v = qkv_ref[:reach, 2 * wide + h * HEAD : 2 * wide + (h + 1) * HEAD]
            s = jnp.where(seen, dot_nt(q, k) * factor, -1e30)
            top = jnp.max(s, axis=-1, keepdims=True)
            e = jnp.exp(s - top)
            total = jnp.sum(e, axis=-1, keepdims=True)
            probs = (e * (1.0 / total)).astype(BF16)
            o_ref[at : at + block, h * HEAD : (h + 1) * HEAD] = dot(probs, v).astype(BF16)
            lse_ref[at : at + block, h : h + 1] = top + jnp.log(total)
    out_ref[...] = dot_nt(o_ref[...], w_ref[:, 3 * wide :]).astype(BF16)


def attend_forward(starts, a_all, w_attn, heads, gain=None):
    seq_len, width = a_all.shape
    wide = heads * HEAD
    spans = starts.shape[1]
    raw = gain is not None
    return pl.pallas_call(
        functools.partial(attend_kernel, heads, spans, PIC, raw),
        out_shape=[
            jax.ShapeDtypeStruct((seq_len, 3 * wide), BF16),
            jax.ShapeDtypeStruct((seq_len, wide), BF16),
            jax.ShapeDtypeStruct((seq_len, heads), F32),
            jax.ShapeDtypeStruct((seq_len, width), BF16),
        ]
        + [jax.ShapeDtypeStruct((seq_len, width), BF16)] * raw,
        in_specs=[pl.BlockSpec(memory_space=pltpu.SMEM)] + [VMEM_SPEC] * (2 + raw),
        out_specs=[VMEM_SPEC] * (4 + raw),
        compiler_params=pltpu.CompilerParams(vmem_limit_bytes=VMEM_LIMIT),
        cost_estimate=pl.CostEstimate(
            flops=8 * seq_len * width * wide + 4 * heads * seq_len * seq_len * HEAD,
            bytes_accessed=6 * seq_len * width,
            transcendentals=heads * seq_len * seq_len,
        ),
        name="attend_forward",
    )(starts, a_all, w_attn, *([gain] if raw else []))


def attend_back_kernel(
    heads, spans, block, starts_ref, g_ref, w_ref, a_ref, qkv_ref, o_ref, lse_ref,
    ga_ref, gw_ref, go_scr, gq_scr, gk_acc, gv_acc,
):
    seq_len = a_ref.shape[0]
    wide = heads * HEAD
    factor = HEAD ** (-0.5)
    go_scr[...] = dot(g_ref[...], w_ref[:, 3 * wide :]).astype(BF16)
    gw_ref[:, 3 * wide :] = dot_tn(g_ref[...], o_ref[...]).astype(BF16)
    gk_acc[...] = jnp.zeros_like(gk_acc)
    gv_acc[...] = jnp.zeros_like(gv_acc)
    for at in range(0, seq_len, block):
        reach = key_extent(at, seq_len, spans)
        seen = span_mask(starts_ref, at, block, reach, spans)
        for h in range(heads):
            own = slice(h * HEAD, (h + 1) * HEAD)
            q = qkv_ref[at : at + block, own]
            k = qkv_ref[:reach, wide + h * HEAD : wide + (h + 1) * HEAD]
            v = qkv_ref[:reach, 2 * wide + h * HEAD : 2 * wide + (h + 1) * HEAD]
            go = go_scr[at : at + block, own]
            s = jnp.where(seen, dot_nt(q, k) * factor, -1e30)
            probs = jnp.exp(s - lse_ref[at : at + block, h : h + 1])
            gp = dot_nt(go, v)
            inner = jnp.sum(probs * gp, axis=-1, keepdims=True)
            gs = (probs * (gp - inner)).astype(BF16)
            gq_scr[at : at + block, own] = (dot(gs, k) * factor).astype(BF16)
            gk_acc[:reach, own] += dot_tn(gs, q) * factor
            gv_acc[:reach, own] += dot_tn(probs.astype(BF16), go)
    gq_scr[:, wide : 2 * wide] = gk_acc[...].astype(BF16)
    gq_scr[:, 2 * wide :] = gv_acc[...].astype(BF16)
    gw_ref[:, : 3 * wide] = dot_tn(a_ref[...], gq_scr[...]).astype(BF16)
    ga_ref[...] = dot_nt(gq_scr[...], w_ref[:, : 3 * wide]).astype(BF16)


def attend_backward(starts, g_all, w_attn, a_all, qkv, o, lse, heads):
    seq_len, width = a_all.shape
    wide = heads * HEAD
    spans = starts.shape[1]
    return pl.pallas_call(
        functools.partial(attend_back_kernel, heads, spans, PIC),
        out_shape=[
            jax.ShapeDtypeStruct((seq_len, width), BF16),
            jax.ShapeDtypeStruct((width, 4 * wide), BF16),
        ],
        in_specs=[pl.BlockSpec(memory_space=pltpu.SMEM)] + [VMEM_SPEC] * 6,
        out_specs=[VMEM_SPEC] * 2,
        scratch_shapes=[
            pltpu.VMEM((seq_len, wide), BF16),
            pltpu.VMEM((seq_len, 3 * wide), BF16),
            pltpu.VMEM((seq_len, wide), F32),
            pltpu.VMEM((seq_len, wide), F32),
        ],
        compiler_params=pltpu.CompilerParams(vmem_limit_bytes=VMEM_LIMIT),
        cost_estimate=pl.CostEstimate(
            flops=16 * seq_len * width * wide + 10 * heads * seq_len * seq_len * HEAD,
            bytes_accessed=12 * seq_len * width,
            transcendentals=heads * seq_len * seq_len,
        ),
        name="attend_backward",
    )(starts, g_all, w_attn, a_all, qkv, o, lse)


def lane_column(values, at):
    lane = lax.broadcasted_iota(jnp.int32, values.shape, 1)
    return jnp.sum(jnp.where(lane == at, values, 0), axis=1, keepdims=True)


def two_parts(values):
    high = values.astype(BF16)
    return high, (values - high.astype(F32)).astype(BF16)


def const_parts(product, wd, layer, at, consts):
    first = EXPERTS + 2
    zero = shift(product, first - at["cmix"] - layer * 2 * consts)
    one = shift(product, first - at["cmix"] - layer * 2 * consts - consts)
    lane = lax.broadcasted_iota(jnp.int32, product.shape, 1)
    here = (lane >= first) & (lane < first + consts)
    gap = jnp.where(here, one - zero, 0.0)
    alpha0 = 1.0 / (1.0 + jnp.exp(gap))
    alpha1 = 1.0 / (1.0 + jnp.exp(-gap))
    gate = jnp.where(here, wd, 0.0)
    keep = jnp.sum(gate * alpha0 + jnp.where(lane == EXPERTS + 1, wd, 0.0), axis=1, keepdims=True)
    return lane, here, alpha0, alpha1, gate, keep


def experts_kernel(
    cap, layer, at, consts, b_ref, w_ref, rowpos_ref, pos_ref, small_ref, rows_ref, mix_ref, zprev_ref,
    mid_ref, x_ref, gu_ref, z_ref, wd_ref, f_ref, extra_ref, pick_scr, y_scr,
):
    e = pl.program_id(0)
    seq_len, width = b_ref.shape
    half = gu_ref.shape[2] // 2

    @pl.when(e == 0)
    def _():
        product = dot(b_ref[...], small_ref[...])
        lane = lax.broadcasted_iota(jnp.int32, product.shape, 1)
        p_high, p_low = two_parts(zprev_ref[...])
        z = (
            jnp.where(lane < NEXP, shift(product, -at["router"] - layer * NEXP), 0.0)
            + dot(p_high, mix_ref[...])
            + dot(p_low, mix_ref[...])
        )
        z_ref[...] = z
        hit = pos_ref[...] >= 0
        top = jnp.max(jnp.where(hit, z, -3e38), axis=1, keepdims=True)
        ez = jnp.where(hit, jnp.exp(jnp.where(hit, z - top, 0.0)), 0.0)
        wd = ez / jnp.sum(ez, axis=1, keepdims=True)
        wd_ref[...] = wd
        _, _, _, alpha1, gate, keep = const_parts(product, wd, layer, at, consts)
        extra = mid_ref[...].astype(F32) + keep * b_ref[...].astype(F32)
        for j in range(consts):
            row = at["cvec"] + layer * consts + j
            extra = extra + lane_column(gate * alpha1, EXPERTS + 2 + j) * rows_ref[row : row + 1, :]
        extra_ref[...] = extra.astype(BF16)

    w = w_ref[...].reshape(width, 3 * half)
    take = (
        lax.broadcasted_iota(jnp.int32, (cap, seq_len), 0) == rowpos_ref[0]
    ).astype(F32).astype(BF16)
    x = dot(take, b_ref[...]).astype(BF16)
    x_ref[0] = x
    gu = dot(x, w[:, : 2 * half])
    gu_ref[0] = gu.astype(BF16)
    g, u = gu[:, :half], gu[:, half:]
    h = (g * jax.nn.sigmoid(g) * u).astype(BF16)
    y = dot_nt(h, w[:, 2 * half :])
    y_scr[pl.ds(pl.multiple_of(e * cap, cap), cap), :] = y.astype(BF16)
    column = lane_column(pos_ref[...], e)
    weight = lane_column(wd_ref[...], e)
    put = jnp.where(
        lax.broadcasted_iota(jnp.int32, (seq_len, cap), 1) == column, weight, 0.0
    ).astype(BF16)
    pick_scr[:, pl.ds(pl.multiple_of(e * cap, cap), cap)] = put

    @pl.when(e == pl.num_programs(0) - 1)
    def _():
        f_ref[...] = dot(pick_scr[...], y_scr[...]).astype(BF16)


def whole(shape):
    return pl.BlockSpec(shape, lambda e: (0,) * len(shape))


def experts_forward(
    layer, at, consts, b_all, w_exp, rowpos, pos, small, rows_t, mix, z_prev, mid, cap
):
    seq_len, width = b_all.shape
    shards_dp, count, rows, wide3 = w_exp.shape
    half = wide3 // 3
    return pl.pallas_call(
        functools.partial(experts_kernel, cap, layer, at, consts),
        grid=(count,),
        out_shape=[
            jax.ShapeDtypeStruct((count, cap, width), BF16),
            jax.ShapeDtypeStruct((count, cap, 2 * half), BF16),
            jax.ShapeDtypeStruct((seq_len, LANES), F32),
            jax.ShapeDtypeStruct((seq_len, LANES), F32),
            jax.ShapeDtypeStruct((seq_len, width), BF16),
            jax.ShapeDtypeStruct((seq_len, width), BF16),
        ],
        in_specs=[
            whole((seq_len, width)),
            pl.BlockSpec((shards_dp, 1, rows, wide3), lambda e: (0, e, 0, 0)),
            pl.BlockSpec((1, 1, seq_len), lambda e: (e, 0, 0)),
            whole((seq_len, LANES)),
            whole((width, LANES)),
            whole(rows_t.shape),
            whole((LANES, LANES)),
            whole((seq_len, LANES)),
            whole((seq_len, width)),
        ],
        out_specs=[
            pl.BlockSpec((1, cap, width), lambda e: (e, 0, 0)),
            pl.BlockSpec((1, cap, 2 * half), lambda e: (e, 0, 0)),
            whole((seq_len, LANES)),
            whole((seq_len, LANES)),
            whole((seq_len, width)),
            whole((seq_len, width)),
        ],
        scratch_shapes=[
            pltpu.VMEM((seq_len, count * cap), BF16),
            pltpu.VMEM((count * cap, width), BF16),
        ],
        compiler_params=pltpu.CompilerParams(vmem_limit_bytes=VMEM_LIMIT),
        cost_estimate=pl.CostEstimate(
            flops=count * (4 * cap * seq_len * width + 6 * cap * width * half),
            bytes_accessed=2 * count * width * wide3,
            transcendentals=0,
        ),
        name="experts_forward",
    )(b_all, w_exp, rowpos, pos, small, rows_t, mix, z_prev, mid)


def experts_back_kernel(
    cap, layer, at, consts, own, top, g_ref, w_ref, x_ref, gu_ref, rowpos_ref, pos_ref, wd_ref,
    b_ref, small_ref, rows_ref, mix_ref, zprev_ref, *refs,
):
    gprev_ref, sums_ref, mixes_ref = (None,) * 3 if top else refs[:3]
    (
        gw_ref, below_ref, gb_ref, sums_out, mixes_out, pick_scr, gx_scr, gg_scr, gb_scr, zs_scr,
        halves, inbox, out_sems, in_sems,
    ) = refs[0 if top else 3 :]
    e = pl.program_id(0)
    last = pl.num_programs(0) - 1
    me = lax.axis_index("dp")
    parity = lax.rem(me, 2)
    partner = me + 1 - 2 * parity

    def to_partner(expert):
        return pltpu.make_async_remote_copy(
            src_ref=halves.at[lax.rem(expert, 2), 1 - parity],
            dst_ref=inbox.at[expert],
            send_sem=out_sems.at[expert],
            recv_sem=in_sems.at[expert],
            device_id={"dp": partner},
            device_id_type=MESH,
        )

    @pl.when(e == 0)
    def _():
        barrier = pltpu.get_barrier_semaphore()
        pl.semaphore_signal(barrier, inc=1, device_id={"dp": partner}, device_id_type=MESH)
        pl.semaphore_wait(barrier, 1)

    @pl.when(e < last)
    def _():
        one_expert_back(
            cap, e, g_ref, w_ref, x_ref, gu_ref, rowpos_ref, pos_ref, wd_ref, pick_scr, gx_scr, gg_scr,
            halves,
        )
        to_partner(e).start()

    @pl.when(e > 0)
    def _():
        before = e - 1
        to_partner(before).wait()
        gw_ref[:, 0] = (
            halves[lax.rem(before, 2), parity].astype(F32) + inbox[before].astype(F32)
        ).astype(BF16)

    @pl.when(e == last)
    def _():
        tokens_back(
            layer, at, consts, own, g_ref, wd_ref, b_ref, small_ref, rows_ref, mix_ref, zprev_ref,
            gprev_ref, sums_ref, mixes_ref, below_ref, gb_ref, sums_out, mixes_out, pick_scr, gx_scr,
            gg_scr, gb_scr, zs_scr,
        )


def one_expert_back(
    cap, e, g_ref, w_ref, x_ref, gu_ref, rowpos_ref, pos_ref, wd_ref, pick_scr, gx_scr, gg_scr, halves,
):
    seq_len, width = g_ref.shape
    shards_dp, _, rows, wide3 = w_ref.shape
    half = wide3 // 3
    slot = lax.rem(e, 2)
    w = w_ref[...].reshape(width, wide3)
    take = (
        lax.broadcasted_iota(jnp.int32, (cap, seq_len), 0) == rowpos_ref[0]
    ).astype(F32).astype(BF16)
    w_high, w_low = two_parts(wd_ref[...])
    weight = lane_column(dot(take, w_high) + dot(take, w_low), e)
    gf = dot(take, g_ref[...])
    gh = dot(gf.astype(BF16), w[:, 2 * half :])
    gu = gu_ref[0].astype(F32)
    g, u = gu[:, :half], gu[:, half:]
    sig = jax.nn.sigmoid(g)
    h = (g * sig * u).astype(BF16)
    slot_grad = jnp.sum(h.astype(F32) * gh, axis=1, keepdims=True)
    gh = gh * weight
    gg = gh * u * sig * (1.0 + g * (1.0 - sig))
    gup = gh * g * sig
    both = jnp.concatenate([gg.astype(BF16), gup.astype(BF16)], axis=1)
    gy = (gf * weight).astype(BF16)
    gw_in = dot_tn(x_ref[0], both).astype(BF16)
    gw_down = dot_tn(gy, h).astype(BF16)
    for shard in range(shards_dp):
        own_rows = slice(shard * rows, (shard + 1) * rows)
        halves[slot, shard % 2, shard // 2, :, : 2 * half] = gw_in[own_rows]
        halves[slot, shard % 2, shard // 2, :, 2 * half :] = gw_down[own_rows]
    here = pl.ds(pl.multiple_of(e * cap, cap), cap)
    gx_scr[here, :] = dot_nt(both, w[:, : 2 * half]).astype(BF16)
    s_high, s_low = two_parts(slot_grad)
    lane = lax.broadcasted_iota(jnp.int32, (cap, LANES), 1)
    gg_scr[here, :LANES] = jnp.where(lane == e, s_high.astype(F32), 0.0).astype(BF16)
    gg_scr[here, LANES:] = jnp.where(lane == e, s_low.astype(F32), 0.0).astype(BF16)
    column = lane_column(pos_ref[...], e)
    pick_scr[:, here] = (
        lax.broadcasted_iota(jnp.int32, (seq_len, cap), 1) == column
    ).astype(F32).astype(BF16)


def tokens_back(
    layer, at, consts, own, g_ref, wd_ref, b_ref, small_ref, rows_ref, mix_ref, zprev_ref, gprev_ref,
    sums_ref, mixes_ref, below_ref, gb_ref, sums_out, mixes_out, pick_scr, gx_scr, gg_scr, gb_scr, zs_scr,
):
    mine = pl.ds(pl.multiple_of(lax.axis_index("tensor") * own, own), own)
    b_own, g_own = b_ref[mine, :], g_ref[mine, :].astype(F32)
    wd_own = wd_ref[mine, :]
    lane, here_own, alpha0, alpha1, gate, keep = const_parts(
        dot(b_own, small_ref[...]), wd_own, layer, at, consts
    )
    b_dot = jnp.sum(b_own.astype(F32) * g_own, axis=1, keepdims=True)
    c_dot = jnp.zeros_like(wd_own)
    for j in range(consts):
        row = at["cvec"] + layer * consts + j
        one = jnp.sum(g_own * rows_ref[row : row + 1, :], axis=1, keepdims=True)
        c_dot = jnp.where(lane == EXPERTS + 2 + j, one, c_dot)
    gw_own = jnp.where(here_own, alpha0 * b_dot + alpha1 * c_dot, 0.0)
    gw_own = jnp.where(lane == EXPERTS + 1, b_dot, gw_own)
    inner = gate * (alpha0 * b_dot + alpha1 * c_dot)
    gt0 = alpha0 * (gate * b_dot - inner)
    gt1 = alpha1 * (gate * c_dot - inner)

    slots = dot(pick_scr[...], gg_scr[...])
    zs_scr[...] = slots[:, :LANES] + slots[:, LANES:]
    zs_scr[mine, :] += gw_own
    gw = zs_scr[...]
    wd = wd_ref[...]
    gz = wd * (gw - jnp.sum(wd * gw, axis=1, keepdims=True))
    if gprev_ref is not None:
        gz = gz + gprev_ref[...]
    z_high, z_low = two_parts(gz)
    below_ref[...] = dot_nt(z_high, mix_ref[...]) + dot_nt(z_low, mix_ref[...])
    p_high, p_low = two_parts(zprev_ref[...])
    mixed = shift(
        dot_tn(p_high, z_high) + dot_tn(p_high, z_low) + dot_tn(p_low, z_high), layer * MIX_STEP
    )
    mixes_out[...] = mixed if mixes_ref is None else mixes_ref[...] + mixed
    zs_scr[...] = shift(gz, at["router"] + layer * NEXP)
    up = at["cmix"] + layer * 2 * consts - EXPERTS - 2
    zs_scr[mine, :] += shift(gt0, up) + shift(gt1, up + consts)
    z_high, z_low = two_parts(zs_scr[...])
    gb_scr[...] = (
        dot(pick_scr[...], gx_scr[...])
        + dot_nt(z_high, small_ref[...])
        + dot_nt(z_low, small_ref[...])
    )
    gb_scr[mine, :] += keep * g_own
    gb_ref[...] = gb_scr[...].astype(BF16)
    i_high, i_low = two_parts(
        shift(gate * alpha1, at["cvec"] + layer * consts - EXPERTS - 2)
    )
    g_low = g_ref[mine, :]
    sums_out[...] = (
        (0.0 if sums_ref is None else sums_ref[...])
        + dot_tn(b_ref[...], z_high)
        + dot_tn(b_ref[...], z_low)
        + dot_tn(g_low, i_high)
        + dot_tn(g_low, i_low)
    )


def experts_backward(
    collective_id, layer, at, consts, own, g_all, w_exp, x, gu, rowpos, pos, wd, b_all, small, rows_t, mix,
    z_prev, above, cap,
):
    seq_len, width = g_all.shape
    shards_dp, count, rows, wide3 = w_exp.shape
    half = wide3 // 3
    weight_spec = pl.BlockSpec(
        (shards_dp, 1, rows, wide3), lambda e: (0, jnp.minimum(e, count - 1), 0, 0)
    )
    half_shape = (shards_dp // 2, 1, rows, wide3)
    return pl.pallas_call(
        functools.partial(experts_back_kernel, cap, layer, at, consts, own, not above),
        grid=(count + 1,),
        out_shape=[
            jax.ShapeDtypeStruct((shards_dp // 2,) + w_exp.shape[1:], BF16),
            jax.ShapeDtypeStruct((seq_len, LANES), F32),
            jax.ShapeDtypeStruct((seq_len, width), BF16),
            jax.ShapeDtypeStruct((width, LANES), F32),
            jax.ShapeDtypeStruct((LANES, LANES), F32),
        ],
        in_specs=[
            whole((seq_len, width)),
            weight_spec,
            pl.BlockSpec((1, cap, width), lambda e: (jnp.minimum(e, count - 1), 0, 0)),
            pl.BlockSpec((1, cap, 2 * half), lambda e: (jnp.minimum(e, count - 1), 0, 0)),
            pl.BlockSpec((1, 1, seq_len), lambda e: (jnp.minimum(e, count - 1), 0, 0)),
            whole((seq_len, LANES)),
            whole((seq_len, LANES)),
            whole((seq_len, width)),
            whole((width, LANES)),
            whole(rows_t.shape),
            whole((LANES, LANES)),
            whole((seq_len, LANES)),
        ]
        + [whole(item.shape) for item in above],
        out_specs=[
            pl.BlockSpec(half_shape, lambda e: (0, jnp.maximum(e - 1, 0), 0, 0)),
            whole((seq_len, LANES)),
            whole((seq_len, width)),
            whole((width, LANES)),
            whole((LANES, LANES)),
        ],
        scratch_shapes=[
            pltpu.VMEM((seq_len, count * cap), BF16),
            pltpu.VMEM((count * cap, width), BF16),
            pltpu.VMEM((count * cap, 2 * LANES), BF16),
            pltpu.VMEM((seq_len, width), F32),
            pltpu.VMEM((seq_len, LANES), F32),
            pltpu.VMEM((2, 2, shards_dp // 2, rows, wide3), BF16),
            pltpu.VMEM((count, shards_dp // 2, rows, wide3), BF16),
            pltpu.SemaphoreType.DMA((count,)),
            pltpu.SemaphoreType.DMA((count,)),
        ],
        compiler_params=pltpu.CompilerParams(
            collective_id=collective_id, has_side_effects=True, vmem_limit_bytes=VMEM_LIMIT
        ),
        cost_estimate=pl.CostEstimate(
            flops=count * (4 * cap * seq_len * width + 12 * cap * width * half),
            bytes_accessed=4 * count * width * wide3,
            transcendentals=0,
        ),
        name="experts_backward",
    )(
        g_all, w_exp, x, gu, rowpos, pos, wd, b_all, small, rows_t, mix, z_prev,
        *above,
    )


def unpack_kernel(half, *refs):
    *in_refs, up_ref, down_ref = refs
    for l, ref in enumerate(in_refs):
        values = ref[0].astype(F32)
        for part in range(2):
            up_ref[l, 0, :, part, :] = values[:, part * half : (part + 1) * half]
        down_ref[l, 0] = values[:, 2 * half :]


def unpack(items):
    count, rows, wide3 = items[0].shape
    half = wide3 // 3
    layers = len(items)
    return pl.pallas_call(
        functools.partial(unpack_kernel, half),
        grid=(count,),
        out_shape=[
            jax.ShapeDtypeStruct((layers, count, rows, 2, half), F32),
            jax.ShapeDtypeStruct((layers, count, rows, half), F32),
        ],
        in_specs=[pl.BlockSpec((1, rows, wide3), lambda e: (e, 0, 0))] * layers,
        out_specs=[
            pl.BlockSpec((layers, 1, rows, 2, half), lambda e: (0, e, 0, 0, 0)),
            pl.BlockSpec((layers, 1, rows, half), lambda e: (0, e, 0, 0)),
        ],
        compiler_params=pltpu.CompilerParams(vmem_limit_bytes=VMEM_LIMIT),
        name="unpack",
    )(*items)


def lanes(values):
    return jnp.pad(values, ((0, 0), (0, LANES - values.shape[1])))


def slot_table(route_ids):
    tokens = route_ids.shape[0]
    codes = jnp.arange(LANES, dtype=jnp.int32)
    hit = jnp.any(route_ids[:, :, None] == codes[None, None, :], axis=1)
    place = jnp.arange(tokens, dtype=jnp.int32)
    before = (place[None, :] < place[:, None]).astype(BF16)
    slots = dot(before, hit.astype(BF16)).astype(jnp.int32)
    return jnp.where(hit, slots, -1)


def shards(
    hidden_in,
    prev_logits,
    routes,
    span_starts,
    attn_norm,
    qkv_weight,
    out_weight,
    moe_norm,
    router,
    gate_mix,
    const_vec,
    const_mix,
    up_weight,
    down_weight,
    out_grad,
):
    layers = qkv_weight.shape[0]
    own, width = hidden_in.shape
    nt = lax.axis_size("tensor")
    ndp = lax.axis_size("dp")
    seq_len = own * nt
    offset = lax.axis_index("tensor") * own
    cap = seq_len // 4
    heads = qkv_weight.shape[3] // HEAD
    wide = heads * HEAD
    half = up_weight.shape[4]
    rows = qkv_weight.shape[1]
    cols = attn_norm.shape[1]
    consts = const_vec.shape[1]

    at = layout(layers, consts)
    packed = jnp.concatenate(
        [attn_norm.T, moe_norm.T]
        + [router[l] for l in range(layers)]
        + [const_vec.reshape(-1, cols).T]
        + [const_mix[l, :, :, k].T for l in range(layers) for k in range(2)],
        axis=1,
    )
    x_all, small = line_exchange("start", [hidden_in, lanes(packed)], own, width, 0)
    small = small.reshape(width, LANES)
    rows_t = small[:, :48].T.astype(F32)

    attn_w, exp_w = [], []
    for l in range(layers):
        local = jnp.concatenate(
            [qkv_weight[l].reshape(rows, 3 * wide), out_weight[l].T], axis=1
        )
        attn_w.append(lax.all_gather(local, "dp", axis=0, tiled=False).reshape(width, 4 * wide))
        local = jnp.concatenate(
            [
                up_weight[l].reshape(EXPERTS, rows, 2 * half),
                jnp.swapaxes(down_weight[l], 1, 2),
            ],
            axis=2,
        )
        exp_w.append(lax.all_gather(local, "dp", axis=0, tiled=False))

    pos = [slot_table(routes[l]) for l in range(layers)]
    rowpos = [p[:, :EXPERTS].T[:, None, :] for p in pos]

    z_prev = lanes(prev_logits)
    hidden, a_all = x_all, None
    grad_all = out_grad
    next_id = 1
    stored = []
    for l in range(layers):
        mix = jnp.pad(gate_mix[l], ((0, LANES - NEXP), (0, LANES - NEXP)))
        if l == 0:
            qkv, o, lse, partial, a_all = attend_forward(
                span_starts, x_all, attn_w[l], heads, rows_t
            )
        else:
            qkv, o, lse, partial = attend_forward(span_starts, a_all, attn_w[l], heads)
        if l == layers - 1:
            partial, grad_all = lax.optimization_barrier((partial, grad_all))
            grad_all = lax.all_gather(grad_all, "tensor", axis=0, tiled=True)
        mid, b_all = join(False, partial, [hidden], rows_t, at["moe"] + l, next_id)
        x, gu, z, wd, partial, extra = experts_forward(
            l, at, consts, b_all, exp_w[l], rowpos[l], pos[l], small, rows_t, mix, z_prev, mid, cap
        )
        stored.append(
            dict(
                hidden=hidden, a_all=a_all, qkv=qkv, o=o, lse=lse, mid=mid, b_all=b_all, x=x, gu=gu,
                wd=wd, z_prev=z_prev, mix=mix,
            )
        )
        if l + 1 < layers:
            hidden, a_all = join(
                False, partial, [extra], rows_t, at["attn"] + l + 1, next_id + 1, APART
            )
        else:
            hidden_out = lax.psum_scatter(partial, "tensor", scatter_dimension=0, tiled=True)
            extra = lax.dynamic_slice_in_dim(extra, offset, own, 0)
        z_prev = z
        next_id += 2

    above = []
    attn_grads, exp_grads = [None] * layers, [None] * layers
    gains_a, gains_m = [None] * layers, [None] * layers
    for l in reversed(range(layers)):
        s = stored[l]
        gw_exp, below, partial, sums, mixes = experts_backward(
            next_id + 2, l, at, consts, own, grad_all, exp_w[l], s["x"], s["gu"], rowpos[l],
            pos[l], s["wd"], s["b_all"], small, rows_t, s["mix"], s["z_prev"], above, cap,
        )
        above = [below, sums, mixes]
        exp_grads[l] = sum_over_pairs(gw_exp)
        if l + 1 < layers:
            partial, exp_grads[l + 1] = lax.optimization_barrier((partial, exp_grads[l + 1]))
        else:
            partial, hidden_out = lax.optimization_barrier((partial, hidden_out))
        grad_mid, gains_m[l] = join(
            True, partial, [s["mid"], grad_all], rows_t, at["moe"] + l, next_id, APART if l > 0 else 0
        )
        partial, gw_attn = attend_backward(
            span_starts, grad_mid, attn_w[l], s["a_all"], s["qkv"], s["o"], s["lse"], heads
        )
        attn_grads[l] = gw_attn.reshape(ndp, rows, 4 * wide)
        if l > 0:
            attn_grads[l] = lax.psum_scatter(attn_grads[l], "dp", scatter_dimension=0, tiled=False)
            grad_all, gains_a[l] = join(
                True, partial, [s["hidden"], grad_mid], rows_t, at["attn"] + l, next_id + 1
            )
        else:
            partial, attn_grads[1:] = lax.optimization_barrier((partial, attn_grads[1:]))
            grad, gains_a[l], attn_grads[l] = line_exchange(
                "end", [partial, hidden_in, grad_mid, rows_t, attn_grads[l]], own, width, next_id + 1
            )
        next_id += 3
    hidden_out = hidden_out.astype(F32) + extra.astype(F32)

    gains = jnp.concatenate(gains_a + gains_m, axis=0)
    sums = sums + jnp.pad(gains, ((0, LANES - 2 * layers), (0, 0))).T
    sums = jnp.concatenate(
        [
            sums.reshape(ndp * nt, cols, LANES),
            jnp.broadcast_to(mixes[None, :MIX_STEP], (ndp * nt, MIX_STEP, LANES)),
        ],
        axis=1,
    )
    attn_g, moe_g, router_g, mix_g, cvec_g, cmix_g, qkv_g, outw_g = closing(
        sums.astype(BF16), attn_grads[0], jnp.stack(attn_grads[1:]), consts, layers, cols, next_id
    )
    up_grad, down_grad = unpack(exp_grads)
    qkv_g = jnp.swapaxes(qkv_g, 1, 2)
    router_g = jnp.transpose(router_g, (1, 2, 0))
    mix_g = jnp.swapaxes(mix_g, 0, 1)
    cmix_g = jnp.swapaxes(cmix_g, 2, 3)
    down_grad = jnp.swapaxes(down_grad, 2, 3)
    return (
        hidden_out,
        grad,
        attn_g,
        qkv_g,
        outw_g,
        moe_g,
        router_g,
        mix_g,
        cvec_g,
        cmix_g,
        up_grad,
        down_grad,
    )


def sum_over_pairs(values):
    members = lax.axis_size("dp")
    groups = [list(range(parity, members, 2)) for parity in range(2)]
    return lax.psum_scatter(
        values, "dp", scatter_dimension=0, axis_index_groups=groups, tiled=False
    )


def solution(mesh):
    return jax.shard_map(
        shards,
        mesh=mesh,
        in_specs=(
            P(("dp", "tensor"), None),
            P("dp", None),
            P(None, "dp", None),
            P("dp", None),
            P(None, ("dp", "tensor")),
            P(None, "dp", None, "tensor"),
            P(None, "tensor", "dp"),
            P(None, ("dp", "tensor")),
            P(None, ("dp", "tensor"), None),
            P(),
            P(None, None, ("dp", "tensor")),
            P(None, None, ("dp", "tensor"), None),
            P(None, None, "dp", None, "tensor"),
            P(None, None, "tensor", "dp"),
            P(("dp", "tensor"), None),
        ),
        out_specs=(
            P(("dp", "tensor"), None),
            P(("dp", "tensor"), None),
            P(None, ("dp", "tensor")),
            P(None, "dp", None, "tensor"),
            P(None, "tensor", "dp"),
            P(None, ("dp", "tensor")),
            P(None, ("dp", "tensor"), None),
            P(),
            P(None, None, ("dp", "tensor")),
            P(None, None, ("dp", "tensor"), None),
            P(None, None, "dp", None, "tensor"),
            P(None, None, "tensor", "dp"),
        ),
        check_vma=False,
    )
```
